32 devices in a mesh: groups: 2 (over y), span: 4 (over z), head: 2 (over x), slab: 2 (over core).
Axes of the slice: x: 2, y: 2, z: 4, core: 2. Of those that a mesh axis runs over, the one named last changes fastest.
Arguments:
- queries: bfloat16 [3072, 5120], P(('groups', 'span'), 'head'), parts along dimension 0, may hold values from -6 to 6
- keys: bfloat16 [3072, 5120], P(('groups', 'span', 'slab'), 'head'), parts along dimension 0, may hold values from -4 to 4
- values: bfloat16 [3072, 5120], P(('groups', 'span', 'slab'), 'head'), parts along dimension 0, may hold values from -240 to 240
- span_mask: int32 [8, 4], P('groups'), parts along dimension 0, may hold values from 0 to 1, as said below
- head_gain: float32 [5120], P('head'), may hold values from 0.5 to 2
- head_shift: float32 [5120], P('head'), may hold values from -3 to 3
- patch_weight: bfloat16 [5120, 64], P('head'), may hold values from -0.078125 to 0.078125
- noisy_latent: float32 [24, 16, 32, 16], P(('groups', 'span'), 'head', 'slab'), parts along dimension 0, may hold values from -6 to 6
- conv_weight: bfloat16 [432, 384], replicated, may hold values from -0.3125 to 0.3125
- conv_bias: float32 [384], replicated, may hold values from -3 to 3
Outputs:
- clean_latent: float32 [24, 16, 32, 16], P(('groups', 'span'), 'head', 'slab'), parts along dimension 0
- decoded: bfloat16 [24, 16, 32, 384], P(('groups', 'span'), 'head', 'slab'), parts along dimension 0
The draws below stay inside these ranges and needn't reach their ends.
There are 2 independent parts, one for each index of `groups`. The reference program is written for one: setup_inputs(seed, part) draws one part's arguments, and reference() takes and returns one part's arrays. A program takes and returns all parts, laid end to end along the dimension named above; an argument that names none is the same for every part. Nothing has to cross between parts.
Inputs may be any that keep to these rules, and one draw needn't show every extreme that they name: span_mask[i, j] is 1 where j = i and 0 where j > i.
All inputs are finite; a program needn't handle non-finite values.
Results may differ from the reference program's by a relative error of at most 0.012.
Values may be sent and summed in bfloat16 or wider, within the bound.
No kernel may reach another device: no remote copies, remote signals or barrier semaphores. Data moves between devices by JAX's collectives and lax.ppermute only.
A program may use at most 128 MiB of HBM per device.

```python
import math
import jax
import jax.numpy as jnp
from jax import lax

HEADS = 40
HD = 128
LAT_CH = 16
DEC_CH = 384
FRAMES_SPAN = 3
TROWS = 8
TCOLS = 16
SPANS = 4
TOKENS = 1536
FRAMES = 12
HL = 16
WL = 32


def query_key_pair(key):
    total_rows = SPANS * FRAMES_SPAN * TROWS * TCOLS
    feature_width = HEADS * HD
    query_key = jax.random.fold_in(key, 11)
    keys_key = jax.random.fold_in(key, 12)
    query_out = jnp.clip(jax.random.normal(query_key, (total_rows, feature_width), jnp.float32), -4.0, 4.0)
    key_out = jnp.clip(jax.random.normal(keys_key, (total_rows, feature_width), jnp.float32), -4.0, 4.0)
    return (query_out, key_out)


def draw_queries(key, part):
    return query_key_pair(key)[0].astype(jnp.bfloat16)


def draw_keys(key, part):
    return query_key_pair(key)[1].astype(jnp.bfloat16)


def draw_values(key, part):
    total_rows = SPANS * FRAMES_SPAN * TROWS * TCOLS
    feature_width = HEADS * HD
    noise_key = jax.random.fold_in(key, 21)
    level_key = jax.random.fold_in(key, 22)
    column = jnp.arange(feature_width, dtype=jnp.int32)
    ramp = 1.0 + 2.0 * (column // HD).astype(jnp.float32) / max(HEADS - 1, 1)
    level = 10.0 ** jax.random.uniform(level_key, (feature_width,), jnp.float32, 0.0, 1.0)
    noise = jnp.clip(jax.random.normal(noise_key, (total_rows, feature_width), jnp.float32), -4.0, 4.0)
    drawn = noise * (level * ramp)[None, :]
    return drawn.astype(jnp.bfloat16)


def draw_span_mask(key, part):
    coins = jax.random.randint(jax.random.fold_in(key, 31), (SPANS, SPANS), 0, 4)
    row_number = jnp.arange(SPANS, dtype=jnp.int32)[:, None]
    col_number = jnp.arange(SPANS, dtype=jnp.int32)[None, :]
    earlier = jnp.logical_and(col_number < row_number, coins > 0)
    return jnp.where(jnp.logical_or(col_number == row_number, earlier), 1, 0).astype(jnp.int32)


def level_of(own_key, extent, cuts, low, top_value):
    level, own = 1.0, jax.random.fold_in(own_key, 6)
    for dim, shards_of in cuts:
        heights = jnp.exp(jax.random.uniform(jax.random.fold_in(own, dim), (shards_of,), jnp.float32, low / len(cuts), top_value / len(cuts)))
        level = level * jnp.repeat(heights, extent[dim] // shards_of).reshape([-1 if axis == dim else 1 for axis in range(len(extent))])
    return level


def gaussian(rng, dims, width, limit, shards=(), kind=jnp.bfloat16):
    loudness = level_of(rng, dims, shards, -0.22, 0.18) if shards else 1.0
    values = jax.random.normal(rng, dims, jnp.float32) * width * loudness
    return jnp.minimum(jnp.maximum(values, -limit), limit).astype(kind)


def setup_inputs(seed: int = 0, part: int = 0) -> dict:
    key_of = jax.random.split(jax.random.key(seed), 11)
    own_keys = jax.random.split(jax.random.fold_in(key_of[10], part), 11)
    queries = draw_queries(jax.random.fold_in(jax.random.fold_in(key_of[10], part), 71), part)
    keys = draw_keys(jax.random.fold_in(jax.random.fold_in(key_of[10], part), 71), part)
    values = draw_values(jax.random.fold_in(jax.random.fold_in(key_of[10], part), 71), part)
    span_mask = draw_span_mask(jax.random.fold_in(jax.random.fold_in(key_of[10], part), 71), part)
    head_gain = jnp.clip(jnp.exp(math.log(2.0) - 1.3862944 * jax.random.uniform(key_of[4], (HEADS * HD,), jnp.float32) ** level_of(key_of[4], (HEADS * HD,), ((0, 2),), -0.2, 0.2)), 0.5, 2.0)
    head_shift = gaussian(key_of[5], (HEADS * HD,), 0.5, 3.0, ((0, 2),), jnp.float32)
    patch_weight = gaussian(key_of[6], (HEADS * HD, 4 * LAT_CH), (HEADS * HD) ** -0.5, 0.078125, ((0, 2),))
    noisy_latent = gaussian(own_keys[7], (FRAMES, HL, WL, LAT_CH), 1.0, 6.0, ((0, 4), (1, 2), (2, 2)), jnp.float32)
    conv_weight = gaussian(key_of[8], (27 * LAT_CH, DEC_CH), (27 * LAT_CH) ** -0.5, 0.3125)
    conv_bias = gaussian(key_of[9], (DEC_CH,), 0.5, 3.0, (), jnp.float32)
    return {"queries": queries, "keys": keys, "values": values, "span_mask": span_mask, "head_gain": head_gain, "head_shift": head_shift, "patch_weight": patch_weight, "noisy_latent": noisy_latent, "conv_weight": conv_weight, "conv_bias": conv_bias}


neg_big = -1e+30
noise_level = 0.75
norm_eps = 1e-06

def reference(queries, keys, values, span_mask, head_gain, head_shift, patch_weight, noisy_latent, conv_weight, conv_bias):
    tok_span = FRAMES_SPAN * TROWS * TCOLS
    feature_width = HEADS * HD
    score_scale = 1.0 / math.sqrt(HD)
    query_heads = queries.reshape(TOKENS, HEADS, HD).transpose(1, 0, 2)
    key_heads = keys.reshape(TOKENS, HEADS, HD).transpose(1, 0, 2)
    value_heads = values.reshape(TOKENS, HEADS, HD).transpose(1, 0, 2)
    outputs = []
    for span_number in range(SPANS):
        key_limit = (span_number + 1) * tok_span
        key_span = (jnp.arange(key_limit, dtype=jnp.int32) // tok_span).astype(jnp.int32)
        allowed = span_mask[span_number][key_span] > 0

        def one_head(operands):
            query_one, key_one, value_one = operands
            scores = jnp.dot(query_one, key_one.T, preferred_element_type=jnp.float32) * score_scale
            scores = jnp.where(allowed[None, :], scores, neg_big)
            row_max = lax.optimization_barrier(jnp.max(scores, axis=1, keepdims=True))
            weights = jnp.where(allowed[None, :], jnp.exp(scores - row_max), 0.0)
            numerator = jnp.dot(weights.astype(jnp.bfloat16), value_one, preferred_element_type=jnp.float32)
            return (numerator / lax.optimization_barrier(jnp.sum(weights, axis=1, keepdims=True))).astype(jnp.bfloat16)
        result = lax.map(one_head, (query_heads[:, span_number * tok_span:key_limit], key_heads[:, :key_limit], value_heads[:, :key_limit]))
        outputs.append(result)
    attended = jnp.concatenate(outputs, axis=1).transpose(1, 0, 2).reshape(TOKENS, feature_width)
    values32 = attended.astype(jnp.float32)
    row_mean = lax.optimization_barrier(jnp.sum(values32, axis=1)) / feature_width
    spread = lax.optimization_barrier(jnp.sum(values32 * values32, axis=1)) / feature_width - row_mean * row_mean
    normed = ((values32 - row_mean[:, None]) * lax.rsqrt(spread + norm_eps)[:, None] * head_gain[None, :] + head_shift[None, :]).astype(jnp.bfloat16)
    velocity = jnp.dot(normed, patch_weight, preferred_element_type=jnp.float32)
    frames = SPANS * FRAMES_SPAN
    height = 2 * TROWS
    breadth = 2 * TCOLS
    patch_cells = velocity.reshape(SPANS, FRAMES_SPAN, TROWS, TCOLS, 2, 2, LAT_CH).transpose(0, 1, 2, 4, 3, 5, 6).reshape(frames, height, breadth, LAT_CH)
    clean_latent = noisy_latent - noise_level * patch_cells
    latent_input = clean_latent.astype(jnp.bfloat16)
    padded = jnp.pad(latent_input, ((2, 0), (1, 1), (1, 1), (0, 0)))
    columns = jnp.concatenate([padded[frame_tap:frame_tap + frames, row_tap:row_tap + height, col_tap:col_tap + breadth, :] for frame_tap in range(3) for row_tap in range(3) for col_tap in range(3)], axis=-1)
    decoded = jnp.dot(columns.reshape(frames * height * breadth, 27 * LAT_CH), conv_weight, preferred_element_type=jnp.float32) + conv_bias[None, :]
    decoded = decoded.astype(jnp.bfloat16).reshape(frames, height, breadth, DEC_CH)
    return (clean_latent, decoded)
```

```python
import functools
import math

import jax
import jax.numpy as jnp
import numpy as np
from jax import lax
from jax.experimental import pallas as pl
from jax.experimental.pallas import tpu as pltpu
from jax.sharding import PartitionSpec as P

HEADS = 40
HD = 128
LAT_CH = 16
FRAMES_SPAN = 3
TROWS = 8
TCOLS = 16


neg_big = -1e30
noise_level = 0.75
norm_eps = 1e-06


def with_halo(cells, sides, width):
    for axis, dim in sides:
        count = lax.axis_size(axis)
        ends = count - 1
        head = lax.slice_in_dim(cells, 0, width, axis=dim)
        tail = lax.slice_in_dim(cells, cells.shape[dim] - width, cells.shape[dim], axis=dim)
        cells = jnp.concatenate(
            [
                lax.ppermute(tail, axis, [(i, (i + 1) % count) for i in range(ends)]),
                cells,
                lax.ppermute(head, axis, [((i + 1) % count, i) for i in range(ends)]),
            ],
            axis=dim,
        )
    return cells


def from_behind(value, axis, by):
    size = lax.axis_size(axis)
    pairs = [(i, i + by) for i in range(size) if 0 <= i + by < size]
    return lax.ppermute(value, axis, pairs)


def block_length(total_rows):
    block_size = total_rows
    while block_size > 768 and block_size % 2 == 0:
        block_size = block_size // 2
    return block_size


def fold_keys(partial_state, key_value, query_block, mask_row, rows_span):
    keys_piece, values_piece = key_value
    heads_dev = query_block.shape[1]
    piece_rows = keys_piece.shape[0]
    length = block_length(piece_rows)
    span_count = mask_row.shape[0]
    score_scale = 1.0 / math.sqrt(HD)
    span_ids = jnp.arange(span_count, dtype=jnp.int32)

    def one_block(carry_state, block_index):
        running_max, running_sum, weighted = carry_state
        offset = block_index * length
        key_block = lax.dynamic_slice_in_dim(keys_piece, offset, length, 0).reshape(
            length, heads_dev, HD
        )
        value_block = lax.dynamic_slice_in_dim(values_piece, offset, length, 0).reshape(
            length, heads_dev, HD
        )
        key_span = (offset + jnp.arange(length, dtype=jnp.int32)) // rows_span
        allowed = (
            jnp.sum(jnp.where(key_span[:, None] == span_ids[None, :], mask_row[None, :], 0), axis=1)
            > 0
        )
        scores = (
            jnp.einsum("qhd,khd->hqk", query_block, key_block, preferred_element_type=jnp.float32)
            * score_scale
        )
        scores = jnp.where(allowed[None, None, :], scores, neg_big)
        new_max = jnp.maximum(running_max, jnp.max(scores, axis=2))
        weights = jnp.where(allowed[None, None, :], jnp.exp(scores - new_max[:, :, None]), 0.0)
        factor = jnp.exp(running_max - new_max)
        running_sum = running_sum * factor + jnp.sum(weights, axis=2)
        weighted = weighted * factor.T[:, :, None] + jnp.einsum(
            "hqk,khd->qhd",
            weights.astype(jnp.bfloat16),
            value_block,
            preferred_element_type=jnp.float32,
        )
        return ((new_max, running_sum, weighted), None)

    result, unused = lax.scan(
        one_block, partial_state, jnp.arange(piece_rows // length, dtype=jnp.int32)
    )
    return result


def gathered_plan(
    queries,
    keys,
    values,
    span_mask,
    head_gain,
    head_shift,
    patch_weight,
    noisy_latent,
    conv_weight,
    conv_bias,
):
    heads_dev = queries.shape[1] // HD
    slab_count = lax.axis_size("slab")
    col_dev = TCOLS // slab_count
    slab_place = lax.axis_index("slab")
    span_place = lax.axis_index("span")
    mask_row = lax.dynamic_slice_in_dim(span_mask, span_place, 1, 0)[0]
    token_grid = queries.reshape(FRAMES_SPAN, TROWS, TCOLS, queries.shape[-1])
    picked = lax.dynamic_slice_in_dim(token_grid, slab_place * col_dev, col_dev, 2)
    own_queries = picked.reshape(FRAMES_SPAN * TROWS * col_dev, queries.shape[-1]).reshape(
        -1, heads_dev, HD
    )
    query_rows = own_queries.shape[0]
    rows_span = keys.shape[0] * slab_count
    running_max, running_sum, weighted = fold_keys(
        (
            jnp.full((heads_dev, query_rows), neg_big, jnp.float32),
            jnp.zeros((heads_dev, query_rows), jnp.float32),
            jnp.zeros((query_rows, heads_dev, HD), jnp.float32),
        ),
        (
            lax.all_gather(keys, ("span", "slab"), axis=0, tiled=True),
            lax.all_gather(values, ("span", "slab"), axis=0, tiled=True),
        ),
        own_queries,
        mask_row,
        rows_span,
    )
    attended = (
        (weighted / running_sum.T[:, :, None])
        .astype(jnp.bfloat16)
        .reshape(query_rows, heads_dev * HD)
    )
    feature_width = HEADS * HD
    values32 = attended.astype(jnp.float32)
    row_total = jnp.sum(values32, axis=1)
    row_squares = jnp.sum(values32 * values32, axis=1)
    row_total, row_squares = lax.psum((row_total, row_squares), "head")
    row_mean = row_total / feature_width
    spread = row_squares / feature_width - row_mean * row_mean
    normed = (
        (values32 - row_mean[:, None]) * lax.rsqrt(spread + norm_eps)[:, None] * head_gain[None, :]
        + head_shift[None, :]
    ).astype(jnp.bfloat16)
    normed_grid = normed.reshape(FRAMES_SPAN, TROWS, col_dev, normed.shape[-1])
    own_rows = TROWS // lax.axis_size("head")
    picked = normed_grid
    product = jnp.dot(
        picked.reshape(-1, picked.shape[-1]), patch_weight, preferred_element_type=jnp.float32
    )
    velocity = lax.psum_scatter(
        product.reshape(
            FRAMES_SPAN, own_rows * lax.axis_size("head"), col_dev * patch_weight.shape[1]
        )
        .transpose(1, 0, 2)
        .reshape(own_rows * lax.axis_size("head"), -1)
        .astype(jnp.bfloat16),
        "head",
        scatter_dimension=0,
        tiled=True,
    ).astype(jnp.float32)
    rows_dev = velocity.shape[0]
    patch_cells = (
        velocity.reshape(rows_dev, FRAMES_SPAN, col_dev, 2, 2, LAT_CH)
        .transpose(1, 0, 3, 2, 4, 5)
        .reshape(FRAMES_SPAN, 2 * rows_dev, 2 * col_dev, LAT_CH)
    )
    clean_latent = noisy_latent - noise_level * patch_cells
    latent_input = clean_latent.astype(jnp.bfloat16)
    framed = with_halo(latent_input, (("head", 1), ("slab", 2)), 1)
    earlier = from_behind(framed[FRAMES_SPAN - 2 :], "span", 1)
    stacked = jnp.concatenate([earlier, framed], axis=0)
    height = clean_latent.shape[1]
    breadth = clean_latent.shape[2]
    columns = jnp.concatenate(
        [
            stacked[
                frame_tap : frame_tap + FRAMES_SPAN,
                row_tap : row_tap + height,
                col_tap : col_tap + breadth,
                :,
            ]
            for frame_tap in range(3)
            for row_tap in range(3)
            for col_tap in range(3)
        ],
        axis=-1,
    )
    decoded = (
        jnp.dot(
            columns.reshape(FRAMES_SPAN * height * breadth, 27 * LAT_CH),
            conv_weight,
            preferred_element_type=jnp.float32,
        )
        + conv_bias[None, :]
    )
    decoded = decoded.astype(jnp.bfloat16).reshape(
        FRAMES_SPAN, height, breadth, conv_weight.shape[1]
    )
    return (clean_latent, decoded)


NEAR_HEADS = 4
MIDDLE_HEADS = 4
FAR_HEADS = 2
EARLY = 3
STAT_ROWS = 8
SLOTS = 3
ABSENT = -1


def plan_fits(heads_dev, span_count, slab_count, head_count):
    return (
        span_count == 4
        and slab_count == 2
        and head_count == 2
        and heads_dev == slab_count * (NEAR_HEADS + MIDDLE_HEADS + FAR_HEADS)
    )


def attend_kernel(plan, meta, mask, *refs):
    (query_own, key_own, value_own, received, weight, gain, sums_in), rest = refs[:7], refs[7:]
    payloads, (sums_out, score, peak, folded, squares) = rest[:-5], rest[-5:]
    query_sources, key_sources, slots, span_count = plan
    rows = query_own.shape[0]
    step = pl.program_id(0)
    base = 2
    to_exp2 = math.log2(math.e) / math.sqrt(HD)

    def key_of(source):
        if source is None:
            return jnp.concatenate([key_own[...], received[: rows // 2]], axis=0)
        ref, start = payloads[source[0]], source[1]
        return ref[start : start + rows]

    def value_of(source):
        if source is None:
            return jnp.concatenate([value_own[...], received[rows // 2 :]], axis=0)
        ref, start = payloads[source[0]], source[1] + rows
        return ref[start : start + rows]

    def allowed(query_index, key_index):
        query_span = meta[base + query_index]
        key_span = meta[base + len(query_sources) + key_index]
        entry = mask[jnp.maximum(query_span, 0) * span_count + jnp.maximum(key_span, 0)]
        return (query_span >= 0) & (key_span >= 0) & (key_span <= query_span) & (entry > 0)

    @pl.when(step == 0)
    def _():
        folded[...] = jnp.zeros_like(folded)
        squares[...] = jnp.zeros_like(squares)
        sums_out[...] = sums_in[...]

    scaled = weight[...].astype(jnp.float32) * gain[...]
    high = scaled.astype(jnp.bfloat16)
    low = (scaled - high.astype(jnp.float32)).astype(jnp.bfloat16)
    projector = jnp.concatenate([high, low, jnp.ones((16, HD), jnp.bfloat16)], axis=0)
    ones_block = jnp.ones((rows, HD), jnp.bfloat16)

    def one_query(query_index, source):
        @pl.when(meta[base + query_index] >= 0)
        def _():
            if source is None:
                query = query_own[...]
            else:
                query = payloads[source[0]][source[1] : source[1] + rows]
            peak[...] = jnp.full_like(peak, neg_big)
            for key_index, key_source in enumerate(key_sources):

                @pl.when(allowed(query_index, key_index))
                def _():
                    block = lax.dot_general(
                        query,
                        key_of(key_source),
                        (((1,), (1,)), ((), ())),
                        preferred_element_type=jnp.float32,
                    )
                    score[key_index] = block
                    best = peak[...]
                    for lane in range(0, rows, HD):
                        best = jnp.maximum(best, block[:, lane : lane + HD])
                    peak[...] = best

            top = jnp.max(peak[...], axis=1, keepdims=True)
            peak[...] = jnp.broadcast_to(top, peak.shape)
            gathered = score.at[len(key_sources)]
            gathered[:, : 2 * HD] = jnp.zeros((rows, 2 * HD), jnp.float32)
            for key_index, key_source in enumerate(key_sources):

                @pl.when(allowed(query_index, key_index))
                def _():
                    shift = peak[...]
                    block = jnp.concatenate(
                        [
                            jnp.exp2((score[key_index, :, lane : lane + HD] - shift) * to_exp2)
                            for lane in range(0, rows, HD)
                        ],
                        axis=1,
                    ).astype(jnp.bfloat16)
                    gathered[:, : 2 * HD] += jnp.dot(
                        block,
                        jnp.concatenate([value_of(key_source), ones_block], axis=1),
                        preferred_element_type=jnp.float32,
                    )

            attended = (gathered[:, :HD] / gathered[:, HD : 2 * HD]).astype(jnp.bfloat16)
            folded[query_index] += lax.dot_general(
                projector, attended, (((1,), (1,)), ((), ())), preferred_element_type=jnp.float32
            )
            wide = attended.astype(jnp.float32)
            squares[query_index] += wide * wide

    for query_index, source in enumerate(query_sources):
        one_query(query_index, source)

    @pl.when(step == pl.num_programs(0) - 1)
    def _():
        ones_rows = jnp.ones((STAT_ROWS, HD), jnp.bfloat16)
        patch = weight.shape[0]
        for query_index, slot in enumerate(slots):
            rest_of = squares[query_index]
            total = jnp.zeros((STAT_ROWS, rows), jnp.float32)
            for _ in range(3):
                piece = rest_of.astype(jnp.bfloat16)
                rest_of = rest_of - piece.astype(jnp.float32)
                total = total + lax.dot_general(
                    ones_rows, piece, (((1,), (1,)), ((), ())), preferred_element_type=jnp.float32
                )
            done = folded[query_index]
            sums_out[slot, :patch] += done[:patch] + done[patch : 2 * patch]
            sums_out[slot, patch : patch + STAT_ROWS] += done[
                2 * patch : 2 * patch + STAT_ROWS
            ]
            sums_out[slot, patch + STAT_ROWS :] += total


def attend(
    heads, meta, mask, own, sums, payloads, query_sources, key_sources, slots, span_count, name
):
    queries, keys, values, received, weight, gain = own
    rows = queries.shape[0]
    patch = weight.shape[0]
    column = lambda height, entry: pl.BlockSpec(
        (height, HD), lambda i, meta, mask: (0, meta[entry] + i)
    )
    sums_spec = pl.BlockSpec(sums.shape, lambda i, meta, mask: (0, 0, 0))
    plan = (query_sources, key_sources, slots, span_count)
    pairs = heads * len(query_sources) * len(key_sources)
    return pl.pallas_call(
        functools.partial(attend_kernel, plan),
        name=name,
        out_shape=jax.ShapeDtypeStruct(sums.shape, sums.dtype),
        grid_spec=pltpu.PrefetchScalarGridSpec(
            num_scalar_prefetch=2,
            grid=(heads,),
            in_specs=[
                column(rows, 0),
                column(rows // 2, 0),
                column(rows // 2, 0),
                column(rows, 1),
                column(patch, 0),
                column(1, 0),
                sums_spec,
            ]
            + [
                pl.BlockSpec((payload.shape[0], HD), lambda i, meta, mask: (0, i))
                for payload in payloads
            ],
            out_specs=sums_spec,
            scratch_shapes=[
                pltpu.VMEM((len(key_sources) + 1, rows, rows), jnp.float32),
                pltpu.VMEM((rows, HD), jnp.float32),
                pltpu.VMEM((len(query_sources), 2 * patch + 16, rows), jnp.float32),
                pltpu.VMEM((len(query_sources), rows, HD), jnp.float32),
            ],
        ),
        compiler_params=pltpu.CompilerParams(vmem_limit_bytes=40 << 20),
        cost_estimate=pl.CostEstimate(
            flops=pairs * 4 * rows * rows * HD,
            bytes_accessed=(heads * HD * 2 * (3 * rows + sum(p.shape[0] for p in payloads))),
            transcendentals=pairs * rows * rows,
        ),
    )(meta, mask, queries, keys, values, received, weight, gain, sums, *payloads)


def meta_table(span_count, first, spans_of):
    return np.array(
        [[first[place], first[place]] + spans_of(place) for place in range(span_count)], np.int32
    )


def token_sums(queries, keys, values, span_mask, head_gain, patch_weight):
    span_count = lax.axis_size("span")
    slab_count = lax.axis_size("slab")
    place = lax.axis_index("span")
    slab = lax.axis_index("slab")
    heads = queries.shape[1] // HD // slab_count
    width = heads * HD
    rows = queries.shape[0]
    first_own = slab * heads
    swap = [(0, 1), (1, 0)]

    def pick(array, head, count):
        return lax.dynamic_slice_in_dim(array, head * HD, count * HD, 1)

    def pick_queries(head, count):
        return pick(queries, first_own + head, count)

    handed = jnp.concatenate(
        [
            lax.dynamic_slice_in_dim(array, (1 - slab) * width, width, 1)
            for array in (keys, values)
        ],
        axis=0,
    )
    received = lax.ppermute(handed, "slab", swap)
    half = rows // 2

    def pick_pair(head, count):
        return [
            pick(keys, first_own + head, count),
            pick(received[:half], head, count),
            pick(values, first_own + head, count),
            pick(received[half:], head, count),
        ]

    near, middle, far = 0, NEAR_HEADS, NEAR_HEADS + MIDDLE_HEADS
    late = NEAR_HEADS - EARLY

    def at(*choices):
        return jnp.array(choices, jnp.int32)[place]

    send = lambda value, *pairs: lax.ppermute(value, "span", list(pairs))
    rows_of = lambda parts: jnp.concatenate(parts, axis=0)

    down_start = at(near, middle, near, middle)
    up_start = at(near, middle, near, near)
    query_down = send(pick_queries(down_start, EARLY), (1, 0), (2, 1), (3, 2))
    query_down_two = send(pick_queries(near, EARLY), (3, 1))
    pair_up = send(rows_of(pick_pair(up_start, EARLY)), (0, 1), (1, 2))
    pair_down = send(rows_of(pick_pair(down_start, EARLY)), (1, 0), (2, 1), (3, 2))
    pair_up_two = send(rows_of(pick_pair(middle, EARLY)), (0, 2))
    pair_down_two = send(rows_of(pick_pair(near, EARLY)), (3, 1))
    far_pair = rows_of(pick_pair(far, FAR_HEADS))
    far_all = rows_of([pick_queries(far, FAR_HEADS), far_pair])
    far_next = send(far_all, (2, 3), (1, 0))
    far_two = send(far_pair, (1, 3))
    far_three = send(far_pair, (0, 3))
    late_down = send(
        rows_of([pick_queries(down_start + EARLY, late)] + pick_pair(down_start + EARLY, late)),
        (1, 0),
        (2, 1),
        (3, 2),
    )
    late_up = send(rows_of(pick_pair(up_start + EARLY, late)), (0, 1), (1, 2))
    late_up_two = send(rows_of(pick_pair(middle + EARLY, late)), (0, 2))
    late_down_two = send(
        rows_of([pick_queries(near + EARLY, late)] + pick_pair(near + EARLY, late)), (3, 1)
    )

    def main_spans(p):
        reach = lambda q: q if 0 <= q < span_count else ABSENT
        query = [p if p in (1, 2) else ABSENT, p + 1 if p < 3 else ABSENT, 3 if p == 1 else ABSENT]
        return query + [p] + [reach(p + d) for d in (-1, -2, 1, 2)]

    def far_spans(p):
        query = [3 if p == 3 else ABSENT, 1 if p == 0 else ABSENT, 2 if p == 3 else ABSENT]
        near_span = {0: 1, 3: 2}.get(p, ABSENT)
        return query + [p, near_span, 1 if p == 3 else ABSENT, 0 if p == 3 else ABSENT]

    main_first = (middle, near, middle, near)

    def meta(first, spans_of):
        row = jnp.array(meta_table(span_count, first, spans_of))[place]
        return row + jnp.where(jnp.arange(row.shape[0]) == 0, first_own, 0)

    mask = span_mask.reshape(-1)
    weight = patch_weight.T
    own = (queries, keys, values, received, weight, head_gain[None, :])
    patch = weight.shape[0]
    sums = jnp.zeros((SLOTS, patch + 2 * STAT_ROWS, rows), jnp.float32)
    run = functools.partial(attend, mask=mask, own=own, span_count=span_count)
    sums = run(
        heads,
        meta((0,) * span_count, lambda p: [0 if p == 0 else ABSENT, p]),
        sums=sums,
        payloads=[],
        query_sources=(None,),
        key_sources=(None,),
        slots=(0,),
        name="first_span",
    )
    sums = run(
        FAR_HEADS,
        meta((far,) * span_count, far_spans),
        sums=sums,
        payloads=[far_next, far_two, far_three],
        query_sources=(None, (0, 0), (0, 0)),
        key_sources=(None, (0, rows), (1, 0), (2, 0)),
        slots=(0, 1, 2),
        name="far_heads",
    )
    sums = run(
        EARLY,
        meta(main_first, main_spans),
        sums=sums,
        payloads=[query_down, query_down_two, pair_up, pair_up_two, pair_down, pair_down_two],
        query_sources=(None, (0, 0), (1, 0)),
        key_sources=(None, (2, 0), (3, 0), (4, 0), (5, 0)),
        slots=(0, 1, 2),
        name="early_heads",
    )
    sums = run(
        late,
        meta(tuple(f + EARLY for f in main_first), main_spans),
        sums=sums,
        payloads=[late_down, late_down_two, late_up, late_up_two],
        query_sources=(None, (0, 0), (1, 0)),
        key_sources=(None, (2, 0), (3, 0), (0, rows), (1, rows)),
        slots=(0, 1, 2),
        name="late_heads",
    )
    return sums


def gather_noise(noisy_latent, swap):
    frames, height, breadth, channels = noisy_latent.shape
    earlier = from_behind(noisy_latent[frames - 2 :].reshape(2, -1), "span", 1)
    grid = jnp.concatenate([earlier, noisy_latent.reshape(frames, -1)], axis=0)
    slab = lax.axis_index("slab")
    head = lax.axis_index("head")
    other = lax.ppermute(grid, "slab", swap)
    grid = grid.reshape(frames + 2, height, breadth * channels)
    other = other.reshape(grid.shape)
    grid = jnp.where(
        slab == 0,
        jnp.concatenate([grid, other], axis=2),
        jnp.concatenate([other, grid], axis=2),
    )
    other = lax.ppermute(grid, "head", swap)
    grid = jnp.where(
        head == 0,
        jnp.concatenate([grid, other], axis=1),
        jnp.concatenate([other, grid], axis=1),
    )
    return grid.reshape(frames + 2, 2 * height, 2 * breadth, channels)


def per_device(
    queries,
    keys,
    values,
    span_mask,
    head_gain,
    head_shift,
    patch_weight,
    noisy_latent,
    conv_weight,
    conv_bias,
):
    heads_dev = queries.shape[1] // HD
    if not plan_fits(
        heads_dev, lax.axis_size("span"), lax.axis_size("slab"), lax.axis_size("head")
    ):
        return gathered_plan(
            queries,
            keys,
            values,
            span_mask,
            head_gain,
            head_shift,
            patch_weight,
            noisy_latent,
            conv_weight,
            conv_bias,
        )
    place = lax.axis_index("span")
    slab = lax.axis_index("slab")
    head = lax.axis_index("head")
    swap = [(0, 1), (1, 0)]
    noise = gather_noise(noisy_latent, swap)
    wide_weight = patch_weight.astype(jnp.float32)
    constants = jnp.stack(
        [
            jnp.sum(wide_weight * head_gain[:, None], axis=0),
            jnp.sum(wide_weight * head_shift[:, None], axis=0),
        ]
    )
    constants = constants + lax.ppermute(constants, "head", swap)

    sums = token_sums(queries, keys, values, span_mask, head_gain, patch_weight)
    half = sums.shape[1] // 2
    mine = lax.dynamic_slice_in_dim(sums, slab * half, half, 1)
    theirs = lax.dynamic_slice_in_dim(sums, (1 - slab) * half, half, 1)
    mine = mine + lax.ppermute(theirs, "slab", swap)
    mine = mine + lax.ppermute(mine, "head", swap)
    own, after, third = mine[0], mine[1], mine[2]
    from_one = lax.ppermute(jnp.stack([after, own]), "span", [(0, 1), (1, 2), (2, 3)])
    from_two = lax.ppermute(jnp.stack([third, after]), "span", [(0, 2), (1, 3)])
    from_next = lax.ppermute(third, "span", [(3, 2)])
    current = own + from_one[0] + from_two[0] + from_next
    before = from_one[1] + from_two[1] + jnp.where(place == 3, third, 0.0)
    both = jnp.stack([before, current])
    other = lax.ppermute(both, "slab", swap)
    both = jnp.where(
        slab == 0,
        jnp.concatenate([both, other], axis=1),
        jnp.concatenate([other, both], axis=1),
    )

    patch = patch_weight.shape[1]
    feature_width = HEADS * HD
    row_mean = both[:, patch] / feature_width
    spread = both[:, patch + STAT_ROWS] / feature_width - row_mean * row_mean
    velocity = (
        lax.rsqrt(spread + norm_eps)[:, None, :]
        * (both[:, :patch] - row_mean[:, None, :] * constants[0][None, :, None])
        + constants[1][None, :, None]
    )
    cells = (
        velocity.reshape(2, 2, 2, LAT_CH, FRAMES_SPAN, TROWS, TCOLS)
        .transpose(0, 4, 5, 1, 6, 2, 3)
        .reshape(2, FRAMES_SPAN, 2 * TROWS, 2 * TCOLS, LAT_CH)
    )
    cells = jnp.concatenate([cells[0, FRAMES_SPAN - 2 :], cells[1]], axis=0)
    latent = noise - noise_level * cells
    frames, height, breadth, channels = noisy_latent.shape
    clean_latent = lax.dynamic_slice(
        latent,
        (2, head * height, slab * breadth, 0),
        (frames, height, breadth, channels),
    )
    latent_input = latent.astype(jnp.bfloat16)
    present = (jnp.arange(frames + 2) >= 2) | (place > 0)
    latent_input = jnp.where(present[:, None, None, None], latent_input, 0)
    padded = jnp.pad(latent_input, ((0, 0), (1, 1), (1, 1), (0, 0)))
    stacked = lax.dynamic_slice(
        padded,
        (0, head * height, slab * breadth, 0),
        (frames + 2, height + 2, breadth + 2, channels),
    )
    columns = jnp.concatenate(
        [
            stacked[
                frame_tap : frame_tap + FRAMES_SPAN,
                row_tap : row_tap + height,
                col_tap : col_tap + breadth,
                :,
            ]
            for frame_tap in range(3)
            for row_tap in range(3)
            for col_tap in range(3)
        ],
        axis=-1,
    )
    decoded = (
        jnp.dot(
            columns.reshape(FRAMES_SPAN * height * breadth, 27 * LAT_CH),
            conv_weight,
            preferred_element_type=jnp.float32,
        )
        + conv_bias[None, :]
    )
    decoded = decoded.astype(jnp.bfloat16).reshape(
        FRAMES_SPAN, height, breadth, conv_weight.shape[1]
    )
    return (clean_latent, decoded)


def solution(mesh):
    placed = (
        P(("groups", "span"), "head"),
        P(("groups", "span", "slab"), "head"),
        P(("groups", "span", "slab"), "head"),
        P("groups", None),
        P("head"),
        P("head"),
        P("head", None),
        P(("groups", "span"), "head", "slab", None),
        P(),
        P(),
    )
    return jax.shard_map(
        per_device,
        mesh=mesh,
        in_specs=placed,
        out_specs=(
            P(("groups", "span"), "head", "slab", None),
            P(("groups", "span"), "head", "slab", None),
        ),
        check_vma=False,
    )
```

```python
import functools
import math

import jax
import jax.numpy as jnp
import numpy as np
from jax import lax
from jax.experimental import pallas as pl
from jax.experimental.pallas import tpu as pltpu
from jax.sharding import PartitionSpec as P

HEADS = 40
HD = 128
LAT_CH = 16
FRAMES_SPAN = 3
TROWS = 8
TCOLS = 16


neg_big = -1e30
noise_level = 0.75
norm_eps = 1e-06


def with_halo(cells, sides, width):
    for axis, dim in sides:
        count = lax.axis_size(axis)
        ends = count - 1
        head = lax.slice_in_dim(cells, 0, width, axis=dim)
        tail = lax.slice_in_dim(cells, cells.shape[dim] - width, cells.shape[dim], axis=dim)
        cells = jnp.concatenate(
            [
                lax.ppermute(tail, axis, [(i, (i + 1) % count) for i in range(ends)]),
                cells,
                lax.ppermute(head, axis, [((i + 1) % count, i) for i in range(ends)]),
            ],
            axis=dim,
        )
    return cells


def from_behind(value, axis, by):
    size = lax.axis_size(axis)
    pairs = [(i, i + by) for i in range(size) if 0 <= i + by < size]
    return lax.ppermute(value, axis, pairs)


def block_length(total_rows):
    block_size = total_rows
    while block_size > 768 and block_size % 2 == 0:
        block_size = block_size // 2
    return block_size


def fold_keys(partial_state, key_value, query_block, mask_row, rows_span):
    keys_piece, values_piece = key_value
    heads_dev = query_block.shape[1]
    piece_rows = keys_piece.shape[0]
    length = block_length(piece_rows)
    span_count = mask_row.shape[0]
    score_scale = 1.0 / math.sqrt(HD)
    span_ids = jnp.arange(span_count, dtype=jnp.int32)

    def one_block(carry_state, block_index):
        running_max, running_sum, weighted = carry_state
        offset = block_index * length
        key_block = lax.dynamic_slice_in_dim(keys_piece, offset, length, 0).reshape(
            length, heads_dev, HD
        )
        value_block = lax.dynamic_slice_in_dim(values_piece, offset, length, 0).reshape(
            length, heads_dev, HD
        )
        key_span = (offset + jnp.arange(length, dtype=jnp.int32)) // rows_span
        allowed = (
            jnp.sum(jnp.where(key_span[:, None] == span_ids[None, :], mask_row[None, :], 0), axis=1)
            > 0
        )
        scores = (
            jnp.einsum("qhd,khd->hqk", query_block, key_block, preferred_element_type=jnp.float32)
            * score_scale
        )
        scores = jnp.where(allowed[None, None, :], scores, neg_big)
        new_max = jnp.maximum(running_max, jnp.max(scores, axis=2))
        weights = jnp.where(allowed[None, None, :], jnp.exp(scores - new_max[:, :, None]), 0.0)
        factor = jnp.exp(running_max - new_max)
        running_sum = running_sum * factor + jnp.sum(weights, axis=2)
        weighted = weighted * factor.T[:, :, None] + jnp.einsum(
            "hqk,khd->qhd",
            weights.astype(jnp.bfloat16),
            value_block,
            preferred_element_type=jnp.float32,
        )
        return ((new_max, running_sum, weighted), None)

    result, unused = lax.scan(
        one_block, partial_state, jnp.arange(piece_rows // length, dtype=jnp.int32)
    )
    return result


def gathered_plan(
    queries,
    keys,
    values,
    span_mask,
    head_gain,
    head_shift,
    patch_weight,
    noisy_latent,
    conv_weight,
    conv_bias,
):
    heads_dev = queries.shape[1] // HD
    slab_count = lax.axis_size("slab")
    col_dev = TCOLS // slab_count
    slab_place = lax.axis_index("slab")
    span_place = lax.axis_index("span")
    mask_row = lax.dynamic_slice_in_dim(span_mask, span_place, 1, 0)[0]
    token_grid = queries.reshape(FRAMES_SPAN, TROWS, TCOLS, queries.shape[-1])
    picked = lax.dynamic_slice_in_dim(token_grid, slab_place * col_dev, col_dev, 2)
    own_queries = picked.reshape(FRAMES_SPAN * TROWS * col_dev, queries.shape[-1]).reshape(
        -1, heads_dev, HD
    )
    query_rows = own_queries.shape[0]
    rows_span = keys.shape[0] * slab_count
    running_max, running_sum, weighted = fold_keys(
        (
            jnp.full((heads_dev, query_rows), neg_big, jnp.float32),
            jnp.zeros((heads_dev, query_rows), jnp.float32),
            jnp.zeros((query_rows, heads_dev, HD), jnp.float32),
        ),
        (
            lax.all_gather(keys, ("span", "slab"), axis=0, tiled=True),
            lax.all_gather(values, ("span", "slab"), axis=0, tiled=True),
        ),
        own_queries,
        mask_row,
        rows_span,
    )
    attended = (
        (weighted / running_sum.T[:, :, None])
        .astype(jnp.bfloat16)
        .reshape(query_rows, heads_dev * HD)
    )
    feature_width = HEADS * HD
    values32 = attended.astype(jnp.float32)
    row_total = jnp.sum(values32, axis=1)
    row_squares = jnp.sum(values32 * values32, axis=1)
    row_total, row_squares = lax.psum((row_total, row_squares), "head")
    row_mean = row_total / feature_width
    spread = row_squares / feature_width - row_mean * row_mean
    normed = (
        (values32 - row_mean[:, None]) * lax.rsqrt(spread + norm_eps)[:, None] * head_gain[None, :]
        + head_shift[None, :]
    ).astype(jnp.bfloat16)
    normed_grid = normed.reshape(FRAMES_SPAN, TROWS, col_dev, normed.shape[-1])
    own_rows = TROWS // lax.axis_size("head")
    picked = normed_grid
    product = jnp.dot(
        picked.reshape(-1, picked.shape[-1]), patch_weight, preferred_element_type=jnp.float32
    )
    velocity = lax.psum_scatter(
        product.reshape(
            FRAMES_SPAN, own_rows * lax.axis_size("head"), col_dev * patch_weight.shape[1]
        )
        .transpose(1, 0, 2)
        .reshape(own_rows * lax.axis_size("head"), -1)
        .astype(jnp.bfloat16),
        "head",
        scatter_dimension=0,
        tiled=True,
    ).astype(jnp.float32)
    rows_dev = velocity.shape[0]
    patch_cells = (
        velocity.reshape(rows_dev, FRAMES_SPAN, col_dev, 2, 2, LAT_CH)
        .transpose(1, 0, 3, 2, 4, 5)
        .reshape(FRAMES_SPAN, 2 * rows_dev, 2 * col_dev, LAT_CH)
    )
    clean_latent = noisy_latent - noise_level * patch_cells
    latent_input = clean_latent.astype(jnp.bfloat16)
    framed = with_halo(latent_input, (("head", 1), ("slab", 2)), 1)
    earlier = from_behind(framed[FRAMES_SPAN - 2 :], "span", 1)
    stacked = jnp.concatenate([earlier, framed], axis=0)
    height = clean_latent.shape[1]
    breadth = clean_latent.shape[2]
    columns = jnp.concatenate(
        [
            stacked[
                frame_tap : frame_tap + FRAMES_SPAN,
                row_tap : row_tap + height,
                col_tap : col_tap + breadth,
                :,
            ]
            for frame_tap in range(3)
            for row_tap in range(3)
            for col_tap in range(3)
        ],
        axis=-1,
    )
    decoded = (
        jnp.dot(
            columns.reshape(FRAMES_SPAN * height * breadth, 27 * LAT_CH),
            conv_weight,
            preferred_element_type=jnp.float32,
        )
        + conv_bias[None, :]
    )
    decoded = decoded.astype(jnp.bfloat16).reshape(
        FRAMES_SPAN, height, breadth, conv_weight.shape[1]
    )
    return (clean_latent, decoded)


NEAR_HEADS = 4
MIDDLE_HEADS = 4
FAR_HEADS = 2
MIDDLE = NEAR_HEADS
FAR = NEAR_HEADS + MIDDLE_HEADS
EARLY = 3
LATE = NEAR_HEADS - EARLY
STAT_ROWS = 8
SLOTS = 3
QUERY_ROWS = 192
SWAP = [(0, 1), (1, 0)]
WINDOW = 32

OWN, OTHER, DOWN, UP, MAIN, PLACE, SLAB = range(7)


def plan_fits(heads_dev, span_count, slab_count, head_count):
    return (
        span_count == 4
        and slab_count == 2
        and head_count == 2
        and heads_dev == slab_count * (NEAR_HEADS + MIDDLE_HEADS + FAR_HEADS)
    )


def scalar_operand(heads):
    by_place = np.array(
        [
            [0, heads, MIDDLE, 0, MIDDLE, 0, 0, 0],
            [0, heads, MIDDLE, MIDDLE, 0, 1, 0, 0],
            [0, heads, 0, 0, MIDDLE, 2, 0, 0],
            [0, heads, MIDDLE, 0, 0, 3, 0, 0],
        ],
        np.int32,
    )
    by_slab = np.array([heads, -heads, 0, 0, 0, 0, 1, 0], np.int32)
    row = lax.dynamic_slice_in_dim(jnp.array(by_place), lax.axis_index("span"), 1, 0)[0]
    return row + lax.axis_index("slab") * jnp.array(by_slab)


def pack_kernel(copies, scalars, *refs):
    ins, outs, semaphores = refs[: copies[0]], refs[copies[0] : -1], refs[-1]
    started = []
    for number, (source, row, rows, entries, shift, target, at, heads) in enumerate(copies[1]):
        head = shift
        for entry in entries:
            head = head + scalars[entry]
        column = pl.multiple_of(head * HD, HD)
        copy = pltpu.make_async_copy(
            ins[source].at[pl.ds(row, rows), pl.ds(column, heads * HD)],
            outs[target].at[pl.ds(at, rows), :],
            semaphores.at[number],
        )
        copy.start()
        started.append(copy)
    for copy in started:
        copy.wait()


def pack(scalars, arrays, shapes, copies, name):
    moved = sum(2 * 2 * rows * heads * HD for _, _, rows, _, _, _, _, heads in copies)
    return pl.pallas_call(
        functools.partial(pack_kernel, (len(arrays), copies)),
        name=name,
        out_shape=[jax.ShapeDtypeStruct(shape, jnp.bfloat16) for shape in shapes],
        grid_spec=pltpu.PrefetchScalarGridSpec(
            num_scalar_prefetch=1,
            grid=(1,),
            in_specs=[pl.BlockSpec(memory_space=pl.ANY)] * len(arrays),
            out_specs=[pl.BlockSpec(memory_space=pl.ANY)] * len(shapes),
            scratch_shapes=[pltpu.SemaphoreType.DMA((len(copies),))],
        ),
        cost_estimate=pl.CostEstimate(flops=0, bytes_accessed=moved, transcendentals=0),
    )(scalars, *arrays)


def pack_messages(scalars, queries, keys, values, received, messages, name):
    rows = queries.shape[0]
    half = rows // 2
    copies, shapes = [], []
    for target, (entry, shift, heads, whole) in enumerate(messages):
        entries = () if entry is None else (entry,)
        at = 0
        if whole:
            copies.append((0, 0, rows, (OWN,) + entries, shift, target, 0, heads))
            at = rows
        for part, array in enumerate((1, 2)):
            copies.append((array, 0, half, (OWN,) + entries, shift, target, at, heads))
            copies.append((3, part * half, half, entries, shift, target, at + half, heads))
            at += rows
        shapes.append((at, heads * HD))
    return pack(scalars, (queries, keys, values, received), shapes, copies, name)


def attend_kernel(variants, extra, span_count, scalars, mask, *refs):
    query_own, key_own, value_own, received, weight, gain, sums_in = refs[:7]
    more = refs[7 : 7 + extra]
    payloads, (sums_out, folded, squares) = refs[7 + extra : -3], refs[-3:]
    rows = query_own.shape[0]
    half = rows // 2
    step = pl.program_id(0)
    to_exp2 = math.log2(math.e) / math.sqrt(HD)

    @pl.when(step == 0)
    def _():
        folded[...] = jnp.zeros_like(folded)
        squares[...] = jnp.zeros_like(squares)

    def query_of(source):
        if source is None:
            return query_own[...]
        if source[0] < 0:
            return more[0][:, source[1] * HD : (source[1] + 1) * HD]
        return payloads[source[0]][:rows]

    def pair_of(source):
        if source is None:
            parts = (key_own[...], received[:half], value_own[...], received[half:])
        elif source[0] < 0:
            lanes = slice(source[1] * HD, (source[1] + 1) * HD)
            parts = (more[1][:, lanes], more[3][:half, lanes], more[2][:, lanes], more[3][half:, lanes])
        else:
            payload = payloads[source[0]]
            start = payload.shape[0] - 2 * rows
            return payload[start : start + rows], payload[start + rows :]
        return jnp.concatenate(parts[:2], axis=0), jnp.concatenate(parts[2:], axis=0)

    def projector(extra_head):
        if extra_head is None:
            scaled = weight[...].astype(jnp.float32) * gain[...]
        else:
            lanes = slice(extra_head * HD, (extra_head + 1) * HD)
            scaled = more[4][:, lanes].astype(jnp.float32) * more[5][:, lanes]
        high = scaled.astype(jnp.bfloat16)
        low = (scaled - high.astype(jnp.float32)).astype(jnp.bfloat16)
        return jnp.concatenate([high, low, jnp.ones((16, HD), jnp.bfloat16)], axis=0)

    def one_query(source, slot, query_span, key_sources):
        query = query_of(source)
        pairs = [pair_of(key_source) for key_source, _ in key_sources]
        open_to = [
            None if key_span == query_span else mask[query_span * span_count + key_span] > 0
            for _, key_span in key_sources
        ]
        keys_in = jnp.concatenate([pair[0] for pair in pairs], axis=0)
        ones_block = jnp.ones((rows, HD), jnp.bfloat16)
        values_in = jnp.concatenate(
            [jnp.concatenate([pair[1], ones_block], axis=1) for pair in pairs], axis=0
        )
        pieces = []
        for row in range(0, rows, QUERY_ROWS):
            score = lax.dot_general(
                query[row : row + QUERY_ROWS],
                keys_in,
                (((1,), (1,)), ((), ())),
                preferred_element_type=jnp.float32,
            )
            best = None
            for number, is_open in enumerate(open_to):
                start = number * rows
                block = score[:, start : start + HD]
                for lane in range(HD, rows, HD):
                    block = jnp.maximum(block, score[:, start + lane : start + lane + HD])
                if is_open is not None:
                    block = jnp.where(is_open, block, neg_big)
                best = block if best is None else jnp.maximum(best, block)
            top = jnp.max(best, axis=1, keepdims=True)
            weights = []
            for number, is_open in enumerate(open_to):
                start = number * rows
                shift = top if is_open is None else jnp.where(is_open, top, -neg_big)
                weights.append(
                    jnp.exp2((score[:, start : start + rows] - shift) * to_exp2).astype(jnp.bfloat16)
                )
            both = jnp.dot(
                jnp.concatenate(weights, axis=1), values_in, preferred_element_type=jnp.float32
            )
            pieces.append((both[:, :HD] / both[:, HD:]).astype(jnp.bfloat16))
        attended = jnp.concatenate(pieces, axis=0)
        extra_head = source[1] if source is not None and source[0] < 0 else None
        folded[slot] += lax.dot_general(
            projector(extra_head),
            attended,
            (((1,), (1,)), ((), ())),
            preferred_element_type=jnp.float32,
        )
        wide = attended.astype(jnp.float32)
        squares[slot] += wide * wide

    for place, tasks in variants.items():

        @pl.when(scalars[PLACE] == place)
        def _():
            for task in tasks:
                one_query(*task)

    @pl.when(step == pl.num_programs(0) - 1)
    def _():
        ones_rows = jnp.ones((STAT_ROWS, HD), jnp.bfloat16)
        patch = weight.shape[0]
        for slot in range(SLOTS):
            left = squares[slot]
            total = jnp.zeros((STAT_ROWS, rows), jnp.float32)
            for _ in range(3):
                piece = left.astype(jnp.bfloat16)
                left = left - piece.astype(jnp.float32)
                total = total + lax.dot_general(
                    ones_rows, piece, (((1,), (1,)), ((), ())), preferred_element_type=jnp.float32
                )
            done = folded[slot]
            sums_out[slot] = sums_in[slot] + jnp.concatenate(
                [
                    done[:patch] + done[patch : 2 * patch],
                    done[2 * patch : 2 * patch + STAT_ROWS],
                    total,
                ],
                axis=0,
            )


def attend(steps, entries, first, own, scalars, mask, sums, payloads, variants, more, name):
    queries, keys, values, received, weight, gain = own
    rows = queries.shape[0]
    half = rows // 2
    patch = weight.shape[0]

    def column(height, own_column):
        def index(i, scalars, mask):
            head = first + i + (scalars[OWN] if own_column else 0)
            for entry in entries:
                head = head + scalars[entry]
            return (0, head)

        return pl.BlockSpec((height, HD), index)

    def two_columns(height, own_column):
        return pl.BlockSpec(
            (height, 2 * HD),
            lambda i, scalars, mask: (0, i + (scalars[OWN] // 2 if own_column else 0)),
        )

    sums_spec = pl.BlockSpec(sums.shape, lambda i, scalars, mask: (0, 0, 0))
    in_specs = [
        column(rows, True),
        column(half, True),
        column(half, True),
        column(rows, False),
        column(patch, True),
        column(1, True),
        sums_spec,
    ]
    arrays = [queries, keys, values, received, weight, gain, sums]
    extra = 0
    if more:
        extra = 6
        in_specs += [
            two_columns(rows, True),
            two_columns(half, True),
            two_columns(half, True),
            two_columns(rows, False),
            two_columns(patch, True),
            two_columns(1, True),
        ]
        arrays += [queries, keys, values, received, weight, gain]
    in_specs += [
        pl.BlockSpec((payload.shape[0], HD), lambda i, scalars, mask: (0, i))
        for payload in payloads
    ]
    arrays += payloads
    pairs = steps * max(sum(len(task[3]) for task in tasks) for tasks in variants.values())
    span_count = math.isqrt(mask.shape[0])
    return pl.pallas_call(
        functools.partial(attend_kernel, variants, extra, span_count),
        name=name,
        out_shape=jax.ShapeDtypeStruct(sums.shape, sums.dtype),
        grid_spec=pltpu.PrefetchScalarGridSpec(
            num_scalar_prefetch=2,
            grid=(steps,),
            in_specs=in_specs,
            out_specs=sums_spec,
            scratch_shapes=[
                pltpu.VMEM((SLOTS, 2 * patch + 16, rows), jnp.float32),
                pltpu.VMEM((SLOTS, rows, HD), jnp.float32),
            ],
        ),
        compiler_params=pltpu.CompilerParams(vmem_limit_bytes=40 << 20),
        cost_estimate=pl.CostEstimate(
            flops=pairs * 4 * rows * rows * HD,
            bytes_accessed=steps * HD * 2 * sum(spec.block_shape[0] for spec in in_specs[:4]),
            transcendentals=pairs * rows * rows,
        ),
    )(scalars, mask, *arrays)


def token_sums(scalars, queries, keys, values, span_mask, head_gain, patch_weight):
    rows = queries.shape[0]
    heads = NEAR_HEADS + MIDDLE_HEADS + FAR_HEADS
    half = rows // 2
    (handed,) = pack(
        scalars,
        (keys, values),
        [(rows, heads * HD)],
        [(0, 0, half, (OTHER,), 0, 0, 0, heads), (1, 0, half, (OTHER,), 0, 0, half, heads)],
        "pack_handed",
    )
    received = lax.ppermute(handed, "slab", SWAP)
    bring = functools.partial(pack_messages, scalars, queries, keys, values, received)
    send = lambda value, *pairs: lax.ppermute(value, "span", list(pairs))

    down, up = bring([(DOWN, 0, EARLY, True), (UP, 0, EARLY, False)], "pack_first")
    anchor = down
    down_two, up_two = bring(
        [(None, 0, EARLY, True), (None, MIDDLE, EARLY, False)], "pack_second"
    )
    far_all, far_pair, late_down, late_down_two, late_up, late_up_two = bring(
        [
            (None, FAR, FAR_HEADS, True),
            (None, FAR, FAR_HEADS, False),
            (DOWN, EARLY, LATE, True),
            (None, EARLY, LATE, True),
            (UP, EARLY, LATE, False),
            (None, MIDDLE + EARLY, LATE, False),
        ],
        "pack_third",
    )
    down = send(down, (1, 0), (2, 1), (3, 2))
    up = send(up, (0, 1), (1, 2))
    down_two = send(down_two, (3, 1))
    up_two = send(up_two, (0, 2))
    far_two = send(far_pair, (1, 3))
    far_three = send(far_pair, (0, 3))
    far_next = send(far_all, (2, 3), (1, 0))
    late_down = send(late_down, (1, 0), (2, 1), (3, 2))
    late_down_two = send(late_down_two, (3, 1))
    late_up = send(late_up, (0, 1), (1, 2))
    late_up_two = send(late_up_two, (0, 2))

    mask = span_mask.reshape(-1)
    weight = patch_weight.T
    own = (queries, keys, values, received, weight, head_gain[None, :])
    sums = jnp.zeros((SLOTS, weight.shape[0] + 2 * STAT_ROWS, rows), jnp.float32)
    on_one, on_two, back_one, back_two = (0, 0), (1, 0), (2, 0), (3, 0)
    main = {
        0: [(None, 0, 0, [(None, 0)]), (on_one, 1, 1, [(None, 0), (on_one, 1)])],
        1: [
            (on_two, 2, 3, [(back_one, 0), (None, 1), (on_one, 2), (on_two, 3)]),
            (on_one, 1, 2, [(back_one, 0), (None, 1), (on_one, 2)]),
            (None, 0, 1, [(back_one, 0), (None, 1)]),
        ],
        2: [
            (on_one, 1, 3, [(back_two, 0), (back_one, 1), (None, 2), (on_one, 3)]),
            (None, 0, 2, [(back_two, 0), (back_one, 1), (None, 2)]),
        ],
    }
    extra = [((-1, lane), 0, 0, [((-1, lane), 0)]) for lane in range(2)]
    far = {
        0: [(None, 0, 0, [(None, 0)]), ((0, 0), 1, 1, [(None, 0), ((0, 0), 1)])] + extra,
        3: [
            (None, 0, 3, [((2, 0), 0), ((1, 0), 1), ((0, 0), 2), (None, 3)]),
            ((0, 0), 2, 2, [((2, 0), 0), ((1, 0), 1), ((0, 0), 2)]),
        ],
    }
    run = functools.partial(attend, own=own, scalars=scalars, mask=mask)
    sums = run(
        FAR_HEADS,
        (),
        FAR,
        sums=sums,
        payloads=[far_next, far_two, far_three],
        variants=far,
        more=True,
        name="far_heads",
    )
    sums = run(
        EARLY,
        (MAIN,),
        0,
        sums=sums,
        payloads=[down, down_two, up, up_two],
        variants=main,
        more=False,
        name="early_heads",
    )
    sums = run(
        LATE,
        (MAIN,),
        EARLY,
        sums=sums,
        payloads=[late_down, late_down_two, late_up, late_up_two],
        variants=main,
        more=False,
        name="late_heads",
    )
    return sums, anchor


def noise_window(noisy_latent):
    frames, height, breadth, channels = noisy_latent.shape
    own = noisy_latent.transpose(1, 2, 0, 3).reshape(height, breadth, frames * channels)
    earlier = from_behind(own[:, :, (frames - 2) * channels :], "span", 1)
    grid = jnp.concatenate([earlier, own], axis=2)
    slab = lax.axis_index("slab")
    edge = jnp.where(slab == 0, grid[:, breadth - 1], grid[:, 0])
    edge = lax.ppermute(edge, "slab", SWAP)[:, None]
    grid = jnp.concatenate(
        [
            jnp.where(slab == 1, edge, 0.0),
            grid,
            jnp.where(slab == 0, edge, 0.0),
            jnp.zeros((height, WINDOW - breadth - 2, grid.shape[2]), grid.dtype),
        ],
        axis=1,
    )
    head = lax.axis_index("head")
    edge = jnp.where(head == 0, grid[height - 1], grid[0])
    edge = lax.ppermute(edge, "head", SWAP)[None]
    grid = jnp.concatenate(
        [jnp.where(head == 1, edge, 0.0), grid, jnp.where(head == 0, edge, 0.0)], axis=0
    )
    return grid.reshape((height + 2) * WINDOW, grid.shape[2])


def cell_selector(height, breadth):
    cell = lax.broadcasted_iota(jnp.int32, ((height + 2) * WINDOW, 4 * TROWS * TCOLS), 0)
    column = lax.broadcasted_iota(jnp.int32, cell.shape, 1)
    y = lax.axis_index("head") * height + cell // WINDOW - 1
    x = lax.axis_index("slab") * breadth + cell % WINDOW - 1
    inside = (y >= 0) & (y < 2 * TROWS) & (x >= 0) & (x < 2 * TCOLS)
    inside = inside & (cell % WINDOW < breadth + 2)
    target = ((y % 2) * 2 + x % 2) * (TROWS * TCOLS) + (y // 2) * TCOLS + x // 2
    return (inside & (column == target)).astype(jnp.bfloat16)


def banded_weight(conv_weight):
    channels = conv_weight.shape[1]
    taps = conv_weight.reshape(3, 3, 3, LAT_CH, channels)
    banded = jnp.stack(
        [
            jnp.pad(taps, ((n, FRAMES_SPAN - 1 - n), (0, 0), (0, 0), (0, 0), (0, 0)))
            for n in range(FRAMES_SPAN)
        ],
        axis=4,
    )
    return banded.transpose(1, 2, 0, 3, 4, 5).reshape(
        3, 3 * (FRAMES_SPAN + 2) * LAT_CH, FRAMES_SPAN * channels
    )


def finish_kernel(
    scalars, mine, other, noise, selector, band, bias, constants, clean, decoded, cells
):
    frames, height, breadth, channels = clean.shape
    patch = constants.shape[0]
    first = scalars[SLAB] == 0
    sums = jnp.concatenate(
        [jnp.where(first, mine[...], other[...]), jnp.where(first, other[...], mine[...])], axis=0
    )
    feature_width = HEADS * HD
    row_mean = sums[patch : patch + 1] / feature_width
    spread = sums[patch + STAT_ROWS : patch + STAT_ROWS + 1] / feature_width - row_mean * row_mean
    velocity = (
        lax.rsqrt(spread + norm_eps) * (sums[:patch] - constants[:, 0:1] * row_mean)
        + constants[:, 1:2]
    )
    tokens = TROWS * TCOLS
    lane = lax.broadcasted_iota(jnp.int32, velocity.shape, 1)
    velocity = jnp.where((lane >= 2 * tokens) | (scalars[PLACE] > 0), velocity, 0.0)
    columns = jnp.concatenate(
        [
            jnp.concatenate(
                [
                    velocity[
                        part * channels : (part + 1) * channels,
                        frame * tokens : (frame + 1) * tokens,
                    ]
                    for part in range(4)
                ],
                axis=1,
            )
            for frame in range(frames + 2)
        ],
        axis=0,
    )
    high = columns.astype(jnp.bfloat16)
    low = (columns - high.astype(jnp.float32)).astype(jnp.bfloat16)
    chosen = sum(
        lax.dot_general(
            selector[...], part, (((1,), (1,)), ((), ())), preferred_element_type=jnp.float32
        )
        for part in (high, low)
    )
    count = (height + 2) * WINDOW
    cells[:count] = noise[...] - noise_level * chosen
    cells[count:] = jnp.zeros_like(cells[count:])
    for frame in range(frames):
        lanes = slice((frame + 2) * channels, (frame + 3) * channels)
        for y in range(height):
            start = (y + 1) * WINDOW + 1
            clean[frame, y] = cells[start : start + breadth, lanes]
    shifted = jnp.concatenate(
        [cells[tap : tap + count] for tap in range(3)], axis=1
    ).astype(jnp.bfloat16)
    total = jnp.broadcast_to(bias[...], (height * breadth, bias.shape[1]))
    for tap in range(3):
        block = jnp.concatenate(
            [
                shifted[(y + tap) * WINDOW : (y + tap) * WINDOW + breadth]
                for y in range(height)
            ],
            axis=0,
        )
        total = total + jnp.dot(block, band[tap], preferred_element_type=jnp.float32)
    outputs = decoded.shape[3]
    total = total.astype(decoded.dtype)
    for frame in range(frames):
        decoded[frame] = total[:, frame * outputs : (frame + 1) * outputs].reshape(
            height, breadth, outputs
        )


def finish(scalars, mine, other, noise, selector, band, bias, constants, shape, outputs):
    whole = pl.BlockSpec(memory_space=pltpu.VMEM)
    frames, height, breadth, channels = shape
    rows = (height + 2) * WINDOW
    return pl.pallas_call(
        finish_kernel,
        name="finish",
        out_shape=(
            jax.ShapeDtypeStruct(shape, jnp.float32),
            jax.ShapeDtypeStruct((frames, height, breadth, outputs), jnp.bfloat16),
        ),
        in_specs=[pl.BlockSpec(memory_space=pltpu.SMEM)] + [whole] * 7,
        out_specs=(whole, whole),
        scratch_shapes=[pltpu.VMEM((rows + 8, (frames + 2) * channels), jnp.float32)],
        compiler_params=pltpu.CompilerParams(vmem_limit_bytes=32 << 20),
    )(scalars, mine, other, noise, selector, band, bias, constants)


def per_device(
    queries,
    keys,
    values,
    span_mask,
    head_gain,
    head_shift,
    patch_weight,
    noisy_latent,
    conv_weight,
    conv_bias,
):
    heads_dev = queries.shape[1] // HD
    if not plan_fits(
        heads_dev, lax.axis_size("span"), lax.axis_size("slab"), lax.axis_size("head")
    ):
        return gathered_plan(
            queries,
            keys,
            values,
            span_mask,
            head_gain,
            head_shift,
            patch_weight,
            noisy_latent,
            conv_weight,
            conv_bias,
        )
    place = lax.axis_index("span")
    slab = lax.axis_index("slab")
    scalars = scalar_operand(heads_dev // lax.axis_size("slab"))
    sums, anchor = token_sums(
        scalars, queries, keys, values, span_mask, head_gain, patch_weight
    )

    noisy, weight, gain, shift, taps, bias, _ = lax.optimization_barrier(
        (noisy_latent, patch_weight, head_gain, head_shift, conv_weight, conv_bias, anchor)
    )
    _, height, breadth, _ = noisy.shape
    noise = noise_window(noisy)
    wide_weight = weight.T.astype(jnp.float32)
    constants = jnp.stack(
        [
            jnp.sum(wide_weight * gain[None, :], axis=1),
            jnp.sum(wide_weight * shift[None, :], axis=1),
        ],
        axis=1,
    )
    constants = constants + lax.ppermute(constants, "head", SWAP)
    selector = cell_selector(height, breadth)
    band = banded_weight(taps)
    bias = jnp.tile(bias, FRAMES_SPAN)[None, :]

    half = sums.shape[1] // 2
    mine = lax.dynamic_slice_in_dim(sums, slab * half, half, 1)
    theirs = lax.dynamic_slice_in_dim(sums, (1 - slab) * half, half, 1)
    mine = mine + lax.ppermute(theirs, "slab", SWAP)
    own, after, third = mine[0], mine[1], mine[2]
    skip = TROWS * TCOLS
    from_one = lax.ppermute(
        jnp.concatenate([own[:, skip:], after], axis=1), "span", [(0, 1), (1, 2), (2, 3)]
    )
    to_current = lax.ppermute(third, "span", [(1, 3), (3, 2)])
    to_before = lax.ppermute(after[:, skip:], "span", [(0, 2), (1, 3)])
    kept = jnp.concatenate([jnp.where(place == 3, third[:, skip:], 0.0), own], axis=1)
    total = kept + from_one + jnp.concatenate([to_before, to_current], axis=1)
    total = total + lax.ppermute(total, "head", SWAP)
    other = lax.ppermute(total, "slab", SWAP)
    return finish(
        scalars,
        total,
        other,
        noise,
        selector,
        band,
        bias,
        constants,
        noisy_latent.shape,
        conv_weight.shape[1],
    )


def solution(mesh):
    placed = (
        P(("groups", "span"), "head"),
        P(("groups", "span", "slab"), "head"),
        P(("groups", "span", "slab"), "head"),
        P("groups", None),
        P("head"),
        P("head"),
        P("head", None),
        P(("groups", "span"), "head", "slab", None),
        P(),
        P(),
    )
    return jax.shard_map(
        per_device,
        mesh=mesh,
        in_specs=placed,
        out_specs=(
            P(("groups", "span"), "head", "slab", None),
            P(("groups", "span"), "head", "slab", None),
        ),
        check_vma=False,
    )
```

```python
import functools
import math

import jax
import jax.numpy as jnp
import numpy as np
from jax import lax
from jax.experimental import pallas as pl
from jax.experimental.pallas import tpu as pltpu
from jax.sharding import PartitionSpec as P

HEADS = 40
HD = 128
LAT_CH = 16
FRAMES_SPAN = 3
TROWS = 8
TCOLS = 16


neg_big = -1e30
noise_level = 0.75
norm_eps = 1e-06


def with_halo(cells, sides, width):
    for axis, dim in sides:
        count = lax.axis_size(axis)
        ends = count - 1
        head = lax.slice_in_dim(cells, 0, width, axis=dim)
        tail = lax.slice_in_dim(cells, cells.shape[dim] - width, cells.shape[dim], axis=dim)
        cells = jnp.concatenate(
            [
                lax.ppermute(tail, axis, [(i, (i + 1) % count) for i in range(ends)]),
                cells,
                lax.ppermute(head, axis, [((i + 1) % count, i) for i in range(ends)]),
            ],
            axis=dim,
        )
    return cells


def from_behind(value, axis, by):
    size = lax.axis_size(axis)
    pairs = [(i, i + by) for i in range(size) if 0 <= i + by < size]
    return lax.ppermute(value, axis, pairs)


def block_length(total_rows):
    block_size = total_rows
    while block_size > 768 and block_size % 2 == 0:
        block_size = block_size // 2
    return block_size


def fold_keys(partial_state, key_value, query_block, mask_row, rows_span):
    keys_piece, values_piece = key_value
    heads_dev = query_block.shape[1]
    piece_rows = keys_piece.shape[0]
    length = block_length(piece_rows)
    span_count = mask_row.shape[0]
    score_scale = 1.0 / math.sqrt(HD)
    span_ids = jnp.arange(span_count, dtype=jnp.int32)

    def one_block(carry_state, block_index):
        running_max, running_sum, weighted = carry_state
        offset = block_index * length
        key_block = lax.dynamic_slice_in_dim(keys_piece, offset, length, 0).reshape(
            length, heads_dev, HD
        )
        value_block = lax.dynamic_slice_in_dim(values_piece, offset, length, 0).reshape(
            length, heads_dev, HD
        )
        key_span = (offset + jnp.arange(length, dtype=jnp.int32)) // rows_span
        allowed = (
            jnp.sum(jnp.where(key_span[:, None] == span_ids[None, :], mask_row[None, :], 0), axis=1)
            > 0
        )
        scores = (
            jnp.einsum("qhd,khd->hqk", query_block, key_block, preferred_element_type=jnp.float32)
            * score_scale
        )
        scores = jnp.where(allowed[None, None, :], scores, neg_big)
        new_max = jnp.maximum(running_max, jnp.max(scores, axis=2))
        weights = jnp.where(allowed[None, None, :], jnp.exp(scores - new_max[:, :, None]), 0.0)
        factor = jnp.exp(running_max - new_max)
        running_sum = running_sum * factor + jnp.sum(weights, axis=2)
        weighted = weighted * factor.T[:, :, None] + jnp.einsum(
            "hqk,khd->qhd",
            weights.astype(jnp.bfloat16),
            value_block,
            preferred_element_type=jnp.float32,
        )
        return ((new_max, running_sum, weighted), None)

    result, unused = lax.scan(
        one_block, partial_state, jnp.arange(piece_rows // length, dtype=jnp.int32)
    )
    return result


def gathered_plan(
    queries,
    keys,
    values,
    span_mask,
    head_gain,
    head_shift,
    patch_weight,
    noisy_latent,
    conv_weight,
    conv_bias,
):
    heads_dev = queries.shape[1] // HD
    slab_count = lax.axis_size("slab")
    col_dev = TCOLS // slab_count
    slab_place = lax.axis_index("slab")
    span_place = lax.axis_index("span")
    mask_row = lax.dynamic_slice_in_dim(span_mask, span_place, 1, 0)[0]
    token_grid = queries.reshape(FRAMES_SPAN, TROWS, TCOLS, queries.shape[-1])
    picked = lax.dynamic_slice_in_dim(token_grid, slab_place * col_dev, col_dev, 2)
    own_queries = picked.reshape(FRAMES_SPAN * TROWS * col_dev, queries.shape[-1]).reshape(
        -1, heads_dev, HD
    )
    query_rows = own_queries.shape[0]
    rows_span = keys.shape[0] * slab_count
    running_max, running_sum, weighted = fold_keys(
        (
            jnp.full((heads_dev, query_rows), neg_big, jnp.float32),
            jnp.zeros((heads_dev, query_rows), jnp.float32),
            jnp.zeros((query_rows, heads_dev, HD), jnp.float32),
        ),
        (
            lax.all_gather(keys, ("span", "slab"), axis=0, tiled=True),
            lax.all_gather(values, ("span", "slab"), axis=0, tiled=True),
        ),
        own_queries,
        mask_row,
        rows_span,
    )
    attended = (
        (weighted / running_sum.T[:, :, None])
        .astype(jnp.bfloat16)
        .reshape(query_rows, heads_dev * HD)
    )
    feature_width = HEADS * HD
    values32 = attended.astype(jnp.float32)
    row_total = jnp.sum(values32, axis=1)
    row_squares = jnp.sum(values32 * values32, axis=1)
    row_total, row_squares = lax.psum((row_total, row_squares), "head")
    row_mean = row_total / feature_width
    spread = row_squares / feature_width - row_mean * row_mean
    normed = (
        (values32 - row_mean[:, None]) * lax.rsqrt(spread + norm_eps)[:, None] * head_gain[None, :]
        + head_shift[None, :]
    ).astype(jnp.bfloat16)
    normed_grid = normed.reshape(FRAMES_SPAN, TROWS, col_dev, normed.shape[-1])
    own_rows = TROWS // lax.axis_size("head")
    picked = normed_grid
    product = jnp.dot(
        picked.reshape(-1, picked.shape[-1]), patch_weight, preferred_element_type=jnp.float32
    )
    velocity = lax.psum_scatter(
        product.reshape(
            FRAMES_SPAN, own_rows * lax.axis_size("head"), col_dev * patch_weight.shape[1]
        )
        .transpose(1, 0, 2)
        .reshape(own_rows * lax.axis_size("head"), -1)
        .astype(jnp.bfloat16),
        "head",
        scatter_dimension=0,
        tiled=True,
    ).astype(jnp.float32)
    rows_dev = velocity.shape[0]
    patch_cells = (
        velocity.reshape(rows_dev, FRAMES_SPAN, col_dev, 2, 2, LAT_CH)
        .transpose(1, 0, 3, 2, 4, 5)
        .reshape(FRAMES_SPAN, 2 * rows_dev, 2 * col_dev, LAT_CH)
    )
    clean_latent = noisy_latent - noise_level * patch_cells
    latent_input = clean_latent.astype(jnp.bfloat16)
    framed = with_halo(latent_input, (("head", 1), ("slab", 2)), 1)
    earlier = from_behind(framed[FRAMES_SPAN - 2 :], "span", 1)
    stacked = jnp.concatenate([earlier, framed], axis=0)
    height = clean_latent.shape[1]
    breadth = clean_latent.shape[2]
    columns = jnp.concatenate(
        [
            stacked[
                frame_tap : frame_tap + FRAMES_SPAN,
                row_tap : row_tap + height,
                col_tap : col_tap + breadth,
                :,
            ]
            for frame_tap in range(3)
            for row_tap in range(3)
            for col_tap in range(3)
        ],
        axis=-1,
    )
    decoded = (
        jnp.dot(
            columns.reshape(FRAMES_SPAN * height * breadth, 27 * LAT_CH),
            conv_weight,
            preferred_element_type=jnp.float32,
        )
        + conv_bias[None, :]
    )
    decoded = decoded.astype(jnp.bfloat16).reshape(
        FRAMES_SPAN, height, breadth, conv_weight.shape[1]
    )
    return (clean_latent, decoded)


NEAR_HEADS = 4
MIDDLE_HEADS = 4
FAR_HEADS = 2
MIDDLE = NEAR_HEADS
FAR = NEAR_HEADS + MIDDLE_HEADS
EARLY = 3
LATE = NEAR_HEADS - EARLY
STAT_ROWS = 8
SLOTS = 3
QUERY_ROWS = 192
SWAP = [(0, 1), (1, 0)]
WINDOW = 32

OWN, OTHER, DOWN, UP, MAIN, PLACE, SLAB = range(7)


def plan_fits(heads_dev, span_count, slab_count, head_count):
    return (
        span_count == 4
        and slab_count == 2
        and head_count == 2
        and heads_dev == slab_count * (NEAR_HEADS + MIDDLE_HEADS + FAR_HEADS)
    )


def scalar_operand(heads):
    by_place = np.array(
        [
            [0, heads, MIDDLE, 0, MIDDLE, 0, 0, 0],
            [0, heads, MIDDLE, MIDDLE, 0, 1, 0, 0],
            [0, heads, 0, 0, MIDDLE, 2, 0, 0],
            [0, heads, MIDDLE, 0, 0, 3, 0, 0],
        ],
        np.int32,
    )
    by_slab = np.array([heads, -heads, 0, 0, 0, 0, 1, 0], np.int32)
    row = lax.dynamic_slice_in_dim(jnp.array(by_place), lax.axis_index("span"), 1, 0)[0]
    return row + lax.axis_index("slab") * jnp.array(by_slab)


def hand_kernel(scalars, keys, values, out):
    half = keys.shape[0]
    out[:half] = keys[...]
    out[half:] = values[...]


def pack_handed(scalars, keys, values, heads):
    half = keys.shape[0]
    wide = heads * HD
    column = pl.BlockSpec((half, wide), lambda i, scalars: (0, 1 - scalars[SLAB]))
    return pl.pallas_call(
        hand_kernel,
        name="pack_handed",
        out_shape=jax.ShapeDtypeStruct((2 * half, wide), keys.dtype),
        grid_spec=pltpu.PrefetchScalarGridSpec(
            num_scalar_prefetch=1,
            grid=(1,),
            in_specs=[column, column],
            out_specs=pl.BlockSpec((2 * half, wide), lambda i, scalars: (0, 0)),
        ),
        compiler_params=pltpu.CompilerParams(vmem_limit_bytes=16 << 20),
        cost_estimate=pl.CostEstimate(
            flops=0, bytes_accessed=8 * half * wide, transcendentals=0
        ),
    )(scalars, keys, values)


def pack_kernel(wholes, scalars, *refs):
    ins, outs = refs[: 4 * len(wholes)], refs[4 * len(wholes) :]
    for number, (whole, out) in enumerate(zip(wholes, outs)):
        queries, keys, values, received = ins[4 * number : 4 * number + 4]
        rows = received.shape[0]
        half = rows // 2
        at = 0
        if whole:
            out[:rows] = queries[...]
            at = rows
        out[at : at + half] = keys[...]
        out[at + half : at + rows] = received[:half]
        out[at + rows : at + rows + half] = values[...]
        out[at + rows + half :] = received[half:]


def pack_messages(scalars, heads, messages, queries, keys, values, received, name):
    rows = queries.shape[0]

    def column(height, entry, shift, own_column):
        def index(i, scalars):
            head = shift + i + (scalars[OWN] if own_column else 0)
            return (0, head if entry is None else head + scalars[entry])

        return pl.BlockSpec((height, HD), index)

    in_specs, arrays, shapes = [], [], []
    for entry, shift, whole in messages:
        in_specs += [
            column(rows, entry, shift, True) if whole else column(16, None, 0, False),
            column(rows // 2, entry, shift, True),
            column(rows // 2, entry, shift, True),
            column(rows, entry, shift, False),
        ]
        arrays += [queries, keys, values, received]
        shapes.append(((3 if whole else 2) * rows, heads * HD))
    wholes = [whole for _, _, whole in messages]
    return pl.pallas_call(
        functools.partial(pack_kernel, wholes),
        name=name,
        out_shape=[jax.ShapeDtypeStruct(shape, queries.dtype) for shape in shapes],
        grid_spec=pltpu.PrefetchScalarGridSpec(
            num_scalar_prefetch=1,
            grid=(heads,),
            in_specs=in_specs,
            out_specs=[
                pl.BlockSpec((shape[0], HD), lambda i, scalars: (0, i)) for shape in shapes
            ],
        ),
        compiler_params=pltpu.CompilerParams(vmem_limit_bytes=16 << 20),
        cost_estimate=pl.CostEstimate(
            flops=0,
            bytes_accessed=4 * sum(shape[0] * shape[1] for shape in shapes),
            transcendentals=0,
        ),
    )(scalars, *arrays)


def attend_kernel(variants, extra, span_count, scalars, mask, *refs):
    query_own, key_own, value_own, received, weight, gain, sums_in = refs[:7]
    more = refs[7 : 7 + extra]
    payloads, (sums_out, folded, squares) = refs[7 + extra : -3], refs[-3:]
    rows = query_own.shape[0]
    half = rows // 2
    step = pl.program_id(0)
    to_exp2 = math.log2(math.e) / math.sqrt(HD)

    @pl.when(step == 0)
    def _():
        folded[...] = jnp.zeros_like(folded)
        squares[...] = jnp.zeros_like(squares)

    def query_of(source):
        if source is None:
            return query_own[...]
        if source[0] < 0:
            return more[0][:, source[1] * HD : (source[1] + 1) * HD]
        return payloads[source[0]][:rows]

    def pair_of(source):
        if source is None:
            parts = (key_own[...], received[:half], value_own[...], received[half:])
        elif source[0] < 0:
            lanes = slice(source[1] * HD, (source[1] + 1) * HD)
            parts = (more[1][:, lanes], more[3][:half, lanes], more[2][:, lanes], more[3][half:, lanes])
        else:
            payload = payloads[source[0]]
            start = payload.shape[0] - 2 * rows
            return payload[start : start + rows], payload[start + rows :]
        return jnp.concatenate(parts[:2], axis=0), jnp.concatenate(parts[2:], axis=0)

    def projector(extra_head):
        if extra_head is None:
            scaled = weight[...].astype(jnp.float32) * gain[...]
        else:
            lanes = slice(extra_head * HD, (extra_head + 1) * HD)
            scaled = more[4][:, lanes].astype(jnp.float32) * more[5][:, lanes]
        high = scaled.astype(jnp.bfloat16)
        low = (scaled - high.astype(jnp.float32)).astype(jnp.bfloat16)
        return jnp.concatenate([high, low, jnp.ones((16, HD), jnp.bfloat16)], axis=0)

    def one_query(source, slot, query_span, key_sources):
        query = query_of(source)
        pairs = [pair_of(key_source) for key_source, _ in key_sources]
        open_to = [
            None if key_span == query_span else mask[query_span * span_count + key_span] > 0
            for _, key_span in key_sources
        ]
        keys_in = jnp.concatenate([pair[0] for pair in pairs], axis=0)
        ones_block = jnp.ones((rows, HD), jnp.bfloat16)
        values_in = jnp.concatenate(
            [jnp.concatenate([pair[1], ones_block], axis=1) for pair in pairs], axis=0
        )
        pieces = []
        for row in range(0, rows, QUERY_ROWS):
            score = lax.dot_general(
                query[row : row + QUERY_ROWS],
                keys_in,
                (((1,), (1,)), ((), ())),
                preferred_element_type=jnp.float32,
            )
            best = None
            for number, is_open in enumerate(open_to):
                start = number * rows
                block = score[:, start : start + HD]
                for lane in range(HD, rows, HD):
                    block = jnp.maximum(block, score[:, start + lane : start + lane + HD])
                if is_open is not None:
                    block = jnp.where(is_open, block, neg_big)
                best = block if best is None else jnp.maximum(best, block)
            top = jnp.max(best, axis=1, keepdims=True)
            weights = []
            for number, is_open in enumerate(open_to):
                start = number * rows
                shift = top if is_open is None else jnp.where(is_open, top, -neg_big)
                weights.append(
                    jnp.exp2((score[:, start : start + rows] - shift) * to_exp2).astype(jnp.bfloat16)
                )
            both = jnp.dot(
                jnp.concatenate(weights, axis=1), values_in, preferred_element_type=jnp.float32
            )
            pieces.append((both[:, :HD] / both[:, HD:]).astype(jnp.bfloat16))
        attended = jnp.concatenate(pieces, axis=0)
        extra_head = source[1] if source is not None and source[0] < 0 else None
        folded[slot] += lax.dot_general(
            projector(extra_head),
            attended,
            (((1,), (1,)), ((), ())),
            preferred_element_type=jnp.float32,
        )
        wide = attended.astype(jnp.float32)
        squares[slot] += wide * wide

    for place, tasks in variants.items():

        @pl.when(scalars[PLACE] == place)
        def _():
            for task in tasks:
                one_query(*task)

    @pl.when(step == pl.num_programs(0) - 1)
    def _():
        ones_rows = jnp.ones((STAT_ROWS, HD), jnp.bfloat16)
        patch = weight.shape[0]
        for slot in range(SLOTS):
            left = squares[slot]
            total = jnp.zeros((STAT_ROWS, rows), jnp.float32)
            for _ in range(3):
                piece = left.astype(jnp.bfloat16)
                left = left - piece.astype(jnp.float32)
                total = total + lax.dot_general(
                    ones_rows, piece, (((1,), (1,)), ((), ())), preferred_element_type=jnp.float32
                )
            done = folded[slot]
            sums_out[slot] = sums_in[slot] + jnp.concatenate(
                [
                    done[:patch] + done[patch : 2 * patch],
                    done[2 * patch : 2 * patch + STAT_ROWS],
                    total,
                ],
                axis=0,
            )


def attend(steps, entries, first, own, scalars, mask, sums, payloads, variants, more, name):
    queries, keys, values, received, weight, gain = own
    rows = queries.shape[0]
    half = rows // 2
    patch = weight.shape[0]

    def column(height, own_column):
        def index(i, scalars, mask):
            head = first + i + (scalars[OWN] if own_column else 0)
            for entry in entries:
                head = head + scalars[entry]
            return (0, head)

        return pl.BlockSpec((height, HD), index)

    def two_columns(height, own_column):
        return pl.BlockSpec(
            (height, 2 * HD),
            lambda i, scalars, mask: (0, i + (scalars[OWN] // 2 if own_column else 0)),
        )

    sums_spec = pl.BlockSpec(sums.shape, lambda i, scalars, mask: (0, 0, 0))
    in_specs = [
        column(rows, True),
        column(half, True),
        column(half, True),
        column(rows, False),
        column(patch, True),
        column(1, True),
        sums_spec,
    ]
    arrays = [queries, keys, values, received, weight, gain, sums]
    extra = 0
    if more:
        extra = 6
        in_specs += [
            two_columns(rows, True),
            two_columns(half, True),
            two_columns(half, True),
            two_columns(rows, False),
            two_columns(patch, True),
            two_columns(1, True),
        ]
        arrays += [queries, keys, values, received, weight, gain]
    in_specs += [
        pl.BlockSpec((payload.shape[0], HD), lambda i, scalars, mask: (0, i))
        for payload in payloads
    ]
    arrays += payloads
    pairs = steps * max(sum(len(task[3]) for task in tasks) for tasks in variants.values())
    span_count = math.isqrt(mask.shape[0])
    return pl.pallas_call(
        functools.partial(attend_kernel, variants, extra, span_count),
        name=name,
        out_shape=jax.ShapeDtypeStruct(sums.shape, sums.dtype),
        grid_spec=pltpu.PrefetchScalarGridSpec(
            num_scalar_prefetch=2,
            grid=(steps,),
            in_specs=in_specs,
            out_specs=sums_spec,
            scratch_shapes=[
                pltpu.VMEM((SLOTS, 2 * patch + 16, rows), jnp.float32),
                pltpu.VMEM((SLOTS, rows, HD), jnp.float32),
            ],
        ),
        compiler_params=pltpu.CompilerParams(vmem_limit_bytes=40 << 20),
        cost_estimate=pl.CostEstimate(
            flops=pairs * 4 * rows * rows * HD,
            bytes_accessed=steps * HD * 2 * sum(spec.block_shape[0] for spec in in_specs[:4]),
            transcendentals=pairs * rows * rows,
        ),
    )(scalars, mask, *arrays)


def token_sums(scalars, queries, keys, values, span_mask, head_gain, patch_weight):
    rows = queries.shape[0]
    heads = NEAR_HEADS + MIDDLE_HEADS + FAR_HEADS
    received = lax.ppermute(pack_handed(scalars, keys, values, heads), "slab", SWAP)
    send = lambda value, *pairs: lax.ppermute(value, "span", list(pairs))

    def bring(heads, messages, source, name):
        return pack_messages(scalars, heads, messages, queries, keys, values, source, name)

    down, up = bring(EARLY, [(DOWN, 0, True), (UP, 0, False)], received, "pack_first")
    anchor = down
    source, _ = lax.optimization_barrier((received, down))
    down_two, up_two = bring(
        EARLY, [(None, 0, True), (None, MIDDLE, False)], source, "pack_second"
    )
    source, _ = lax.optimization_barrier((received, down_two))
    far_all, far_pair = bring(
        FAR_HEADS, [(None, FAR, True), (None, FAR, False)], source, "pack_far"
    )
    source, _ = lax.optimization_barrier((received, far_all))
    late_down, late_down_two, late_up, late_up_two = bring(
        LATE,
        [
            (DOWN, EARLY, True),
            (None, EARLY, True),
            (UP, EARLY, False),
            (None, MIDDLE + EARLY, False),
        ],
        source,
        "pack_late",
    )
    down = send(down, (1, 0), (2, 1), (3, 2))
    up = send(up, (0, 1), (1, 2))
    down_two = send(down_two, (3, 1))
    up_two = send(up_two, (0, 2))
    far_two = send(far_pair, (1, 3))
    far_three = send(far_pair, (0, 3))
    far_next = send(far_all, (2, 3), (1, 0))
    late_down = send(late_down, (1, 0), (2, 1), (3, 2))
    late_down_two = send(late_down_two, (3, 1))
    late_up = send(late_up, (0, 1), (1, 2))
    late_up_two = send(late_up_two, (0, 2))

    mask = span_mask.reshape(-1)
    weight = patch_weight.T
    own = (queries, keys, values, received, weight, head_gain[None, :])
    sums = jnp.zeros((SLOTS, weight.shape[0] + 2 * STAT_ROWS, rows), jnp.float32)
    on_one, on_two, back_one, back_two = (0, 0), (1, 0), (2, 0), (3, 0)
    main = {
        0: [(None, 0, 0, [(None, 0)]), (on_one, 1, 1, [(None, 0), (on_one, 1)])],
        1: [
            (on_two, 2, 3, [(back_one, 0), (None, 1), (on_one, 2), (on_two, 3)]),
            (on_one, 1, 2, [(back_one, 0), (None, 1), (on_one, 2)]),
            (None, 0, 1, [(back_one, 0), (None, 1)]),
        ],
        2: [
            (on_one, 1, 3, [(back_two, 0), (back_one, 1), (None, 2), (on_one, 3)]),
            (None, 0, 2, [(back_two, 0), (back_one, 1), (None, 2)]),
        ],
    }
    extra = [((-1, lane), 0, 0, [((-1, lane), 0)]) for lane in range(2)]
    far = {
        0: [(None, 0, 0, [(None, 0)]), ((0, 0), 1, 1, [(None, 0), ((0, 0), 1)])] + extra,
        3: [
            (None, 0, 3, [((2, 0), 0), ((1, 0), 1), ((0, 0), 2), (None, 3)]),
            ((0, 0), 2, 2, [((2, 0), 0), ((1, 0), 1), ((0, 0), 2)]),
        ],
    }
    run = functools.partial(attend, own=own, scalars=scalars, mask=mask)
    sums = run(
        FAR_HEADS,
        (),
        FAR,
        sums=sums,
        payloads=[far_next, far_two, far_three],
        variants=far,
        more=True,
        name="far_heads",
    )
    sums = run(
        EARLY,
        (MAIN,),
        0,
        sums=sums,
        payloads=[down, down_two, up, up_two],
        variants=main,
        more=False,
        name="early_heads",
    )
    sums = run(
        LATE,
        (MAIN,),
        EARLY,
        sums=sums,
        payloads=[late_down, late_down_two, late_up, late_up_two],
        variants=main,
        more=False,
        name="late_heads",
    )
    return sums, anchor


def noise_window(noisy_latent):
    frames, height, breadth, channels = noisy_latent.shape
    own = noisy_latent.transpose(1, 2, 0, 3).reshape(height, breadth, frames * channels)
    earlier = from_behind(own[:, :, (frames - 2) * channels :], "span", 1)
    grid = jnp.concatenate([earlier, own], axis=2)
    slab = lax.axis_index("slab")
    edge = jnp.where(slab == 0, grid[:, breadth - 1], grid[:, 0])
    edge = lax.ppermute(edge, "slab", SWAP)[:, None]
    grid = jnp.concatenate(
        [
            jnp.where(slab == 1, edge, 0.0),
            grid,
            jnp.where(slab == 0, edge, 0.0),
            jnp.zeros((height, WINDOW - breadth - 2, grid.shape[2]), grid.dtype),
        ],
        axis=1,
    )
    head = lax.axis_index("head")
    edge = jnp.where(head == 0, grid[height - 1], grid[0])
    edge = lax.ppermute(edge, "head", SWAP)[None]
    grid = jnp.concatenate(
        [jnp.where(head == 1, edge, 0.0), grid, jnp.where(head == 0, edge, 0.0)], axis=0
    )
    return grid.reshape((height + 2) * WINDOW, grid.shape[2])


def cell_selector(height, breadth):
    cell = lax.broadcasted_iota(jnp.int32, ((height + 2) * WINDOW, 4 * TROWS * TCOLS), 0)
    column = lax.broadcasted_iota(jnp.int32, cell.shape, 1)
    y = lax.axis_index("head") * height + cell // WINDOW - 1
    x = lax.axis_index("slab") * breadth + cell % WINDOW - 1
    inside = (y >= 0) & (y < 2 * TROWS) & (x >= 0) & (x < 2 * TCOLS)
    inside = inside & (cell % WINDOW < breadth + 2)
    target = ((y % 2) * 2 + x % 2) * (TROWS * TCOLS) + (y // 2) * TCOLS + x // 2
    return (inside & (column == target)).astype(jnp.bfloat16)


def banded_weight(conv_weight):
    channels = conv_weight.shape[1]
    taps = conv_weight.reshape(3, 3, 3, LAT_CH, channels)
    banded = jnp.stack(
        [
            jnp.pad(taps, ((n, FRAMES_SPAN - 1 - n), (0, 0), (0, 0), (0, 0), (0, 0)))
            for n in range(FRAMES_SPAN)
        ],
        axis=4,
    )
    return banded.transpose(1, 2, 0, 3, 4, 5).reshape(
        3, 3 * (FRAMES_SPAN + 2) * LAT_CH, FRAMES_SPAN * channels
    )


def finish_kernel(
    scalars, mine, other, noise, selector, band, bias, constants, clean, decoded, cells
):
    frames, height, breadth, channels = clean.shape
    patch = constants.shape[0]
    first = scalars[SLAB] == 0
    sums = jnp.concatenate(
        [jnp.where(first, mine[...], other[...]), jnp.where(first, other[...], mine[...])], axis=0
    )
    feature_width = HEADS * HD
    row_mean = sums[patch : patch + 1] / feature_width
    spread = sums[patch + STAT_ROWS : patch + STAT_ROWS + 1] / feature_width - row_mean * row_mean
    velocity = (
        lax.rsqrt(spread + norm_eps) * (sums[:patch] - constants[:, 0:1] * row_mean)
        + constants[:, 1:2]
    )
    tokens = TROWS * TCOLS
    lane = lax.broadcasted_iota(jnp.int32, velocity.shape, 1)
    velocity = jnp.where((lane >= 2 * tokens) | (scalars[PLACE] > 0), velocity, 0.0)
    columns = jnp.concatenate(
        [
            jnp.concatenate(
                [
                    velocity[
                        part * channels : (part + 1) * channels,
                        frame * tokens : (frame + 1) * tokens,
                    ]
                    for part in range(4)
                ],
                axis=1,
            )
            for frame in range(frames + 2)
        ],
        axis=0,
    )
    high = columns.astype(jnp.bfloat16)
    low = (columns - high.astype(jnp.float32)).astype(jnp.bfloat16)
    chosen = sum(
        lax.dot_general(
            selector[...], part, (((1,), (1,)), ((), ())), preferred_element_type=jnp.float32
        )
        for part in (high, low)
    )
    count = (height + 2) * WINDOW
    cells[:count] = noise[...] - noise_level * chosen
    cells[count:] = jnp.zeros_like(cells[count:])
    for frame in range(frames):
        lanes = slice((frame + 2) * channels, (frame + 3) * channels)
        for y in range(height):
            start = (y + 1) * WINDOW + 1
            clean[frame, y] = cells[start : start + breadth, lanes]
    shifted = jnp.concatenate(
        [cells[tap : tap + count] for tap in range(3)], axis=1
    ).astype(jnp.bfloat16)
    total = jnp.broadcast_to(bias[...], (height * breadth, bias.shape[1]))
    for tap in range(3):
        block = jnp.concatenate(
            [
                shifted[(y + tap) * WINDOW : (y + tap) * WINDOW + breadth]
                for y in range(height)
            ],
            axis=0,
        )
        total = total + jnp.dot(block, band[tap], preferred_element_type=jnp.float32)
    outputs = decoded.shape[3]
    total = total.astype(decoded.dtype)
    for frame in range(frames):
        decoded[frame] = total[:, frame * outputs : (frame + 1) * outputs].reshape(
            height, breadth, outputs
        )


def finish(scalars, mine, other, noise, selector, band, bias, constants, shape, outputs):
    whole = pl.BlockSpec(memory_space=pltpu.VMEM)
    frames, height, breadth, channels = shape
    rows = (height + 2) * WINDOW
    return pl.pallas_call(
        finish_kernel,
        name="finish",
        out_shape=(
            jax.ShapeDtypeStruct(shape, jnp.float32),
            jax.ShapeDtypeStruct((frames, height, breadth, outputs), jnp.bfloat16),
        ),
        in_specs=[pl.BlockSpec(memory_space=pltpu.SMEM)] + [whole] * 7,
        out_specs=(whole, whole),
        scratch_shapes=[pltpu.VMEM((rows + 8, (frames + 2) * channels), jnp.float32)],
        compiler_params=pltpu.CompilerParams(vmem_limit_bytes=32 << 20),
    )(scalars, mine, other, noise, selector, band, bias, constants)


def per_device(
    queries,
    keys,
    values,
    span_mask,
    head_gain,
    head_shift,
    patch_weight,
    noisy_latent,
    conv_weight,
    conv_bias,
):
    heads_dev = queries.shape[1] // HD
    if not plan_fits(
        heads_dev, lax.axis_size("span"), lax.axis_size("slab"), lax.axis_size("head")
    ):
        return gathered_plan(
            queries,
            keys,
            values,
            span_mask,
            head_gain,
            head_shift,
            patch_weight,
            noisy_latent,
            conv_weight,
            conv_bias,
        )
    place = lax.axis_index("span")
    slab = lax.axis_index("slab")
    scalars = scalar_operand(heads_dev // lax.axis_size("slab"))
    sums, anchor = token_sums(
        scalars, queries, keys, values, span_mask, head_gain, patch_weight
    )

    noisy, weight, gain, shift, taps, bias, _ = lax.optimization_barrier(
        (noisy_latent, patch_weight, head_gain, head_shift, conv_weight, conv_bias, anchor)
    )
    _, height, breadth, _ = noisy.shape
    noise = noise_window(noisy)
    wide_weight = weight.T.astype(jnp.float32)
    constants = jnp.stack(
        [
            jnp.sum(wide_weight * gain[None, :], axis=1),
            jnp.sum(wide_weight * shift[None, :], axis=1),
        ],
        axis=1,
    )
    constants = constants + lax.ppermute(constants, "head", SWAP)
    selector = cell_selector(height, breadth)
    band = banded_weight(taps)
    bias = jnp.tile(bias, FRAMES_SPAN)[None, :]

    half = sums.shape[1] // 2
    mine = lax.dynamic_slice_in_dim(sums, slab * half, half, 1)
    theirs = lax.dynamic_slice_in_dim(sums, (1 - slab) * half, half, 1)
    mine = mine + lax.ppermute(theirs, "slab", SWAP)
    own, after, third = mine[0], mine[1], mine[2]
    skip = TROWS * TCOLS
    from_one = lax.ppermute(
        jnp.concatenate([own[:, skip:], after], axis=1), "span", [(0, 1), (1, 2), (2, 3)]
    )
    to_current = lax.ppermute(third, "span", [(1, 3), (3, 2)])
    to_before = lax.ppermute(after[:, skip:], "span", [(0, 2), (1, 3)])
    kept = jnp.concatenate([jnp.where(place == 3, third[:, skip:], 0.0), own], axis=1)
    total = kept + from_one + jnp.concatenate([to_before, to_current], axis=1)
    total = total + lax.ppermute(total, "head", SWAP)
    other = lax.ppermute(total, "slab", SWAP)
    return finish(
        scalars,
        total,
        other,
        noise,
        selector,
        band,
        bias,
        constants,
        noisy_latent.shape,
        conv_weight.shape[1],
    )


def solution(mesh):
    placed = (
        P(("groups", "span"), "head"),
        P(("groups", "span", "slab"), "head"),
        P(("groups", "span", "slab"), "head"),
        P("groups", None),
        P("head"),
        P("head"),
        P("head", None),
        P(("groups", "span"), "head", "slab", None),
        P(),
        P(),
    )
    return jax.shard_map(
        per_device,
        mesh=mesh,
        in_specs=placed,
        out_specs=(
            P(("groups", "span"), "head", "slab", None),
            P(("groups", "span"), "head", "slab", None),
        ),
        check_vma=False,
    )
```

```python
import functools
import math

import jax
import jax.numpy as jnp
import numpy as np
from jax import lax
from jax.experimental import pallas as pl
from jax.experimental.pallas import tpu as pltpu
from jax.sharding import PartitionSpec as P

HEADS = 40
HD = 128
LAT_CH = 16
FRAMES_SPAN = 3
TROWS = 8
TCOLS = 16


neg_big = -1e30
noise_level = 0.75
norm_eps = 1e-06


def with_halo(cells, sides, width):
    for axis, dim in sides:
        count = lax.axis_size(axis)
        ends = count - 1
        head = lax.slice_in_dim(cells, 0, width, axis=dim)
        tail = lax.slice_in_dim(cells, cells.shape[dim] - width, cells.shape[dim], axis=dim)
        cells = jnp.concatenate(
            [
                lax.ppermute(tail, axis, [(i, (i + 1) % count) for i in range(ends)]),
                cells,
                lax.ppermute(head, axis, [((i + 1) % count, i) for i in range(ends)]),
            ],
            axis=dim,
        )
    return cells


def from_behind(value, axis, by):
    size = lax.axis_size(axis)
    pairs = [(i, i + by) for i in range(size) if 0 <= i + by < size]
    return lax.ppermute(value, axis, pairs)


def block_length(total_rows):
    block_size = total_rows
    while block_size > 768 and block_size % 2 == 0:
        block_size = block_size // 2
    return block_size


def fold_keys(partial_state, key_value, query_block, mask_row, rows_span):
    keys_piece, values_piece = key_value
    heads_dev = query_block.shape[1]
    piece_rows = keys_piece.shape[0]
    length = block_length(piece_rows)
    span_count = mask_row.shape[0]
    score_scale = 1.0 / math.sqrt(HD)
    span_ids = jnp.arange(span_count, dtype=jnp.int32)

    def one_block(carry_state, block_index):
        running_max, running_sum, weighted = carry_state
        offset = block_index * length
        key_block = lax.dynamic_slice_in_dim(keys_piece, offset, length, 0).reshape(
            length, heads_dev, HD
        )
        value_block = lax.dynamic_slice_in_dim(values_piece, offset, length, 0).reshape(
            length, heads_dev, HD
        )
        key_span = (offset + jnp.arange(length, dtype=jnp.int32)) // rows_span
        allowed = (
            jnp.sum(jnp.where(key_span[:, None] == span_ids[None, :], mask_row[None, :], 0), axis=1)
            > 0
        )
        scores = (
            jnp.einsum("qhd,khd->hqk", query_block, key_block, preferred_element_type=jnp.float32)
            * score_scale
        )
        scores = jnp.where(allowed[None, None, :], scores, neg_big)
        new_max = jnp.maximum(running_max, jnp.max(scores, axis=2))
        weights = jnp.where(allowed[None, None, :], jnp.exp(scores - new_max[:, :, None]), 0.0)
        factor = jnp.exp(running_max - new_max)
        running_sum = running_sum * factor + jnp.sum(weights, axis=2)
        weighted = weighted * factor.T[:, :, None] + jnp.einsum(
            "hqk,khd->qhd",
            weights.astype(jnp.bfloat16),
            value_block,
            preferred_element_type=jnp.float32,
        )
        return ((new_max, running_sum, weighted), None)

    result, unused = lax.scan(
        one_block, partial_state, jnp.arange(piece_rows // length, dtype=jnp.int32)
    )
    return result


def gathered_plan(
    queries,
    keys,
    values,
    span_mask,
    head_gain,
    head_shift,
    patch_weight,
    noisy_latent,
    conv_weight,
    conv_bias,
):
    heads_dev = queries.shape[1] // HD
    slab_count = lax.axis_size("slab")
    col_dev = TCOLS // slab_count
    slab_place = lax.axis_index("slab")
    span_place = lax.axis_index("span")
    mask_row = lax.dynamic_slice_in_dim(span_mask, span_place, 1, 0)[0]
    token_grid = queries.reshape(FRAMES_SPAN, TROWS, TCOLS, queries.shape[-1])
    picked = lax.dynamic_slice_in_dim(token_grid, slab_place * col_dev, col_dev, 2)
    own_queries = picked.reshape(FRAMES_SPAN * TROWS * col_dev, queries.shape[-1]).reshape(
        -1, heads_dev, HD
    )
    query_rows = own_queries.shape[0]
    rows_span = keys.shape[0] * slab_count
    running_max, running_sum, weighted = fold_keys(
        (
            jnp.full((heads_dev, query_rows), neg_big, jnp.float32),
            jnp.zeros((heads_dev, query_rows), jnp.float32),
            jnp.zeros((query_rows, heads_dev, HD), jnp.float32),
        ),
        (
            lax.all_gather(keys, ("span", "slab"), axis=0, tiled=True),
            lax.all_gather(values, ("span", "slab"), axis=0, tiled=True),
        ),
        own_queries,
        mask_row,
        rows_span,
    )
    attended = (
        (weighted / running_sum.T[:, :, None])
        .astype(jnp.bfloat16)
        .reshape(query_rows, heads_dev * HD)
    )
    feature_width = HEADS * HD
    values32 = attended.astype(jnp.float32)
    row_total = jnp.sum(values32, axis=1)
    row_squares = jnp.sum(values32 * values32, axis=1)
    row_total, row_squares = lax.psum((row_total, row_squares), "head")
    row_mean = row_total / feature_width
    spread = row_squares / feature_width - row_mean * row_mean
    normed = (
        (values32 - row_mean[:, None]) * lax.rsqrt(spread + norm_eps)[:, None] * head_gain[None, :]
        + head_shift[None, :]
    ).astype(jnp.bfloat16)
    normed_grid = normed.reshape(FRAMES_SPAN, TROWS, col_dev, normed.shape[-1])
    own_rows = TROWS // lax.axis_size("head")
    picked = normed_grid
    product = jnp.dot(
        picked.reshape(-1, picked.shape[-1]), patch_weight, preferred_element_type=jnp.float32
    )
    velocity = lax.psum_scatter(
        product.reshape(
            FRAMES_SPAN, own_rows * lax.axis_size("head"), col_dev * patch_weight.shape[1]
        )
        .transpose(1, 0, 2)
        .reshape(own_rows * lax.axis_size("head"), -1)
        .astype(jnp.bfloat16),
        "head",
        scatter_dimension=0,
        tiled=True,
    ).astype(jnp.float32)
    rows_dev = velocity.shape[0]
    patch_cells = (
        velocity.reshape(rows_dev, FRAMES_SPAN, col_dev, 2, 2, LAT_CH)
        .transpose(1, 0, 3, 2, 4, 5)
        .reshape(FRAMES_SPAN, 2 * rows_dev, 2 * col_dev, LAT_CH)
    )
    clean_latent = noisy_latent - noise_level * patch_cells
    latent_input = clean_latent.astype(jnp.bfloat16)
    framed = with_halo(latent_input, (("head", 1), ("slab", 2)), 1)
    earlier = from_behind(framed[FRAMES_SPAN - 2 :], "span", 1)
    stacked = jnp.concatenate([earlier, framed], axis=0)
    height = clean_latent.shape[1]
    breadth = clean_latent.shape[2]
    columns = jnp.concatenate(
        [
            stacked[
                frame_tap : frame_tap + FRAMES_SPAN,
                row_tap : row_tap + height,
                col_tap : col_tap + breadth,
                :,
            ]
            for frame_tap in range(3)
            for row_tap in range(3)
            for col_tap in range(3)
        ],
        axis=-1,
    )
    decoded = (
        jnp.dot(
            columns.reshape(FRAMES_SPAN * height * breadth, 27 * LAT_CH),
            conv_weight,
            preferred_element_type=jnp.float32,
        )
        + conv_bias[None, :]
    )
    decoded = decoded.astype(jnp.bfloat16).reshape(
        FRAMES_SPAN, height, breadth, conv_weight.shape[1]
    )
    return (clean_latent, decoded)


NEAR_HEADS = 4
MIDDLE_HEADS = 4
FAR_HEADS = 2
MIDDLE = NEAR_HEADS
FAR = NEAR_HEADS + MIDDLE_HEADS
EARLY = 3
LATE = NEAR_HEADS - EARLY
STAT_ROWS = 8
SLOTS = 3
QUERY_ROWS = 192
SWAP = [(0, 1), (1, 0)]
WINDOW = 32
GRANT = 20 << 20

OWN, OTHER, DOWN, UP, MAIN, PLACE, SLAB = range(7)


def plan_fits(heads_dev, span_count, slab_count, head_count):
    return (
        span_count == 4
        and slab_count == 2
        and head_count == 2
        and heads_dev == slab_count * (NEAR_HEADS + MIDDLE_HEADS + FAR_HEADS)
    )


def scalar_operand(heads):
    by_place = np.array(
        [
            [0, heads, MIDDLE, 0, MIDDLE, 0, 0, 0],
            [0, heads, MIDDLE, MIDDLE, 0, 1, 0, 0],
            [0, heads, 0, 0, MIDDLE, 2, 0, 0],
            [0, heads, MIDDLE, 0, 0, 3, 0, 0],
        ],
        np.int32,
    )
    by_slab = np.array([heads, -heads, 0, 0, 0, 0, 1, 0], np.int32)
    row = lax.dynamic_slice_in_dim(jnp.array(by_place), lax.axis_index("span"), 1, 0)[0]
    return row + lax.axis_index("slab") * jnp.array(by_slab)


def pack_kernel(inputs, copies, scalars, *refs):
    ins, outs, semaphores = refs[:inputs], refs[inputs:-1], refs[-1]
    started = []
    for number, (source, row, rows, entries, shift, target, at, heads) in enumerate(copies):
        head = shift
        for entry in entries:
            head = head + scalars[entry]
        column = pl.multiple_of(head * HD, HD)
        copy = pltpu.make_async_copy(
            ins[source].at[pl.ds(row, rows), pl.ds(column, heads * HD)],
            outs[target].at[pl.ds(at, rows), :],
            semaphores.at[number],
        )
        copy.start()
        started.append(copy)
    for copy in started:
        copy.wait()


def pack(scalars, arrays, shapes, copies, name):
    moved = sum(2 * 2 * rows * heads * HD for _, _, rows, _, _, _, _, heads in copies)
    return pl.pallas_call(
        functools.partial(pack_kernel, len(arrays), copies),
        name=name,
        out_shape=[jax.ShapeDtypeStruct(shape, jnp.bfloat16) for shape in shapes],
        grid_spec=pltpu.PrefetchScalarGridSpec(
            num_scalar_prefetch=1,
            grid=(1,),
            in_specs=[pl.BlockSpec(memory_space=pl.ANY)] * len(arrays),
            out_specs=[pl.BlockSpec(shape, lambda i, scalars: (0, 0)) for shape in shapes],
            scratch_shapes=[pltpu.SemaphoreType.DMA((len(copies),))],
        ),
        compiler_params=pltpu.CompilerParams(vmem_limit_bytes=GRANT),
        cost_estimate=pl.CostEstimate(flops=0, bytes_accessed=moved, transcendentals=0),
    )(scalars, *arrays)


def pack_messages(scalars, messages, queries, keys, values, received, name):
    rows = queries.shape[0]
    half = rows // 2
    copies, shapes = [], []
    for target, (entry, shift, heads, whole) in enumerate(messages):
        entries = () if entry is None else (entry,)
        at = 0
        if whole:
            copies.append((0, 0, rows, (OWN,) + entries, shift, target, 0, heads))
            at = rows
        for part, array in enumerate((1, 2)):
            copies.append((array, 0, half, (OWN,) + entries, shift, target, at, heads))
            copies.append((3, part * half, half, entries, shift, target, at + half, heads))
            at += rows
        shapes.append((at, heads * HD))
    return pack(scalars, (queries, keys, values, received), shapes, copies, name)


def attend_kernel(variants, extra, span_count, scalars, mask, *refs):
    query_own, key_own, value_own, received, weight, gain, sums_in = refs[:7]
    more = refs[7 : 7 + extra]
    payloads, (sums_out, folded, squares) = refs[7 + extra : -3], refs[-3:]
    rows = query_own.shape[0]
    half = rows // 2
    step = pl.program_id(0)
    to_exp2 = math.log2(math.e) / math.sqrt(HD)

    @pl.when(step == 0)
    def _():
        folded[...] = jnp.zeros_like(folded)
        squares[...] = jnp.zeros_like(squares)

    def query_of(source):
        if source is None:
            return query_own[...]
        if source[0] < 0:
            return more[0][:, source[1] * HD : (source[1] + 1) * HD]
        return payloads[source[0]][:rows]

    def pair_of(source):
        if source is None:
            parts = (key_own[...], received[:half], value_own[...], received[half:])
        elif source[0] < 0:
            lanes = slice(source[1] * HD, (source[1] + 1) * HD)
            parts = (more[1][:, lanes], more[3][:half, lanes], more[2][:, lanes], more[3][half:, lanes])
        else:
            payload = payloads[source[0]]
            start = payload.shape[0] - 2 * rows
            return payload[start : start + rows], payload[start + rows :]
        return jnp.concatenate(parts[:2], axis=0), jnp.concatenate(parts[2:], axis=0)

    def projector(extra_head):
        if extra_head is None:
            scaled = weight[...].astype(jnp.float32) * gain[...]
        else:
            lanes = slice(extra_head * HD, (extra_head + 1) * HD)
            scaled = more[4][:, lanes].astype(jnp.float32) * more[5][:, lanes]
        high = scaled.astype(jnp.bfloat16)
        low = (scaled - high.astype(jnp.float32)).astype(jnp.bfloat16)
        return jnp.concatenate([high, low, jnp.ones((16, HD), jnp.bfloat16)], axis=0)

    def one_query(source, slot, query_span, key_sources):
        query = query_of(source)
        pairs = [pair_of(key_source) for key_source, _ in key_sources]
        open_to = [
            None if key_span == query_span else mask[query_span * span_count + key_span] > 0
            for _, key_span in key_sources
        ]
        keys_in = jnp.concatenate([pair[0] for pair in pairs], axis=0)
        ones_block = jnp.ones((rows, HD), jnp.bfloat16)
        values_in = jnp.concatenate(
            [jnp.concatenate([pair[1], ones_block], axis=1) for pair in pairs], axis=0
        )
        pieces = []
        for row in range(0, rows, QUERY_ROWS):
            score = lax.dot_general(
                query[row : row + QUERY_ROWS],
                keys_in,
                (((1,), (1,)), ((), ())),
                preferred_element_type=jnp.float32,
            )
            best = None
            for number, is_open in enumerate(open_to):
                start = number * rows
                block = score[:, start : start + HD]
                for lane in range(HD, rows, HD):
                    block = jnp.maximum(block, score[:, start + lane : start + lane + HD])
                if is_open is not None:
                    block = jnp.where(is_open, block, neg_big)
                best = block if best is None else jnp.maximum(best, block)
            top = jnp.max(best, axis=1, keepdims=True)
            weights = []
            for number, is_open in enumerate(open_to):
                start = number * rows
                shift = top if is_open is None else jnp.where(is_open, top, -neg_big)
                weights.append(
                    jnp.exp2((score[:, start : start + rows] - shift) * to_exp2).astype(jnp.bfloat16)
                )
            both = jnp.dot(
                jnp.concatenate(weights, axis=1), values_in, preferred_element_type=jnp.float32
            )
            pieces.append((both[:, :HD] / both[:, HD:]).astype(jnp.bfloat16))
        attended = jnp.concatenate(pieces, axis=0)
        extra_head = source[1] if source is not None and source[0] < 0 else None
        folded[slot] += lax.dot_general(
            projector(extra_head),
            attended,
            (((1,), (1,)), ((), ())),
            preferred_element_type=jnp.float32,
        )
        wide = attended.astype(jnp.float32)
        squares[slot] += wide * wide

    for place, tasks in variants.items():

        @pl.when(scalars[PLACE] == place)
        def _():
            for task in tasks:
                one_query(*task)

    @pl.when(step == pl.num_programs(0) - 1)
    def _():
        ones_rows = jnp.ones((STAT_ROWS, HD), jnp.bfloat16)
        patch = weight.shape[0]
        for slot in range(SLOTS):
            left = squares[slot]
            total = jnp.zeros((STAT_ROWS, rows), jnp.float32)
            for _ in range(3):
                piece = left.astype(jnp.bfloat16)
                left = left - piece.astype(jnp.float32)
                total = total + lax.dot_general(
                    ones_rows, piece, (((1,), (1,)), ((), ())), preferred_element_type=jnp.float32
                )
            done = folded[slot]
            sums_out[slot] = sums_in[slot] + jnp.concatenate(
                [
                    done[:patch] + done[patch : 2 * patch],
                    done[2 * patch : 2 * patch + STAT_ROWS],
                    total,
                ],
                axis=0,
            )


def attend(steps, entries, first, own, scalars, mask, sums, payloads, variants, more, name):
    queries, keys, values, received, weight, gain = own
    rows = queries.shape[0]
    half = rows // 2
    patch = weight.shape[0]

    def column(height, own_column):
        def index(i, scalars, mask):
            head = first + i + (scalars[OWN] if own_column else 0)
            for entry in entries:
                head = head + scalars[entry]
            return (0, head)

        return pl.BlockSpec((height, HD), index)

    def two_columns(height, own_column):
        return pl.BlockSpec(
            (height, 2 * HD),
            lambda i, scalars, mask: (0, i + (scalars[OWN] // 2 if own_column else 0)),
        )

    sums_spec = pl.BlockSpec(sums.shape, lambda i, scalars, mask: (0, 0, 0))
    in_specs = [
        column(rows, True),
        column(half, True),
        column(half, True),
        column(rows, False),
        column(patch, True),
        column(1, True),
        sums_spec,
    ]
    arrays = [queries, keys, values, received, weight, gain, sums]
    extra = 0
    if more:
        extra = 6
        in_specs += [
            two_columns(rows, True),
            two_columns(half, True),
            two_columns(half, True),
            two_columns(rows, False),
            two_columns(patch, True),
            two_columns(1, True),
        ]
        arrays += [queries, keys, values, received, weight, gain]
    in_specs += [
        pl.BlockSpec(
            (payload.shape[0], HD), lambda i, scalars, mask, start=start: (0, start + i)
        )
        for payload, start in payloads
    ]
    arrays += [payload for payload, _ in payloads]
    pairs = steps * max(sum(len(task[3]) for task in tasks) for tasks in variants.values())
    span_count = math.isqrt(mask.shape[0])
    return pl.pallas_call(
        functools.partial(attend_kernel, variants, extra, span_count),
        name=name,
        out_shape=jax.ShapeDtypeStruct(sums.shape, sums.dtype),
        grid_spec=pltpu.PrefetchScalarGridSpec(
            num_scalar_prefetch=2,
            grid=(steps,),
            in_specs=in_specs,
            out_specs=sums_spec,
            scratch_shapes=[
                pltpu.VMEM((SLOTS, 2 * patch + 16, rows), jnp.float32),
                pltpu.VMEM((SLOTS, rows, HD), jnp.float32),
            ],
        ),
        compiler_params=pltpu.CompilerParams(vmem_limit_bytes=GRANT),
        cost_estimate=pl.CostEstimate(
            flops=pairs * 4 * rows * rows * HD,
            bytes_accessed=steps * HD * 2 * sum(spec.block_shape[0] for spec in in_specs[:4]),
            transcendentals=pairs * rows * rows,
        ),
    )(scalars, mask, *arrays)


def token_sums(scalars, queries, keys, values, span_mask, head_gain, patch_weight):
    rows = queries.shape[0]
    heads = NEAR_HEADS + MIDDLE_HEADS + FAR_HEADS
    queries, keys, values = (
        pltpu.with_memory_space_constraint(array, pltpu.HBM) for array in (queries, keys, values)
    )
    half = rows // 2
    (handed,) = pack(
        scalars,
        (keys, values),
        [(rows, heads * HD)],
        [(0, 0, half, (OTHER,), 0, 0, 0, heads), (1, 0, half, (OTHER,), 0, 0, half, heads)],
        "pack_handed",
    )
    received = lax.ppermute(handed, "slab", SWAP)
    send = lambda value, *pairs: lax.ppermute(value, "span", list(pairs))

    def bring(messages, source, name):
        return pack_messages(scalars, messages, queries, keys, values, source, name)

    down, up, down_two, up_two = bring(
        [
            (DOWN, 0, EARLY, True),
            (UP, 0, NEAR_HEADS, False),
            (None, 0, EARLY, True),
            (None, MIDDLE, EARLY, False),
        ],
        received,
        "pack_first",
    )
    down = send(down, (1, 0), (2, 1), (3, 2))
    up = send(up, (0, 1), (1, 2))
    down_two = send(down_two, (3, 1))
    up_two = send(up_two, (0, 2))
    source, _ = lax.optimization_barrier((received, up))
    far_all, far_pair, late_down, late_down_two, late_up_two = bring(
        [
            (None, FAR, FAR_HEADS, True),
            (None, FAR, FAR_HEADS, False),
            (DOWN, EARLY, LATE, True),
            (None, EARLY, LATE, True),
            (None, MIDDLE + EARLY, LATE, False),
        ],
        source,
        "pack_second",
    )
    far_two = send(far_pair, (1, 3))
    far_three = send(far_pair, (0, 3))
    far_next = send(far_all, (2, 3), (1, 0))
    late_down, late_down_two, late_up_two, _ = lax.optimization_barrier(
        (late_down, late_down_two, late_up_two, down)
    )
    late_down = send(late_down, (1, 0), (2, 1), (3, 2))
    late_down_two = send(late_down_two, (3, 1))
    late_up_two = send(late_up_two, (0, 2))

    mask = span_mask.reshape(-1)
    weight = patch_weight.T
    own = (queries, keys, values, received, weight, head_gain[None, :])
    sums = jnp.zeros((SLOTS, weight.shape[0] + 2 * STAT_ROWS, rows), jnp.float32)
    on_one, on_two, back_one, back_two = (0, 0), (1, 0), (2, 0), (3, 0)
    main = {
        0: [(None, 0, 0, [(None, 0)]), (on_one, 1, 1, [(None, 0), (on_one, 1)])],
        1: [
            (on_two, 2, 3, [(back_one, 0), (None, 1), (on_one, 2), (on_two, 3)]),
            (on_one, 1, 2, [(back_one, 0), (None, 1), (on_one, 2)]),
            (None, 0, 1, [(back_one, 0), (None, 1)]),
        ],
        2: [
            (on_one, 1, 3, [(back_two, 0), (back_one, 1), (None, 2), (on_one, 3)]),
            (None, 0, 2, [(back_two, 0), (back_one, 1), (None, 2)]),
        ],
    }
    extra = [((-1, lane), 0, 0, [((-1, lane), 0)]) for lane in range(2)]
    far = {
        0: [(None, 0, 0, [(None, 0)]), ((0, 0), 1, 1, [(None, 0), ((0, 0), 1)])] + extra,
        3: [
            (None, 0, 3, [((2, 0), 0), ((1, 0), 1), ((0, 0), 2), (None, 3)]),
            ((0, 0), 2, 2, [((2, 0), 0), ((1, 0), 1), ((0, 0), 2)]),
        ],
    }
    run = functools.partial(attend, own=own, scalars=scalars, mask=mask)
    sums = run(
        EARLY,
        (MAIN,),
        0,
        sums=sums,
        payloads=[(down, 0), (down_two, 0), (up, 0), (up_two, 0)],
        variants=main,
        more=False,
        name="early_heads",
    )
    sums = run(
        FAR_HEADS,
        (),
        FAR,
        sums=sums,
        payloads=[(far_next, 0), (far_two, 0), (far_three, 0)],
        variants=far,
        more=True,
        name="far_heads",
    )

    def last(sums):
        return run(
            LATE,
            (MAIN,),
            EARLY,
            sums=sums,
            payloads=[(late_down, 0), (late_down_two, 0), (up, EARLY), (late_up_two, 0)],
            variants=main,
            more=False,
            name="late_heads",
        )

    return sums, last, up_two


def noise_window(noisy_latent):
    frames, height, breadth, channels = noisy_latent.shape
    own = noisy_latent.transpose(1, 2, 0, 3).reshape(height, breadth, frames * channels)
    earlier = from_behind(own[:, :, (frames - 2) * channels :], "span", 1)
    grid = jnp.concatenate([earlier, own], axis=2)
    slab = lax.axis_index("slab")
    edge = jnp.where(slab == 0, grid[:, breadth - 1], grid[:, 0])
    edge = lax.ppermute(edge, "slab", SWAP)[:, None]
    grid = jnp.concatenate(
        [
            jnp.where(slab == 1, edge, 0.0),
            grid,
            jnp.where(slab == 0, edge, 0.0),
            jnp.zeros((height, WINDOW - breadth - 2, grid.shape[2]), grid.dtype),
        ],
        axis=1,
    )
    head = lax.axis_index("head")
    edge = jnp.where(head == 0, grid[height - 1], grid[0])
    edge = lax.ppermute(edge, "head", SWAP)[None]
    grid = jnp.concatenate(
        [jnp.where(head == 1, edge, 0.0), grid, jnp.where(head == 0, edge, 0.0)], axis=0
    )
    return grid.reshape((height + 2) * WINDOW, grid.shape[2])


def cell_selector(height, breadth):
    cell = lax.broadcasted_iota(jnp.int32, ((height + 2) * WINDOW, 4 * TROWS * TCOLS), 0)
    column = lax.broadcasted_iota(jnp.int32, cell.shape, 1)
    y = lax.axis_index("head") * height + cell // WINDOW - 1
    x = lax.axis_index("slab") * breadth + cell % WINDOW - 1
    inside = (y >= 0) & (y < 2 * TROWS) & (x >= 0) & (x < 2 * TCOLS)
    inside = inside & (cell % WINDOW < breadth + 2)
    target = ((y % 2) * 2 + x % 2) * (TROWS * TCOLS) + (y // 2) * TCOLS + x // 2
    return (inside & (column == target)).astype(jnp.bfloat16)


def banded_weight(conv_weight):
    channels = conv_weight.shape[1]
    taps = conv_weight.reshape(3, 3, 3, LAT_CH, channels)
    banded = jnp.stack(
        [
            jnp.pad(taps, ((n, FRAMES_SPAN - 1 - n), (0, 0), (0, 0), (0, 0), (0, 0)))
            for n in range(FRAMES_SPAN)
        ],
        axis=4,
    )
    return banded.transpose(1, 2, 0, 3, 4, 5).reshape(
        3, 3 * (FRAMES_SPAN + 2) * LAT_CH, FRAMES_SPAN * channels
    )


def finish_kernel(
    scalars, mine, other, noise, selector, band, bias, constants, clean, decoded, cells
):
    frames, height, breadth, channels = clean.shape
    patch = constants.shape[0]
    first = scalars[SLAB] == 0
    sums = jnp.concatenate(
        [jnp.where(first, mine[...], other[...]), jnp.where(first, other[...], mine[...])], axis=0
    )
    feature_width = HEADS * HD
    row_mean = sums[patch : patch + 1] / feature_width
    spread = sums[patch + STAT_ROWS : patch + STAT_ROWS + 1] / feature_width - row_mean * row_mean
    velocity = (
        lax.rsqrt(spread + norm_eps) * (sums[:patch] - constants[:, 0:1] * row_mean)
        + constants[:, 1:2]
    )
    tokens = TROWS * TCOLS
    lane = lax.broadcasted_iota(jnp.int32, velocity.shape, 1)
    velocity = jnp.where((lane >= 2 * tokens) | (scalars[PLACE] > 0), velocity, 0.0)
    columns = jnp.concatenate(
        [
            jnp.concatenate(
                [
                    velocity[
                        part * channels : (part + 1) * channels,
                        frame * tokens : (frame + 1) * tokens,
                    ]
                    for part in range(4)
                ],
                axis=1,
            )
            for frame in range(frames + 2)
        ],
        axis=0,
    )
    high = columns.astype(jnp.bfloat16)
    low = (columns - high.astype(jnp.float32)).astype(jnp.bfloat16)
    chosen = sum(
        lax.dot_general(
            selector[...], part, (((1,), (1,)), ((), ())), preferred_element_type=jnp.float32
        )
        for part in (high, low)
    )
    count = (height + 2) * WINDOW
    cells[:count] = noise[...] - noise_level * chosen
    cells[count:] = jnp.zeros_like(cells[count:])
    for frame in range(frames):
        lanes = slice((frame + 2) * channels, (frame + 3) * channels)
        for y in range(height):
            start = (y + 1) * WINDOW + 1
            clean[frame, y] = cells[start : start + breadth, lanes]
    shifted = jnp.concatenate(
        [cells[tap : tap + count] for tap in range(3)], axis=1
    ).astype(jnp.bfloat16)
    total = jnp.broadcast_to(bias[...], (height * breadth, bias.shape[1]))
    for tap in range(3):
        block = jnp.concatenate(
            [
                shifted[(y + tap) * WINDOW : (y + tap) * WINDOW + breadth]
                for y in range(height)
            ],
            axis=0,
        )
        total = total + jnp.dot(block, band[tap], preferred_element_type=jnp.float32)
    outputs = decoded.shape[3]
    total = total.astype(decoded.dtype)
    for frame in range(frames):
        decoded[frame] = total[:, frame * outputs : (frame + 1) * outputs].reshape(
            height, breadth, outputs
        )


def finish(scalars, mine, other, noise, selector, band, bias, constants, shape, outputs):
    whole = pl.BlockSpec(memory_space=pltpu.VMEM)
    frames, height, breadth, channels = shape
    rows = (height + 2) * WINDOW
    return pl.pallas_call(
        finish_kernel,
        name="finish",
        out_shape=(
            jax.ShapeDtypeStruct(shape, jnp.float32),
            jax.ShapeDtypeStruct((frames, height, breadth, outputs), jnp.bfloat16),
        ),
        in_specs=[pl.BlockSpec(memory_space=pltpu.SMEM)] + [whole] * 7,
        out_specs=(whole, whole),
        scratch_shapes=[pltpu.VMEM((rows + 8, (frames + 2) * channels), jnp.float32)],
        compiler_params=pltpu.CompilerParams(vmem_limit_bytes=GRANT),
    )(scalars, mine, other, noise, selector, band, bias, constants)


def per_device(
    queries,
    keys,
    values,
    span_mask,
    head_gain,
    head_shift,
    patch_weight,
    noisy_latent,
    conv_weight,
    conv_bias,
):
    heads_dev = queries.shape[1] // HD
    if not plan_fits(
        heads_dev, lax.axis_size("span"), lax.axis_size("slab"), lax.axis_size("head")
    ):
        return gathered_plan(
            queries,
            keys,
            values,
            span_mask,
            head_gain,
            head_shift,
            patch_weight,
            noisy_latent,
            conv_weight,
            conv_bias,
        )
    place = lax.axis_index("span")
    slab = lax.axis_index("slab")
    scalars = scalar_operand(heads_dev // lax.axis_size("slab"))
    sums, last, anchor = token_sums(
        scalars, queries, keys, values, span_mask, head_gain, patch_weight
    )

    noisy, weight, gain, shift, taps, bias, _ = lax.optimization_barrier(
        (noisy_latent, patch_weight, head_gain, head_shift, conv_weight, conv_bias, anchor)
    )
    _, height, breadth, _ = noisy.shape
    noise = noise_window(noisy)
    wide_weight = weight.T.astype(jnp.float32)
    constants = jnp.stack(
        [
            jnp.sum(wide_weight * gain[None, :], axis=1),
            jnp.sum(wide_weight * shift[None, :], axis=1),
        ],
        axis=1,
    )
    constants = constants + lax.ppermute(constants, "head", SWAP)
    selector = cell_selector(height, breadth)
    band = banded_weight(taps)
    bias = jnp.tile(bias, FRAMES_SPAN)[None, :]
    sums, noise, constants, selector, band, bias = lax.optimization_barrier(
        (sums, noise, constants, selector, band, bias)
    )

    sums = last(sums)
    half = sums.shape[1] // 2
    mine = lax.dynamic_slice_in_dim(sums, slab * half, half, 1)
    theirs = lax.dynamic_slice_in_dim(sums, (1 - slab) * half, half, 1)
    mine = mine + lax.ppermute(theirs, "slab", SWAP)
    own, after, third = mine[0], mine[1], mine[2]
    skip = TROWS * TCOLS
    from_one = lax.ppermute(
        jnp.concatenate([own[:, skip:], after], axis=1), "span", [(0, 1), (1, 2), (2, 3)]
    )
    to_current = lax.ppermute(third, "span", [(1, 3), (3, 2)])
    to_before = lax.ppermute(after[:, skip:], "span", [(0, 2), (1, 3)])
    kept = jnp.concatenate([jnp.where(place == 3, third[:, skip:], 0.0), own], axis=1)
    total = kept + from_one + jnp.concatenate([to_before, to_current], axis=1)
    total = total + lax.ppermute(total, "head", SWAP)
    other = lax.ppermute(total, "slab", SWAP)
    return finish(
        scalars,
        total,
        other,
        noise,
        selector,
        band,
        bias,
        constants,
        noisy_latent.shape,
        conv_weight.shape[1],
    )


def solution(mesh):
    placed = (
        P(("groups", "span"), "head"),
        P(("groups", "span", "slab"), "head"),
        P(("groups", "span", "slab"), "head"),
        P("groups", None),
        P("head"),
        P("head"),
        P("head", None),
        P(("groups", "span"), "head", "slab", None),
        P(),
        P(),
    )
    return jax.shard_map(
        per_device,
        mesh=mesh,
        in_specs=placed,
        out_specs=(
            P(("groups", "span"), "head", "slab", None),
            P(("groups", "span"), "head", "slab", None),
        ),
        check_vma=False,
    )
```

```python
import functools
import math
import typing

import jax
import jax.numpy as jnp
import numpy as np
from jax import lax
from jax.experimental import pallas as pl
from jax.experimental.pallas import tpu as pltpu
from jax.sharding import PartitionSpec as P

HEADS = 40
HD = 128
LAT_CH = 16
FRAMES_SPAN = 3
TROWS = 8
TCOLS = 16


neg_big = -1e30
noise_level = 0.75
norm_eps = 1e-06


def with_halo(cells, sides, width):
    for axis, dim in sides:
        count = lax.axis_size(axis)
        ends = count - 1
        head = lax.slice_in_dim(cells, 0, width, axis=dim)
        tail = lax.slice_in_dim(cells, cells.shape[dim] - width, cells.shape[dim], axis=dim)
        cells = jnp.concatenate(
            [
                lax.ppermute(tail, axis, [(i, (i + 1) % count) for i in range(ends)]),
                cells,
                lax.ppermute(head, axis, [((i + 1) % count, i) for i in range(ends)]),
            ],
            axis=dim,
        )
    return cells


def from_behind(value, axis, by):
    size = lax.axis_size(axis)
    pairs = [(i, i + by) for i in range(size) if 0 <= i + by < size]
    return lax.ppermute(value, axis, pairs)


def block_length(total_rows):
    block_size = total_rows
    while block_size > 768 and block_size % 2 == 0:
        block_size = block_size // 2
    return block_size


def fold_keys(partial_state, key_value, query_block, mask_row, rows_span):
    keys_piece, values_piece = key_value
    heads_dev = query_block.shape[1]
    piece_rows = keys_piece.shape[0]
    length = block_length(piece_rows)
    span_count = mask_row.shape[0]
    score_scale = 1.0 / math.sqrt(HD)
    span_ids = jnp.arange(span_count, dtype=jnp.int32)

    def one_block(carry_state, block_index):
        running_max, running_sum, weighted = carry_state
        offset = block_index * length
        key_block = lax.dynamic_slice_in_dim(keys_piece, offset, length, 0).reshape(
            length, heads_dev, HD
        )
        value_block = lax.dynamic_slice_in_dim(values_piece, offset, length, 0).reshape(
            length, heads_dev, HD
        )
        key_span = (offset + jnp.arange(length, dtype=jnp.int32)) // rows_span
        allowed = (
            jnp.sum(jnp.where(key_span[:, None] == span_ids[None, :], mask_row[None, :], 0), axis=1)
            > 0
        )
        scores = (
            jnp.einsum("qhd,khd->hqk", query_block, key_block, preferred_element_type=jnp.float32)
            * score_scale
        )
        scores = jnp.where(allowed[None, None, :], scores, neg_big)
        new_max = jnp.maximum(running_max, jnp.max(scores, axis=2))
        weights = jnp.where(allowed[None, None, :], jnp.exp(scores - new_max[:, :, None]), 0.0)
        factor = jnp.exp(running_max - new_max)
        running_sum = running_sum * factor + jnp.sum(weights, axis=2)
        weighted = weighted * factor.T[:, :, None] + jnp.einsum(
            "hqk,khd->qhd",
            weights.astype(jnp.bfloat16),
            value_block,
            preferred_element_type=jnp.float32,
        )
        return ((new_max, running_sum, weighted), None)

    result, unused = lax.scan(
        one_block, partial_state, jnp.arange(piece_rows // length, dtype=jnp.int32)
    )
    return result


def gathered_plan(
    queries,
    keys,
    values,
    span_mask,
    head_gain,
    head_shift,
    patch_weight,
    noisy_latent,
    conv_weight,
    conv_bias,
):
    heads_dev = queries.shape[1] // HD
    slab_count = lax.axis_size("slab")
    col_dev = TCOLS // slab_count
    slab_place = lax.axis_index("slab")
    span_place = lax.axis_index("span")
    mask_row = lax.dynamic_slice_in_dim(span_mask, span_place, 1, 0)[0]
    token_grid = queries.reshape(FRAMES_SPAN, TROWS, TCOLS, queries.shape[-1])
    picked = lax.dynamic_slice_in_dim(token_grid, slab_place * col_dev, col_dev, 2)
    own_queries = picked.reshape(FRAMES_SPAN * TROWS * col_dev, queries.shape[-1]).reshape(
        -1, heads_dev, HD
    )
    query_rows = own_queries.shape[0]
    rows_span = keys.shape[0] * slab_count
    running_max, running_sum, weighted = fold_keys(
        (
            jnp.full((heads_dev, query_rows), neg_big, jnp.float32),
            jnp.zeros((heads_dev, query_rows), jnp.float32),
            jnp.zeros((query_rows, heads_dev, HD), jnp.float32),
        ),
        (
            lax.all_gather(keys, ("span", "slab"), axis=0, tiled=True),
            lax.all_gather(values, ("span", "slab"), axis=0, tiled=True),
        ),
        own_queries,
        mask_row,
        rows_span,
    )
    attended = (
        (weighted / running_sum.T[:, :, None])
        .astype(jnp.bfloat16)
        .reshape(query_rows, heads_dev * HD)
    )
    feature_width = HEADS * HD
    values32 = attended.astype(jnp.float32)
    row_total = jnp.sum(values32, axis=1)
    row_squares = jnp.sum(values32 * values32, axis=1)
    row_total, row_squares = lax.psum((row_total, row_squares), "head")
    row_mean = row_total / feature_width
    spread = row_squares / feature_width - row_mean * row_mean
    normed = (
        (values32 - row_mean[:, None]) * lax.rsqrt(spread + norm_eps)[:, None] * head_gain[None, :]
        + head_shift[None, :]
    ).astype(jnp.bfloat16)
    normed_grid = normed.reshape(FRAMES_SPAN, TROWS, col_dev, normed.shape[-1])
    own_rows = TROWS // lax.axis_size("head")
    picked = normed_grid
    product = jnp.dot(
        picked.reshape(-1, picked.shape[-1]), patch_weight, preferred_element_type=jnp.float32
    )
    velocity = lax.psum_scatter(
        product.reshape(
            FRAMES_SPAN, own_rows * lax.axis_size("head"), col_dev * patch_weight.shape[1]
        )
        .transpose(1, 0, 2)
        .reshape(own_rows * lax.axis_size("head"), -1)
        .astype(jnp.bfloat16),
        "head",
        scatter_dimension=0,
        tiled=True,
    ).astype(jnp.float32)
    rows_dev = velocity.shape[0]
    patch_cells = (
        velocity.reshape(rows_dev, FRAMES_SPAN, col_dev, 2, 2, LAT_CH)
        .transpose(1, 0, 3, 2, 4, 5)
        .reshape(FRAMES_SPAN, 2 * rows_dev, 2 * col_dev, LAT_CH)
    )
    clean_latent = noisy_latent - noise_level * patch_cells
    latent_input = clean_latent.astype(jnp.bfloat16)
    framed = with_halo(latent_input, (("head", 1), ("slab", 2)), 1)
    earlier = from_behind(framed[FRAMES_SPAN - 2 :], "span", 1)
    stacked = jnp.concatenate([earlier, framed], axis=0)
    height = clean_latent.shape[1]
    breadth = clean_latent.shape[2]
    columns = jnp.concatenate(
        [
            stacked[
                frame_tap : frame_tap + FRAMES_SPAN,
                row_tap : row_tap + height,
                col_tap : col_tap + breadth,
                :,
            ]
            for frame_tap in range(3)
            for row_tap in range(3)
            for col_tap in range(3)
        ],
        axis=-1,
    )
    decoded = (
        jnp.dot(
            columns.reshape(FRAMES_SPAN * height * breadth, 27 * LAT_CH),
            conv_weight,
            preferred_element_type=jnp.float32,
        )
        + conv_bias[None, :]
    )
    decoded = decoded.astype(jnp.bfloat16).reshape(
        FRAMES_SPAN, height, breadth, conv_weight.shape[1]
    )
    return (clean_latent, decoded)


NEAR_HEADS = 4
MIDDLE_HEADS = 4
FAR_HEADS = 2
MIDDLE = NEAR_HEADS
FAR = NEAR_HEADS + MIDDLE_HEADS
STAT_ROWS = 8
SLOTS = 3
QUERY_ROWS = 192
SWAP = [(0, 1), (1, 0)]
WINDOW = 32
GRANT = 20 << 20

OWN, OTHER, DOWN, UP, MAIN, LAST, LAST_COLUMN, PLACE, SLAB = range(9)
STEPS = 9


def plan_fits(heads_dev, span_count, slab_count, head_count):
    return (
        span_count == 4
        and slab_count == 2
        and head_count == 2
        and heads_dev == slab_count * (NEAR_HEADS + MIDDLE_HEADS + FAR_HEADS)
    )


def scalar_operand(heads):
    by_place = np.zeros((4, 12), np.int32)
    by_place[:, OTHER] = heads
    by_place[:, DOWN] = [MIDDLE, MIDDLE, 0, MIDDLE]
    by_place[:, UP] = [0, MIDDLE, 0, 0]
    by_place[:, MAIN] = [MIDDLE, 0, MIDDLE, 0]
    by_place[:, LAST] = [0, 2, MIDDLE + 3, 0]
    by_place[:, LAST_COLUMN] = [0, 2, 3, 0]
    by_place[:, PLACE] = range(4)
    by_slab = np.zeros(12, np.int32)
    by_slab[[OWN, OTHER, SLAB]] = heads, -heads, 1
    row = lax.dynamic_slice_in_dim(jnp.array(by_place), lax.axis_index("span"), 1, 0)[0]
    return row + lax.axis_index("slab") * jnp.array(by_slab)


def pack_kernel(inputs, copies, scalars, *refs):
    ins, outs, semaphores = refs[:inputs], refs[inputs:-1], refs[-1]
    started = []
    for number, (source, row, rows, entries, shift, target, at, heads) in enumerate(copies):
        head = shift
        for entry in entries:
            head = head + scalars[entry]
        column = pl.multiple_of(head * HD, HD)
        copy = pltpu.make_async_copy(
            ins[source].at[pl.ds(row, rows), pl.ds(column, heads * HD)],
            outs[target].at[pl.ds(at, rows), :],
            semaphores.at[number],
        )
        copy.start()
        started.append(copy)
    for copy in started:
        copy.wait()


def pack(scalars, arrays, shapes, copies, name):
    moved = sum(2 * 2 * rows * heads * HD for _, _, rows, _, _, _, _, heads in copies)
    return pl.pallas_call(
        functools.partial(pack_kernel, len(arrays), copies),
        name=name,
        out_shape=[jax.ShapeDtypeStruct(shape, jnp.bfloat16) for shape in shapes],
        grid_spec=pltpu.PrefetchScalarGridSpec(
            num_scalar_prefetch=1,
            grid=(1,),
            in_specs=[pl.BlockSpec(memory_space=pl.ANY)] * len(arrays),
            out_specs=[pl.BlockSpec(shape, lambda i, scalars: (0, 0)) for shape in shapes],
            scratch_shapes=[pltpu.SemaphoreType.DMA((len(copies),))],
        ),
        compiler_params=pltpu.CompilerParams(vmem_limit_bytes=GRANT),
        cost_estimate=pl.CostEstimate(flops=0, bytes_accessed=moved, transcendentals=0),
    )(scalars, *arrays)


def message(scalars, pieces, arrays, name):
    copies, shapes = [], []
    for target, parts in enumerate(pieces):
        at = 0
        for source, row, rows, entries, shift, heads in parts:
            copies.append((source, row, rows, entries, shift, target, at, heads))
            at += rows
        shapes.append((at, parts[0][5] * HD))
    return pack(scalars, arrays, shapes, copies, name)


class Tokens(typing.NamedTuple):
    query: int | None = None
    pairs: tuple = ()
    extra: int | None = None


OWN_TOKENS = Tokens()


def attend_kernel(variants, extra, span_count, scalars, mask, *refs):
    query_own, key_own, value_own, received, weight, gain, sums_in = refs[:7]
    more = refs[7 : 7 + extra]
    payloads, (sums_out, folded, squares) = refs[7 + extra : -3], refs[-3:]
    rows = query_own.shape[0]
    half = rows // 2
    step = pl.program_id(0)
    to_exp2 = math.log2(math.e) / math.sqrt(HD)
    active = functools.reduce(
        lambda a, b: a | b, [scalars[PLACE] == place for place in variants]
    )

    @pl.when(step == 0)
    def _():
        folded[...] = jnp.zeros_like(folded)
        squares[...] = jnp.zeros_like(squares)

    def query_of(source):
        if source is OWN_TOKENS:
            return query_own[...]
        if source.extra is not None:
            return more[0][:, source.extra * HD : (source.extra + 1) * HD]
        return payloads[source.query][:rows]

    def pair_of(source):
        if source is OWN_TOKENS:
            parts = (key_own[...], received[:half], value_own[...], received[half:])
        elif source.extra is not None:
            lanes = slice(source.extra * HD, (source.extra + 1) * HD)
            parts = (more[1][:, lanes], more[3][:half, lanes], more[2][:, lanes], more[3][half:, lanes])
        elif len(source.pairs) == 2:
            one, two = (payloads[number] for number in source.pairs)
            parts = (one[:half], two[:half], one[half:], two[half:])
        else:
            payload = payloads[source.pairs[0]]
            start = payload.shape[0] - 2 * rows
            return payload[start : start + rows], payload[start + rows :]
        return jnp.concatenate(parts[:2], axis=0), jnp.concatenate(parts[2:], axis=0)

    def projector(extra_head):
        if extra_head is None:
            scaled = weight[...].astype(jnp.float32) * gain[...]
        else:
            lanes = slice(extra_head * HD, (extra_head + 1) * HD)
            scaled = more[4][:, lanes].astype(jnp.float32) * more[5][:, lanes]
        high = scaled.astype(jnp.bfloat16)
        low = (scaled - high.astype(jnp.float32)).astype(jnp.bfloat16)
        return jnp.concatenate([high, low, jnp.ones((16, HD), jnp.bfloat16)], axis=0)

    def one_query(source, slot, query_span, key_sources):
        query = query_of(source)
        pairs = [pair_of(key_source) for key_source, _ in key_sources]
        open_to = [
            None if key_span == query_span else mask[query_span * span_count + key_span] > 0
            for _, key_span in key_sources
        ]
        keys_in = jnp.concatenate([pair[0] for pair in pairs], axis=0)
        ones_block = jnp.ones((rows, HD), jnp.bfloat16)
        values_in = jnp.concatenate(
            [jnp.concatenate([pair[1], ones_block], axis=1) for pair in pairs], axis=0
        )
        pieces = []
        for row in range(0, rows, QUERY_ROWS):
            score = lax.dot_general(
                query[row : row + QUERY_ROWS],
                keys_in,
                (((1,), (1,)), ((), ())),
                preferred_element_type=jnp.float32,
            )
            best = None
            for number, is_open in enumerate(open_to):
                start = number * rows
                block = score[:, start : start + HD]
                for lane in range(HD, rows, HD):
                    block = jnp.maximum(block, score[:, start + lane : start + lane + HD])
                if is_open is not None:
                    block = jnp.where(is_open, block, neg_big)
                best = block if best is None else jnp.maximum(best, block)
            top = jnp.max(best, axis=1, keepdims=True)
            weights = []
            for number, is_open in enumerate(open_to):
                start = number * rows
                shift = top if is_open is None else jnp.where(is_open, top, -neg_big)
                weights.append(
                    jnp.exp2((score[:, start : start + rows] - shift) * to_exp2).astype(jnp.bfloat16)
                )
            both = jnp.dot(
                jnp.concatenate(weights, axis=1), values_in, preferred_element_type=jnp.float32
            )
            pieces.append((both[:, :HD] / both[:, HD:]).astype(jnp.bfloat16))
        attended = jnp.concatenate(pieces, axis=0)
        folded[slot] += lax.dot_general(
            projector(source.extra),
            attended,
            (((1,), (1,)), ((), ())),
            preferred_element_type=jnp.float32,
        )
        wide = attended.astype(jnp.float32)
        squares[slot] += wide * wide

    for place, (steps, tasks) in variants.items():

        @pl.when((scalars[PLACE] == place) & (step < steps))
        def _():
            for task in tasks:
                one_query(*task)

    @pl.when((step == pl.num_programs(0) - 1) & jnp.logical_not(active))
    def _():
        sums_out[...] = sums_in[...]

    @pl.when((step == pl.num_programs(0) - 1) & active)
    def _():
        ones_rows = jnp.ones((STAT_ROWS, HD), jnp.bfloat16)
        patch = weight.shape[0]
        for slot in range(SLOTS):
            left = squares[slot]
            total = jnp.zeros((STAT_ROWS, rows), jnp.float32)
            for _ in range(3):
                piece = left.astype(jnp.bfloat16)
                left = left - piece.astype(jnp.float32)
                total = total + lax.dot_general(
                    ones_rows, piece, (((1,), (1,)), ((), ())), preferred_element_type=jnp.float32
                )
            done = folded[slot]
            sums_out[slot] = sums_in[slot] + jnp.concatenate(
                [
                    done[:patch] + done[patch : 2 * patch],
                    done[2 * patch : 2 * patch + STAT_ROWS],
                    total,
                ],
                axis=0,
            )


def attend(steps, entries, first, own, scalars, mask, sums, payloads, variants, more, name):
    queries, keys, values, received, weight, gain = own
    rows = queries.shape[0]
    half = rows // 2
    patch = weight.shape[0]

    def moving(i, scalars):
        used = functools.reduce(
            lambda a, b: a | b, [scalars[PLACE] == place for place in variants]
        )
        return jnp.where(used, i, 0)

    def column(height, own_column):
        def index(i, scalars, mask):
            head = first + moving(i, scalars) + (scalars[OWN] if own_column else 0)
            for entry in entries:
                head = head + scalars[entry]
            return (0, head)

        return pl.BlockSpec((height, HD), index)

    def two_columns(height, own_column):
        return pl.BlockSpec(
            (height, 2 * HD),
            lambda i, scalars, mask: (
                0,
                moving(i, scalars) + (scalars[OWN] // 2 if own_column else 0),
            ),
        )

    def payload_column(payload, entry, shift):
        last = payload.shape[1] // HD - 1

        def index(i, scalars, mask):
            at = shift + moving(i, scalars)
            return (0, jnp.minimum(at if entry is None else at + scalars[entry], last))

        return pl.BlockSpec((payload.shape[0], HD), index)

    sums_spec = pl.BlockSpec(sums.shape, lambda i, scalars, mask: (0, 0, 0))
    in_specs = [
        column(rows, True),
        column(half, True),
        column(half, True),
        column(rows, False),
        column(patch, True),
        column(1, True),
        sums_spec,
    ]
    arrays = [queries, keys, values, received, weight, gain, sums]
    extra = 0
    if more:
        extra = 6
        in_specs += [
            two_columns(rows, True),
            two_columns(half, True),
            two_columns(half, True),
            two_columns(rows, False),
            two_columns(patch, True),
            two_columns(1, True),
        ]
        arrays += [queries, keys, values, received, weight, gain]
    in_specs += [payload_column(*payload) for payload in payloads]
    arrays += [payload[0] for payload in payloads]
    pairs = max(
        count * sum(len(task[3]) for task in tasks) for count, tasks in variants.values()
    )
    span_count = math.isqrt(mask.shape[0])
    return pl.pallas_call(
        functools.partial(attend_kernel, variants, extra, span_count),
        name=name,
        out_shape=jax.ShapeDtypeStruct(sums.shape, sums.dtype),
        grid_spec=pltpu.PrefetchScalarGridSpec(
            num_scalar_prefetch=2,
            grid=(steps,),
            in_specs=in_specs,
            out_specs=sums_spec,
            scratch_shapes=[
                pltpu.VMEM((SLOTS, 2 * patch + 16, rows), jnp.float32),
                pltpu.VMEM((SLOTS, rows, HD), jnp.float32),
            ],
        ),
        compiler_params=pltpu.CompilerParams(vmem_limit_bytes=GRANT),
        cost_estimate=pl.CostEstimate(
            flops=pairs * 4 * rows * rows * HD,
            bytes_accessed=steps * HD * 2 * sum(spec.block_shape[0] for spec in in_specs[:4]),
            transcendentals=pairs * rows * rows,
        ),
    )(scalars, mask, *arrays)


def token_sums(scalars, queries, keys, values, span_mask, head_gain, patch_weight):
    rows = queries.shape[0]
    half = rows // 2
    heads = NEAR_HEADS + MIDDLE_HEADS + FAR_HEADS
    queries, keys, values = (
        pltpu.with_memory_space_constraint(array, pltpu.HBM) for array in (queries, keys, values)
    )

    def send(value, *pairs):
        return lax.ppermute(value, "span", list(pairs))

    def send_across(value, *pairs):
        slabs = lax.axis_size("slab")
        return lax.ppermute(
            value,
            ("span", "slab"),
            [(a * slabs + s, b * slabs + 1 - s) for a, b in pairs for s in range(slabs)],
        )

    def tokens(entry, shift, count):
        return [(0, 0, rows, (OWN, entry) if entry else (OWN,), shift, count)]

    def own_half(slab_entry, entry, shift, count):
        return [(part, 0, half, (slab_entry, entry), shift, count) for part in (1, 2)]

    def pairs_of(entry, shift, count):
        entries = (entry,) if entry else ()
        return [
            piece
            for part in (1, 2)
            for piece in (
                (part, 0, half, (OWN,) + entries, shift, count),
                (3, (part - 1) * half, half, entries, shift, count),
            )
        ]

    handed, up_same, up_across, query_down, query_two = message(
        scalars,
        [
            [(part, 0, half, (OTHER,), 0, heads) for part in (1, 2)],
            own_half(OWN, UP, 0, NEAR_HEADS),
            own_half(OTHER, UP, 0, NEAR_HEADS),
            tokens(DOWN, 0, MIDDLE_HEADS),
            tokens(None, 0, NEAR_HEADS),
        ],
        (queries, keys, values),
        "pack_first",
    )
    anchor = handed
    received = lax.ppermute(handed, "slab", SWAP)
    up_same = send(up_same, (0, 1), (1, 2))
    up_across = send_across(up_across, (0, 1), (1, 2))
    query_down = send(query_down, (1, 0), (2, 1), (3, 2))
    query_two = send(query_two, (3, 1))

    arrays = (queries, keys, values, received)
    pair_down, pair_two, up_two = message(
        scalars,
        [pairs_of(DOWN, 0, MIDDLE_HEADS), pairs_of(None, 0, 2), pairs_of(None, MIDDLE, 3)],
        arrays,
        "pack_second",
    )
    pair_down = send(pair_down, (1, 0), (2, 1), (3, 2))
    pair_two = send(pair_two, (3, 1))
    up_two = send(up_two, (0, 2))

    source, _ = lax.optimization_barrier((received, up_same))
    far_all, far_pair, last_two, last_up = message(
        scalars,
        [
            tokens(None, FAR, FAR_HEADS) + pairs_of(None, FAR, FAR_HEADS),
            pairs_of(None, FAR, FAR_HEADS),
            pairs_of(None, 2, 2),
            pairs_of(None, MIDDLE + 3, 1),
        ],
        (queries, keys, values, source),
        "pack_third",
    )
    far_two = send(far_pair, (1, 3))
    far_three = send(far_pair, (0, 3))
    far_next = send(far_all, (2, 3), (1, 0))
    last_two, last_up, _ = lax.optimization_barrier((last_two, last_up, pair_down))
    last_two = send(last_two, (3, 1))
    last_up = send(last_up, (0, 2))

    mask = span_mask.reshape(-1)
    weight = patch_weight.T
    own = (queries, keys, values, received, weight, head_gain[None, :])
    sums = jnp.zeros((SLOTS, weight.shape[0] + 2 * STAT_ROWS, rows), jnp.float32)
    run = functools.partial(attend, own=own, scalars=scalars, mask=mask)

    on_one, back_one, back_two = Tokens(0, (1,)), Tokens(None, (2, 3)), Tokens(None, (4,))
    here = OWN_TOKENS
    middle = [
        (on_one, 1, 3, [(back_two, 0), (back_one, 1), (here, 2), (on_one, 3)]),
        (here, 0, 2, [(back_two, 0), (back_one, 1), (here, 2)]),
    ]
    sums = run(
        MIDDLE_HEADS,
        (MAIN,),
        0,
        sums=sums,
        payloads=[
            (query_down, None, 0),
            (pair_down, None, 0),
            (up_same, None, 0),
            (up_across, None, 0),
            (up_two, None, 0),
        ],
        variants={
            0: (4, [(here, 0, 0, [(here, 0)]), (on_one, 1, 1, [(here, 0), (on_one, 1)])]),
            1: (
                4,
                [
                    (on_one, 1, 2, [(back_one, 0), (here, 1), (on_one, 2)]),
                    (here, 0, 1, [(back_one, 0), (here, 1)]),
                ],
            ),
            2: (3, middle),
        },
        more=False,
        name="main_heads",
    )
    on_two = Tokens(5, (6,))
    last_span = [(on_two, 2, 3, [(back_one, 0), (here, 1), (on_one, 2), (on_two, 3)])]
    sums = run(
        2,
        (MAIN,),
        0,
        sums=sums,
        payloads=[
            (query_down, None, 0),
            (pair_down, None, 0),
            (up_same, None, 0),
            (up_across, None, 0),
            (up_two, None, 0),
            (query_two, None, 0),
            (pair_two, None, 0),
        ],
        variants={1: (2, last_span)},
        more=False,
        name="near_heads",
    )
    beside, two_back, three_back = Tokens(0, (0,)), Tokens(None, (1,)), Tokens(None, (2,))
    extras = [Tokens(None, (), lane) for lane in range(2)]
    sums = run(
        FAR_HEADS,
        (),
        FAR,
        sums=sums,
        payloads=[(far_next, None, 0), (far_two, None, 0), (far_three, None, 0)],
        variants={
            0: (
                FAR_HEADS,
                [(here, 0, 0, [(here, 0)]), (beside, 1, 1, [(here, 0), (beside, 1)])]
                + [(head, 0, 0, [(head, 0)]) for head in extras],
            ),
            3: (
                FAR_HEADS,
                [
                    (here, 0, 3, [(three_back, 0), (two_back, 1), (beside, 2), (here, 3)]),
                    (beside, 2, 2, [(three_back, 0), (two_back, 1), (beside, 2)]),
                ],
            ),
        },
        more=True,
        name="far_heads",
    )

    def last(sums):
        return run(
            2,
            (LAST,),
            0,
            sums=sums,
            payloads=[
                (query_down, LAST_COLUMN, 0),
                (pair_down, LAST_COLUMN, 0),
                (up_same, LAST_COLUMN, 0),
                (up_across, LAST_COLUMN, 0),
                (last_up, None, 0),
                (query_two, LAST_COLUMN, 0),
                (last_two, None, 0),
            ],
            variants={1: (2, last_span), 2: (1, middle)},
            more=False,
            name="last_heads",
        )

    return sums, last, anchor, pair_down


def noise_window(noisy_latent):
    frames, height, breadth, channels = noisy_latent.shape
    own = noisy_latent.transpose(1, 2, 0, 3).reshape(height, breadth, frames * channels)
    earlier = from_behind(own[:, :, (frames - 2) * channels :], "span", 1)
    grid = jnp.concatenate([earlier, own], axis=2)
    slab = lax.axis_index("slab")
    edge = jnp.where(slab == 0, grid[:, breadth - 1], grid[:, 0])
    edge = lax.ppermute(edge, "slab", SWAP)[:, None]
    grid = jnp.concatenate(
        [
            jnp.where(slab == 1, edge, 0.0),
            grid,
            jnp.where(slab == 0, edge, 0.0),
            jnp.zeros((height, WINDOW - breadth - 2, grid.shape[2]), grid.dtype),
        ],
        axis=1,
    )
    head = lax.axis_index("head")
    edge = jnp.where(head == 0, grid[height - 1], grid[0])
    edge = lax.ppermute(edge, "head", SWAP)[None]
    grid = jnp.concatenate(
        [jnp.where(head == 1, edge, 0.0), grid, jnp.where(head == 0, edge, 0.0)], axis=0
    )
    return grid.reshape((height + 2) * WINDOW, grid.shape[2])


def cell_selector(height, breadth):
    cell = lax.broadcasted_iota(jnp.int32, ((height + 2) * WINDOW, 4 * TROWS * TCOLS), 0)
    column = lax.broadcasted_iota(jnp.int32, cell.shape, 1)
    y = lax.axis_index("head") * height + cell // WINDOW - 1
    x = lax.axis_index("slab") * breadth + cell % WINDOW - 1
    inside = (y >= 0) & (y < 2 * TROWS) & (x >= 0) & (x < 2 * TCOLS)
    inside = inside & (cell % WINDOW < breadth + 2)
    target = ((y % 2) * 2 + x % 2) * (TROWS * TCOLS) + (y // 2) * TCOLS + x // 2
    return (inside & (column == target)).astype(jnp.bfloat16)


def banded_weight(conv_weight):
    channels = conv_weight.shape[1]
    taps = conv_weight.reshape(3, 3, 3, LAT_CH, channels)
    banded = jnp.stack(
        [
            jnp.pad(taps, ((n, FRAMES_SPAN - 1 - n), (0, 0), (0, 0), (0, 0), (0, 0)))
            for n in range(FRAMES_SPAN)
        ],
        axis=4,
    )
    return banded.transpose(1, 2, 0, 3, 4, 5).reshape(
        3, 3 * (FRAMES_SPAN + 2) * LAT_CH, FRAMES_SPAN * channels
    )


def finish_kernel(
    scalars, mine, other, noise, selector, band, bias, constants, clean, decoded, cells
):
    frames, height, breadth, channels = clean.shape
    patch = constants.shape[0]
    first = scalars[SLAB] == 0
    sums = jnp.concatenate(
        [jnp.where(first, mine[...], other[...]), jnp.where(first, other[...], mine[...])], axis=0
    )
    feature_width = HEADS * HD
    row_mean = sums[patch : patch + 1] / feature_width
    spread = sums[patch + STAT_ROWS : patch + STAT_ROWS + 1] / feature_width - row_mean * row_mean
    velocity = (
        lax.rsqrt(spread + norm_eps) * (sums[:patch] - constants[:, 0:1] * row_mean)
        + constants[:, 1:2]
    )
    tokens = TROWS * TCOLS
    lane = lax.broadcasted_iota(jnp.int32, velocity.shape, 1)
    velocity = jnp.where((lane >= 2 * tokens) | (scalars[PLACE] > 0), velocity, 0.0)
    columns = jnp.concatenate(
        [
            jnp.concatenate(
                [
                    velocity[
                        part * channels : (part + 1) * channels,
                        frame * tokens : (frame + 1) * tokens,
                    ]
                    for part in range(4)
                ],
                axis=1,
            )
            for frame in range(frames + 2)
        ],
        axis=0,
    )
    high = columns.astype(jnp.bfloat16)
    low = (columns - high.astype(jnp.float32)).astype(jnp.bfloat16)
    chosen = sum(
        lax.dot_general(
            selector[...], part, (((1,), (1,)), ((), ())), preferred_element_type=jnp.float32
        )
        for part in (high, low)
    )
    count = (height + 2) * WINDOW
    cells[:count] = noise[...] - noise_level * chosen
    cells[count:] = jnp.zeros_like(cells[count:])
    for frame in range(frames):
        lanes = slice((frame + 2) * channels, (frame + 3) * channels)
        for y in range(height):
            start = (y + 1) * WINDOW + 1
            clean[frame, y] = cells[start : start + breadth, lanes]
    shifted = jnp.concatenate(
        [cells[tap : tap + count] for tap in range(3)], axis=1
    ).astype(jnp.bfloat16)
    total = jnp.broadcast_to(bias[...], (height * breadth, bias.shape[1]))
    for tap in range(3):
        block = jnp.concatenate(
            [
                shifted[(y + tap) * WINDOW : (y + tap) * WINDOW + breadth]
                for y in range(height)
            ],
            axis=0,
        )
        total = total + jnp.dot(block, band[tap], preferred_element_type=jnp.float32)
    outputs = decoded.shape[3]
    total = total.astype(decoded.dtype)
    for frame in range(frames):
        decoded[frame] = total[:, frame * outputs : (frame + 1) * outputs].reshape(
            height, breadth, outputs
        )


def finish(scalars, mine, other, noise, selector, band, bias, constants, shape, outputs):
    whole = pl.BlockSpec(memory_space=pltpu.VMEM)
    frames, height, breadth, channels = shape
    rows = (height + 2) * WINDOW
    return pl.pallas_call(
        finish_kernel,
        name="finish",
        out_shape=(
            jax.ShapeDtypeStruct(shape, jnp.float32),
            jax.ShapeDtypeStruct((frames, height, breadth, outputs), jnp.bfloat16),
        ),
        in_specs=[pl.BlockSpec(memory_space=pltpu.SMEM)] + [whole] * 7,
        out_specs=(whole, whole),
        scratch_shapes=[pltpu.VMEM((rows + 8, (frames + 2) * channels), jnp.float32)],
        compiler_params=pltpu.CompilerParams(vmem_limit_bytes=GRANT),
    )(scalars, mine, other, noise, selector, band, bias, constants)


def per_device(
    queries,
    keys,
    values,
    span_mask,
    head_gain,
    head_shift,
    patch_weight,
    noisy_latent,
    conv_weight,
    conv_bias,
):
    heads_dev = queries.shape[1] // HD
    if not plan_fits(
        heads_dev, lax.axis_size("span"), lax.axis_size("slab"), lax.axis_size("head")
    ):
        return gathered_plan(
            queries,
            keys,
            values,
            span_mask,
            head_gain,
            head_shift,
            patch_weight,
            noisy_latent,
            conv_weight,
            conv_bias,
        )
    place = lax.axis_index("span")
    slab = lax.axis_index("slab")
    scalars = scalar_operand(heads_dev // lax.axis_size("slab"))
    sums, last, anchor, later = token_sums(
        scalars, queries, keys, values, span_mask, head_gain, patch_weight
    )

    noisy, weight, gain, shift, taps, bias, _ = lax.optimization_barrier(
        (noisy_latent, patch_weight, head_gain, head_shift, conv_weight, conv_bias, anchor)
    )
    _, height, breadth, _ = noisy.shape
    noise = noise_window(noisy)
    wide_weight = weight.T.astype(jnp.float32)
    constants = jnp.stack(
        [
            jnp.sum(wide_weight * gain[None, :], axis=1),
            jnp.sum(wide_weight * shift[None, :], axis=1),
        ],
        axis=1,
    )
    constants = constants + lax.ppermute(constants, "head", SWAP)
    selector = cell_selector(height, breadth)
    band = banded_weight(taps)
    bias = jnp.tile(bias, FRAMES_SPAN)[None, :]
    sums, noise, constants, selector, band, bias = lax.optimization_barrier(
        (sums, noise, constants, selector, band, bias)
    )

    sums = last(sums)
    half = sums.shape[1] // 2
    mine = lax.dynamic_slice_in_dim(sums, slab * half, half, 1)
    theirs = lax.dynamic_slice_in_dim(sums, (1 - slab) * half, half, 1)
    mine = mine + lax.ppermute(theirs, "slab", SWAP)
    own, after, third = mine[0], mine[1], mine[2]
    skip = TROWS * TCOLS
    from_one = lax.ppermute(
        jnp.concatenate([own[:, skip:], after], axis=1), "span", [(0, 1), (1, 2), (2, 3)]
    )
    to_current = lax.ppermute(third, "span", [(1, 3), (3, 2)])
    to_before = lax.ppermute(after[:, skip:], "span", [(0, 2), (1, 3)])
    kept = jnp.concatenate([jnp.where(place == 3, third[:, skip:], 0.0), own], axis=1)
    total = kept + from_one + jnp.concatenate([to_before, to_current], axis=1)
    total = total + lax.ppermute(total, "head", SWAP)
    other = lax.ppermute(total, "slab", SWAP)
    return finish(
        scalars,
        total,
        other,
        noise,
        selector,
        band,
        bias,
        constants,
        noisy_latent.shape,
        conv_weight.shape[1],
    )


def solution(mesh):
    placed = (
        P(("groups", "span"), "head"),
        P(("groups", "span", "slab"), "head"),
        P(("groups", "span", "slab"), "head"),
        P("groups", None),
        P("head"),
        P("head"),
        P("head", None),
        P(("groups", "span"), "head", "slab", None),
        P(),
        P(),
    )
    return jax.shard_map(
        per_device,
        mesh=mesh,
        in_specs=placed,
        out_specs=(
            P(("groups", "span"), "head", "slab", None),
            P(("groups", "span"), "head", "slab", None),
        ),
        check_vma=False,
    )
```

```python
import functools
import math
import typing

import jax
import jax.numpy as jnp
import numpy as np
from jax import lax
from jax.experimental import pallas as pl
from jax.experimental.pallas import tpu as pltpu
from jax.sharding import PartitionSpec as P

HEADS = 40
HD = 128
LAT_CH = 16
FRAMES_SPAN = 3
TROWS = 8
TCOLS = 16


neg_big = -1e30
noise_level = 0.75
norm_eps = 1e-06


def with_halo(cells, sides, width):
    for axis, dim in sides:
        count = lax.axis_size(axis)
        ends = count - 1
        head = lax.slice_in_dim(cells, 0, width, axis=dim)
        tail = lax.slice_in_dim(cells, cells.shape[dim] - width, cells.shape[dim], axis=dim)
        cells = jnp.concatenate(
            [
                lax.ppermute(tail, axis, [(i, (i + 1) % count) for i in range(ends)]),
                cells,
                lax.ppermute(head, axis, [((i + 1) % count, i) for i in range(ends)]),
            ],
            axis=dim,
        )
    return cells


def from_behind(value, axis, by):
    size = lax.axis_size(axis)
    pairs = [(i, i + by) for i in range(size) if 0 <= i + by < size]
    return lax.ppermute(value, axis, pairs)


def block_length(total_rows):
    block_size = total_rows
    while block_size > 768 and block_size % 2 == 0:
        block_size = block_size // 2
    return block_size


def fold_keys(partial_state, key_value, query_block, mask_row, rows_span):
    keys_piece, values_piece = key_value
    heads_dev = query_block.shape[1]
    piece_rows = keys_piece.shape[0]
    length = block_length(piece_rows)
    span_count = mask_row.shape[0]
    score_scale = 1.0 / math.sqrt(HD)
    span_ids = jnp.arange(span_count, dtype=jnp.int32)

    def one_block(carry_state, block_index):
        running_max, running_sum, weighted = carry_state
        offset = block_index * length
        key_block = lax.dynamic_slice_in_dim(keys_piece, offset, length, 0).reshape(
            length, heads_dev, HD
        )
        value_block = lax.dynamic_slice_in_dim(values_piece, offset, length, 0).reshape(
            length, heads_dev, HD
        )
        key_span = (offset + jnp.arange(length, dtype=jnp.int32)) // rows_span
        allowed = (
            jnp.sum(jnp.where(key_span[:, None] == span_ids[None, :], mask_row[None, :], 0), axis=1)
            > 0
        )
        scores = (
            jnp.einsum("qhd,khd->hqk", query_block, key_block, preferred_element_type=jnp.float32)
            * score_scale
        )
        scores = jnp.where(allowed[None, None, :], scores, neg_big)
        new_max = jnp.maximum(running_max, jnp.max(scores, axis=2))
        weights = jnp.where(allowed[None, None, :], jnp.exp(scores - new_max[:, :, None]), 0.0)
        factor = jnp.exp(running_max - new_max)
        running_sum = running_sum * factor + jnp.sum(weights, axis=2)
        weighted = weighted * factor.T[:, :, None] + jnp.einsum(
            "hqk,khd->qhd",
            weights.astype(jnp.bfloat16),
            value_block,
            preferred_element_type=jnp.float32,
        )
        return ((new_max, running_sum, weighted), None)

    result, unused = lax.scan(
        one_block, partial_state, jnp.arange(piece_rows // length, dtype=jnp.int32)
    )
    return result


def gathered_plan(
    queries,
    keys,
    values,
    span_mask,
    head_gain,
    head_shift,
    patch_weight,
    noisy_latent,
    conv_weight,
    conv_bias,
):
    heads_dev = queries.shape[1] // HD
    slab_count = lax.axis_size("slab")
    col_dev = TCOLS // slab_count
    slab_place = lax.axis_index("slab")
    span_place = lax.axis_index("span")
    mask_row = lax.dynamic_slice_in_dim(span_mask, span_place, 1, 0)[0]
    token_grid = queries.reshape(FRAMES_SPAN, TROWS, TCOLS, queries.shape[-1])
    picked = lax.dynamic_slice_in_dim(token_grid, slab_place * col_dev, col_dev, 2)
    own_queries = picked.reshape(FRAMES_SPAN * TROWS * col_dev, queries.shape[-1]).reshape(
        -1, heads_dev, HD
    )
    query_rows = own_queries.shape[0]
    rows_span = keys.shape[0] * slab_count
    running_max, running_sum, weighted = fold_keys(
        (
            jnp.full((heads_dev, query_rows), neg_big, jnp.float32),
            jnp.zeros((heads_dev, query_rows), jnp.float32),
            jnp.zeros((query_rows, heads_dev, HD), jnp.float32),
        ),
        (
            lax.all_gather(keys, ("span", "slab"), axis=0, tiled=True),
            lax.all_gather(values, ("span", "slab"), axis=0, tiled=True),
        ),
        own_queries,
        mask_row,
        rows_span,
    )
    attended = (
        (weighted / running_sum.T[:, :, None])
        .astype(jnp.bfloat16)
        .reshape(query_rows, heads_dev * HD)
    )
    feature_width = HEADS * HD
    values32 = attended.astype(jnp.float32)
    row_total = jnp.sum(values32, axis=1)
    row_squares = jnp.sum(values32 * values32, axis=1)
    row_total, row_squares = lax.psum((row_total, row_squares), "head")
    row_mean = row_total / feature_width
    spread = row_squares / feature_width - row_mean * row_mean
    normed = (
        (values32 - row_mean[:, None]) * lax.rsqrt(spread + norm_eps)[:, None] * head_gain[None, :]
        + head_shift[None, :]
    ).astype(jnp.bfloat16)
    normed_grid = normed.reshape(FRAMES_SPAN, TROWS, col_dev, normed.shape[-1])
    own_rows = TROWS // lax.axis_size("head")
    picked = normed_grid
    product = jnp.dot(
        picked.reshape(-1, picked.shape[-1]), patch_weight, preferred_element_type=jnp.float32
    )
    velocity = lax.psum_scatter(
        product.reshape(
            FRAMES_SPAN, own_rows * lax.axis_size("head"), col_dev * patch_weight.shape[1]
        )
        .transpose(1, 0, 2)
        .reshape(own_rows * lax.axis_size("head"), -1)
        .astype(jnp.bfloat16),
        "head",
        scatter_dimension=0,
        tiled=True,
    ).astype(jnp.float32)
    rows_dev = velocity.shape[0]
    patch_cells = (
        velocity.reshape(rows_dev, FRAMES_SPAN, col_dev, 2, 2, LAT_CH)
        .transpose(1, 0, 3, 2, 4, 5)
        .reshape(FRAMES_SPAN, 2 * rows_dev, 2 * col_dev, LAT_CH)
    )
    clean_latent = noisy_latent - noise_level * patch_cells
    latent_input = clean_latent.astype(jnp.bfloat16)
    framed = with_halo(latent_input, (("head", 1), ("slab", 2)), 1)
    earlier = from_behind(framed[FRAMES_SPAN - 2 :], "span", 1)
    stacked = jnp.concatenate([earlier, framed], axis=0)
    height = clean_latent.shape[1]
    breadth = clean_latent.shape[2]
    columns = jnp.concatenate(
        [
            stacked[
                frame_tap : frame_tap + FRAMES_SPAN,
                row_tap : row_tap + height,
                col_tap : col_tap + breadth,
                :,
            ]
            for frame_tap in range(3)
            for row_tap in range(3)
            for col_tap in range(3)
        ],
        axis=-1,
    )
    decoded = (
        jnp.dot(
            columns.reshape(FRAMES_SPAN * height * breadth, 27 * LAT_CH),
            conv_weight,
            preferred_element_type=jnp.float32,
        )
        + conv_bias[None, :]
    )
    decoded = decoded.astype(jnp.bfloat16).reshape(
        FRAMES_SPAN, height, breadth, conv_weight.shape[1]
    )
    return (clean_latent, decoded)


NEAR_HEADS = 4
MIDDLE_HEADS = 4
FAR_HEADS = 2
MIDDLE = NEAR_HEADS
FAR = NEAR_HEADS + MIDDLE_HEADS
STAT_ROWS = 8
SLOTS = 3
QUERY_ROWS = 192
SWAP = [(0, 1), (1, 0)]
WINDOW = 32
GRANT = 20 << 20

OWN, OTHER, DOWN, UP, MAIN, LAST, LAST_COLUMN, PLACE, SLAB = range(9)
STEPS = 9


def plan_fits(heads_dev, span_count, slab_count, head_count):
    return (
        span_count == 4
        and slab_count == 2
        and head_count == 2
        and heads_dev == slab_count * (NEAR_HEADS + MIDDLE_HEADS + FAR_HEADS)
    )


def scalar_operand(heads):
    by_place = np.zeros((4, 12), np.int32)
    by_place[:, OTHER] = heads
    by_place[:, DOWN] = [MIDDLE, MIDDLE, 0, MIDDLE]
    by_place[:, UP] = [0, MIDDLE, 0, 0]
    by_place[:, MAIN] = [MIDDLE, 0, MIDDLE, 0]
    by_place[:, LAST] = [0, 2, MIDDLE + 3, 0]
    by_place[:, LAST_COLUMN] = [0, 2, 3, 0]
    by_place[:, PLACE] = range(4)
    by_slab = np.zeros(12, np.int32)
    by_slab[[OWN, OTHER, SLAB]] = heads, -heads, 1
    row = lax.dynamic_slice_in_dim(jnp.array(by_place), lax.axis_index("span"), 1, 0)[0]
    return row + lax.axis_index("slab") * jnp.array(by_slab)


def pack_kernel(inputs, copies, with_noise, scalars, *refs):
    ins, outs, semaphores = refs[:inputs], refs[inputs:-1], refs[-1]
    started = []
    for number, (source, row, rows, entries, shift, target, at, heads) in enumerate(copies):
        head = shift
        for entry in entries:
            head = head + scalars[entry]
        column = pl.multiple_of(head * HD, HD)
        copy = pltpu.make_async_copy(
            ins[source].at[pl.ds(row, rows), pl.ds(column, heads * HD)],
            outs[target].at[pl.ds(at, rows), :],
            semaphores.at[number],
        )
        copy.start()
        started.append(copy)
    if with_noise:
        noisy, out = ins[-1], outs[-1]
        frames = noisy.shape[0]
        out[...] = jnp.concatenate([noisy[frame] for frame in range(frames)], axis=-1)
    for copy in started:
        copy.wait()


def pack(scalars, arrays, shapes, copies, name, noisy=None):
    moved = sum(2 * 2 * rows * heads * HD for _, _, rows, _, _, _, _, heads in copies)
    out_shape = [pltpu.HBM(shape, jnp.bfloat16) for shape in shapes]
    in_specs = [pl.BlockSpec(memory_space=pl.ANY)] * len(arrays)
    out_specs = [pl.BlockSpec(shape, lambda i, scalars: (0, 0)) for shape in shapes]
    if noisy is not None:
        frames, height, breadth, channels = noisy.shape
        lanes = frames * channels
        arrays = arrays + (noisy,)
        in_specs.append(pl.BlockSpec(noisy.shape, lambda i, scalars: (0, 0, 0, 0)))
        out_shape.append(jax.ShapeDtypeStruct((height, breadth, lanes), noisy.dtype))
        out_specs.append(pl.BlockSpec((height, breadth, lanes), lambda i, scalars: (0, 0, 0)))
    return pl.pallas_call(
        functools.partial(pack_kernel, len(arrays), copies, noisy is not None),
        name=name,
        out_shape=out_shape,
        grid_spec=pltpu.PrefetchScalarGridSpec(
            num_scalar_prefetch=1,
            grid=(1,),
            in_specs=in_specs,
            out_specs=out_specs,
            scratch_shapes=[pltpu.SemaphoreType.DMA((len(copies),))],
        ),
        compiler_params=pltpu.CompilerParams(vmem_limit_bytes=GRANT),
        cost_estimate=pl.CostEstimate(flops=0, bytes_accessed=moved, transcendentals=0),
    )(scalars, *arrays)


def message(scalars, pieces, arrays, name, noisy=None):
    copies, shapes = [], []
    for target, parts in enumerate(pieces):
        at = 0
        for source, row, rows, entries, shift, heads in parts:
            copies.append((source, row, rows, entries, shift, target, at, heads))
            at += rows
        shapes.append((at, parts[0][5] * HD))
    return pack(scalars, arrays, shapes, copies, name, noisy)


class Tokens(typing.NamedTuple):
    query: int | None = None
    pairs: tuple = ()
    extra: int | None = None


OWN_TOKENS = Tokens()


def attend_kernel(variants, extra, span_count, scalars, mask, *refs):
    query_own, key_own, value_own, received, weight, gain, sums_in = refs[:7]
    more = refs[7 : 7 + extra]
    payloads, (sums_out, folded, squares) = refs[7 + extra : -3], refs[-3:]
    rows = query_own.shape[0]
    half = rows // 2
    step = pl.program_id(0)
    to_exp2 = math.log2(math.e) / math.sqrt(HD)
    active = functools.reduce(
        lambda a, b: a | b, [scalars[PLACE] == place for place in variants]
    )

    @pl.when(step == 0)
    def _():
        folded[...] = jnp.zeros_like(folded)
        squares[...] = jnp.zeros_like(squares)

    def query_of(source):
        if source is OWN_TOKENS:
            return query_own[...]
        if source.extra is not None:
            return more[0][:, source.extra * HD : (source.extra + 1) * HD]
        return payloads[source.query][:rows]

    def pair_of(source):
        if source is OWN_TOKENS:
            parts = (key_own[...], received[:half], value_own[...], received[half:])
        elif source.extra is not None:
            lanes = slice(source.extra * HD, (source.extra + 1) * HD)
            parts = (more[1][:, lanes], more[3][:half, lanes], more[2][:, lanes], more[3][half:, lanes])
        elif len(source.pairs) == 2:
            one, two = (payloads[number] for number in source.pairs)
            parts = (one[:half], two[:half], one[half:], two[half:])
        else:
            payload = payloads[source.pairs[0]]
            start = payload.shape[0] - 2 * rows
            return payload[start : start + rows], payload[start + rows :]
        return jnp.concatenate(parts[:2], axis=0), jnp.concatenate(parts[2:], axis=0)

    def projector(extra_head):
        if extra_head is None:
            scaled = weight[...].astype(jnp.float32) * gain[...]
        else:
            lanes = slice(extra_head * HD, (extra_head + 1) * HD)
            scaled = more[4][:, lanes].astype(jnp.float32) * more[5][:, lanes]
        high = scaled.astype(jnp.bfloat16)
        low = (scaled - high.astype(jnp.float32)).astype(jnp.bfloat16)
        return jnp.concatenate([high, low, jnp.ones((16, HD), jnp.bfloat16)], axis=0)

    def one_query(source, slot, query_span, key_sources):
        query = query_of(source)
        pairs = [pair_of(key_source) for key_source, _ in key_sources]
        open_to = [
            None if key_span == query_span else mask[query_span * span_count + key_span] > 0
            for _, key_span in key_sources
        ]
        keys_in = jnp.concatenate([pair[0] for pair in pairs], axis=0)
        ones_block = jnp.ones((rows, HD), jnp.bfloat16)
        values_in = jnp.concatenate(
            [jnp.concatenate([pair[1], ones_block], axis=1) for pair in pairs], axis=0
        )
        pieces = []
        for row in range(0, rows, QUERY_ROWS):
            score = lax.dot_general(
                query[row : row + QUERY_ROWS],
                keys_in,
                (((1,), (1,)), ((), ())),
                preferred_element_type=jnp.float32,
            )
            best = None
            for number, is_open in enumerate(open_to):
                start = number * rows
                block = score[:, start : start + HD]
                for lane in range(HD, rows, HD):
                    block = jnp.maximum(block, score[:, start + lane : start + lane + HD])
                if is_open is not None:
                    block = jnp.where(is_open, block, neg_big)
                best = block if best is None else jnp.maximum(best, block)
            top = jnp.max(best, axis=1, keepdims=True)
            weights = []
            for number, is_open in enumerate(open_to):
                start = number * rows
                shift = top if is_open is None else jnp.where(is_open, top, -neg_big)
                weights.append(
                    jnp.exp2((score[:, start : start + rows] - shift) * to_exp2).astype(jnp.bfloat16)
                )
            both = jnp.dot(
                jnp.concatenate(weights, axis=1), values_in, preferred_element_type=jnp.float32
            )
            pieces.append((both[:, :HD] / both[:, HD:]).astype(jnp.bfloat16))
        attended = jnp.concatenate(pieces, axis=0)
        folded[slot] += lax.dot_general(
            projector(source.extra),
            attended,
            (((1,), (1,)), ((), ())),
            preferred_element_type=jnp.float32,
        )
        wide = attended.astype(jnp.float32)
        squares[slot] += wide * wide

    for place, (steps, tasks) in variants.items():

        @pl.when((scalars[PLACE] == place) & (step < steps))
        def _():
            for task in tasks:
                one_query(*task)

    @pl.when((step == pl.num_programs(0) - 1) & jnp.logical_not(active))
    def _():
        sums_out[...] = sums_in[...]

    @pl.when((step == pl.num_programs(0) - 1) & active)
    def _():
        ones_rows = jnp.ones((STAT_ROWS, HD), jnp.bfloat16)
        patch = weight.shape[0]
        for slot in range(SLOTS):
            left = squares[slot]
            total = jnp.zeros((STAT_ROWS, rows), jnp.float32)
            for _ in range(3):
                piece = left.astype(jnp.bfloat16)
                left = left - piece.astype(jnp.float32)
                total = total + lax.dot_general(
                    ones_rows, piece, (((1,), (1,)), ((), ())), preferred_element_type=jnp.float32
                )
            done = folded[slot]
            sums_out[slot] = sums_in[slot] + jnp.concatenate(
                [
                    done[:patch] + done[patch : 2 * patch],
                    done[2 * patch : 2 * patch + STAT_ROWS],
                    total,
                ],
                axis=0,
            )


def attend(steps, entries, first, own, scalars, mask, sums, payloads, variants, more, name):
    queries, keys, values, received, weight, gain = own
    rows = queries.shape[0]
    half = rows // 2
    patch = weight.shape[0]

    def moving(i, scalars):
        used = functools.reduce(
            lambda a, b: a | b, [scalars[PLACE] == place for place in variants]
        )
        return jnp.where(used, i, 0)

    def column(height, own_column):
        def index(i, scalars, mask):
            head = first + moving(i, scalars) + (scalars[OWN] if own_column else 0)
            for entry in entries:
                head = head + scalars[entry]
            return (0, head)

        return pl.BlockSpec((height, HD), index)

    def two_columns(height, own_column):
        return pl.BlockSpec(
            (height, 2 * HD),
            lambda i, scalars, mask: (
                0,
                moving(i, scalars) + (scalars[OWN] // 2 if own_column else 0),
            ),
        )

    def payload_column(payload, entry, shift):
        last = payload.shape[1] // HD - 1

        def index(i, scalars, mask):
            at = shift + moving(i, scalars)
            return (0, jnp.minimum(at if entry is None else at + scalars[entry], last))

        return pl.BlockSpec((payload.shape[0], HD), index)

    sums_spec = pl.BlockSpec(sums.shape, lambda i, scalars, mask: (0, 0, 0))
    in_specs = [
        column(rows, True),
        column(half, True),
        column(half, True),
        column(rows, False),
        column(patch, True),
        column(1, True),
        sums_spec,
    ]
    arrays = [queries, keys, values, received, weight, gain, sums]
    extra = 0
    if more:
        extra = 6
        in_specs += [
            two_columns(rows, True),
            two_columns(half, True),
            two_columns(half, True),
            two_columns(rows, False),
            two_columns(patch, True),
            two_columns(1, True),
        ]
        arrays += [queries, keys, values, received, weight, gain]
    in_specs += [payload_column(*payload) for payload in payloads]
    arrays += [payload[0] for payload in payloads]
    pairs = max(
        count * sum(len(task[3]) for task in tasks) for count, tasks in variants.values()
    )
    span_count = math.isqrt(mask.shape[0])
    return pl.pallas_call(
        functools.partial(attend_kernel, variants, extra, span_count),
        name=name,
        out_shape=jax.ShapeDtypeStruct(sums.shape, sums.dtype),
        grid_spec=pltpu.PrefetchScalarGridSpec(
            num_scalar_prefetch=2,
            grid=(steps,),
            in_specs=in_specs,
            out_specs=sums_spec,
            scratch_shapes=[
                pltpu.VMEM((SLOTS, 2 * patch + 16, rows), jnp.float32),
                pltpu.VMEM((SLOTS, rows, HD), jnp.float32),
            ],
        ),
        compiler_params=pltpu.CompilerParams(vmem_limit_bytes=GRANT),
        cost_estimate=pl.CostEstimate(
            flops=pairs * 4 * rows * rows * HD,
            bytes_accessed=steps * HD * 2 * sum(spec.block_shape[0] for spec in in_specs[:4]),
            transcendentals=pairs * rows * rows,
        ),
    )(scalars, mask, *arrays)


def token_sums(scalars, queries, keys, values, span_mask, head_gain, patch_weight, noisy):
    rows = queries.shape[0]
    half = rows // 2
    heads = NEAR_HEADS + MIDDLE_HEADS + FAR_HEADS
    queries, keys, values = (
        pltpu.with_memory_space_constraint(array, pltpu.HBM) for array in (queries, keys, values)
    )

    def send(value, *pairs):
        return lax.ppermute(value, "span", list(pairs))

    def send_across(value, *pairs):
        slabs = lax.axis_size("slab")
        return lax.ppermute(
            value,
            ("span", "slab"),
            [(a * slabs + s, b * slabs + 1 - s) for a, b in pairs for s in range(slabs)],
        )

    def tokens(entry, shift, count):
        return [(0, 0, rows, (OWN, entry) if entry else (OWN,), shift, count)]

    def own_half(slab_entry, entry, shift, count):
        return [(part, 0, half, (slab_entry, entry), shift, count) for part in (1, 2)]

    def pairs_of(entry, shift, count):
        entries = (entry,) if entry else ()
        return [
            piece
            for part in (1, 2)
            for piece in (
                (part, 0, half, (OWN,) + entries, shift, count),
                (3, (part - 1) * half, half, entries, shift, count),
            )
        ]

    handed, up_same, up_across, query_down, query_two, noise = message(
        scalars,
        [
            [(part, 0, half, (OTHER,), 0, heads) for part in (1, 2)],
            own_half(OWN, UP, 0, NEAR_HEADS),
            own_half(OTHER, UP, 0, NEAR_HEADS),
            tokens(DOWN, 0, MIDDLE_HEADS),
            tokens(None, 0, NEAR_HEADS),
        ],
        (queries, keys, values),
        "pack_first",
        noisy,
    )
    lanes = 2 * noisy.shape[3]
    noise = jnp.concatenate([from_behind(noise[:, :, -lanes:], "span", 1), noise], axis=2)
    received = lax.ppermute(handed, "slab", SWAP)
    up_same = send(up_same, (0, 1), (1, 2))
    up_across = send_across(up_across, (0, 1), (1, 2))
    query_down = send(query_down, (1, 0), (2, 1), (3, 2))
    query_two = send(query_two, (3, 1))

    arrays = (queries, keys, values, received)
    pair_down, pair_two, up_two = message(
        scalars,
        [pairs_of(DOWN, 0, MIDDLE_HEADS), pairs_of(None, 0, 2), pairs_of(None, MIDDLE, 3)],
        arrays,
        "pack_second",
    )
    anchor = pair_down
    pair_down = send(pair_down, (1, 0), (2, 1), (3, 2))
    pair_two = send(pair_two, (3, 1))
    up_two = send(up_two, (0, 2))

    source, _ = lax.optimization_barrier((received, up_same))
    far_all, far_pair, last_two, last_up = message(
        scalars,
        [
            tokens(None, FAR, FAR_HEADS) + pairs_of(None, FAR, FAR_HEADS),
            pairs_of(None, FAR, FAR_HEADS),
            pairs_of(None, 2, 2),
            pairs_of(None, MIDDLE + 3, 1),
        ],
        (queries, keys, values, source),
        "pack_third",
    )
    far_two = send(far_pair, (1, 3))
    far_three = send(far_pair, (0, 3))
    far_next = send(far_all, (2, 3), (1, 0))
    span_mask, head_gain, patch_weight, _ = lax.optimization_barrier(
        (span_mask, head_gain, patch_weight, anchor)
    )
    mask = span_mask.reshape(-1)
    weight = patch_weight.T
    own = (queries, keys, values, received, weight, head_gain[None, :])
    sums = jnp.zeros((SLOTS, weight.shape[0] + 2 * STAT_ROWS, rows), jnp.float32)
    run = functools.partial(attend, own=own, scalars=scalars, mask=mask)

    on_one, back_one, back_two = Tokens(0, (1,)), Tokens(None, (2, 3)), Tokens(None, (4,))
    here = OWN_TOKENS
    middle = [
        (on_one, 1, 3, [(back_two, 0), (back_one, 1), (here, 2), (on_one, 3)]),
        (here, 0, 2, [(back_two, 0), (back_one, 1), (here, 2)]),
    ]
    sums = run(
        MIDDLE_HEADS,
        (MAIN,),
        0,
        sums=sums,
        payloads=[
            (query_down, None, 0),
            (pair_down, None, 0),
            (up_same, None, 0),
            (up_across, None, 0),
            (up_two, None, 0),
        ],
        variants={
            0: (4, [(here, 0, 0, [(here, 0)]), (on_one, 1, 1, [(here, 0), (on_one, 1)])]),
            1: (
                4,
                [
                    (on_one, 1, 2, [(back_one, 0), (here, 1), (on_one, 2)]),
                    (here, 0, 1, [(back_one, 0), (here, 1)]),
                ],
            ),
            2: (3, middle),
        },
        more=False,
        name="main_heads",
    )
    last_two, last_up, sums = lax.optimization_barrier((last_two, last_up, sums))
    last_two = send(last_two, (3, 1))
    last_up = send(last_up, (0, 2))
    on_two = Tokens(5, (6,))
    last_span = [(on_two, 2, 3, [(back_one, 0), (here, 1), (on_one, 2), (on_two, 3)])]
    sums = run(
        2,
        (MAIN,),
        0,
        sums=sums,
        payloads=[
            (query_down, None, 0),
            (pair_down, None, 0),
            (up_same, None, 0),
            (up_across, None, 0),
            (up_two, None, 0),
            (query_two, None, 0),
            (pair_two, None, 0),
        ],
        variants={1: (2, last_span)},
        more=False,
        name="near_heads",
    )
    beside, two_back, three_back = Tokens(0, (0,)), Tokens(None, (1,)), Tokens(None, (2,))
    extras = [Tokens(None, (), lane) for lane in range(2)]
    sums = run(
        FAR_HEADS,
        (),
        FAR,
        sums=sums,
        payloads=[(far_next, None, 0), (far_two, None, 0), (far_three, None, 0)],
        variants={
            0: (
                FAR_HEADS,
                [(here, 0, 0, [(here, 0)]), (beside, 1, 1, [(here, 0), (beside, 1)])]
                + [(head, 0, 0, [(head, 0)]) for head in extras],
            ),
            3: (
                FAR_HEADS,
                [
                    (here, 0, 3, [(three_back, 0), (two_back, 1), (beside, 2), (here, 3)]),
                    (beside, 2, 2, [(three_back, 0), (two_back, 1), (beside, 2)]),
                ],
            ),
        },
        more=True,
        name="far_heads",
    )

    def last(sums):
        return run(
            2,
            (LAST,),
            0,
            sums=sums,
            payloads=[
                (query_down, LAST_COLUMN, 0),
                (pair_down, LAST_COLUMN, 0),
                (up_same, LAST_COLUMN, 0),
                (up_across, LAST_COLUMN, 0),
                (last_up, None, 0),
                (query_two, LAST_COLUMN, 0),
                (last_two, None, 0),
            ],
            variants={1: (2, last_span), 2: (1, middle)},
            more=False,
            name="last_heads",
        )

    return sums, last, anchor, noise


def noise_window(grid):
    height, breadth, _ = grid.shape
    slab = lax.axis_index("slab")
    edge = jnp.where(slab == 0, grid[:, breadth - 1], grid[:, 0])
    edge = lax.ppermute(edge, "slab", SWAP)[:, None]
    grid = jnp.concatenate(
        [
            jnp.where(slab == 1, edge, 0.0),
            grid,
            jnp.where(slab == 0, edge, 0.0),
            jnp.zeros((height, WINDOW - breadth - 2, grid.shape[2]), grid.dtype),
        ],
        axis=1,
    )
    head = lax.axis_index("head")
    edge = jnp.where(head == 0, grid[height - 1], grid[0])
    edge = lax.ppermute(edge, "head", SWAP)[None]
    grid = jnp.concatenate(
        [jnp.where(head == 1, edge, 0.0), grid, jnp.where(head == 0, edge, 0.0)], axis=0
    )
    return grid.reshape((height + 2) * WINDOW, grid.shape[2])


def cell_selector(height, breadth):
    cell = lax.broadcasted_iota(jnp.int32, ((height + 2) * WINDOW, 4 * TROWS * TCOLS), 0)
    column = lax.broadcasted_iota(jnp.int32, cell.shape, 1)
    y = lax.axis_index("head") * height + cell // WINDOW - 1
    x = lax.axis_index("slab") * breadth + cell % WINDOW - 1
    inside = (y >= 0) & (y < 2 * TROWS) & (x >= 0) & (x < 2 * TCOLS)
    inside = inside & (cell % WINDOW < breadth + 2)
    target = ((y % 2) * 2 + x % 2) * (TROWS * TCOLS) + (y // 2) * TCOLS + x // 2
    return (inside & (column == target)).astype(jnp.bfloat16)


def banded_weight(conv_weight):
    channels = conv_weight.shape[1]
    taps = conv_weight.reshape(3, 3, 3, LAT_CH, channels)
    banded = jnp.stack(
        [
            jnp.pad(taps, ((n, FRAMES_SPAN - 1 - n), (0, 0), (0, 0), (0, 0), (0, 0)))
            for n in range(FRAMES_SPAN)
        ],
        axis=4,
    )
    return banded.transpose(1, 2, 0, 3, 4, 5).reshape(
        3, 3 * (FRAMES_SPAN + 2) * LAT_CH, FRAMES_SPAN * channels
    )


def finish_kernel(
    scalars, mine, other, noise, selector, band, bias, constants, clean, decoded, cells
):
    frames, height, breadth, channels = clean.shape
    patch = constants.shape[0]
    first = scalars[SLAB] == 0
    sums = jnp.concatenate(
        [jnp.where(first, mine[...], other[...]), jnp.where(first, other[...], mine[...])], axis=0
    )
    feature_width = HEADS * HD
    row_mean = sums[patch : patch + 1] / feature_width
    spread = sums[patch + STAT_ROWS : patch + STAT_ROWS + 1] / feature_width - row_mean * row_mean
    velocity = (
        lax.rsqrt(spread + norm_eps) * (sums[:patch] - constants[:, 0:1] * row_mean)
        + constants[:, 1:2]
    )
    tokens = TROWS * TCOLS
    lane = lax.broadcasted_iota(jnp.int32, velocity.shape, 1)
    velocity = jnp.where((lane >= 2 * tokens) | (scalars[PLACE] > 0), velocity, 0.0)
    columns = jnp.concatenate(
        [
            jnp.concatenate(
                [
                    velocity[
                        part * channels : (part + 1) * channels,
                        frame * tokens : (frame + 1) * tokens,
                    ]
                    for part in range(4)
                ],
                axis=1,
            )
            for frame in range(frames + 2)
        ],
        axis=0,
    )
    high = columns.astype(jnp.bfloat16)
    low = (columns - high.astype(jnp.float32)).astype(jnp.bfloat16)
    chosen = sum(
        lax.dot_general(
            selector[...], part, (((1,), (1,)), ((), ())), preferred_element_type=jnp.float32
        )
        for part in (high, low)
    )
    count = (height + 2) * WINDOW
    cells[:count] = noise[...] - noise_level * chosen
    cells[count:] = jnp.zeros_like(cells[count:])
    for frame in range(frames):
        lanes = slice((frame + 2) * channels, (frame + 3) * channels)
        for y in range(height):
            start = (y + 1) * WINDOW + 1
            clean[frame, y] = cells[start : start + breadth, lanes]
    shifted = jnp.concatenate(
        [cells[tap : tap + count] for tap in range(3)], axis=1
    ).astype(jnp.bfloat16)
    total = jnp.broadcast_to(bias[...], (height * breadth, bias.shape[1]))
    for tap in range(3):
        block = jnp.concatenate(
            [
                shifted[(y + tap) * WINDOW : (y + tap) * WINDOW + breadth]
                for y in range(height)
            ],
            axis=0,
        )
        total = total + jnp.dot(block, band[tap], preferred_element_type=jnp.float32)
    outputs = decoded.shape[3]
    total = total.astype(decoded.dtype)
    for frame in range(frames):
        decoded[frame] = total[:, frame * outputs : (frame + 1) * outputs].reshape(
            height, breadth, outputs
        )


def finish(scalars, mine, other, noise, selector, band, bias, constants, shape, outputs):
    whole = pl.BlockSpec(memory_space=pltpu.VMEM)
    frames, height, breadth, channels = shape
    rows = (height + 2) * WINDOW
    return pl.pallas_call(
        finish_kernel,
        name="finish",
        out_shape=(
            jax.ShapeDtypeStruct(shape, jnp.float32),
            jax.ShapeDtypeStruct((frames, height, breadth, outputs), jnp.bfloat16),
        ),
        in_specs=[pl.BlockSpec(memory_space=pltpu.SMEM)] + [whole] * 7,
        out_specs=(whole, whole),
        scratch_shapes=[pltpu.VMEM((rows + 8, (frames + 2) * channels), jnp.float32)],
        compiler_params=pltpu.CompilerParams(vmem_limit_bytes=GRANT),
    )(scalars, mine, other, noise, selector, band, bias, constants)


def per_device(
    queries,
    keys,
    values,
    span_mask,
    head_gain,
    head_shift,
    patch_weight,
    noisy_latent,
    conv_weight,
    conv_bias,
):
    heads_dev = queries.shape[1] // HD
    if not plan_fits(
        heads_dev, lax.axis_size("span"), lax.axis_size("slab"), lax.axis_size("head")
    ):
        return gathered_plan(
            queries,
            keys,
            values,
            span_mask,
            head_gain,
            head_shift,
            patch_weight,
            noisy_latent,
            conv_weight,
            conv_bias,
        )
    place = lax.axis_index("span")
    slab = lax.axis_index("slab")
    scalars = scalar_operand(heads_dev // lax.axis_size("slab"))
    sums, last, anchor, noise = token_sums(
        scalars, queries, keys, values, span_mask, head_gain, patch_weight, noisy_latent
    )

    noise, weight, gain, shift, taps, bias, _ = lax.optimization_barrier(
        (noise, patch_weight, head_gain, head_shift, conv_weight, conv_bias, anchor)
    )
    height, breadth, _ = noise.shape
    noise = noise_window(noise)
    wide_weight = weight.T.astype(jnp.float32)
    constants = jnp.stack(
        [
            jnp.sum(wide_weight * gain[None, :], axis=1),
            jnp.sum(wide_weight * shift[None, :], axis=1),
        ],
        axis=1,
    )
    constants = constants + lax.ppermute(constants, "head", SWAP)
    selector = cell_selector(height, breadth)
    band = banded_weight(taps)
    bias = jnp.tile(bias, FRAMES_SPAN)[None, :]
    sums, noise, constants, selector, band, bias = lax.optimization_barrier(
        (sums, noise, constants, selector, band, bias)
    )

    sums = last(sums)
    half = sums.shape[1] // 2
    mine = lax.dynamic_slice_in_dim(sums, slab * half, half, 1)
    theirs = lax.dynamic_slice_in_dim(sums, (1 - slab) * half, half, 1)
    mine = mine + lax.ppermute(theirs, "slab", SWAP)
    own, after, third = mine[0], mine[1], mine[2]
    skip = TROWS * TCOLS
    from_one = lax.ppermute(
        jnp.concatenate([own[:, skip:], after], axis=1), "span", [(0, 1), (1, 2), (2, 3)]
    )
    to_current = lax.ppermute(third, "span", [(1, 3), (3, 2)])
    to_before = lax.ppermute(after[:, skip:], "span", [(0, 2), (1, 3)])
    kept = jnp.concatenate([jnp.where(place == 3, third[:, skip:], 0.0), own], axis=1)
    total = kept + from_one + jnp.concatenate([to_before, to_current], axis=1)
    total = total + lax.ppermute(total, "head", SWAP)
    other = lax.ppermute(total, "slab", SWAP)
    return finish(
        scalars,
        total,
        other,
        noise,
        selector,
        band,
        bias,
        constants,
        noisy_latent.shape,
        conv_weight.shape[1],
    )


def solution(mesh):
    placed = (
        P(("groups", "span"), "head"),
        P(("groups", "span", "slab"), "head"),
        P(("groups", "span", "slab"), "head"),
        P("groups", None),
        P("head"),
        P("head"),
        P("head", None),
        P(("groups", "span"), "head", "slab", None),
        P(),
        P(),
    )
    return jax.shard_map(
        per_device,
        mesh=mesh,
        in_specs=placed,
        out_specs=(
            P(("groups", "span"), "head", "slab", None),
            P(("groups", "span"), "head", "slab", None),
        ),
        check_vma=False,
    )
```

```python
import functools
import math
import typing

import jax
import jax.numpy as jnp
import numpy as np
from jax import lax
from jax.experimental import pallas as pl
from jax.experimental.pallas import tpu as pltpu
from jax.sharding import PartitionSpec as P

HEADS = 40
HD = 128
LAT_CH = 16
FRAMES_SPAN = 3
TROWS = 8
TCOLS = 16


neg_big = -1e30
noise_level = 0.75
norm_eps = 1e-06


def with_halo(cells, sides, width):
    for axis, dim in sides:
        count = lax.axis_size(axis)
        ends = count - 1
        head = lax.slice_in_dim(cells, 0, width, axis=dim)
        tail = lax.slice_in_dim(cells, cells.shape[dim] - width, cells.shape[dim], axis=dim)
        cells = jnp.concatenate(
            [
                lax.ppermute(tail, axis, [(i, (i + 1) % count) for i in range(ends)]),
                cells,
                lax.ppermute(head, axis, [((i + 1) % count, i) for i in range(ends)]),
            ],
            axis=dim,
        )
    return cells


def from_behind(value, axis, by):
    size = lax.axis_size(axis)
    pairs = [(i, i + by) for i in range(size) if 0 <= i + by < size]
    return lax.ppermute(value, axis, pairs)


def block_length(total_rows):
    block_size = total_rows
    while block_size > 768 and block_size % 2 == 0:
        block_size = block_size // 2
    return block_size


def fold_keys(partial_state, key_value, query_block, mask_row, rows_span):
    keys_piece, values_piece = key_value
    heads_dev = query_block.shape[1]
    piece_rows = keys_piece.shape[0]
    length = block_length(piece_rows)
    span_count = mask_row.shape[0]
    score_scale = 1.0 / math.sqrt(HD)
    span_ids = jnp.arange(span_count, dtype=jnp.int32)

    def one_block(carry_state, block_index):
        running_max, running_sum, weighted = carry_state
        offset = block_index * length
        key_block = lax.dynamic_slice_in_dim(keys_piece, offset, length, 0).reshape(
            length, heads_dev, HD
        )
        value_block = lax.dynamic_slice_in_dim(values_piece, offset, length, 0).reshape(
            length, heads_dev, HD
        )
        key_span = (offset + jnp.arange(length, dtype=jnp.int32)) // rows_span
        allowed = (
            jnp.sum(jnp.where(key_span[:, None] == span_ids[None, :], mask_row[None, :], 0), axis=1)
            > 0
        )
        scores = (
            jnp.einsum("qhd,khd->hqk", query_block, key_block, preferred_element_type=jnp.float32)
            * score_scale
        )
        scores = jnp.where(allowed[None, None, :], scores, neg_big)
        new_max = jnp.maximum(running_max, jnp.max(scores, axis=2))
        weights = jnp.where(allowed[None, None, :], jnp.exp(scores - new_max[:, :, None]), 0.0)
        factor = jnp.exp(running_max - new_max)
        running_sum = running_sum * factor + jnp.sum(weights, axis=2)
        weighted = weighted * factor.T[:, :, None] + jnp.einsum(
            "hqk,khd->qhd",
            weights.astype(jnp.bfloat16),
            value_block,
            preferred_element_type=jnp.float32,
        )
        return ((new_max, running_sum, weighted), None)

    result, unused = lax.scan(
        one_block, partial_state, jnp.arange(piece_rows // length, dtype=jnp.int32)
    )
    return result


def gathered_plan(
    queries,
    keys,
    values,
    span_mask,
    head_gain,
    head_shift,
    patch_weight,
    noisy_latent,
    conv_weight,
    conv_bias,
):
    heads_dev = queries.shape[1] // HD
    slab_count = lax.axis_size("slab")
    col_dev = TCOLS // slab_count
    slab_place = lax.axis_index("slab")
    span_place = lax.axis_index("span")
    mask_row = lax.dynamic_slice_in_dim(span_mask, span_place, 1, 0)[0]
    token_grid = queries.reshape(FRAMES_SPAN, TROWS, TCOLS, queries.shape[-1])
    picked = lax.dynamic_slice_in_dim(token_grid, slab_place * col_dev, col_dev, 2)
    own_queries = picked.reshape(FRAMES_SPAN * TROWS * col_dev, queries.shape[-1]).reshape(
        -1, heads_dev, HD
    )
    query_rows = own_queries.shape[0]
    rows_span = keys.shape[0] * slab_count
    running_max, running_sum, weighted = fold_keys(
        (
            jnp.full((heads_dev, query_rows), neg_big, jnp.float32),
            jnp.zeros((heads_dev, query_rows), jnp.float32),
            jnp.zeros((query_rows, heads_dev, HD), jnp.float32),
        ),
        (
            lax.all_gather(keys, ("span", "slab"), axis=0, tiled=True),
            lax.all_gather(values, ("span", "slab"), axis=0, tiled=True),
        ),
        own_queries,
        mask_row,
        rows_span,
    )
    attended = (
        (weighted / running_sum.T[:, :, None])
        .astype(jnp.bfloat16)
        .reshape(query_rows, heads_dev * HD)
    )
    feature_width = HEADS * HD
    values32 = attended.astype(jnp.float32)
    row_total = jnp.sum(values32, axis=1)
    row_squares = jnp.sum(values32 * values32, axis=1)
    row_total, row_squares = lax.psum((row_total, row_squares), "head")
    row_mean = row_total / feature_width
    spread = row_squares / feature_width - row_mean * row_mean
    normed = (
        (values32 - row_mean[:, None]) * lax.rsqrt(spread + norm_eps)[:, None] * head_gain[None, :]
        + head_shift[None, :]
    ).astype(jnp.bfloat16)
    normed_grid = normed.reshape(FRAMES_SPAN, TROWS, col_dev, normed.shape[-1])
    own_rows = TROWS // lax.axis_size("head")
    picked = normed_grid
    product = jnp.dot(
        picked.reshape(-1, picked.shape[-1]), patch_weight, preferred_element_type=jnp.float32
    )
    velocity = lax.psum_scatter(
        product.reshape(
            FRAMES_SPAN, own_rows * lax.axis_size("head"), col_dev * patch_weight.shape[1]
        )
        .transpose(1, 0, 2)
        .reshape(own_rows * lax.axis_size("head"), -1)
        .astype(jnp.bfloat16),
        "head",
        scatter_dimension=0,
        tiled=True,
    ).astype(jnp.float32)
    rows_dev = velocity.shape[0]
    patch_cells = (
        velocity.reshape(rows_dev, FRAMES_SPAN, col_dev, 2, 2, LAT_CH)
        .transpose(1, 0, 3, 2, 4, 5)
        .reshape(FRAMES_SPAN, 2 * rows_dev, 2 * col_dev, LAT_CH)
    )
    clean_latent = noisy_latent - noise_level * patch_cells
    latent_input = clean_latent.astype(jnp.bfloat16)
    framed = with_halo(latent_input, (("head", 1), ("slab", 2)), 1)
    earlier = from_behind(framed[FRAMES_SPAN - 2 :], "span", 1)
    stacked = jnp.concatenate([earlier, framed], axis=0)
    height = clean_latent.shape[1]
    breadth = clean_latent.shape[2]
    columns = jnp.concatenate(
        [
            stacked[
                frame_tap : frame_tap + FRAMES_SPAN,
                row_tap : row_tap + height,
                col_tap : col_tap + breadth,
                :,
            ]
            for frame_tap in range(3)
            for row_tap in range(3)
            for col_tap in range(3)
        ],
        axis=-1,
    )
    decoded = (
        jnp.dot(
            columns.reshape(FRAMES_SPAN * height * breadth, 27 * LAT_CH),
            conv_weight,
            preferred_element_type=jnp.float32,
        )
        + conv_bias[None, :]
    )
    decoded = decoded.astype(jnp.bfloat16).reshape(
        FRAMES_SPAN, height, breadth, conv_weight.shape[1]
    )
    return (clean_latent, decoded)


NEAR_HEADS = 4
MIDDLE_HEADS = 4
FAR_HEADS = 2
MIDDLE = NEAR_HEADS
FAR = NEAR_HEADS + MIDDLE_HEADS
STAT_ROWS = 8
SLOTS = 3
QUERY_ROWS = 192
SWAP = [(0, 1), (1, 0)]
WINDOW = 32
GRANT = 20 << 20

OWN, OTHER, DOWN, UP, MAIN, LAST, LAST_COLUMN, PLACE, SLAB = range(9)
STEPS = 9


def plan_fits(heads_dev, span_count, slab_count, head_count):
    return (
        span_count == 4
        and slab_count == 2
        and head_count == 2
        and heads_dev == slab_count * (NEAR_HEADS + MIDDLE_HEADS + FAR_HEADS)
    )


def scalar_operand(heads):
    by_place = np.zeros((4, 12), np.int32)
    by_place[:, OTHER] = heads
    by_place[:, DOWN] = [MIDDLE, MIDDLE, 0, MIDDLE]
    by_place[:, UP] = [0, MIDDLE, 0, 0]
    by_place[:, MAIN] = [MIDDLE, 0, MIDDLE, 0]
    by_place[:, LAST] = [0, 2, MIDDLE + 3, 0]
    by_place[:, LAST_COLUMN] = [0, 2, 3, 0]
    by_place[:, PLACE] = range(4)
    by_slab = np.zeros(12, np.int32)
    by_slab[[OWN, OTHER, SLAB]] = heads, -heads, 1
    row = lax.dynamic_slice_in_dim(jnp.array(by_place), lax.axis_index("span"), 1, 0)[0]
    return row + lax.axis_index("slab") * jnp.array(by_slab)


def pack_kernel(inputs, messages, copies, with_noise, scalars, *refs):
    ins, rest = refs[:inputs], refs[inputs:]
    outs = rest[: messages + with_noise]
    staged = rest[messages + with_noise : -2]
    arrive, leave = rest[-2:]
    arriving = [[] for _ in range(messages)]
    for number, (source, row, rows, entries, shift, target, at, heads) in enumerate(copies):
        head = shift
        for entry in entries:
            head = head + scalars[entry]
        column = pl.multiple_of(head * HD, HD)
        copy = pltpu.make_async_copy(
            ins[source].at[pl.ds(row, rows), pl.ds(column, heads * HD)],
            staged[target].at[pl.ds(at, rows), :],
            arrive.at[number],
        )
        copy.start()
        arriving[target].append(copy)
    if with_noise:
        noisy, out = ins[-1], outs[-1]
        frames = noisy.shape[0]
        out[...] = jnp.concatenate([noisy[frame] for frame in range(frames)], axis=-1)
    leaving = []
    for target in range(messages):
        for copy in arriving[target]:
            copy.wait()
        copy = pltpu.make_async_copy(staged[target], outs[target], leave.at[target])
        copy.start()
        leaving.append(copy)
    for copy in leaving:
        copy.wait()


def pack(scalars, arrays, shapes, copies, name, noisy=None):
    moved = sum(2 * 2 * rows * heads * HD for _, _, rows, _, _, _, _, heads in copies)
    out_shape = [pltpu.HBM(shape, jnp.bfloat16) for shape in shapes]
    in_specs = [pl.BlockSpec(memory_space=pl.ANY)] * len(arrays)
    out_specs = [pl.BlockSpec(memory_space=pl.ANY)] * len(shapes)
    if noisy is not None:
        frames, height, breadth, channels = noisy.shape
        lanes = frames * channels
        arrays = arrays + (noisy,)
        in_specs.append(pl.BlockSpec(noisy.shape, lambda i, scalars: (0, 0, 0, 0)))
        out_shape.append(jax.ShapeDtypeStruct((height, breadth, lanes), noisy.dtype))
        out_specs.append(pl.BlockSpec((height, breadth, lanes), lambda i, scalars: (0, 0, 0)))
    return pl.pallas_call(
        functools.partial(
            pack_kernel, len(arrays), len(shapes), copies, noisy is not None
        ),
        name=name,
        out_shape=out_shape,
        grid_spec=pltpu.PrefetchScalarGridSpec(
            num_scalar_prefetch=1,
            grid=(1,),
            in_specs=in_specs,
            out_specs=out_specs,
            scratch_shapes=[pltpu.VMEM(shape, jnp.bfloat16) for shape in shapes]
            + [
                pltpu.SemaphoreType.DMA((len(copies),)),
                pltpu.SemaphoreType.DMA((len(shapes),)),
            ],
        ),
        compiler_params=pltpu.CompilerParams(vmem_limit_bytes=GRANT),
        cost_estimate=pl.CostEstimate(flops=0, bytes_accessed=moved, transcendentals=0),
    )(scalars, *arrays)


def message(scalars, pieces, arrays, name, noisy=None):
    copies, shapes = [], []
    for target, parts in enumerate(pieces):
        at = 0
        for source, row, rows, entries, shift, heads in parts:
            copies.append((source, row, rows, entries, shift, target, at, heads))
            at += rows
        shapes.append((at, parts[0][5] * HD))
    return pack(scalars, arrays, shapes, copies, name, noisy)


class Tokens(typing.NamedTuple):
    query: int | None = None
    pairs: tuple = ()
    extra: int | None = None


OWN_TOKENS = Tokens()


def attend_kernel(variants, extra, span_count, fresh, scalars, mask, *refs):
    query_own, key_own, value_own, received, weight, gain = refs[:6]
    more = refs[6 : 6 + extra]
    sums_out, folded, squares, carried, fetched, stored = refs[-6:]
    payloads = refs[6 + extra : -6] if fresh else refs[6 + extra : -7]
    rows = query_own.shape[0]
    half = rows // 2
    step = pl.program_id(0)
    to_exp2 = math.log2(math.e) / math.sqrt(HD)
    active = functools.reduce(
        lambda a, b: a | b, [scalars[PLACE] == place for place in variants]
    )

    last_step = step == pl.num_programs(0) - 1
    fetch = None if fresh else pltpu.make_async_copy(refs[-7], carried, fetched)

    @pl.when((step == 0) & active)
    def _():
        folded[...] = jnp.zeros_like(folded)
        squares[...] = jnp.zeros_like(squares)
        if fetch is not None:
            fetch.start()

    def query_of(source):
        if source is OWN_TOKENS:
            return query_own[...]
        if source.extra is not None:
            return more[0][:, source.extra * HD : (source.extra + 1) * HD]
        return payloads[source.query][:rows]

    def pair_of(source):
        if source is OWN_TOKENS:
            parts = (key_own[...], received[:half], value_own[...], received[half:])
        elif source.extra is not None:
            lanes = slice(source.extra * HD, (source.extra + 1) * HD)
            parts = (more[1][:, lanes], more[3][:half, lanes], more[2][:, lanes], more[3][half:, lanes])
        elif len(source.pairs) == 2:
            one, two = (payloads[number] for number in source.pairs)
            parts = (one[:half], two[:half], one[half:], two[half:])
        else:
            payload = payloads[source.pairs[0]]
            start = payload.shape[0] - 2 * rows
            return payload[start : start + rows], payload[start + rows :]
        return jnp.concatenate(parts[:2], axis=0), jnp.concatenate(parts[2:], axis=0)

    def projector(extra_head):
        if extra_head is None:
            scaled = weight[...].astype(jnp.float32) * gain[...]
        else:
            lanes = slice(extra_head * HD, (extra_head + 1) * HD)
            scaled = more[4][:, lanes].astype(jnp.float32) * more[5][:, lanes]
        high = scaled.astype(jnp.bfloat16)
        low = (scaled - high.astype(jnp.float32)).astype(jnp.bfloat16)
        return jnp.concatenate([high, low, jnp.ones((16, HD), jnp.bfloat16)], axis=0)

    def one_query(source, slot, query_span, key_sources):
        query = query_of(source)
        pairs = [pair_of(key_source) for key_source, _ in key_sources]
        open_to = [
            None if key_span == query_span else mask[query_span * span_count + key_span] > 0
            for _, key_span in key_sources
        ]
        keys_in = jnp.concatenate([pair[0] for pair in pairs], axis=0)
        ones_block = jnp.ones((rows, HD), jnp.bfloat16)
        values_in = jnp.concatenate(
            [jnp.concatenate([pair[1], ones_block], axis=1) for pair in pairs], axis=0
        )
        pieces = []
        for row in range(0, rows, QUERY_ROWS):
            score = lax.dot_general(
                query[row : row + QUERY_ROWS],
                keys_in,
                (((1,), (1,)), ((), ())),
                preferred_element_type=jnp.float32,
            )
            best = None
            for number, is_open in enumerate(open_to):
                start = number * rows
                block = score[:, start : start + HD]
                for lane in range(HD, rows, HD):
                    block = jnp.maximum(block, score[:, start + lane : start + lane + HD])
                if is_open is not None:
                    block = jnp.where(is_open, block, neg_big)
                best = block if best is None else jnp.maximum(best, block)
            top = jnp.max(best, axis=1, keepdims=True)
            weights = []
            for number, is_open in enumerate(open_to):
                start = number * rows
                shift = top if is_open is None else jnp.where(is_open, top, -neg_big)
                weights.append(
                    jnp.exp2((score[:, start : start + rows] - shift) * to_exp2).astype(jnp.bfloat16)
                )
            both = jnp.dot(
                jnp.concatenate(weights, axis=1), values_in, preferred_element_type=jnp.float32
            )
            pieces.append((both[:, :HD] / both[:, HD:]).astype(jnp.bfloat16))
        attended = jnp.concatenate(pieces, axis=0)
        folded[slot] += lax.dot_general(
            projector(source.extra),
            attended,
            (((1,), (1,)), ((), ())),
            preferred_element_type=jnp.float32,
        )
        wide = attended.astype(jnp.float32)
        squares[slot] += wide * wide

    for place, (steps, tasks) in variants.items():

        @pl.when((scalars[PLACE] == place) & (step < steps))
        def _():
            for task in tasks:
                one_query(*task)

    def store():
        copy = pltpu.make_async_copy(carried, sums_out, stored)
        copy.start()
        copy.wait()

    if fresh:

        @pl.when(last_step & jnp.logical_not(active))
        def _():
            carried[...] = jnp.zeros_like(carried)
            store()

    @pl.when(last_step & active)
    def _():
        ones_rows = jnp.ones((STAT_ROWS, HD), jnp.bfloat16)
        patch = weight.shape[0]
        used = sorted({task[1] for _, tasks in variants.values() for task in tasks})
        if fetch is not None:
            fetch.wait()
        for slot in range(SLOTS):
            if slot not in used:
                if fresh:
                    carried[slot] = jnp.zeros(carried.shape[1:], carried.dtype)
                continue
            left = squares[slot]
            total = jnp.zeros((STAT_ROWS, rows), jnp.float32)
            for _ in range(3):
                piece = left.astype(jnp.bfloat16)
                left = left - piece.astype(jnp.float32)
                total = total + lax.dot_general(
                    ones_rows, piece, (((1,), (1,)), ((), ())), preferred_element_type=jnp.float32
                )
            done = folded[slot]
            new = jnp.concatenate(
                [
                    done[:patch] + done[patch : 2 * patch],
                    done[2 * patch : 2 * patch + STAT_ROWS],
                    total,
                ],
                axis=0,
            )
            carried[slot] = new if fresh else carried[slot] + new
        store()


def attend(
    steps, entries, first, own, scalars, mask, sums, payloads, variants, more, name, cost=1
):
    queries, keys, values, received, weight, gain = own
    rows = queries.shape[0]
    half = rows // 2
    patch = weight.shape[0]

    def moving(i, scalars):
        used = functools.reduce(
            lambda a, b: a | b, [scalars[PLACE] == place for place in variants]
        )
        return jnp.where(used, i, 0)

    def column(height, own_column):
        def index(i, scalars, mask):
            head = first + moving(i, scalars) + (scalars[OWN] if own_column else 0)
            for entry in entries:
                head = head + scalars[entry]
            return (0, head)

        return pl.BlockSpec((height, HD), index)

    def two_columns(height, own_column):
        return pl.BlockSpec(
            (height, 2 * HD),
            lambda i, scalars, mask: (
                0,
                moving(i, scalars) + (scalars[OWN] // 2 if own_column else 0),
            ),
        )

    def payload_column(payload, entry, shift):
        last = payload.shape[1] // HD - 1

        def index(i, scalars, mask):
            at = shift + moving(i, scalars)
            return (0, jnp.minimum(at if entry is None else at + scalars[entry], last))

        return pl.BlockSpec((payload.shape[0], HD), index)

    in_specs = [
        column(rows, True),
        column(half, True),
        column(half, True),
        column(rows, False),
        column(patch, True),
        column(1, True),
    ]
    arrays = [queries, keys, values, received, weight, gain]
    extra = 0
    if more:
        extra = 6
        in_specs += [
            two_columns(rows, True),
            two_columns(half, True),
            two_columns(half, True),
            two_columns(rows, False),
            two_columns(patch, True),
            two_columns(1, True),
        ]
        arrays += [queries, keys, values, received, weight, gain]
    in_specs += [payload_column(*payload) for payload in payloads]
    arrays += [payload[0] for payload in payloads]
    fresh = sums is None
    sums_shape = (SLOTS, patch + 2 * STAT_ROWS, rows)
    aliases = {}
    if not fresh:
        aliases = {2 + len(arrays): 0}
        in_specs.append(pl.BlockSpec(memory_space=pl.ANY))
        arrays.append(sums)
    pairs = max(
        count * sum(len(task[3]) for task in tasks) for count, tasks in variants.values()
    )
    span_count = math.isqrt(mask.shape[0])
    return pl.pallas_call(
        functools.partial(attend_kernel, variants, extra, span_count, fresh),
        name=name,
        out_shape=pltpu.HBM(sums_shape, jnp.float32),
        input_output_aliases=aliases,
        grid_spec=pltpu.PrefetchScalarGridSpec(
            num_scalar_prefetch=2,
            grid=(steps,),
            in_specs=in_specs,
            out_specs=pl.BlockSpec(memory_space=pl.ANY),
            scratch_shapes=[
                pltpu.VMEM((SLOTS, 2 * patch + 16, rows), jnp.float32),
                pltpu.VMEM((SLOTS, rows, HD), jnp.float32),
                pltpu.VMEM(sums_shape, jnp.float32),
                pltpu.SemaphoreType.DMA,
                pltpu.SemaphoreType.DMA,
            ],
        ),
        compiler_params=pltpu.CompilerParams(vmem_limit_bytes=GRANT),
        cost_estimate=pl.CostEstimate(
            flops=cost * pairs * 4 * rows * rows * HD,
            bytes_accessed=steps * HD * 2 * sum(spec.block_shape[0] for spec in in_specs[:4]),
            transcendentals=cost * pairs * rows * rows,
        ),
    )(scalars, mask, *arrays)


def token_sums(
    scalars, queries, keys, values, span_mask, head_gain, patch_weight, noisy, prepare
):
    rows = queries.shape[0]
    half = rows // 2
    heads = NEAR_HEADS + MIDDLE_HEADS + FAR_HEADS
    queries, keys, values = (
        pltpu.with_memory_space_constraint(array, pltpu.HBM) for array in (queries, keys, values)
    )

    def send(value, *pairs):
        return lax.ppermute(value, "span", list(pairs))

    def send_across(value, *pairs):
        slabs = lax.axis_size("slab")
        return lax.ppermute(
            value,
            ("span", "slab"),
            [(a * slabs + s, b * slabs + 1 - s) for a, b in pairs for s in range(slabs)],
        )

    def tokens(entry, shift, count):
        return [(0, 0, rows, (OWN, entry) if entry else (OWN,), shift, count)]

    def own_half(slab_entry, entry, shift, count):
        return [(part, 0, half, (slab_entry, entry), shift, count) for part in (1, 2)]

    def pairs_of(entry, shift, count):
        entries = (entry,) if entry else ()
        return [
            piece
            for part in (1, 2)
            for piece in (
                (part, 0, half, (OWN,) + entries, shift, count),
                (3, (part - 1) * half, half, entries, shift, count),
            )
        ]

    handed, up_same, up_across, query_down, noise = message(
        scalars,
        [
            [(part, 0, half, (OTHER,), 0, heads) for part in (1, 2)],
            own_half(OWN, UP, 0, NEAR_HEADS),
            own_half(OTHER, UP, 0, NEAR_HEADS),
            tokens(DOWN, 0, MIDDLE_HEADS),
        ],
        (queries, keys, values),
        "pack_first",
        noisy,
    )
    lanes = 2 * noisy.shape[3]
    noise = jnp.concatenate([from_behind(noise[:, :, -lanes:], "span", 1), noise], axis=2)
    received = lax.ppermute(handed, "slab", SWAP)
    up_same = send(up_same, (0, 1), (1, 2))
    up_across = send_across(up_across, (0, 1), (1, 2))
    query_down = send(query_down, (1, 0), (2, 1), (3, 2))

    arrays = (queries, keys, values, received)
    pair_down, up_two = message(
        scalars,
        [pairs_of(DOWN, 0, MIDDLE_HEADS), pairs_of(None, MIDDLE, 3)],
        arrays,
        "pack_second",
    )
    source, _ = lax.optimization_barrier((received, pair_down))
    two, far_all, far_pair, last_two, last_up = message(
        scalars,
        [
            tokens(None, 0, 2) + pairs_of(None, 0, 2),
            tokens(None, FAR, FAR_HEADS) + pairs_of(None, FAR, FAR_HEADS),
            pairs_of(None, FAR, FAR_HEADS),
            tokens(None, 2, 2) + pairs_of(None, 2, 2),
            pairs_of(None, MIDDLE + 3, 1),
        ],
        (queries, keys, values, source),
        "pack_third",
    )
    anchor = two
    pair_down = send(pair_down, (1, 0), (2, 1), (3, 2))
    up_two = send(up_two, (0, 2))
    two = send(two, (3, 1))
    far_next = send(far_all, (2, 3), (1, 0))
    far_pair, prepared = lax.optimization_barrier((far_pair, prepare(noise, anchor)))
    far_two = send(far_pair, (1, 3))
    far_three = send(far_pair, (0, 3))

    span_mask, head_gain, patch_weight, _ = lax.optimization_barrier(
        (span_mask, head_gain, patch_weight, anchor)
    )
    mask = span_mask.reshape(-1)
    weight = patch_weight.T
    own = (queries, keys, values, received, weight, head_gain[None, :])
    run = functools.partial(attend, own=own, scalars=scalars, mask=mask)

    on_one, back_one, back_two = Tokens(0, (1,)), Tokens(None, (2, 3)), Tokens(None, (4,))
    here = OWN_TOKENS
    middle = [
        (on_one, 1, 3, [(back_two, 0), (back_one, 1), (here, 2), (on_one, 3)]),
        (here, 0, 2, [(back_two, 0), (back_one, 1), (here, 2)]),
    ]
    sums = run(
        MIDDLE_HEADS,
        (MAIN,),
        0,
        sums=None,
        payloads=[
            (query_down, None, 0),
            (pair_down, None, 0),
            (up_same, None, 0),
            (up_across, None, 0),
            (up_two, None, 0),
        ],
        variants={
            0: (4, [(here, 0, 0, [(here, 0)]), (on_one, 1, 1, [(here, 0), (on_one, 1)])]),
            1: (
                4,
                [
                    (on_one, 1, 2, [(back_one, 0), (here, 1), (on_one, 2)]),
                    (here, 0, 1, [(back_one, 0), (here, 1)]),
                ],
            ),
            2: (3, middle),
        },
        more=False,
        name="main_heads",
    )
    last_two, last_up, sums = lax.optimization_barrier((last_two, last_up, sums))
    last_two = send(last_two, (3, 1))
    last_up = send(last_up, (0, 2))
    on_two = Tokens(5, (5,))
    last_span = [(on_two, 2, 3, [(back_one, 0), (here, 1), (on_one, 2), (on_two, 3)])]
    sums = run(
        2,
        (MAIN,),
        0,
        sums=sums,
        payloads=[
            (query_down, None, 0),
            (pair_down, None, 0),
            (up_same, None, 0),
            (up_across, None, 0),
            (up_two, None, 0),
            (two, None, 0),
        ],
        variants={1: (2, last_span)},
        more=False,
        name="near_heads",
    )
    beside, two_back, three_back = Tokens(0, (0,)), Tokens(None, (1,)), Tokens(None, (2,))
    extras = [Tokens(None, (), lane) for lane in range(2)]
    sums = run(
        FAR_HEADS,
        (),
        FAR,
        sums=sums,
        payloads=[(far_next, None, 0), (far_two, None, 0), (far_three, None, 0)],
        variants={
            0: (
                FAR_HEADS,
                [(here, 0, 0, [(here, 0)]), (beside, 1, 1, [(here, 0), (beside, 1)])]
                + [(head, 0, 0, [(head, 0)]) for head in extras],
            ),
            3: (
                FAR_HEADS,
                [
                    (here, 0, 3, [(three_back, 0), (two_back, 1), (beside, 2), (here, 3)]),
                    (beside, 2, 2, [(three_back, 0), (two_back, 1), (beside, 2)]),
                ],
            ),
        },
        more=True,
        name="far_heads",
        cost=4,
    )

    def last(sums):
        return run(
            2,
            (LAST,),
            0,
            sums=sums,
            payloads=[
                (query_down, LAST_COLUMN, 0),
                (pair_down, LAST_COLUMN, 0),
                (up_same, LAST_COLUMN, 0),
                (up_across, LAST_COLUMN, 0),
                (last_up, None, 0),
                (last_two, None, 0),
            ],
            variants={1: (2, last_span), 2: (1, middle)},
            more=False,
            name="last_heads",
        )

    sums, prepared = lax.optimization_barrier((sums, prepared))
    return last(sums), prepared


def noise_window(grid):
    height, breadth, _ = grid.shape
    slab = lax.axis_index("slab")
    edge = jnp.where(slab == 0, grid[:, breadth - 1], grid[:, 0])
    edge = lax.ppermute(edge, "slab", SWAP)[:, None]
    grid = jnp.concatenate(
        [
            jnp.where(slab == 1, edge, 0.0),
            grid,
            jnp.where(slab == 0, edge, 0.0),
            jnp.zeros((height, WINDOW - breadth - 2, grid.shape[2]), grid.dtype),
        ],
        axis=1,
    )
    head = lax.axis_index("head")
    edge = jnp.where(head == 0, grid[height - 1], grid[0])
    edge = lax.ppermute(edge, "head", SWAP)[None]
    grid = jnp.concatenate(
        [jnp.where(head == 1, edge, 0.0), grid, jnp.where(head == 0, edge, 0.0)], axis=0
    )
    return grid.reshape((height + 2) * WINDOW, grid.shape[2])


def cell_selector(height, breadth):
    cell = lax.broadcasted_iota(jnp.int32, ((height + 2) * WINDOW, 4 * TROWS * TCOLS), 0)
    column = lax.broadcasted_iota(jnp.int32, cell.shape, 1)
    y = lax.axis_index("head") * height + cell // WINDOW - 1
    x = lax.axis_index("slab") * breadth + cell % WINDOW - 1
    inside = (y >= 0) & (y < 2 * TROWS) & (x >= 0) & (x < 2 * TCOLS)
    inside = inside & (cell % WINDOW < breadth + 2)
    target = ((y % 2) * 2 + x % 2) * (TROWS * TCOLS) + (y // 2) * TCOLS + x // 2
    return (inside & (column == target)).astype(jnp.bfloat16)


def band_kernel(weight, band):
    outputs = weight.shape[1]
    band[...] = jnp.zeros_like(band)
    for row_tap in range(3):
        for col_tap in range(3):
            for frame_tap in range(3):
                start = ((3 * frame_tap + row_tap) * 3 + col_tap) * LAT_CH
                block = weight[start : start + LAT_CH]
                for frame in range(FRAMES_SPAN):
                    at = (col_tap * (FRAMES_SPAN + 2) + frame + frame_tap) * LAT_CH
                    band[
                        row_tap, at : at + LAT_CH, frame * outputs : (frame + 1) * outputs
                    ] = block


def banded_weight(conv_weight):
    shape = (3, 3 * (FRAMES_SPAN + 2) * LAT_CH, FRAMES_SPAN * conv_weight.shape[1])
    return pl.pallas_call(
        band_kernel,
        name="band",
        out_shape=jax.ShapeDtypeStruct(shape, conv_weight.dtype),
        in_specs=[pl.BlockSpec(memory_space=pltpu.VMEM)],
        out_specs=pl.BlockSpec(memory_space=pltpu.VMEM),
        compiler_params=pltpu.CompilerParams(vmem_limit_bytes=GRANT),
        cost_estimate=pl.CostEstimate(
            flops=0, bytes_accessed=2 * math.prod(shape), transcendentals=0
        ),
    )(conv_weight)


def finish_kernel(
    scalars, mine, other, noise, selector, band, bias, constants, clean, decoded, cells
):
    frames, height, breadth, channels = clean.shape
    patch = constants.shape[0]
    first = scalars[SLAB] == 0
    sums = jnp.concatenate(
        [jnp.where(first, mine[...], other[...]), jnp.where(first, other[...], mine[...])], axis=0
    )
    feature_width = HEADS * HD
    row_mean = sums[patch : patch + 1] / feature_width
    spread = sums[patch + STAT_ROWS : patch + STAT_ROWS + 1] / feature_width - row_mean * row_mean
    velocity = (
        lax.rsqrt(spread + norm_eps) * (sums[:patch] - constants[:, 0:1] * row_mean)
        + constants[:, 1:2]
    )
    tokens = TROWS * TCOLS
    lane = lax.broadcasted_iota(jnp.int32, velocity.shape, 1)
    velocity = jnp.where((lane >= 2 * tokens) | (scalars[PLACE] > 0), velocity, 0.0)
    columns = jnp.concatenate(
        [
            jnp.concatenate(
                [
                    velocity[
                        part * channels : (part + 1) * channels,
                        frame * tokens : (frame + 1) * tokens,
                    ]
                    for part in range(4)
                ],
                axis=1,
            )
            for frame in range(frames + 2)
        ],
        axis=0,
    )
    high = columns.astype(jnp.bfloat16)
    low = (columns - high.astype(jnp.float32)).astype(jnp.bfloat16)
    chosen = sum(
        lax.dot_general(
            selector[...], part, (((1,), (1,)), ((), ())), preferred_element_type=jnp.float32
        )
        for part in (high, low)
    )
    count = (height + 2) * WINDOW
    cells[:count] = noise[...] - noise_level * chosen
    cells[count:] = jnp.zeros_like(cells[count:])
    for frame in range(frames):
        lanes = slice((frame + 2) * channels, (frame + 3) * channels)
        for y in range(height):
            start = (y + 1) * WINDOW + 1
            clean[frame, y] = cells[start : start + breadth, lanes]
    shifted = jnp.concatenate(
        [cells[tap : tap + count] for tap in range(3)], axis=1
    ).astype(jnp.bfloat16)
    total = jnp.broadcast_to(bias[...], (height * breadth, bias.shape[1]))
    for tap in range(3):
        block = jnp.concatenate(
            [
                shifted[(y + tap) * WINDOW : (y + tap) * WINDOW + breadth]
                for y in range(height)
            ],
            axis=0,
        )
        total = total + jnp.dot(block, band[tap], preferred_element_type=jnp.float32)
    outputs = decoded.shape[3]
    total = total.astype(decoded.dtype)
    for frame in range(frames):
        decoded[frame] = total[:, frame * outputs : (frame + 1) * outputs].reshape(
            height, breadth, outputs
        )


def finish(scalars, mine, other, noise, selector, band, bias, constants, shape, outputs):
    whole = pl.BlockSpec(memory_space=pltpu.VMEM)
    frames, height, breadth, channels = shape
    rows = (height + 2) * WINDOW
    return pl.pallas_call(
        finish_kernel,
        name="finish",
        out_shape=(
            jax.ShapeDtypeStruct(shape, jnp.float32),
            jax.ShapeDtypeStruct((frames, height, breadth, outputs), jnp.bfloat16),
        ),
        in_specs=[pl.BlockSpec(memory_space=pltpu.SMEM)] + [whole] * 7,
        out_specs=(whole, whole),
        scratch_shapes=[pltpu.VMEM((rows + 8, (frames + 2) * channels), jnp.float32)],
        compiler_params=pltpu.CompilerParams(vmem_limit_bytes=GRANT),
    )(scalars, mine, other, noise, selector, band, bias, constants)


def per_device(
    queries,
    keys,
    values,
    span_mask,
    head_gain,
    head_shift,
    patch_weight,
    noisy_latent,
    conv_weight,
    conv_bias,
):
    heads_dev = queries.shape[1] // HD
    if not plan_fits(
        heads_dev, lax.axis_size("span"), lax.axis_size("slab"), lax.axis_size("head")
    ):
        return gathered_plan(
            queries,
            keys,
            values,
            span_mask,
            head_gain,
            head_shift,
            patch_weight,
            noisy_latent,
            conv_weight,
            conv_bias,
        )
    place = lax.axis_index("span")
    slab = lax.axis_index("slab")
    scalars = scalar_operand(heads_dev // lax.axis_size("slab"))
    def prepare(noise, anchor):
        noise, weight, gain, shift, taps, bias, _ = lax.optimization_barrier(
            (noise, patch_weight, head_gain, head_shift, conv_weight, conv_bias, anchor)
        )
        height, breadth, _ = noise.shape
        wide_weight = weight.T.astype(jnp.float32)
        constants = jnp.stack(
            [
                jnp.sum(wide_weight * gain[None, :], axis=1),
                jnp.sum(wide_weight * shift[None, :], axis=1),
            ],
            axis=1,
        )
        return (
            noise_window(noise),
            constants + lax.ppermute(constants, "head", SWAP),
            cell_selector(height, breadth),
            banded_weight(taps),
            jnp.tile(bias, FRAMES_SPAN)[None, :],
        )

    sums, (noise, constants, selector, band, bias) = token_sums(
        scalars,
        queries,
        keys,
        values,
        span_mask,
        head_gain,
        patch_weight,
        noisy_latent,
        prepare,
    )
    half = sums.shape[1] // 2
    mine = lax.dynamic_slice_in_dim(sums, slab * half, half, 1)
    theirs = lax.dynamic_slice_in_dim(sums, (1 - slab) * half, half, 1)
    mine = mine + lax.ppermute(theirs, "slab", SWAP)
    own, after, third = mine[0], mine[1], mine[2]
    skip = TROWS * TCOLS
    from_one = lax.ppermute(
        jnp.concatenate([own[:, skip:], after], axis=1), "span", [(0, 1), (1, 2), (2, 3)]
    )
    to_current = lax.ppermute(third, "span", [(1, 3), (3, 2)])
    to_before = lax.ppermute(after[:, skip:], "span", [(0, 2), (1, 3)])
    kept = jnp.concatenate([jnp.where(place == 3, third[:, skip:], 0.0), own], axis=1)
    total = kept + from_one + jnp.concatenate([to_before, to_current], axis=1)
    total = total + lax.ppermute(total, "head", SWAP)
    other = lax.ppermute(total, "slab", SWAP)
    return finish(
        scalars,
        total,
        other,
        noise,
        selector,
        band,
        bias,
        constants,
        noisy_latent.shape,
        conv_weight.shape[1],
    )


def solution(mesh):
    placed = (
        P(("groups", "span"), "head"),
        P(("groups", "span", "slab"), "head"),
        P(("groups", "span", "slab"), "head"),
        P("groups", None),
        P("head"),
        P("head"),
        P("head", None),
        P(("groups", "span"), "head", "slab", None),
        P(),
        P(),
    )
    return jax.shard_map(
        per_device,
        mesh=mesh,
        in_specs=placed,
        out_specs=(
            P(("groups", "span"), "head", "slab", None),
            P(("groups", "span"), "head", "slab", None),
        ),
        check_vma=False,
    )
```

```python
import functools
import math
import typing

import jax
import jax.numpy as jnp
import numpy as np
from jax import lax
from jax.experimental import pallas as pl
from jax.experimental.pallas import tpu as pltpu
from jax.sharding import PartitionSpec as P

HEADS = 40
HD = 128
LAT_CH = 16
FRAMES_SPAN = 3
TROWS = 8
TCOLS = 16


neg_big = -1e30
noise_level = 0.75
norm_eps = 1e-06


def with_halo(cells, sides, width):
    for axis, dim in sides:
        count = lax.axis_size(axis)
        ends = count - 1
        head = lax.slice_in_dim(cells, 0, width, axis=dim)
        tail = lax.slice_in_dim(cells, cells.shape[dim] - width, cells.shape[dim], axis=dim)
        cells = jnp.concatenate(
            [
                lax.ppermute(tail, axis, [(i, (i + 1) % count) for i in range(ends)]),
                cells,
                lax.ppermute(head, axis, [((i + 1) % count, i) for i in range(ends)]),
            ],
            axis=dim,
        )
    return cells


def from_behind(value, axis, by):
    size = lax.axis_size(axis)
    pairs = [(i, i + by) for i in range(size) if 0 <= i + by < size]
    return lax.ppermute(value, axis, pairs)


def block_length(total_rows):
    block_size = total_rows
    while block_size > 768 and block_size % 2 == 0:
        block_size = block_size // 2
    return block_size


def fold_keys(partial_state, key_value, query_block, mask_row, rows_span):
    keys_piece, values_piece = key_value
    heads_dev = query_block.shape[1]
    piece_rows = keys_piece.shape[0]
    length = block_length(piece_rows)
    span_count = mask_row.shape[0]
    score_scale = 1.0 / math.sqrt(HD)
    span_ids = jnp.arange(span_count, dtype=jnp.int32)

    def one_block(carry_state, block_index):
        running_max, running_sum, weighted = carry_state
        offset = block_index * length
        key_block = lax.dynamic_slice_in_dim(keys_piece, offset, length, 0).reshape(
            length, heads_dev, HD
        )
        value_block = lax.dynamic_slice_in_dim(values_piece, offset, length, 0).reshape(
            length, heads_dev, HD
        )
        key_span = (offset + jnp.arange(length, dtype=jnp.int32)) // rows_span
        allowed = (
            jnp.sum(jnp.where(key_span[:, None] == span_ids[None, :], mask_row[None, :], 0), axis=1)
            > 0
        )
        scores = (
            jnp.einsum("qhd,khd->hqk", query_block, key_block, preferred_element_type=jnp.float32)
            * score_scale
        )
        scores = jnp.where(allowed[None, None, :], scores, neg_big)
        new_max = jnp.maximum(running_max, jnp.max(scores, axis=2))
        weights = jnp.where(allowed[None, None, :], jnp.exp(scores - new_max[:, :, None]), 0.0)
        factor = jnp.exp(running_max - new_max)
        running_sum = running_sum * factor + jnp.sum(weights, axis=2)
        weighted = weighted * factor.T[:, :, None] + jnp.einsum(
            "hqk,khd->qhd",
            weights.astype(jnp.bfloat16),
            value_block,
            preferred_element_type=jnp.float32,
        )
        return ((new_max, running_sum, weighted), None)

    result, unused = lax.scan(
        one_block, partial_state, jnp.arange(piece_rows // length, dtype=jnp.int32)
    )
    return result


def gathered_plan(
    queries,
    keys,
    values,
    span_mask,
    head_gain,
    head_shift,
    patch_weight,
    noisy_latent,
    conv_weight,
    conv_bias,
):
    heads_dev = queries.shape[1] // HD
    slab_count = lax.axis_size("slab")
    col_dev = TCOLS // slab_count
    slab_place = lax.axis_index("slab")
    span_place = lax.axis_index("span")
    mask_row = lax.dynamic_slice_in_dim(span_mask, span_place, 1, 0)[0]
    token_grid = queries.reshape(FRAMES_SPAN, TROWS, TCOLS, queries.shape[-1])
    picked = lax.dynamic_slice_in_dim(token_grid, slab_place * col_dev, col_dev, 2)
    own_queries = picked.reshape(FRAMES_SPAN * TROWS * col_dev, queries.shape[-1]).reshape(
        -1, heads_dev, HD
    )
    query_rows = own_queries.shape[0]
    rows_span = keys.shape[0] * slab_count
    running_max, running_sum, weighted = fold_keys(
        (
            jnp.full((heads_dev, query_rows), neg_big, jnp.float32),
            jnp.zeros((heads_dev, query_rows), jnp.float32),
            jnp.zeros((query_rows, heads_dev, HD), jnp.float32),
        ),
        (
            lax.all_gather(keys, ("span", "slab"), axis=0, tiled=True),
            lax.all_gather(values, ("span", "slab"), axis=0, tiled=True),
        ),
        own_queries,
        mask_row,
        rows_span,
    )
    attended = (
        (weighted / running_sum.T[:, :, None])
        .astype(jnp.bfloat16)
        .reshape(query_rows, heads_dev * HD)
    )
    feature_width = HEADS * HD
    values32 = attended.astype(jnp.float32)
    row_total = jnp.sum(values32, axis=1)
    row_squares = jnp.sum(values32 * values32, axis=1)
    row_total, row_squares = lax.psum((row_total, row_squares), "head")
    row_mean = row_total / feature_width
    spread = row_squares / feature_width - row_mean * row_mean
    normed = (
        (values32 - row_mean[:, None]) * lax.rsqrt(spread + norm_eps)[:, None] * head_gain[None, :]
        + head_shift[None, :]
    ).astype(jnp.bfloat16)
    normed_grid = normed.reshape(FRAMES_SPAN, TROWS, col_dev, normed.shape[-1])
    own_rows = TROWS // lax.axis_size("head")
    picked = normed_grid
    product = jnp.dot(
        picked.reshape(-1, picked.shape[-1]), patch_weight, preferred_element_type=jnp.float32
    )
    velocity = lax.psum_scatter(
        product.reshape(
            FRAMES_SPAN, own_rows * lax.axis_size("head"), col_dev * patch_weight.shape[1]
        )
        .transpose(1, 0, 2)
        .reshape(own_rows * lax.axis_size("head"), -1)
        .astype(jnp.bfloat16),
        "head",
        scatter_dimension=0,
        tiled=True,
    ).astype(jnp.float32)
    rows_dev = velocity.shape[0]
    patch_cells = (
        velocity.reshape(rows_dev, FRAMES_SPAN, col_dev, 2, 2, LAT_CH)
        .transpose(1, 0, 3, 2, 4, 5)
        .reshape(FRAMES_SPAN, 2 * rows_dev, 2 * col_dev, LAT_CH)
    )
    clean_latent = noisy_latent - noise_level * patch_cells
    latent_input = clean_latent.astype(jnp.bfloat16)
    framed = with_halo(latent_input, (("head", 1), ("slab", 2)), 1)
    earlier = from_behind(framed[FRAMES_SPAN - 2 :], "span", 1)
    stacked = jnp.concatenate([earlier, framed], axis=0)
    height = clean_latent.shape[1]
    breadth = clean_latent.shape[2]
    columns = jnp.concatenate(
        [
            stacked[
                frame_tap : frame_tap + FRAMES_SPAN,
                row_tap : row_tap + height,
                col_tap : col_tap + breadth,
                :,
            ]
            for frame_tap in range(3)
            for row_tap in range(3)
            for col_tap in range(3)
        ],
        axis=-1,
    )
    decoded = (
        jnp.dot(
            columns.reshape(FRAMES_SPAN * height * breadth, 27 * LAT_CH),
            conv_weight,
            preferred_element_type=jnp.float32,
        )
        + conv_bias[None, :]
    )
    decoded = decoded.astype(jnp.bfloat16).reshape(
        FRAMES_SPAN, height, breadth, conv_weight.shape[1]
    )
    return (clean_latent, decoded)


NEAR_HEADS = 4
MIDDLE_HEADS = 4
FAR_HEADS = 2
MIDDLE = NEAR_HEADS
FAR = NEAR_HEADS + MIDDLE_HEADS
STAT_ROWS = 8
SLOTS = 3
QUERY_ROWS = 192
SWAP = [(0, 1), (1, 0)]
WINDOW = 32
GRANT = 20 << 20

OWN, OTHER, DOWN, UP, MAIN, PLACE, SLAB = range(7)


def plan_fits(heads_dev, span_count, slab_count, head_count):
    return (
        span_count == 4
        and slab_count == 2
        and head_count == 2
        and heads_dev == slab_count * (NEAR_HEADS + MIDDLE_HEADS + FAR_HEADS)
    )


def scalar_operand(heads):
    by_place = np.zeros((4, 8), np.int32)
    by_place[:, OTHER] = heads
    by_place[:, DOWN] = [MIDDLE, MIDDLE, 0, MIDDLE]
    by_place[:, UP] = [0, MIDDLE, 0, 0]
    by_place[:, MAIN] = [MIDDLE, 0, MIDDLE, 0]
    by_place[:, PLACE] = range(4)
    by_slab = np.zeros(8, np.int32)
    by_slab[[OWN, OTHER, SLAB]] = heads, -heads, 1
    row = lax.dynamic_slice_in_dim(jnp.array(by_place), lax.axis_index("span"), 1, 0)[0]
    return row + lax.axis_index("slab") * jnp.array(by_slab)


def pack_kernel(inputs, messages, copies, with_noise, scalars, *refs):
    ins, rest = refs[:inputs], refs[inputs:]
    outs = rest[: messages + with_noise]
    staged = rest[messages + with_noise : -2]
    arrive, leave = rest[-2:]
    arriving = [[] for _ in range(messages)]
    for number, (source, row, rows, entries, shift, target, at, heads) in enumerate(copies):
        head = shift
        for entry in entries:
            head = head + scalars[entry]
        column = pl.multiple_of(head * HD, HD)
        copy = pltpu.make_async_copy(
            ins[source].at[pl.ds(row, rows), pl.ds(column, heads * HD)],
            staged[target].at[pl.ds(at, rows), :],
            arrive.at[number],
        )
        copy.start()
        arriving[target].append(copy)
    if with_noise:
        noisy, out = ins[-1], outs[-1]
        frames = noisy.shape[0]
        out[...] = jnp.concatenate([noisy[frame] for frame in range(frames)], axis=-1)
    leaving = []
    for target in range(messages):
        for copy in arriving[target]:
            copy.wait()
        copy = pltpu.make_async_copy(staged[target], outs[target], leave.at[target])
        copy.start()
        leaving.append(copy)
    for copy in leaving:
        copy.wait()


def pack(scalars, arrays, shapes, copies, name, noisy=None):
    moved = sum(2 * 2 * rows * heads * HD for _, _, rows, _, _, _, _, heads in copies)
    out_shape = [pltpu.HBM(shape, jnp.bfloat16) for shape in shapes]
    in_specs = [pl.BlockSpec(memory_space=pl.ANY)] * len(arrays)
    out_specs = [pl.BlockSpec(memory_space=pl.ANY)] * len(shapes)
    if noisy is not None:
        frames, height, breadth, channels = noisy.shape
        lanes = frames * channels
        arrays = arrays + (noisy,)
        in_specs.append(pl.BlockSpec(noisy.shape, lambda i, scalars: (0, 0, 0, 0)))
        out_shape.append(jax.ShapeDtypeStruct((height, breadth, lanes), noisy.dtype))
        out_specs.append(pl.BlockSpec((height, breadth, lanes), lambda i, scalars: (0, 0, 0)))
    return pl.pallas_call(
        functools.partial(
            pack_kernel, len(arrays), len(shapes), copies, noisy is not None
        ),
        name=name,
        out_shape=out_shape,
        grid_spec=pltpu.PrefetchScalarGridSpec(
            num_scalar_prefetch=1,
            grid=(1,),
            in_specs=in_specs,
            out_specs=out_specs,
            scratch_shapes=[pltpu.VMEM(shape, jnp.bfloat16) for shape in shapes]
            + [
                pltpu.SemaphoreType.DMA((len(copies),)),
                pltpu.SemaphoreType.DMA((len(shapes),)),
            ],
        ),
        compiler_params=pltpu.CompilerParams(vmem_limit_bytes=GRANT),
        cost_estimate=pl.CostEstimate(flops=0, bytes_accessed=moved, transcendentals=0),
    )(scalars, *arrays)


def message(scalars, pieces, arrays, name, noisy=None):
    copies, shapes = [], []
    for target, parts in enumerate(pieces):
        at = 0
        for source, row, rows, entries, shift, heads in parts:
            copies.append((source, row, rows, entries, shift, target, at, heads))
            at += rows
        shapes.append((at, parts[0][5] * HD))
    return pack(scalars, arrays, shapes, copies, name, noisy)


class Tokens(typing.NamedTuple):
    query: int | None = None
    pairs: tuple = ()
    extra: int | None = None


OWN_TOKENS = Tokens()


def attend_kernel(variants, extra, span_count, fresh, scalars, mask, *refs):
    query_own, key_own, value_own, received, weight, gain = refs[:6]
    more = refs[6 : 6 + extra]
    mine_out, theirs_out, folded, squares, carried, moved = refs[-6:]
    payloads = refs[6 + extra : -6] if fresh else refs[6 + extra : -8]
    rows = query_own.shape[0]
    half = rows // 2
    step = pl.program_id(0)
    to_exp2 = math.log2(math.e) / math.sqrt(HD)
    active = functools.reduce(
        lambda a, b: a | b, [scalars[PLACE] == place for place in variants]
    )

    last_step = step == pl.num_programs(0) - 1
    part = carried.shape[1] // 2
    halves = [
        carried.at[:, pl.ds(pl.multiple_of(number * part, part), part)]
        for number in (scalars[SLAB], 1 - scalars[SLAB])
    ]
    fetches = (
        []
        if fresh
        else [
            pltpu.make_async_copy(refs[number - 8], halves[number], moved.at[number])
            for number in range(2)
        ]
    )

    @pl.when((step == 0) & active)
    def _():
        folded[...] = jnp.zeros_like(folded)
        squares[...] = jnp.zeros_like(squares)
        for fetch in fetches:
            fetch.start()

    def query_of(source):
        if source is OWN_TOKENS:
            return query_own[...]
        if source.extra is not None:
            return more[0][:, source.extra * HD : (source.extra + 1) * HD]
        return payloads[source.query][:rows]

    def pair_of(source):
        if source is OWN_TOKENS:
            parts = (key_own[...], received[:half], value_own[...], received[half:])
        elif source.extra is not None:
            lanes = slice(source.extra * HD, (source.extra + 1) * HD)
            parts = (more[1][:, lanes], more[3][:half, lanes], more[2][:, lanes], more[3][half:, lanes])
        elif len(source.pairs) == 2:
            one, two = (payloads[number] for number in source.pairs)
            parts = (one[:half], two[:half], one[half:], two[half:])
        else:
            payload = payloads[source.pairs[0]]
            start = payload.shape[0] - 2 * rows
            return payload[start : start + rows], payload[start + rows :]
        return jnp.concatenate(parts[:2], axis=0), jnp.concatenate(parts[2:], axis=0)

    def projector(extra_head):
        if extra_head is None:
            scaled = weight[...].astype(jnp.float32) * gain[...]
        else:
            lanes = slice(extra_head * HD, (extra_head + 1) * HD)
            scaled = more[4][:, lanes].astype(jnp.float32) * more[5][:, lanes]
        high = scaled.astype(jnp.bfloat16)
        low = (scaled - high.astype(jnp.float32)).astype(jnp.bfloat16)
        return jnp.concatenate([high, low, jnp.ones((16, HD), jnp.bfloat16)], axis=0)

    def one_query(source, slot, query_span, key_sources):
        query = query_of(source)
        pairs = [pair_of(key_source) for key_source, _ in key_sources]
        open_to = [
            None if key_span == query_span else mask[query_span * span_count + key_span] > 0
            for _, key_span in key_sources
        ]
        keys_in = jnp.concatenate([pair[0] for pair in pairs], axis=0)
        ones_block = jnp.ones((rows, HD), jnp.bfloat16)
        values_in = jnp.concatenate(
            [jnp.concatenate([pair[1], ones_block], axis=1) for pair in pairs], axis=0
        )
        pieces = []
        for row in range(0, rows, QUERY_ROWS):
            score = lax.dot_general(
                query[row : row + QUERY_ROWS],
                keys_in,
                (((1,), (1,)), ((), ())),
                preferred_element_type=jnp.float32,
            )
            best = None
            for number, is_open in enumerate(open_to):
                start = number * rows
                block = score[:, start : start + HD]
                for lane in range(HD, rows, HD):
                    block = jnp.maximum(block, score[:, start + lane : start + lane + HD])
                if is_open is not None:
                    block = jnp.where(is_open, block, neg_big)
                best = block if best is None else jnp.maximum(best, block)
            top = jnp.max(best, axis=1, keepdims=True)
            weights = []
            for number, is_open in enumerate(open_to):
                start = number * rows
                shift = top if is_open is None else jnp.where(is_open, top, -neg_big)
                weights.append(
                    jnp.exp2((score[:, start : start + rows] - shift) * to_exp2).astype(jnp.bfloat16)
                )
            both = jnp.dot(
                jnp.concatenate(weights, axis=1), values_in, preferred_element_type=jnp.float32
            )
            pieces.append((both[:, :HD] / both[:, HD:]).astype(jnp.bfloat16))
        attended = jnp.concatenate(pieces, axis=0)
        folded[slot] += lax.dot_general(
            projector(source.extra),
            attended,
            (((1,), (1,)), ((), ())),
            preferred_element_type=jnp.float32,
        )
        wide = attended.astype(jnp.float32)
        squares[slot] += wide * wide

    for place, tasks in variants.items():

        @pl.when(scalars[PLACE] == place)
        def _():
            for task in tasks:
                one_query(*task)

    def store():
        copies = [
            pltpu.make_async_copy(halves[number], out, moved.at[2 + number])
            for number, out in enumerate((mine_out, theirs_out))
        ]
        for copy in copies:
            copy.start()
        for copy in copies:
            copy.wait()

    if fresh:

        @pl.when(last_step & jnp.logical_not(active))
        def _():
            carried[...] = jnp.zeros_like(carried)
            store()

    @pl.when(last_step & active)
    def _():
        ones_rows = jnp.ones((STAT_ROWS, HD), jnp.bfloat16)
        patch = weight.shape[0]
        used = sorted({task[1] for tasks in variants.values() for task in tasks})
        for fetch in fetches:
            fetch.wait()
        for slot in range(SLOTS):
            if slot not in used:
                if fresh:
                    carried[slot] = jnp.zeros(carried.shape[1:], carried.dtype)
                continue
            left = squares[slot]
            total = jnp.zeros((STAT_ROWS, rows), jnp.float32)
            for _ in range(3):
                piece = left.astype(jnp.bfloat16)
                left = left - piece.astype(jnp.float32)
                total = total + lax.dot_general(
                    ones_rows, piece, (((1,), (1,)), ((), ())), preferred_element_type=jnp.float32
                )
            done = folded[slot]
            new = jnp.concatenate(
                [
                    done[:patch] + done[patch : 2 * patch],
                    done[2 * patch : 2 * patch + STAT_ROWS],
                    total,
                ],
                axis=0,
            )
            carried[slot] = new if fresh else carried[slot] + new
        store()


def attend(
    steps, entries, first, own, scalars, mask, sums, payloads, variants, more, name, cost=1
):
    queries, keys, values, received, weight, gain = own
    rows = queries.shape[0]
    half = rows // 2
    patch = weight.shape[0]

    def moving(i, scalars):
        used = functools.reduce(
            lambda a, b: a | b, [scalars[PLACE] == place for place in variants]
        )
        return jnp.where(used, i, 0)

    def column(height, own_column):
        def index(i, scalars, mask):
            head = first + moving(i, scalars) + (scalars[OWN] if own_column else 0)
            for entry in entries:
                head = head + scalars[entry]
            return (0, head)

        return pl.BlockSpec((height, HD), index)

    def two_columns(height, own_column):
        return pl.BlockSpec(
            (height, 2 * HD),
            lambda i, scalars, mask: (
                0,
                moving(i, scalars) + (scalars[OWN] // 2 if own_column else 0),
            ),
        )

    def payload_column(payload):
        return pl.BlockSpec(
            (payload.shape[0], HD), lambda i, scalars, mask: (0, moving(i, scalars))
        )

    in_specs = [
        column(rows, True),
        column(half, True),
        column(half, True),
        column(rows, False),
        column(patch, True),
        column(1, True),
    ]
    arrays = [queries, keys, values, received, weight, gain]
    extra = 0
    if more:
        extra = 6
        in_specs += [
            two_columns(rows, True),
            two_columns(half, True),
            two_columns(half, True),
            two_columns(rows, False),
            two_columns(patch, True),
            two_columns(1, True),
        ]
        arrays += [queries, keys, values, received, weight, gain]
    in_specs += [payload_column(payload) for payload in payloads]
    arrays += payloads
    fresh = sums is None
    sums_shape = (SLOTS, patch + 2 * STAT_ROWS, rows)
    aliases = {}
    if not fresh:
        aliases = {2 + len(arrays): 0, 3 + len(arrays): 1}
        in_specs += [pl.BlockSpec(memory_space=pl.ANY)] * 2
        arrays += sums
    pairs = steps * max(sum(len(task[3]) for task in tasks) for tasks in variants.values())
    span_count = math.isqrt(mask.shape[0])
    return pl.pallas_call(
        functools.partial(attend_kernel, variants, extra, span_count, fresh),
        name=name,
        out_shape=[pltpu.HBM((SLOTS, sums_shape[1] // 2, rows), jnp.float32)] * 2,
        input_output_aliases=aliases,
        grid_spec=pltpu.PrefetchScalarGridSpec(
            num_scalar_prefetch=2,
            grid=(steps,),
            in_specs=in_specs,
            out_specs=[pl.BlockSpec(memory_space=pl.ANY)] * 2,
            scratch_shapes=[
                pltpu.VMEM((SLOTS, 2 * patch + 16, rows), jnp.float32),
                pltpu.VMEM((SLOTS, rows, HD), jnp.float32),
                pltpu.VMEM(sums_shape, jnp.float32),
                pltpu.SemaphoreType.DMA((4,)),
            ],
        ),
        compiler_params=pltpu.CompilerParams(vmem_limit_bytes=GRANT),
        cost_estimate=pl.CostEstimate(
            flops=cost * pairs * 4 * rows * rows * HD,
            bytes_accessed=steps * HD * 2 * sum(spec.block_shape[0] for spec in in_specs[:4]),
            transcendentals=cost * pairs * rows * rows,
        ),
    )(scalars, mask, *arrays)


def token_sums(
    scalars, queries, keys, values, span_mask, head_gain, patch_weight, noisy, prepare
):
    rows = queries.shape[0]
    half = rows // 2
    heads = NEAR_HEADS + MIDDLE_HEADS + FAR_HEADS
    in_place = lambda array: pltpu.with_memory_space_constraint(array, pltpu.HBM)
    queries, keys, values = (in_place(array) for array in (queries, keys, values))

    def send(value, *pairs):
        return in_place(lax.ppermute(value, "span", list(pairs)))

    def send_across(value, *pairs):
        slabs = lax.axis_size("slab")
        flipped = [(a * slabs + s, b * slabs + 1 - s) for a, b in pairs for s in range(slabs)]
        return in_place(lax.ppermute(value, ("span", "slab"), flipped))

    def tokens(entry, shift, count):
        return [(0, 0, rows, (OWN, entry) if entry else (OWN,), shift, count)]

    def own_half(slab_entry, entry, shift, count):
        return [(part, 0, half, (slab_entry, entry), shift, count) for part in (1, 2)]

    def pairs_of(entry, shift, count):
        entries = (entry,) if entry else ()
        return [
            piece
            for part in (1, 2)
            for piece in (
                (part, 0, half, (OWN,) + entries, shift, count),
                (3, (part - 1) * half, half, entries, shift, count),
            )
        ]

    handed, up_same, up_across, query_down, noise = message(
        scalars,
        [
            [(part, 0, half, (OTHER,), 0, heads) for part in (1, 2)],
            own_half(OWN, UP, 0, NEAR_HEADS),
            own_half(OTHER, UP, 0, NEAR_HEADS),
            tokens(DOWN, 0, MIDDLE_HEADS),
        ],
        (queries, keys, values),
        "pack_first",
        noisy,
    )
    lanes = 2 * noisy.shape[3]
    noise = jnp.concatenate([from_behind(noise[:, :, -lanes:], "span", 1), noise], axis=2)
    received = in_place(lax.ppermute(handed, "slab", SWAP))
    up_same = send(up_same, (0, 1), (1, 2))
    up_across = send_across(up_across, (0, 1), (1, 2))
    query_down = send(query_down, (1, 0), (2, 1), (3, 2))

    arrays = (queries, keys, values, received)
    pair_down, up_two = message(
        scalars,
        [pairs_of(DOWN, 0, MIDDLE_HEADS), pairs_of(None, MIDDLE, MIDDLE_HEADS)],
        arrays,
        "pack_second",
    )
    source, _ = lax.optimization_barrier((received, pair_down))
    two, far_all, far_pair = message(
        scalars,
        [
            tokens(None, 0, NEAR_HEADS) + pairs_of(None, 0, NEAR_HEADS),
            tokens(None, FAR, FAR_HEADS) + pairs_of(None, FAR, FAR_HEADS),
            pairs_of(None, FAR, FAR_HEADS),
        ],
        (queries, keys, values, source),
        "pack_third",
    )
    anchor = two
    pair_down = send(pair_down, (1, 0), (2, 1), (3, 2))
    up_two = send(up_two, (0, 2))
    two = send(two, (3, 1))
    far_next = send(far_all, (2, 3), (1, 0))
    far_pair, prepared = lax.optimization_barrier((far_pair, prepare(noise, anchor)))
    far_two = send(far_pair, (1, 3))
    far_three = send(far_pair, (0, 3))

    span_mask, head_gain, patch_weight, _ = lax.optimization_barrier(
        (span_mask, head_gain, patch_weight, anchor)
    )
    mask = span_mask.reshape(-1)
    weight = patch_weight.T
    own = (queries, keys, values, received, weight, head_gain[None, :])
    run = functools.partial(attend, own=own, scalars=scalars, mask=mask)

    on_one, back_one, back_two = Tokens(0, (1,)), Tokens(None, (2, 3)), Tokens(None, (4,))
    here = OWN_TOKENS
    payloads = [query_down, pair_down, up_same, up_across, up_two]
    sums = run(
        MIDDLE_HEADS,
        (MAIN,),
        0,
        sums=None,
        payloads=payloads,
        variants={
            0: [(here, 0, 0, [(here, 0)]), (on_one, 1, 1, [(here, 0), (on_one, 1)])],
            1: [
                (on_one, 1, 2, [(back_one, 0), (here, 1), (on_one, 2)]),
                (here, 0, 1, [(back_one, 0), (here, 1)]),
            ],
            2: [
                (on_one, 1, 3, [(back_two, 0), (back_one, 1), (here, 2), (on_one, 3)]),
                (here, 0, 2, [(back_two, 0), (back_one, 1), (here, 2)]),
            ],
        },
        more=False,
        name="main_heads",
    )
    beside, two_back, three_back = Tokens(0, (0,)), Tokens(None, (1,)), Tokens(None, (2,))
    extras = [Tokens(None, (), lane) for lane in range(2)]
    sums = run(
        FAR_HEADS,
        (),
        FAR,
        sums=sums,
        payloads=[far_next, far_two, far_three],
        variants={
            0: [(here, 0, 0, [(here, 0)]), (beside, 1, 1, [(here, 0), (beside, 1)])]
            + [(head, 0, 0, [(head, 0)]) for head in extras],
            3: [
                (here, 0, 3, [(three_back, 0), (two_back, 1), (beside, 2), (here, 3)]),
                (beside, 2, 2, [(three_back, 0), (two_back, 1), (beside, 2)]),
            ],
        },
        more=True,
        name="far_heads",
        cost=4,
    )
    on_two = Tokens(5, (5,))
    sums, prepared = lax.optimization_barrier((sums, prepared))
    sums = run(
        NEAR_HEADS,
        (MAIN,),
        0,
        sums=sums,
        payloads=payloads + [two],
        variants={1: [(on_two, 2, 3, [(back_one, 0), (here, 1), (on_one, 2), (on_two, 3)])]},
        more=False,
        name="near_heads",
    )
    return sums, prepared


def noise_window(grid, constants):
    height, breadth, _ = grid.shape
    slab = lax.axis_index("slab")
    edge = jnp.where(slab == 0, grid[:, breadth - 1], grid[:, 0])
    edge = lax.ppermute(edge, "slab", SWAP)[:, None]
    grid = jnp.concatenate(
        [
            jnp.where(slab == 1, edge, 0.0),
            grid,
            jnp.where(slab == 0, edge, 0.0),
            jnp.zeros((height, WINDOW - breadth - 2, grid.shape[2]), grid.dtype),
        ],
        axis=1,
    )
    head = lax.axis_index("head")
    edge = jnp.where(head == 0, grid[height - 1], grid[0])
    count = constants.shape[1]
    extra = jnp.pad(constants, ((0, 8 - constants.shape[0]), (0, edge.shape[1] - count)))
    sent = lax.ppermute(jnp.concatenate([edge, extra], axis=0), "head", SWAP)
    edge = sent[None, :WINDOW]
    constants = constants + sent[WINDOW : WINDOW + constants.shape[0], :count]
    grid = jnp.concatenate(
        [jnp.where(head == 1, edge, 0.0), grid, jnp.where(head == 0, edge, 0.0)], axis=0
    )
    return grid.reshape((height + 2) * WINDOW, grid.shape[2]), constants.T


def cell_selector(height, breadth):
    cell = lax.broadcasted_iota(jnp.int32, ((height + 2) * WINDOW, 4 * TROWS * TCOLS), 0)
    column = lax.broadcasted_iota(jnp.int32, cell.shape, 1)
    y = lax.axis_index("head") * height + cell // WINDOW - 1
    x = lax.axis_index("slab") * breadth + cell % WINDOW - 1
    inside = (y >= 0) & (y < 2 * TROWS) & (x >= 0) & (x < 2 * TCOLS)
    inside = inside & (cell % WINDOW < breadth + 2)
    target = ((y % 2) * 2 + x % 2) * (TROWS * TCOLS) + (y // 2) * TCOLS + x // 2
    return (inside & (column == target)).astype(jnp.bfloat16)


def band_kernel(weight, band):
    outputs = weight.shape[1]
    band[...] = jnp.zeros_like(band)
    for row_tap in range(3):
        for col_tap in range(3):
            for frame_tap in range(3):
                start = ((3 * frame_tap + row_tap) * 3 + col_tap) * LAT_CH
                block = weight[start : start + LAT_CH]
                for frame in range(FRAMES_SPAN):
                    at = (col_tap * (FRAMES_SPAN + 2) + frame + frame_tap) * LAT_CH
                    band[
                        row_tap, at : at + LAT_CH, frame * outputs : (frame + 1) * outputs
                    ] = block


def banded_weight(conv_weight):
    shape = (3, 3 * (FRAMES_SPAN + 2) * LAT_CH, FRAMES_SPAN * conv_weight.shape[1])
    return pl.pallas_call(
        band_kernel,
        name="band",
        out_shape=jax.ShapeDtypeStruct(shape, conv_weight.dtype),
        in_specs=[pl.BlockSpec(memory_space=pltpu.VMEM)],
        out_specs=pl.BlockSpec(memory_space=pltpu.VMEM),
        compiler_params=pltpu.CompilerParams(vmem_limit_bytes=GRANT),
        cost_estimate=pl.CostEstimate(
            flops=0, bytes_accessed=2 * math.prod(shape), transcendentals=0
        ),
    )(conv_weight)


def finish_kernel(
    scalars, mine, other, noise, selector, band, bias, constants, clean, decoded, cells
):
    frames, height, breadth, channels = clean.shape
    patch = constants.shape[0]
    first = scalars[SLAB] == 0
    sums = jnp.concatenate(
        [jnp.where(first, mine[...], other[...]), jnp.where(first, other[...], mine[...])], axis=0
    )
    feature_width = HEADS * HD
    row_mean = sums[patch : patch + 1] / feature_width
    spread = sums[patch + STAT_ROWS : patch + STAT_ROWS + 1] / feature_width - row_mean * row_mean
    velocity = (
        lax.rsqrt(spread + norm_eps) * (sums[:patch] - constants[:, 0:1] * row_mean)
        + constants[:, 1:2]
    )
    tokens = TROWS * TCOLS
    lane = lax.broadcasted_iota(jnp.int32, velocity.shape, 1)
    velocity = jnp.where((lane >= 2 * tokens) | (scalars[PLACE] > 0), velocity, 0.0)
    columns = jnp.concatenate(
        [
            jnp.concatenate(
                [
                    velocity[
                        part * channels : (part + 1) * channels,
                        frame * tokens : (frame + 1) * tokens,
                    ]
                    for part in range(4)
                ],
                axis=1,
            )
            for frame in range(frames + 2)
        ],
        axis=0,
    )
    high = columns.astype(jnp.bfloat16)
    low = (columns - high.astype(jnp.float32)).astype(jnp.bfloat16)
    chosen = sum(
        lax.dot_general(
            selector[...], part, (((1,), (1,)), ((), ())), preferred_element_type=jnp.float32
        )
        for part in (high, low)
    )
    count = (height + 2) * WINDOW
    cells[:count] = noise[...] - noise_level * chosen
    cells[count:] = jnp.zeros_like(cells[count:])
    for frame in range(frames):
        lanes = slice((frame + 2) * channels, (frame + 3) * channels)
        for y in range(height):
            start = (y + 1) * WINDOW + 1
            clean[frame, y] = cells[start : start + breadth, lanes]
    shifted = jnp.concatenate(
        [cells[tap : tap + count] for tap in range(3)], axis=1
    ).astype(jnp.bfloat16)
    total = jnp.broadcast_to(bias[...], (height * breadth, bias.shape[1]))
    for tap in range(3):
        block = jnp.concatenate(
            [
                shifted[(y + tap) * WINDOW : (y + tap) * WINDOW + breadth]
                for y in range(height)
            ],
            axis=0,
        )
        total = total + jnp.dot(block, band[tap], preferred_element_type=jnp.float32)
    outputs = decoded.shape[3]
    total = total.astype(decoded.dtype)
    for frame in range(frames):
        decoded[frame] = total[:, frame * outputs : (frame + 1) * outputs].reshape(
            height, breadth, outputs
        )


def finish(scalars, mine, other, noise, selector, band, bias, constants, shape, outputs):
    whole = pl.BlockSpec(memory_space=pltpu.VMEM)
    frames, height, breadth, channels = shape
    rows = (height + 2) * WINDOW
    return pl.pallas_call(
        finish_kernel,
        name="finish",
        out_shape=(
            jax.ShapeDtypeStruct(shape, jnp.float32),
            jax.ShapeDtypeStruct((frames, height, breadth, outputs), jnp.bfloat16),
        ),
        in_specs=[pl.BlockSpec(memory_space=pltpu.SMEM)] + [whole] * 7,
        out_specs=(whole, whole),
        scratch_shapes=[pltpu.VMEM((rows + 8, (frames + 2) * channels), jnp.float32)],
        compiler_params=pltpu.CompilerParams(vmem_limit_bytes=GRANT),
    )(scalars, mine, other, noise, selector, band, bias, constants)


def per_device(
    queries,
    keys,
    values,
    span_mask,
    head_gain,
    head_shift,
    patch_weight,
    noisy_latent,
    conv_weight,
    conv_bias,
):
    heads_dev = queries.shape[1] // HD
    if not plan_fits(
        heads_dev, lax.axis_size("span"), lax.axis_size("slab"), lax.axis_size("head")
    ):
        return gathered_plan(
            queries,
            keys,
            values,
            span_mask,
            head_gain,
            head_shift,
            patch_weight,
            noisy_latent,
            conv_weight,
            conv_bias,
        )
    place = lax.axis_index("span")
    slab = lax.axis_index("slab")
    scalars = scalar_operand(heads_dev // lax.axis_size("slab"))
    def prepare(noise, anchor):
        noise, weight, gain, shift, taps, bias, _ = lax.optimization_barrier(
            (noise, patch_weight, head_gain, head_shift, conv_weight, conv_bias, anchor)
        )
        height, breadth, _ = noise.shape
        wide_weight = weight.T.astype(jnp.float32)
        constants = jnp.stack(
            [
                jnp.sum(wide_weight * gain[None, :], axis=1),
                jnp.sum(wide_weight * shift[None, :], axis=1),
            ]
        )
        window, constants = noise_window(noise, constants)
        return (
            window,
            constants,
            cell_selector(height, breadth),
            banded_weight(taps),
            jnp.tile(bias, FRAMES_SPAN)[None, :],
        )

    (mine, theirs), (noise, constants, selector, band, bias) = token_sums(
        scalars,
        queries,
        keys,
        values,
        span_mask,
        head_gain,
        patch_weight,
        noisy_latent,
        prepare,
    )
    mine = mine + lax.ppermute(theirs, "slab", SWAP)
    own, after, third = mine[0], mine[1], mine[2]
    skip = TROWS * TCOLS
    from_one = lax.ppermute(
        jnp.concatenate([own[:, skip:], after], axis=1), "span", [(0, 1), (1, 2), (2, 3)]
    )
    to_current = lax.ppermute(third, "span", [(1, 3), (3, 2)])
    to_before = lax.ppermute(after[:, skip:], "span", [(0, 2), (1, 3)])
    kept = jnp.concatenate([jnp.where(place == 3, third[:, skip:], 0.0), own], axis=1)
    total = kept + from_one + jnp.concatenate([to_before, to_current], axis=1)
    total = total + lax.ppermute(total, "head", SWAP)
    other = lax.ppermute(total, "slab", SWAP)
    return finish(
        scalars,
        total,
        other,
        noise,
        selector,
        band,
        bias,
        constants,
        noisy_latent.shape,
        conv_weight.shape[1],
    )


def solution(mesh):
    placed = (
        P(("groups", "span"), "head"),
        P(("groups", "span", "slab"), "head"),
        P(("groups", "span", "slab"), "head"),
        P("groups", None),
        P("head"),
        P("head"),
        P("head", None),
        P(("groups", "span"), "head", "slab", None),
        P(),
        P(),
    )
    return jax.shard_map(
        per_device,
        mesh=mesh,
        in_specs=placed,
        out_specs=(
            P(("groups", "span"), "head", "slab", None),
            P(("groups", "span"), "head", "slab", None),
        ),
        check_vma=False,
    )
```

```python
import functools
import math
import typing

import jax
import jax.numpy as jnp
import numpy as np
from jax import lax
from jax.experimental import pallas as pl
from jax.experimental.pallas import tpu as pltpu
from jax.sharding import PartitionSpec as P

HEADS = 40
HD = 128
LAT_CH = 16
FRAMES_SPAN = 3
TROWS = 8
TCOLS = 16


neg_big = -1e30
noise_level = 0.75
norm_eps = 1e-06


def with_halo(cells, sides, width):
    for axis, dim in sides:
        count = lax.axis_size(axis)
        ends = count - 1
        head = lax.slice_in_dim(cells, 0, width, axis=dim)
        tail = lax.slice_in_dim(cells, cells.shape[dim] - width, cells.shape[dim], axis=dim)
        cells = jnp.concatenate(
            [
                lax.ppermute(tail, axis, [(i, (i + 1) % count) for i in range(ends)]),
                cells,
                lax.ppermute(head, axis, [((i + 1) % count, i) for i in range(ends)]),
            ],
            axis=dim,
        )
    return cells


def from_behind(value, axis, by):
    size = lax.axis_size(axis)
    pairs = [(i, i + by) for i in range(size) if 0 <= i + by < size]
    return lax.ppermute(value, axis, pairs)


def block_length(total_rows):
    block_size = total_rows
    while block_size > 768 and block_size % 2 == 0:
        block_size = block_size // 2
    return block_size


def fold_keys(partial_state, key_value, query_block, mask_row, rows_span):
    keys_piece, values_piece = key_value
    heads_dev = query_block.shape[1]
    piece_rows = keys_piece.shape[0]
    length = block_length(piece_rows)
    span_count = mask_row.shape[0]
    score_scale = 1.0 / math.sqrt(HD)
    span_ids = jnp.arange(span_count, dtype=jnp.int32)

    def one_block(carry_state, block_index):
        running_max, running_sum, weighted = carry_state
        offset = block_index * length
        key_block = lax.dynamic_slice_in_dim(keys_piece, offset, length, 0).reshape(
            length, heads_dev, HD
        )
        value_block = lax.dynamic_slice_in_dim(values_piece, offset, length, 0).reshape(
            length, heads_dev, HD
        )
        key_span = (offset + jnp.arange(length, dtype=jnp.int32)) // rows_span
        allowed = (
            jnp.sum(jnp.where(key_span[:, None] == span_ids[None, :], mask_row[None, :], 0), axis=1)
            > 0
        )
        scores = (
            jnp.einsum("qhd,khd->hqk", query_block, key_block, preferred_element_type=jnp.float32)
            * score_scale
        )
        scores = jnp.where(allowed[None, None, :], scores, neg_big)
        new_max = jnp.maximum(running_max, jnp.max(scores, axis=2))
        weights = jnp.where(allowed[None, None, :], jnp.exp(scores - new_max[:, :, None]), 0.0)
        factor = jnp.exp(running_max - new_max)
        running_sum = running_sum * factor + jnp.sum(weights, axis=2)
        weighted = weighted * factor.T[:, :, None] + jnp.einsum(
            "hqk,khd->qhd",
            weights.astype(jnp.bfloat16),
            value_block,
            preferred_element_type=jnp.float32,
        )
        return ((new_max, running_sum, weighted), None)

    result, unused = lax.scan(
        one_block, partial_state, jnp.arange(piece_rows // length, dtype=jnp.int32)
    )
    return result


def gathered_plan(
    queries,
    keys,
    values,
    span_mask,
    head_gain,
    head_shift,
    patch_weight,
    noisy_latent,
    conv_weight,
    conv_bias,
):
    heads_dev = queries.shape[1] // HD
    slab_count = lax.axis_size("slab")
    col_dev = TCOLS // slab_count
    slab_place = lax.axis_index("slab")
    span_place = lax.axis_index("span")
    mask_row = lax.dynamic_slice_in_dim(span_mask, span_place, 1, 0)[0]
    token_grid = queries.reshape(FRAMES_SPAN, TROWS, TCOLS, queries.shape[-1])
    picked = lax.dynamic_slice_in_dim(token_grid, slab_place * col_dev, col_dev, 2)
    own_queries = picked.reshape(FRAMES_SPAN * TROWS * col_dev, queries.shape[-1]).reshape(
        -1, heads_dev, HD
    )
    query_rows = own_queries.shape[0]
    rows_span = keys.shape[0] * slab_count
    running_max, running_sum, weighted = fold_keys(
        (
            jnp.full((heads_dev, query_rows), neg_big, jnp.float32),
            jnp.zeros((heads_dev, query_rows), jnp.float32),
            jnp.zeros((query_rows, heads_dev, HD), jnp.float32),
        ),
        (
            lax.all_gather(keys, ("span", "slab"), axis=0, tiled=True),
            lax.all_gather(values, ("span", "slab"), axis=0, tiled=True),
        ),
        own_queries,
        mask_row,
        rows_span,
    )
    attended = (
        (weighted / running_sum.T[:, :, None])
        .astype(jnp.bfloat16)
        .reshape(query_rows, heads_dev * HD)
    )
    feature_width = HEADS * HD
    values32 = attended.astype(jnp.float32)
    row_total = jnp.sum(values32, axis=1)
    row_squares = jnp.sum(values32 * values32, axis=1)
    row_total, row_squares = lax.psum((row_total, row_squares), "head")
    row_mean = row_total / feature_width
    spread = row_squares / feature_width - row_mean * row_mean
    normed = (
        (values32 - row_mean[:, None]) * lax.rsqrt(spread + norm_eps)[:, None] * head_gain[None, :]
        + head_shift[None, :]
    ).astype(jnp.bfloat16)
    normed_grid = normed.reshape(FRAMES_SPAN, TROWS, col_dev, normed.shape[-1])
    own_rows = TROWS // lax.axis_size("head")
    picked = normed_grid
    product = jnp.dot(
        picked.reshape(-1, picked.shape[-1]), patch_weight, preferred_element_type=jnp.float32
    )
    velocity = lax.psum_scatter(
        product.reshape(
            FRAMES_SPAN, own_rows * lax.axis_size("head"), col_dev * patch_weight.shape[1]
        )
        .transpose(1, 0, 2)
        .reshape(own_rows * lax.axis_size("head"), -1)
        .astype(jnp.bfloat16),
        "head",
        scatter_dimension=0,
        tiled=True,
    ).astype(jnp.float32)
    rows_dev = velocity.shape[0]
    patch_cells = (
        velocity.reshape(rows_dev, FRAMES_SPAN, col_dev, 2, 2, LAT_CH)
        .transpose(1, 0, 3, 2, 4, 5)
        .reshape(FRAMES_SPAN, 2 * rows_dev, 2 * col_dev, LAT_CH)
    )
    clean_latent = noisy_latent - noise_level * patch_cells
    latent_input = clean_latent.astype(jnp.bfloat16)
    framed = with_halo(latent_input, (("head", 1), ("slab", 2)), 1)
    earlier = from_behind(framed[FRAMES_SPAN - 2 :], "span", 1)
    stacked = jnp.concatenate([earlier, framed], axis=0)
    height = clean_latent.shape[1]
    breadth = clean_latent.shape[2]
    columns = jnp.concatenate(
        [
            stacked[
                frame_tap : frame_tap + FRAMES_SPAN,
                row_tap : row_tap + height,
                col_tap : col_tap + breadth,
                :,
            ]
            for frame_tap in range(3)
            for row_tap in range(3)
            for col_tap in range(3)
        ],
        axis=-1,
    )
    decoded = (
        jnp.dot(
            columns.reshape(FRAMES_SPAN * height * breadth, 27 * LAT_CH),
            conv_weight,
            preferred_element_type=jnp.float32,
        )
        + conv_bias[None, :]
    )
    decoded = decoded.astype(jnp.bfloat16).reshape(
        FRAMES_SPAN, height, breadth, conv_weight.shape[1]
    )
    return (clean_latent, decoded)


NEAR_HEADS = 4
MIDDLE_HEADS = 4
FAR_HEADS = 2
MIDDLE = NEAR_HEADS
FAR = NEAR_HEADS + MIDDLE_HEADS
STAT_ROWS = 8
SLOTS = 3
QUERY_ROWS = 192
SWAP = [(0, 1), (1, 0)]
WINDOW = 32
GRANT = 20 << 20

OWN, OTHER, DOWN, UP, MAIN, MAIN_CAP, FINAL, FINAL_CAP, PLACE, SLAB = range(10)


def plan_fits(heads_dev, span_count, slab_count, head_count):
    return (
        span_count == 4
        and slab_count == 2
        and head_count == 2
        and heads_dev == slab_count * (NEAR_HEADS + MIDDLE_HEADS + FAR_HEADS)
    )


def scalar_operand(heads):
    by_place = np.zeros((4, 12), np.int32)
    by_place[:, OTHER] = heads
    by_place[:, DOWN] = [MIDDLE, MIDDLE, 0, MIDDLE]
    by_place[:, UP] = [0, MIDDLE, 0, 0]
    by_place[:, MAIN] = [MIDDLE, 0, MIDDLE, 0]
    by_place[:, MAIN_CAP] = [3, 3, 3, 0]
    by_place[:, FINAL] = [FAR, 0, 0, FAR]
    by_place[:, FINAL_CAP] = [1, 3, 0, 1]
    by_place[:, PLACE] = range(4)
    by_slab = np.zeros(12, np.int32)
    by_slab[[OWN, OTHER, SLAB]] = heads, -heads, 1
    row = lax.dynamic_slice_in_dim(jnp.array(by_place), lax.axis_index("span"), 1, 0)[0]
    return row + lax.axis_index("slab") * jnp.array(by_slab)


def pack_kernel(inputs, messages, copies, with_noise, scalars, *refs):
    ins, rest = refs[:inputs], refs[inputs:]
    outs = rest[: messages + with_noise]
    staged = rest[messages + with_noise : -2]
    arrive, leave = rest[-2:]
    arriving = [[] for _ in range(messages)]
    for number, (source, row, rows, entries, shift, target, at, heads) in enumerate(copies):
        head = shift
        for entry in entries:
            head = head + scalars[entry]
        column = pl.multiple_of(head * HD, HD)
        copy = pltpu.make_async_copy(
            ins[source].at[pl.ds(row, rows), pl.ds(column, heads * HD)],
            staged[target].at[pl.ds(at, rows), :],
            arrive.at[number],
        )
        copy.start()
        arriving[target].append(copy)
    if with_noise:
        noisy, out = ins[-1], outs[-1]
        frames = noisy.shape[0]
        out[...] = jnp.concatenate([noisy[frame] for frame in range(frames)], axis=-1)
    leaving = []
    for target in range(messages):
        for copy in arriving[target]:
            copy.wait()
        copy = pltpu.make_async_copy(staged[target], outs[target], leave.at[target])
        copy.start()
        leaving.append(copy)
    for copy in leaving:
        copy.wait()


def pack(scalars, arrays, shapes, copies, name, noisy=None):
    moved = sum(2 * 2 * rows * heads * HD for _, _, rows, _, _, _, _, heads in copies)
    out_shape = [pltpu.HBM(shape, jnp.bfloat16) for shape in shapes]
    in_specs = [pl.BlockSpec(memory_space=pl.ANY)] * len(arrays)
    out_specs = [pl.BlockSpec(memory_space=pl.ANY)] * len(shapes)
    if noisy is not None:
        frames, height, breadth, channels = noisy.shape
        lanes = frames * channels
        arrays = arrays + (noisy,)
        in_specs.append(pl.BlockSpec(noisy.shape, lambda i, scalars: (0, 0, 0, 0)))
        out_shape.append(jax.ShapeDtypeStruct((height, breadth, lanes), noisy.dtype))
        out_specs.append(pl.BlockSpec((height, breadth, lanes), lambda i, scalars: (0, 0, 0)))
    return pl.pallas_call(
        functools.partial(
            pack_kernel, len(arrays), len(shapes), copies, noisy is not None
        ),
        name=name,
        out_shape=out_shape,
        grid_spec=pltpu.PrefetchScalarGridSpec(
            num_scalar_prefetch=1,
            grid=(1,),
            in_specs=in_specs,
            out_specs=out_specs,
            scratch_shapes=[pltpu.VMEM(shape, jnp.bfloat16) for shape in shapes]
            + [
                pltpu.SemaphoreType.DMA((len(copies),)),
                pltpu.SemaphoreType.DMA((len(shapes),)),
            ],
        ),
        compiler_params=pltpu.CompilerParams(vmem_limit_bytes=GRANT),
        cost_estimate=pl.CostEstimate(flops=0, bytes_accessed=moved, transcendentals=0),
    )(scalars, *arrays)


def message(scalars, pieces, arrays, name, noisy=None):
    copies, shapes = [], []
    for target, parts in enumerate(pieces):
        at = 0
        for source, row, rows, entries, shift, heads in parts:
            copies.append((source, row, rows, entries, shift, target, at, heads))
            at += rows
        shapes.append((at, parts[0][5] * HD))
    return pack(scalars, arrays, shapes, copies, name, noisy)


class Tokens(typing.NamedTuple):
    query: int | None = None
    pairs: tuple = ()
    extra: int | None = None


OWN_TOKENS = Tokens()


def attend_kernel(variants, extra, span_count, fresh, scalars, mask, *refs):
    query_own, key_own, value_own, received, weight, gain = refs[:6]
    more = refs[6 : 6 + extra]
    mine_out, theirs_out, folded, squares, carried, moved = refs[-6:]
    payloads = refs[6 + extra : -6] if fresh else refs[6 + extra : -8]
    rows = query_own.shape[0]
    half = rows // 2
    step = pl.program_id(0)
    to_exp2 = math.log2(math.e) / math.sqrt(HD)
    active = functools.reduce(
        lambda a, b: a | b, [scalars[PLACE] == place for place in variants]
    )

    last_step = step == pl.num_programs(0) - 1
    part = carried.shape[1] // 2
    halves = [
        carried.at[:, pl.ds(pl.multiple_of(number * part, part), part)]
        for number in (scalars[SLAB], 1 - scalars[SLAB])
    ]
    fetches = (
        []
        if fresh
        else [
            pltpu.make_async_copy(refs[number - 8], halves[number], moved.at[number])
            for number in range(2)
        ]
    )

    @pl.when((step == 0) & active)
    def _():
        folded[...] = jnp.zeros_like(folded)
        squares[...] = jnp.zeros_like(squares)
        for fetch in fetches:
            fetch.start()

    def query_of(source):
        if source is OWN_TOKENS:
            return query_own[...]
        if source.extra is not None:
            return more[0][:, source.extra * HD : (source.extra + 1) * HD]
        return payloads[source.query][:rows]

    def pair_of(source):
        if source is OWN_TOKENS:
            parts = (key_own[...], received[:half], value_own[...], received[half:])
        elif source.extra is not None:
            lanes = slice(source.extra * HD, (source.extra + 1) * HD)
            parts = (more[1][:, lanes], more[3][:half, lanes], more[2][:, lanes], more[3][half:, lanes])
        elif len(source.pairs) == 2:
            one, two = (payloads[number] for number in source.pairs)
            parts = (one[:half], two[:half], one[half:], two[half:])
        else:
            payload = payloads[source.pairs[0]]
            start = payload.shape[0] - 2 * rows
            return payload[start : start + rows], payload[start + rows :]
        return jnp.concatenate(parts[:2], axis=0), jnp.concatenate(parts[2:], axis=0)

    def projector(extra_head):
        if extra_head is None:
            scaled = weight[...].astype(jnp.float32) * gain[...]
        else:
            lanes = slice(extra_head * HD, (extra_head + 1) * HD)
            scaled = more[4][:, lanes].astype(jnp.float32) * more[5][:, lanes]
        high = scaled.astype(jnp.bfloat16)
        low = (scaled - high.astype(jnp.float32)).astype(jnp.bfloat16)
        return jnp.concatenate([high, low, jnp.ones((16, HD), jnp.bfloat16)], axis=0)

    def one_query(source, slot, query_span, key_sources):
        query = query_of(source)
        pairs = [pair_of(key_source) for key_source, _ in key_sources]
        open_to = [
            None if key_span == query_span else mask[query_span * span_count + key_span] > 0
            for _, key_span in key_sources
        ]
        keys_in = jnp.concatenate([pair[0] for pair in pairs], axis=0)
        ones_block = jnp.ones((rows, HD), jnp.bfloat16)
        values_in = jnp.concatenate(
            [jnp.concatenate([pair[1], ones_block], axis=1) for pair in pairs], axis=0
        )
        pieces = []
        for row in range(0, rows, QUERY_ROWS):
            score = lax.dot_general(
                query[row : row + QUERY_ROWS],
                keys_in,
                (((1,), (1,)), ((), ())),
                preferred_element_type=jnp.float32,
            )
            best = None
            for number, is_open in enumerate(open_to):
                start = number * rows
                block = score[:, start : start + HD]
                for lane in range(HD, rows, HD):
                    block = jnp.maximum(block, score[:, start + lane : start + lane + HD])
                if is_open is not None:
                    block = jnp.where(is_open, block, neg_big)
                best = block if best is None else jnp.maximum(best, block)
            top = jnp.max(best, axis=1, keepdims=True)
            weights = []
            for number, is_open in enumerate(open_to):
                start = number * rows
                shift = top if is_open is None else jnp.where(is_open, top, -neg_big)
                weights.append(
                    jnp.exp2((score[:, start : start + rows] - shift) * to_exp2).astype(jnp.bfloat16)
                )
            both = jnp.dot(
                jnp.concatenate(weights, axis=1), values_in, preferred_element_type=jnp.float32
            )
            pieces.append((both[:, :HD] / both[:, HD:]).astype(jnp.bfloat16))
        attended = jnp.concatenate(pieces, axis=0)
        folded[slot] += lax.dot_general(
            projector(source.extra),
            attended,
            (((1,), (1,)), ((), ())),
            preferred_element_type=jnp.float32,
        )
        wide = attended.astype(jnp.float32)
        squares[slot] += wide * wide

    for place, (steps, tasks) in variants.items():

        @pl.when((scalars[PLACE] == place) & (step < steps))
        def _():
            for task in tasks:
                one_query(*task)

    def store():
        copies = [
            pltpu.make_async_copy(halves[number], out, moved.at[2 + number])
            for number, out in enumerate((mine_out, theirs_out))
        ]
        for copy in copies:
            copy.start()
        for copy in copies:
            copy.wait()

    if fresh:

        @pl.when(last_step & jnp.logical_not(active))
        def _():
            carried[...] = jnp.zeros_like(carried)
            store()

    @pl.when(last_step & active)
    def _():
        ones_rows = jnp.ones((STAT_ROWS, HD), jnp.bfloat16)
        patch = weight.shape[0]
        used = sorted({task[1] for _, tasks in variants.values() for task in tasks})
        for fetch in fetches:
            fetch.wait()
        for slot in range(SLOTS):
            if slot not in used:
                if fresh:
                    carried[slot] = jnp.zeros(carried.shape[1:], carried.dtype)
                continue
            left = squares[slot]
            total = jnp.zeros((STAT_ROWS, rows), jnp.float32)
            for _ in range(3):
                piece = left.astype(jnp.bfloat16)
                left = left - piece.astype(jnp.float32)
                total = total + lax.dot_general(
                    ones_rows, piece, (((1,), (1,)), ((), ())), preferred_element_type=jnp.float32
                )
            done = folded[slot]
            new = jnp.concatenate(
                [
                    done[:patch] + done[patch : 2 * patch],
                    done[2 * patch : 2 * patch + STAT_ROWS],
                    total,
                ],
                axis=0,
            )
            carried[slot] = new if fresh else carried[slot] + new
        store()


def attend(steps, first, cap, own, scalars, mask, sums, payloads, variants, more, name, cost=1):
    queries, keys, values, received, weight, gain = own
    rows = queries.shape[0]
    half = rows // 2
    patch = weight.shape[0]

    def moving(i, scalars):
        return jnp.minimum(i, scalars[cap])

    def column(height, own_column):
        def index(i, scalars, mask):
            head = scalars[first] + moving(i, scalars)
            return (0, head + scalars[OWN] if own_column else head)

        return pl.BlockSpec((height, HD), index)

    def two_columns(height, own_column):
        def index(i, scalars, mask):
            pair = jnp.minimum(moving(i, scalars), 1)
            return (0, pair + scalars[OWN] // 2 if own_column else pair)

        return pl.BlockSpec((height, 2 * HD), index)

    def payload_column(payload):
        last = payload.shape[1] // HD - 1

        def index(i, scalars, mask):
            return (0, jnp.minimum(moving(i, scalars), last))

        return pl.BlockSpec((payload.shape[0], HD), index)

    in_specs = [
        column(rows, True),
        column(half, True),
        column(half, True),
        column(rows, False),
        column(patch, True),
        column(1, True),
    ]
    arrays = [queries, keys, values, received, weight, gain]
    extra = 0
    if more:
        extra = 6
        in_specs += [
            two_columns(rows, True),
            two_columns(half, True),
            two_columns(half, True),
            two_columns(rows, False),
            two_columns(patch, True),
            two_columns(1, True),
        ]
        arrays += [queries, keys, values, received, weight, gain]
    in_specs += [payload_column(payload) for payload in payloads]
    arrays += payloads
    fresh = sums is None
    sums_shape = (SLOTS, patch + 2 * STAT_ROWS, rows)
    aliases = {}
    if not fresh:
        aliases = {2 + len(arrays): 0, 3 + len(arrays): 1}
        in_specs += [pl.BlockSpec(memory_space=pl.ANY)] * 2
        arrays += sums
    pairs = max(
        count * sum(len(task[3]) for task in tasks) for count, tasks in variants.values()
    )
    span_count = math.isqrt(mask.shape[0])
    return pl.pallas_call(
        functools.partial(attend_kernel, variants, extra, span_count, fresh),
        name=name,
        out_shape=[pltpu.HBM((SLOTS, sums_shape[1] // 2, rows), jnp.float32)] * 2,
        input_output_aliases=aliases,
        grid_spec=pltpu.PrefetchScalarGridSpec(
            num_scalar_prefetch=2,
            grid=(steps,),
            in_specs=in_specs,
            out_specs=[pl.BlockSpec(memory_space=pl.ANY)] * 2,
            scratch_shapes=[
                pltpu.VMEM((SLOTS, 2 * patch + 16, rows), jnp.float32),
                pltpu.VMEM((SLOTS, rows, HD), jnp.float32),
                pltpu.VMEM(sums_shape, jnp.float32),
                pltpu.SemaphoreType.DMA((4,)),
            ],
        ),
        compiler_params=pltpu.CompilerParams(vmem_limit_bytes=GRANT),
        cost_estimate=pl.CostEstimate(
            flops=cost * pairs * 4 * rows * rows * HD,
            bytes_accessed=steps * HD * 2 * sum(spec.block_shape[0] for spec in in_specs[:4]),
            transcendentals=cost * pairs * rows * rows,
        ),
    )(scalars, mask, *arrays)


def token_sums(
    scalars, queries, keys, values, span_mask, head_gain, patch_weight, prepare
):
    rows = queries.shape[0]
    half = rows // 2
    heads = NEAR_HEADS + MIDDLE_HEADS + FAR_HEADS
    in_place = lambda array: pltpu.with_memory_space_constraint(array, pltpu.HBM)
    queries, keys, values = (in_place(array) for array in (queries, keys, values))

    def send(value, *pairs):
        return in_place(lax.ppermute(value, "span", list(pairs)))

    def tokens(entry, shift, count):
        return [(0, 0, rows, (OWN, entry) if entry else (OWN,), shift, count)]

    def pairs_of(entry, shift, count):
        entries = (entry,) if entry else ()
        return [
            piece
            for part in (1, 2)
            for piece in (
                (part, 0, half, (OWN,) + entries, shift, count),
                (3, (part - 1) * half, half, entries, shift, count),
            )
        ]

    (handed,) = message(
        scalars,
        [[(part, 0, half, (OTHER,), 0, heads) for part in (1, 2)]],
        (queries, keys, values),
        "pack_handed",
    )
    received = lax.ppermute(handed, "slab", SWAP)
    down, up = message(
        scalars,
        [
            tokens(DOWN, 0, MIDDLE_HEADS) + pairs_of(DOWN, 0, MIDDLE_HEADS),
            pairs_of(UP, 0, NEAR_HEADS),
        ],
        (queries, keys, values, received),
        "pack_first",
    )
    source, _ = lax.optimization_barrier((received, down))
    down = send(down, (1, 0), (2, 1), (3, 2))
    up = send(up, (0, 1), (1, 2))
    up_two, two, far_all, far_pair = message(
        scalars,
        [
            pairs_of(None, MIDDLE, MIDDLE_HEADS),
            tokens(None, 0, NEAR_HEADS) + pairs_of(None, 0, NEAR_HEADS),
            tokens(None, FAR, FAR_HEADS) + pairs_of(None, FAR, FAR_HEADS),
            pairs_of(None, FAR, FAR_HEADS),
        ],
        (queries, keys, values, source),
        "pack_second",
    )
    anchor = two
    up_two = send(up_two, (0, 2))
    two = send(two, (3, 1))
    far_next = send(far_all, (2, 3), (1, 0))
    far_pair, prepared = lax.optimization_barrier((far_pair, prepare(anchor)))
    far_two = send(far_pair, (1, 3))
    far_three = send(far_pair, (0, 3))

    span_mask, head_gain, patch_weight, _ = lax.optimization_barrier(
        (span_mask, head_gain, patch_weight, anchor)
    )
    mask = span_mask.reshape(-1)
    weight = patch_weight.T
    own = (queries, keys, values, received, weight, head_gain[None, :])
    run = functools.partial(attend, own=own, scalars=scalars, mask=mask)

    here, on_one, back_one = OWN_TOKENS, Tokens(0, (0,)), Tokens(None, (1,))
    back_two = Tokens(None, (2,))
    sums = run(
        MIDDLE_HEADS,
        MAIN,
        MAIN_CAP,
        sums=None,
        payloads=[down, up, up_two],
        variants={
            0: (4, [(here, 0, 0, [(here, 0)]), (on_one, 1, 1, [(here, 0), (on_one, 1)])]),
            1: (
                4,
                [
                    (on_one, 1, 2, [(back_one, 0), (here, 1), (on_one, 2)]),
                    (here, 0, 1, [(back_one, 0), (here, 1)]),
                ],
            ),
            2: (
                4,
                [
                    (on_one, 1, 3, [(back_two, 0), (back_one, 1), (here, 2), (on_one, 3)]),
                    (here, 0, 2, [(back_two, 0), (back_one, 1), (here, 2)]),
                ],
            ),
        },
        more=False,
        name="main_heads",
    )
    noise, *prepared = prepared
    sums, noise = lax.optimization_barrier((sums, noise))
    lanes = 2 * LAT_CH
    before = from_behind(noise[:, -lanes:].reshape(-1, HD), "span", 1).reshape(-1, lanes)
    on_two, beside = Tokens(2, (2,)), Tokens(3, (3,))
    two_back, three_back = Tokens(None, (4,)), Tokens(None, (5,))
    extras = [Tokens(None, (), lane) for lane in range(2)]
    sums, before, prepared = lax.optimization_barrier((sums, before, prepared))
    sums = run(
        NEAR_HEADS,
        FINAL,
        FINAL_CAP,
        sums=sums,
        payloads=[down, up, two, far_next, far_two, far_three],
        variants={
            0: (
                FAR_HEADS,
                [(here, 0, 0, [(here, 0)]), (beside, 1, 1, [(here, 0), (beside, 1)])]
                + [(head, 0, 0, [(head, 0)]) for head in extras],
            ),
            1: (
                NEAR_HEADS,
                [(on_two, 2, 3, [(back_one, 0), (here, 1), (on_one, 2), (on_two, 3)])],
            ),
            3: (
                FAR_HEADS,
                [
                    (here, 0, 3, [(three_back, 0), (two_back, 1), (beside, 2), (here, 3)]),
                    (beside, 2, 2, [(three_back, 0), (two_back, 1), (beside, 2)]),
                ],
            ),
        },
        more=True,
        name="final_heads",
        cost=4,
    )
    return sums, (noise, before, *prepared)


def noise_window(grid, constants):
    height, breadth, _ = grid.shape
    slab = lax.axis_index("slab")
    edge = jnp.where(slab == 0, grid[:, breadth - 1], grid[:, 0])
    edge = lax.ppermute(edge, "slab", SWAP)[:, None]
    grid = jnp.concatenate(
        [
            jnp.where(slab == 1, edge, 0.0),
            grid,
            jnp.where(slab == 0, edge, 0.0),
            jnp.zeros((height, WINDOW - breadth - 2, grid.shape[2]), grid.dtype),
        ],
        axis=1,
    )
    head = lax.axis_index("head")
    edge = jnp.where(head == 0, grid[height - 1], grid[0])
    count = constants.shape[1]
    extra = jnp.pad(constants, ((0, 8 - constants.shape[0]), (0, HD - count)))
    edge = jnp.pad(edge, ((0, 0), (0, HD - edge.shape[1])))
    sent = lax.ppermute(jnp.concatenate([edge, extra], axis=0), "head", SWAP)
    edge = sent[None, :WINDOW, : grid.shape[2]]
    constants = constants + sent[WINDOW : WINDOW + constants.shape[0], :count]
    grid = jnp.concatenate(
        [jnp.where(head == 1, edge, 0.0), grid, jnp.where(head == 0, edge, 0.0)], axis=0
    )
    return grid.reshape((height + 2) * WINDOW, grid.shape[2]), constants.T


def cell_selector(height, breadth):
    cell = lax.broadcasted_iota(jnp.int32, ((height + 2) * WINDOW, 4 * TROWS * TCOLS), 0)
    column = lax.broadcasted_iota(jnp.int32, cell.shape, 1)
    y = lax.axis_index("head") * height + cell // WINDOW - 1
    x = lax.axis_index("slab") * breadth + cell % WINDOW - 1
    inside = (y >= 0) & (y < 2 * TROWS) & (x >= 0) & (x < 2 * TCOLS)
    inside = inside & (cell % WINDOW < breadth + 2)
    target = ((y % 2) * 2 + x % 2) * (TROWS * TCOLS) + (y // 2) * TCOLS + x // 2
    return (inside & (column == target)).astype(jnp.bfloat16)


def band_kernel(weight, band):
    outputs = weight.shape[1]
    band[...] = jnp.zeros_like(band)
    for row_tap in range(3):
        for col_tap in range(3):
            for frame_tap in range(3):
                start = ((3 * frame_tap + row_tap) * 3 + col_tap) * LAT_CH
                block = weight[start : start + LAT_CH]
                for frame in range(FRAMES_SPAN):
                    at = (col_tap * (FRAMES_SPAN + 2) + frame + frame_tap) * LAT_CH
                    band[
                        row_tap, at : at + LAT_CH, frame * outputs : (frame + 1) * outputs
                    ] = block


def banded_weight(conv_weight):
    shape = (3, 3 * (FRAMES_SPAN + 2) * LAT_CH, FRAMES_SPAN * conv_weight.shape[1])
    return pl.pallas_call(
        band_kernel,
        name="band",
        out_shape=jax.ShapeDtypeStruct(shape, conv_weight.dtype),
        in_specs=[pl.BlockSpec(memory_space=pltpu.VMEM)],
        out_specs=pl.BlockSpec(memory_space=pltpu.VMEM),
        compiler_params=pltpu.CompilerParams(vmem_limit_bytes=GRANT),
        cost_estimate=pl.CostEstimate(
            flops=0, bytes_accessed=2 * math.prod(shape), transcendentals=0
        ),
    )(conv_weight)


def finish_kernel(
    scalars, mine, other, noise, before, selector, band, bias, constants, clean, decoded, cells
):
    frames, height, breadth, channels = clean.shape
    patch = constants.shape[0]
    first = scalars[SLAB] == 0
    sums = jnp.concatenate(
        [jnp.where(first, mine[...], other[...]), jnp.where(first, other[...], mine[...])], axis=0
    )
    feature_width = HEADS * HD
    row_mean = sums[patch : patch + 1] / feature_width
    spread = sums[patch + STAT_ROWS : patch + STAT_ROWS + 1] / feature_width - row_mean * row_mean
    velocity = (
        lax.rsqrt(spread + norm_eps) * (sums[:patch] - constants[:, 0:1] * row_mean)
        + constants[:, 1:2]
    )
    tokens = TROWS * TCOLS
    lane = lax.broadcasted_iota(jnp.int32, velocity.shape, 1)
    velocity = jnp.where((lane >= 2 * tokens) | (scalars[PLACE] > 0), velocity, 0.0)
    columns = jnp.concatenate(
        [
            jnp.concatenate(
                [
                    velocity[
                        part * channels : (part + 1) * channels,
                        frame * tokens : (frame + 1) * tokens,
                    ]
                    for part in range(4)
                ],
                axis=1,
            )
            for frame in range(frames + 2)
        ],
        axis=0,
    )
    high = columns.astype(jnp.bfloat16)
    low = (columns - high.astype(jnp.float32)).astype(jnp.bfloat16)
    chosen = sum(
        lax.dot_general(
            selector[...], part, (((1,), (1,)), ((), ())), preferred_element_type=jnp.float32
        )
        for part in (high, low)
    )
    count = (height + 2) * WINDOW
    cells[:count] = (
        jnp.concatenate([before[...], noise[...]], axis=1) - noise_level * chosen
    )
    cells[count:] = jnp.zeros_like(cells[count:])
    for frame in range(frames):
        lanes = slice((frame + 2) * channels, (frame + 3) * channels)
        for y in range(height):
            start = (y + 1) * WINDOW + 1
            clean[frame, y] = cells[start : start + breadth, lanes]
    shifted = jnp.concatenate(
        [cells[tap : tap + count] for tap in range(3)], axis=1
    ).astype(jnp.bfloat16)
    total = jnp.broadcast_to(bias[...], (height * breadth, bias.shape[1]))
    for tap in range(3):
        block = jnp.concatenate(
            [
                shifted[(y + tap) * WINDOW : (y + tap) * WINDOW + breadth]
                for y in range(height)
            ],
            axis=0,
        )
        total = total + jnp.dot(block, band[tap], preferred_element_type=jnp.float32)
    outputs = decoded.shape[3]
    total = total.astype(decoded.dtype)
    for frame in range(frames):
        decoded[frame] = total[:, frame * outputs : (frame + 1) * outputs].reshape(
            height, breadth, outputs
        )


def finish(
    scalars, mine, other, noise, before, selector, band, bias, constants, shape, outputs
):
    whole = pl.BlockSpec(memory_space=pltpu.VMEM)
    frames, height, breadth, channels = shape
    rows = (height + 2) * WINDOW
    return pl.pallas_call(
        finish_kernel,
        name="finish",
        out_shape=(
            jax.ShapeDtypeStruct(shape, jnp.float32),
            jax.ShapeDtypeStruct((frames, height, breadth, outputs), jnp.bfloat16),
        ),
        in_specs=[pl.BlockSpec(memory_space=pltpu.SMEM)] + [whole] * 8,
        out_specs=(whole, whole),
        scratch_shapes=[pltpu.VMEM((rows + 8, (frames + 2) * channels), jnp.float32)],
        compiler_params=pltpu.CompilerParams(vmem_limit_bytes=GRANT),
    )(scalars, mine, other, noise, before, selector, band, bias, constants)


def per_device(
    queries,
    keys,
    values,
    span_mask,
    head_gain,
    head_shift,
    patch_weight,
    noisy_latent,
    conv_weight,
    conv_bias,
):
    heads_dev = queries.shape[1] // HD
    if not plan_fits(
        heads_dev, lax.axis_size("span"), lax.axis_size("slab"), lax.axis_size("head")
    ):
        return gathered_plan(
            queries,
            keys,
            values,
            span_mask,
            head_gain,
            head_shift,
            patch_weight,
            noisy_latent,
            conv_weight,
            conv_bias,
        )
    place = lax.axis_index("span")
    slab = lax.axis_index("slab")
    scalars = scalar_operand(heads_dev // lax.axis_size("slab"))
    def prepare(anchor):
        noise, weight, gain, shift, taps, bias, _ = lax.optimization_barrier(
            (noisy_latent, patch_weight, head_gain, head_shift, conv_weight, conv_bias, anchor)
        )
        _, height, breadth, _ = noise.shape
        noise = noise.transpose(1, 2, 0, 3).reshape(height, breadth, -1)
        wide_weight = weight.T.astype(jnp.float32)
        constants = jnp.stack(
            [
                jnp.sum(wide_weight * gain[None, :], axis=1),
                jnp.sum(wide_weight * shift[None, :], axis=1),
            ]
        )
        window, constants = noise_window(noise, constants)
        return (
            window,
            constants,
            cell_selector(height, breadth),
            banded_weight(taps),
            jnp.tile(bias, FRAMES_SPAN)[None, :],
        )

    (mine, theirs), (noise, before, constants, selector, band, bias) = token_sums(
        scalars,
        queries,
        keys,
        values,
        span_mask,
        head_gain,
        patch_weight,
        prepare,
    )
    mine = mine + lax.ppermute(theirs, "slab", SWAP)
    own, after, third = mine[0], mine[1], mine[2]
    skip = TROWS * TCOLS
    from_one = lax.ppermute(
        jnp.concatenate([own[:, skip:], after], axis=1), "span", [(0, 1), (1, 2), (2, 3)]
    )
    to_current = lax.ppermute(third, "span", [(1, 3), (3, 2)])
    to_before = lax.ppermute(after[:, skip:], "span", [(0, 2), (1, 3)])
    kept = jnp.concatenate([jnp.where(place == 3, third[:, skip:], 0.0), own], axis=1)
    total = kept + from_one + jnp.concatenate([to_before, to_current], axis=1)
    total = total + lax.ppermute(total, "head", SWAP)
    other = lax.ppermute(total, "slab", SWAP)
    return finish(
        scalars,
        total,
        other,
        noise,
        before,
        selector,
        band,
        bias,
        constants,
        noisy_latent.shape,
        conv_weight.shape[1],
    )


def solution(mesh):
    placed = (
        P(("groups", "span"), "head"),
        P(("groups", "span", "slab"), "head"),
        P(("groups", "span", "slab"), "head"),
        P("groups", None),
        P("head"),
        P("head"),
        P("head", None),
        P(("groups", "span"), "head", "slab", None),
        P(),
        P(),
    )
    return jax.shard_map(
        per_device,
        mesh=mesh,
        in_specs=placed,
        out_specs=(
            P(("groups", "span"), "head", "slab", None),
            P(("groups", "span"), "head", "slab", None),
        ),
        check_vma=False,
    )
```

```python
import functools
import math
import typing

import jax
import jax.numpy as jnp
import numpy as np
from jax import lax
from jax.experimental import pallas as pl
from jax.experimental.pallas import tpu as pltpu
from jax.sharding import PartitionSpec as P

HEADS = 40
HD = 128
LAT_CH = 16
FRAMES_SPAN = 3
TROWS = 8
TCOLS = 16


neg_big = -1e30
noise_level = 0.75
norm_eps = 1e-06


def with_halo(cells, sides, width):
    for axis, dim in sides:
        count = lax.axis_size(axis)
        ends = count - 1
        head = lax.slice_in_dim(cells, 0, width, axis=dim)
        tail = lax.slice_in_dim(cells, cells.shape[dim] - width, cells.shape[dim], axis=dim)
        cells = jnp.concatenate(
            [
                lax.ppermute(tail, axis, [(i, (i + 1) % count) for i in range(ends)]),
                cells,
                lax.ppermute(head, axis, [((i + 1) % count, i) for i in range(ends)]),
            ],
            axis=dim,
        )
    return cells


def from_behind(value, axis, by):
    size = lax.axis_size(axis)
    pairs = [(i, i + by) for i in range(size) if 0 <= i + by < size]
    return lax.ppermute(value, axis, pairs)


def block_length(total_rows):
    block_size = total_rows
    while block_size > 768 and block_size % 2 == 0:
        block_size = block_size // 2
    return block_size


def fold_keys(partial_state, key_value, query_block, mask_row, rows_span):
    keys_piece, values_piece = key_value
    heads_dev = query_block.shape[1]
    piece_rows = keys_piece.shape[0]
    length = block_length(piece_rows)
    span_count = mask_row.shape[0]
    score_scale = 1.0 / math.sqrt(HD)
    span_ids = jnp.arange(span_count, dtype=jnp.int32)

    def one_block(carry_state, block_index):
        running_max, running_sum, weighted = carry_state
        offset = block_index * length
        key_block = lax.dynamic_slice_in_dim(keys_piece, offset, length, 0).reshape(
            length, heads_dev, HD
        )
        value_block = lax.dynamic_slice_in_dim(values_piece, offset, length, 0).reshape(
            length, heads_dev, HD
        )
        key_span = (offset + jnp.arange(length, dtype=jnp.int32)) // rows_span
        allowed = (
            jnp.sum(jnp.where(key_span[:, None] == span_ids[None, :], mask_row[None, :], 0), axis=1)
            > 0
        )
        scores = (
            jnp.einsum("qhd,khd->hqk", query_block, key_block, preferred_element_type=jnp.float32)
            * score_scale
        )
        scores = jnp.where(allowed[None, None, :], scores, neg_big)
        new_max = jnp.maximum(running_max, jnp.max(scores, axis=2))
        weights = jnp.where(allowed[None, None, :], jnp.exp(scores - new_max[:, :, None]), 0.0)
        factor = jnp.exp(running_max - new_max)
        running_sum = running_sum * factor + jnp.sum(weights, axis=2)
        weighted = weighted * factor.T[:, :, None] + jnp.einsum(
            "hqk,khd->qhd",
            weights.astype(jnp.bfloat16),
            value_block,
            preferred_element_type=jnp.float32,
        )
        return ((new_max, running_sum, weighted), None)

    result, unused = lax.scan(
        one_block, partial_state, jnp.arange(piece_rows // length, dtype=jnp.int32)
    )
    return result


def gathered_plan(
    queries,
    keys,
    values,
    span_mask,
    head_gain,
    head_shift,
    patch_weight,
    noisy_latent,
    conv_weight,
    conv_bias,
):
    heads_dev = queries.shape[1] // HD
    slab_count = lax.axis_size("slab")
    col_dev = TCOLS // slab_count
    slab_place = lax.axis_index("slab")
    span_place = lax.axis_index("span")
    mask_row = lax.dynamic_slice_in_dim(span_mask, span_place, 1, 0)[0]
    token_grid = queries.reshape(FRAMES_SPAN, TROWS, TCOLS, queries.shape[-1])
    picked = lax.dynamic_slice_in_dim(token_grid, slab_place * col_dev, col_dev, 2)
    own_queries = picked.reshape(FRAMES_SPAN * TROWS * col_dev, queries.shape[-1]).reshape(
        -1, heads_dev, HD
    )
    query_rows = own_queries.shape[0]
    rows_span = keys.shape[0] * slab_count
    running_max, running_sum, weighted = fold_keys(
        (
            jnp.full((heads_dev, query_rows), neg_big, jnp.float32),
            jnp.zeros((heads_dev, query_rows), jnp.float32),
            jnp.zeros((query_rows, heads_dev, HD), jnp.float32),
        ),
        (
            lax.all_gather(keys, ("span", "slab"), axis=0, tiled=True),
            lax.all_gather(values, ("span", "slab"), axis=0, tiled=True),
        ),
        own_queries,
        mask_row,
        rows_span,
    )
    attended = (
        (weighted / running_sum.T[:, :, None])
        .astype(jnp.bfloat16)
        .reshape(query_rows, heads_dev * HD)
    )
    feature_width = HEADS * HD
    values32 = attended.astype(jnp.float32)
    row_total = jnp.sum(values32, axis=1)
    row_squares = jnp.sum(values32 * values32, axis=1)
    row_total, row_squares = lax.psum((row_total, row_squares), "head")
    row_mean = row_total / feature_width
    spread = row_squares / feature_width - row_mean * row_mean
    normed = (
        (values32 - row_mean[:, None]) * lax.rsqrt(spread + norm_eps)[:, None] * head_gain[None, :]
        + head_shift[None, :]
    ).astype(jnp.bfloat16)
    normed_grid = normed.reshape(FRAMES_SPAN, TROWS, col_dev, normed.shape[-1])
    own_rows = TROWS // lax.axis_size("head")
    picked = normed_grid
    product = jnp.dot(
        picked.reshape(-1, picked.shape[-1]), patch_weight, preferred_element_type=jnp.float32
    )
    velocity = lax.psum_scatter(
        product.reshape(
            FRAMES_SPAN, own_rows * lax.axis_size("head"), col_dev * patch_weight.shape[1]
        )
        .transpose(1, 0, 2)
        .reshape(own_rows * lax.axis_size("head"), -1)
        .astype(jnp.bfloat16),
        "head",
        scatter_dimension=0,
        tiled=True,
    ).astype(jnp.float32)
    rows_dev = velocity.shape[0]
    patch_cells = (
        velocity.reshape(rows_dev, FRAMES_SPAN, col_dev, 2, 2, LAT_CH)
        .transpose(1, 0, 3, 2, 4, 5)
        .reshape(FRAMES_SPAN, 2 * rows_dev, 2 * col_dev, LAT_CH)
    )
    clean_latent = noisy_latent - noise_level * patch_cells
    latent_input = clean_latent.astype(jnp.bfloat16)
    framed = with_halo(latent_input, (("head", 1), ("slab", 2)), 1)
    earlier = from_behind(framed[FRAMES_SPAN - 2 :], "span", 1)
    stacked = jnp.concatenate([earlier, framed], axis=0)
    height = clean_latent.shape[1]
    breadth = clean_latent.shape[2]
    columns = jnp.concatenate(
        [
            stacked[
                frame_tap : frame_tap + FRAMES_SPAN,
                row_tap : row_tap + height,
                col_tap : col_tap + breadth,
                :,
            ]
            for frame_tap in range(3)
            for row_tap in range(3)
            for col_tap in range(3)
        ],
        axis=-1,
    )
    decoded = (
        jnp.dot(
            columns.reshape(FRAMES_SPAN * height * breadth, 27 * LAT_CH),
            conv_weight,
            preferred_element_type=jnp.float32,
        )
        + conv_bias[None, :]
    )
    decoded = decoded.astype(jnp.bfloat16).reshape(
        FRAMES_SPAN, height, breadth, conv_weight.shape[1]
    )
    return (clean_latent, decoded)


NEAR_HEADS = 4
MIDDLE_HEADS = 4
FAR_HEADS = 2
MIDDLE = NEAR_HEADS
FAR = NEAR_HEADS + MIDDLE_HEADS
STAT_ROWS = 8
SLOTS = 3
QUERY_ROWS = 192
SWAP = [(0, 1), (1, 0)]
WINDOW = 32
GRANT = 20 << 20

OWN, OTHER, DOWN, UP, MAIN, MAIN_CAP, FINAL, FINAL_CAP, PLACE, SLAB = range(10)


def plan_fits(heads_dev, span_count, slab_count, head_count):
    return (
        span_count == 4
        and slab_count == 2
        and head_count == 2
        and heads_dev == slab_count * (NEAR_HEADS + MIDDLE_HEADS + FAR_HEADS)
    )


def scalar_operand(heads):
    by_place = np.zeros((4, 12), np.int32)
    by_place[:, OTHER] = heads
    by_place[:, DOWN] = [MIDDLE, MIDDLE, 0, MIDDLE]
    by_place[:, UP] = [0, MIDDLE, 0, 0]
    by_place[:, MAIN] = [MIDDLE, 0, MIDDLE, 0]
    by_place[:, MAIN_CAP] = [3, 3, 3, 0]
    by_place[:, FINAL] = [FAR, 0, 0, FAR]
    by_place[:, FINAL_CAP] = [1, 3, 0, 1]
    by_place[:, PLACE] = range(4)
    by_slab = np.zeros(12, np.int32)
    by_slab[[OWN, OTHER, SLAB]] = heads, -heads, 1
    row = lax.dynamic_slice_in_dim(jnp.array(by_place), lax.axis_index("span"), 1, 0)[0]
    return row + lax.axis_index("slab") * jnp.array(by_slab)


def pack_kernel(inputs, messages, copies, scalars, *refs):
    ins, rest = refs[:inputs], refs[inputs:]
    outs, staged = rest[:messages], rest[messages:-2]
    arrive, leave = rest[-2:]
    arriving = []
    for number, (source, row, rows, entries, shift, target, at, heads) in enumerate(copies):
        head = shift
        for entry in entries:
            head = head + scalars[entry]
        column = pl.multiple_of(head * HD, HD)
        place = staged[target].at[pl.ds(at, rows), :]
        copy = pltpu.make_async_copy(
            ins[source].at[pl.ds(row, rows), pl.ds(column, heads * HD)], place, arrive.at[number]
        )
        copy.start()
        onward = pltpu.make_async_copy(
            place, outs[target].at[pl.ds(at, rows), :], leave.at[number]
        )
        arriving.append((copy, onward))
    for copy, onward in arriving:
        copy.wait()
        onward.start()
    for _, onward in arriving:
        onward.wait()


def pack(scalars, arrays, shapes, copies, name):
    moved = sum(2 * 2 * rows * heads * HD for _, _, rows, _, _, _, _, heads in copies)
    out_shape = [pltpu.HBM(shape, jnp.bfloat16) for shape in shapes]
    in_specs = [pl.BlockSpec(memory_space=pl.ANY)] * len(arrays)
    out_specs = [pl.BlockSpec(memory_space=pl.ANY)] * len(shapes)
    return pl.pallas_call(
        functools.partial(pack_kernel, len(arrays), len(shapes), copies),
        name=name,
        out_shape=out_shape,
        grid_spec=pltpu.PrefetchScalarGridSpec(
            num_scalar_prefetch=1,
            grid=(1,),
            in_specs=in_specs,
            out_specs=out_specs,
            scratch_shapes=[pltpu.VMEM(shape, jnp.bfloat16) for shape in shapes]
            + [
                pltpu.SemaphoreType.DMA((len(copies),)),
                pltpu.SemaphoreType.DMA((len(copies),)),
            ],
        ),
        compiler_params=pltpu.CompilerParams(vmem_limit_bytes=GRANT),
        cost_estimate=pl.CostEstimate(flops=0, bytes_accessed=moved, transcendentals=0),
    )(scalars, *arrays)


def message(scalars, pieces, arrays, name):
    copies, shapes = [], []
    for target, parts in enumerate(pieces):
        at = 0
        for source, row, rows, entries, shift, heads in parts:
            copies.append((source, row, rows, entries, shift, target, at, heads))
            at += rows
        shapes.append((at, parts[0][5] * HD))
    return pack(scalars, arrays, shapes, copies, name)


class Tokens(typing.NamedTuple):
    query: int | None = None
    pairs: tuple = ()
    extra: int | None = None


OWN_TOKENS = Tokens()


def attend_kernel(variants, extra, span_count, fresh, scalars, mask, *refs):
    query_own, key_own, value_own, received, weight, gain = refs[:6]
    more = refs[6 : 6 + extra]
    mine_out, theirs_out, folded, squares, carried, moved = refs[-6:]
    payloads = refs[6 + extra : -6] if fresh else refs[6 + extra : -8]
    rows = query_own.shape[0]
    half = rows // 2
    step = pl.program_id(0)
    to_exp2 = math.log2(math.e) / math.sqrt(HD)
    active = functools.reduce(
        lambda a, b: a | b, [scalars[PLACE] == place for place in variants]
    )

    last_step = step == pl.num_programs(0) - 1
    part = carried.shape[1] // 2
    halves = [
        carried.at[:, pl.ds(pl.multiple_of(number * part, part), part)]
        for number in (scalars[SLAB], 1 - scalars[SLAB])
    ]
    fetches = (
        []
        if fresh
        else [
            pltpu.make_async_copy(refs[number - 8], halves[number], moved.at[number])
            for number in range(2)
        ]
    )

    @pl.when((step == 0) & active)
    def _():
        folded[...] = jnp.zeros_like(folded)
        squares[...] = jnp.zeros_like(squares)
        for fetch in fetches:
            fetch.start()

    def query_of(source):
        if source is OWN_TOKENS:
            return query_own[...]
        if source.extra is not None:
            return more[0][:, source.extra * HD : (source.extra + 1) * HD]
        return payloads[source.query][:rows]

    def pair_of(source):
        if source is OWN_TOKENS:
            parts = (key_own[...], received[:half], value_own[...], received[half:])
        elif source.extra is not None:
            lanes = slice(source.extra * HD, (source.extra + 1) * HD)
            parts = (more[1][:, lanes], more[3][:half, lanes], more[2][:, lanes], more[3][half:, lanes])
        elif len(source.pairs) == 2:
            one, two = (payloads[number] for number in source.pairs)
            parts = (one[:half], two[:half], one[half:], two[half:])
        else:
            payload = payloads[source.pairs[0]]
            start = payload.shape[0] - 2 * rows
            return payload[start : start + rows], payload[start + rows :]
        return jnp.concatenate(parts[:2], axis=0), jnp.concatenate(parts[2:], axis=0)

    def projector(extra_head):
        if extra_head is None:
            scaled = weight[...].astype(jnp.float32) * gain[...]
        else:
            lanes = slice(extra_head * HD, (extra_head + 1) * HD)
            scaled = more[4][:, lanes].astype(jnp.float32) * more[5][:, lanes]
        high = scaled.astype(jnp.bfloat16)
        low = (scaled - high.astype(jnp.float32)).astype(jnp.bfloat16)
        return jnp.concatenate([high, low, jnp.ones((16, HD), jnp.bfloat16)], axis=0)

    def one_query(source, slot, query_span, key_sources):
        query = query_of(source)
        pairs = [pair_of(key_source) for key_source, _ in key_sources]
        open_to = [
            None if key_span == query_span else mask[query_span * span_count + key_span] > 0
            for _, key_span in key_sources
        ]
        keys_in = jnp.concatenate([pair[0] for pair in pairs], axis=0)
        ones_block = jnp.ones((rows, HD), jnp.bfloat16)
        values_in = jnp.concatenate(
            [jnp.concatenate([pair[1], ones_block], axis=1) for pair in pairs], axis=0
        )
        pieces = []
        for row in range(0, rows, QUERY_ROWS):
            score = lax.dot_general(
                query[row : row + QUERY_ROWS],
                keys_in,
                (((1,), (1,)), ((), ())),
                preferred_element_type=jnp.float32,
            )
            best = None
            for number, is_open in enumerate(open_to):
                start = number * rows
                block = score[:, start : start + HD]
                for lane in range(HD, rows, HD):
                    block = jnp.maximum(block, score[:, start + lane : start + lane + HD])
                if is_open is not None:
                    block = jnp.where(is_open, block, neg_big)
                best = block if best is None else jnp.maximum(best, block)
            top = jnp.max(best, axis=1, keepdims=True)
            weights = []
            for number, is_open in enumerate(open_to):
                start = number * rows
                shift = top if is_open is None else jnp.where(is_open, top, -neg_big)
                weights.append(
                    jnp.exp2((score[:, start : start + rows] - shift) * to_exp2).astype(jnp.bfloat16)
                )
            both = jnp.dot(
                jnp.concatenate(weights, axis=1), values_in, preferred_element_type=jnp.float32
            )
            pieces.append((both[:, :HD] / both[:, HD:]).astype(jnp.bfloat16))
        attended = jnp.concatenate(pieces, axis=0)
        folded[slot] += lax.dot_general(
            projector(source.extra),
            attended,
            (((1,), (1,)), ((), ())),
            preferred_element_type=jnp.float32,
        )
        wide = attended.astype(jnp.float32)
        squares[slot] += wide * wide

    for place, (steps, tasks) in variants.items():

        @pl.when((scalars[PLACE] == place) & (step < steps))
        def _():
            for task in tasks:
                one_query(*task)

    def store():
        copies = [
            pltpu.make_async_copy(halves[number], out, moved.at[2 + number])
            for number, out in enumerate((mine_out, theirs_out))
        ]
        for copy in copies:
            copy.start()
        for copy in copies:
            copy.wait()

    if fresh:

        @pl.when(last_step & jnp.logical_not(active))
        def _():
            carried[...] = jnp.zeros_like(carried)
            store()

    @pl.when(last_step & active)
    def _():
        ones_rows = jnp.ones((STAT_ROWS, HD), jnp.bfloat16)
        patch = weight.shape[0]
        used = sorted({task[1] for _, tasks in variants.values() for task in tasks})
        for fetch in fetches:
            fetch.wait()
        for slot in range(SLOTS):
            if slot not in used:
                if fresh:
                    carried[slot] = jnp.zeros(carried.shape[1:], carried.dtype)
                continue
            left = squares[slot]
            total = jnp.zeros((STAT_ROWS, rows), jnp.float32)
            for _ in range(3):
                piece = left.astype(jnp.bfloat16)
                left = left - piece.astype(jnp.float32)
                total = total + lax.dot_general(
                    ones_rows, piece, (((1,), (1,)), ((), ())), preferred_element_type=jnp.float32
                )
            done = folded[slot]
            new = jnp.concatenate(
                [
                    done[:patch] + done[patch : 2 * patch],
                    done[2 * patch : 2 * patch + STAT_ROWS],
                    total,
                ],
                axis=0,
            )
            carried[slot] = new if fresh else carried[slot] + new
        store()


def attend(steps, first, cap, own, scalars, mask, sums, payloads, variants, more, name, cost=1):
    queries, keys, values, received, weight, gain = own
    rows = queries.shape[0]
    half = rows // 2
    patch = weight.shape[0]

    def moving(i, scalars):
        return jnp.minimum(i, scalars[cap])

    def column(height, own_column):
        def index(i, scalars, mask):
            head = scalars[first] + moving(i, scalars)
            return (0, head + scalars[OWN] if own_column else head)

        return pl.BlockSpec((height, HD), index)

    def two_columns(height, own_column):
        def index(i, scalars, mask):
            pair = jnp.minimum(moving(i, scalars), 1)
            return (0, pair + scalars[OWN] // 2 if own_column else pair)

        return pl.BlockSpec((height, 2 * HD), index)

    def payload_column(payload):
        last = payload.shape[1] // HD - 1

        def index(i, scalars, mask):
            return (0, jnp.minimum(moving(i, scalars), last))

        return pl.BlockSpec((payload.shape[0], HD), index)

    in_specs = [
        column(rows, True),
        column(half, True),
        column(half, True),
        column(rows, False),
        column(patch, True),
        column(1, True),
    ]
    arrays = [queries, keys, values, received, weight, gain]
    extra = 0
    if more:
        extra = 6
        in_specs += [
            two_columns(rows, True),
            two_columns(half, True),
            two_columns(half, True),
            two_columns(rows, False),
            two_columns(patch, True),
            two_columns(1, True),
        ]
        arrays += [queries, keys, values, received, weight, gain]
    in_specs += [payload_column(payload) for payload in payloads]
    arrays += payloads
    fresh = sums is None
    sums_shape = (SLOTS, patch + 2 * STAT_ROWS, rows)
    aliases = {}
    if not fresh:
        aliases = {2 + len(arrays): 0, 3 + len(arrays): 1}
        in_specs += [pl.BlockSpec(memory_space=pl.ANY)] * 2
        arrays += sums
    pairs = max(
        count * sum(len(task[3]) for task in tasks) for count, tasks in variants.values()
    )
    span_count = math.isqrt(mask.shape[0])
    return pl.pallas_call(
        functools.partial(attend_kernel, variants, extra, span_count, fresh),
        name=name,
        out_shape=[pltpu.HBM((SLOTS, sums_shape[1] // 2, rows), jnp.float32)] * 2,
        input_output_aliases=aliases,
        grid_spec=pltpu.PrefetchScalarGridSpec(
            num_scalar_prefetch=2,
            grid=(steps,),
            in_specs=in_specs,
            out_specs=[pl.BlockSpec(memory_space=pl.ANY)] * 2,
            scratch_shapes=[
                pltpu.VMEM((SLOTS, 2 * patch + 16, rows), jnp.float32),
                pltpu.VMEM((SLOTS, rows, HD), jnp.float32),
                pltpu.VMEM(sums_shape, jnp.float32),
                pltpu.SemaphoreType.DMA((4,)),
            ],
        ),
        compiler_params=pltpu.CompilerParams(vmem_limit_bytes=GRANT),
        cost_estimate=pl.CostEstimate(
            flops=cost * pairs * 4 * rows * rows * HD,
            bytes_accessed=steps * HD * 2 * sum(spec.block_shape[0] for spec in in_specs[:4]),
            transcendentals=cost * pairs * rows * rows,
        ),
    )(scalars, mask, *arrays)


def token_sums(
    scalars, queries, keys, values, span_mask, head_gain, patch_weight, prepare
):
    rows = queries.shape[0]
    half = rows // 2
    heads = NEAR_HEADS + MIDDLE_HEADS + FAR_HEADS
    in_place = lambda array: pltpu.with_memory_space_constraint(array, pltpu.HBM)
    queries, keys, values = (in_place(array) for array in (queries, keys, values))

    def send(value, *pairs):
        return in_place(lax.ppermute(value, "span", list(pairs)))

    def tokens(entry, shift, count):
        return [(0, 0, rows, (OWN, entry) if entry else (OWN,), shift, count)]

    def pairs_of(entry, shift, count):
        entries = (entry,) if entry else ()
        return [
            piece
            for part in (1, 2)
            for piece in (
                (part, 0, half, (OWN,) + entries, shift, count),
                (3, (part - 1) * half, half, entries, shift, count),
            )
        ]

    (handed,) = message(
        scalars,
        [
            [
                (part, row, half // 2, (OTHER,), 0, heads)
                for part in (1, 2)
                for row in (0, half // 2)
            ]
        ],
        (queries, keys, values),
        "pack_handed",
    )
    received = lax.ppermute(handed, "slab", SWAP)
    down, up = message(
        scalars,
        [
            tokens(DOWN, 0, MIDDLE_HEADS) + pairs_of(DOWN, 0, MIDDLE_HEADS),
            pairs_of(UP, 0, NEAR_HEADS),
        ],
        (queries, keys, values, received),
        "pack_first",
    )
    source, _ = lax.optimization_barrier((received, down))
    down = send(down, (1, 0), (2, 1), (3, 2))
    up = send(up, (0, 1), (1, 2))
    up_two, two, far_all, far_pair = message(
        scalars,
        [
            pairs_of(None, MIDDLE, MIDDLE_HEADS),
            tokens(None, 0, NEAR_HEADS) + pairs_of(None, 0, NEAR_HEADS),
            tokens(None, FAR, FAR_HEADS) + pairs_of(None, FAR, FAR_HEADS),
            pairs_of(None, FAR, FAR_HEADS),
        ],
        (queries, keys, values, source),
        "pack_second",
    )
    anchor = two
    up_two = send(up_two, (0, 2))
    two = send(two, (3, 1))
    far_next = send(far_all, (2, 3), (1, 0))
    far_pair, prepared = lax.optimization_barrier((far_pair, prepare(anchor)))
    far_two = send(far_pair, (1, 3))
    far_three = send(far_pair, (0, 3))

    span_mask, head_gain, patch_weight, _ = lax.optimization_barrier(
        (span_mask, head_gain, patch_weight, anchor)
    )
    mask = span_mask.reshape(-1)
    weight = patch_weight.T
    own = (queries, keys, values, received, weight, head_gain[None, :])
    run = functools.partial(attend, own=own, scalars=scalars, mask=mask)

    here, on_one, back_one = OWN_TOKENS, Tokens(0, (0,)), Tokens(None, (1,))
    back_two = Tokens(None, (2,))
    sums = run(
        MIDDLE_HEADS,
        MAIN,
        MAIN_CAP,
        sums=None,
        payloads=[down, up, up_two],
        variants={
            0: (4, [(here, 0, 0, [(here, 0)]), (on_one, 1, 1, [(here, 0), (on_one, 1)])]),
            1: (
                4,
                [
                    (on_one, 1, 2, [(back_one, 0), (here, 1), (on_one, 2)]),
                    (here, 0, 1, [(back_one, 0), (here, 1)]),
                ],
            ),
            2: (
                4,
                [
                    (on_one, 1, 3, [(back_two, 0), (back_one, 1), (here, 2), (on_one, 3)]),
                    (here, 0, 2, [(back_two, 0), (back_one, 1), (here, 2)]),
                ],
            ),
        },
        more=False,
        name="main_heads",
    )
    on_two, beside = Tokens(2, (2,)), Tokens(3, (3,))
    two_back, three_back = Tokens(None, (4,)), Tokens(None, (5,))
    extras = [Tokens(None, (), lane) for lane in range(2)]
    sums, prepared = lax.optimization_barrier((sums, prepared))
    sums = run(
        NEAR_HEADS,
        FINAL,
        FINAL_CAP,
        sums=sums,
        payloads=[down, up, two, far_next, far_two, far_three],
        variants={
            0: (
                FAR_HEADS,
                [(here, 0, 0, [(here, 0)]), (beside, 1, 1, [(here, 0), (beside, 1)])]
                + [(head, 0, 0, [(head, 0)]) for head in extras],
            ),
            1: (
                NEAR_HEADS,
                [(on_two, 2, 3, [(back_one, 0), (here, 1), (on_one, 2), (on_two, 3)])],
            ),
            3: (
                FAR_HEADS,
                [
                    (here, 0, 3, [(three_back, 0), (two_back, 1), (beside, 2), (here, 3)]),
                    (beside, 2, 2, [(three_back, 0), (two_back, 1), (beside, 2)]),
                ],
            ),
        },
        more=True,
        name="final_heads",
        cost=4,
    )
    return sums, prepared


def noise_window(grid, constants):
    height, breadth, _ = grid.shape
    slab = lax.axis_index("slab")
    edge = jnp.where(slab == 0, grid[:, breadth - 1], grid[:, 0])
    edge = lax.ppermute(edge, "slab", SWAP)[:, None]
    grid = jnp.concatenate(
        [
            jnp.where(slab == 1, edge, 0.0),
            grid,
            jnp.where(slab == 0, edge, 0.0),
            jnp.zeros((height, WINDOW - breadth - 2, grid.shape[2]), grid.dtype),
        ],
        axis=1,
    )
    head = lax.axis_index("head")
    edge = jnp.where(head == 0, grid[height - 1], grid[0])
    count = constants.shape[1]
    extra = jnp.pad(constants, ((0, 8 - constants.shape[0]), (0, HD - count)))
    edge = jnp.pad(edge, ((0, 0), (0, HD - edge.shape[1])))
    sent = lax.ppermute(jnp.concatenate([edge, extra], axis=0), "head", SWAP)
    edge = sent[None, :WINDOW, : grid.shape[2]]
    constants = constants + sent[WINDOW : WINDOW + constants.shape[0], :count]
    grid = jnp.concatenate(
        [jnp.where(head == 1, edge, 0.0), grid, jnp.where(head == 0, edge, 0.0)], axis=0
    )
    return grid.reshape((height + 2) * WINDOW, grid.shape[2]), constants.T


def cell_selector(height, breadth):
    cell = lax.broadcasted_iota(jnp.int32, ((height + 2) * WINDOW, 4 * TROWS * TCOLS), 0)
    column = lax.broadcasted_iota(jnp.int32, cell.shape, 1)
    y = lax.axis_index("head") * height + cell // WINDOW - 1
    x = lax.axis_index("slab") * breadth + cell % WINDOW - 1
    inside = (y >= 0) & (y < 2 * TROWS) & (x >= 0) & (x < 2 * TCOLS)
    inside = inside & (cell % WINDOW < breadth + 2)
    target = ((y % 2) * 2 + x % 2) * (TROWS * TCOLS) + (y // 2) * TCOLS + x // 2
    return (inside & (column == target)).astype(jnp.bfloat16)


def band_kernel(weight, band):
    outputs = weight.shape[1]
    band[...] = jnp.zeros_like(band)
    for row_tap in range(3):
        for col_tap in range(3):
            for frame_tap in range(3):
                start = ((3 * frame_tap + row_tap) * 3 + col_tap) * LAT_CH
                block = weight[start : start + LAT_CH]
                for frame in range(FRAMES_SPAN):
                    at = (col_tap * (FRAMES_SPAN + 2) + frame + frame_tap) * LAT_CH
                    band[
                        row_tap, at : at + LAT_CH, frame * outputs : (frame + 1) * outputs
                    ] = block


def banded_weight(conv_weight):
    shape = (3, 3 * (FRAMES_SPAN + 2) * LAT_CH, FRAMES_SPAN * conv_weight.shape[1])
    return pl.pallas_call(
        band_kernel,
        name="band",
        out_shape=jax.ShapeDtypeStruct(shape, conv_weight.dtype),
        in_specs=[pl.BlockSpec(memory_space=pltpu.VMEM)],
        out_specs=pl.BlockSpec(memory_space=pltpu.VMEM),
        compiler_params=pltpu.CompilerParams(vmem_limit_bytes=GRANT),
        cost_estimate=pl.CostEstimate(
            flops=0, bytes_accessed=2 * math.prod(shape), transcendentals=0
        ),
    )(conv_weight)


def finish_kernel(
    scalars, mine, other, noise, before, selector, band, bias, constants, clean, decoded, cells
):
    frames, height, breadth, channels = clean.shape
    patch = constants.shape[0]
    first = scalars[SLAB] == 0
    sums = jnp.concatenate(
        [jnp.where(first, mine[...], other[...]), jnp.where(first, other[...], mine[...])], axis=0
    )
    feature_width = HEADS * HD
    row_mean = sums[patch : patch + 1] / feature_width
    spread = sums[patch + STAT_ROWS : patch + STAT_ROWS + 1] / feature_width - row_mean * row_mean
    velocity = (
        lax.rsqrt(spread + norm_eps) * (sums[:patch] - constants[:, 0:1] * row_mean)
        + constants[:, 1:2]
    )
    tokens = TROWS * TCOLS
    lane = lax.broadcasted_iota(jnp.int32, velocity.shape, 1)
    velocity = jnp.where((lane >= 2 * tokens) | (scalars[PLACE] > 0), velocity, 0.0)
    columns = jnp.concatenate(
        [
            jnp.concatenate(
                [
                    velocity[
                        part * channels : (part + 1) * channels,
                        frame * tokens : (frame + 1) * tokens,
                    ]
                    for part in range(4)
                ],
                axis=1,
            )
            for frame in range(frames + 2)
        ],
        axis=0,
    )
    high = columns.astype(jnp.bfloat16)
    low = (columns - high.astype(jnp.float32)).astype(jnp.bfloat16)
    chosen = sum(
        lax.dot_general(
            selector[...], part, (((1,), (1,)), ((), ())), preferred_element_type=jnp.float32
        )
        for part in (high, low)
    )
    count = (height + 2) * WINDOW
    cells[:count] = (
        jnp.concatenate([before[...], noise[...]], axis=1) - noise_level * chosen
    )
    cells[count:] = jnp.zeros_like(cells[count:])
    for frame in range(frames):
        lanes = slice((frame + 2) * channels, (frame + 3) * channels)
        for y in range(height):
            start = (y + 1) * WINDOW + 1
            clean[frame, y] = cells[start : start + breadth, lanes]
    shifted = jnp.concatenate(
        [cells[tap : tap + count] for tap in range(3)], axis=1
    ).astype(jnp.bfloat16)
    total = jnp.broadcast_to(bias[...], (height * breadth, bias.shape[1]))
    for tap in range(3):
        block = jnp.concatenate(
            [
                shifted[(y + tap) * WINDOW : (y + tap) * WINDOW + breadth]
                for y in range(height)
            ],
            axis=0,
        )
        total = total + jnp.dot(block, band[tap], preferred_element_type=jnp.float32)
    outputs = decoded.shape[3]
    total = total.astype(decoded.dtype)
    for frame in range(frames):
        decoded[frame] = total[:, frame * outputs : (frame + 1) * outputs].reshape(
            height, breadth, outputs
        )


def finish(
    scalars, mine, other, noise, before, selector, band, bias, constants, shape, outputs
):
    whole = pl.BlockSpec(memory_space=pltpu.VMEM)
    frames, height, breadth, channels = shape
    rows = (height + 2) * WINDOW
    return pl.pallas_call(
        finish_kernel,
        name="finish",
        out_shape=(
            jax.ShapeDtypeStruct(shape, jnp.float32),
            jax.ShapeDtypeStruct((frames, height, breadth, outputs), jnp.bfloat16),
        ),
        in_specs=[pl.BlockSpec(memory_space=pltpu.SMEM)] + [whole] * 8,
        out_specs=(whole, whole),
        scratch_shapes=[pltpu.VMEM((rows + 8, (frames + 2) * channels), jnp.float32)],
        compiler_params=pltpu.CompilerParams(vmem_limit_bytes=GRANT),
    )(scalars, mine, other, noise, before, selector, band, bias, constants)


def per_device(
    queries,
    keys,
    values,
    span_mask,
    head_gain,
    head_shift,
    patch_weight,
    noisy_latent,
    conv_weight,
    conv_bias,
):
    heads_dev = queries.shape[1] // HD
    if not plan_fits(
        heads_dev, lax.axis_size("span"), lax.axis_size("slab"), lax.axis_size("head")
    ):
        return gathered_plan(
            queries,
            keys,
            values,
            span_mask,
            head_gain,
            head_shift,
            patch_weight,
            noisy_latent,
            conv_weight,
            conv_bias,
        )
    place = lax.axis_index("span")
    slab = lax.axis_index("slab")
    scalars = scalar_operand(heads_dev // lax.axis_size("slab"))
    def prepare(anchor):
        noise, weight, gain, shift, taps, bias, _ = lax.optimization_barrier(
            (noisy_latent, patch_weight, head_gain, head_shift, conv_weight, conv_bias, anchor)
        )
        _, height, breadth, _ = noise.shape
        noise = noise.transpose(1, 2, 0, 3).reshape(height, breadth, -1)
        wide_weight = weight.T.astype(jnp.float32)
        constants = jnp.stack(
            [
                jnp.sum(wide_weight * gain[None, :], axis=1),
                jnp.sum(wide_weight * shift[None, :], axis=1),
            ]
        )
        window, constants = noise_window(noise, constants)
        return (
            window,
            window[:, -2 * LAT_CH :].reshape(16, -1),
            constants,
            cell_selector(height, breadth),
            banded_weight(taps),
            jnp.tile(bias, FRAMES_SPAN)[None, :],
        )

    (mine, theirs), (noise, ahead, constants, selector, band, bias) = token_sums(
        scalars,
        queries,
        keys,
        values,
        span_mask,
        head_gain,
        patch_weight,
        prepare,
    )
    mine = mine + lax.ppermute(theirs, "slab", SWAP)
    own, after, third = mine[0], mine[1], mine[2]
    skip = TROWS * TCOLS
    from_one = lax.ppermute(
        jnp.concatenate([jnp.concatenate([own[:, skip:], after], axis=1), ahead], axis=0),
        "span",
        [(0, 1), (1, 2), (2, 3)],
    )
    before = from_one[own.shape[0] :].reshape(-1, 2 * LAT_CH)
    from_one = from_one[: own.shape[0]]
    to_current = lax.ppermute(third, "span", [(1, 3), (3, 2)])
    to_before = lax.ppermute(after[:, skip:], "span", [(0, 2), (1, 3)])
    kept = jnp.concatenate([jnp.where(place == 3, third[:, skip:], 0.0), own], axis=1)
    total = kept + from_one + jnp.concatenate([to_before, to_current], axis=1)
    total = total + lax.ppermute(total, "head", SWAP)
    other = lax.ppermute(total, "slab", SWAP)
    return finish(
        scalars,
        total,
        other,
        noise,
        before,
        selector,
        band,
        bias,
        constants,
        noisy_latent.shape,
        conv_weight.shape[1],
    )


def solution(mesh):
    placed = (
        P(("groups", "span"), "head"),
        P(("groups", "span", "slab"), "head"),
        P(("groups", "span", "slab"), "head"),
        P("groups", None),
        P("head"),
        P("head"),
        P("head", None),
        P(("groups", "span"), "head", "slab", None),
        P(),
        P(),
    )
    return jax.shard_map(
        per_device,
        mesh=mesh,
        in_specs=placed,
        out_specs=(
            P(("groups", "span"), "head", "slab", None),
            P(("groups", "span"), "head", "slab", None),
        ),
        check_vma=False,
    )
```

```python
import functools
import math
import typing

import jax
import jax.numpy as jnp
import numpy as np
from jax import lax
from jax.experimental import pallas as pl
from jax.experimental.pallas import tpu as pltpu
from jax.sharding import PartitionSpec as P

HEADS = 40
HD = 128
LAT_CH = 16
FRAMES_SPAN = 3
TROWS = 8
TCOLS = 16


neg_big = -1e30
noise_level = 0.75
norm_eps = 1e-06


def with_halo(cells, sides, width):
    for axis, dim in sides:
        count = lax.axis_size(axis)
        ends = count - 1
        head = lax.slice_in_dim(cells, 0, width, axis=dim)
        tail = lax.slice_in_dim(cells, cells.shape[dim] - width, cells.shape[dim], axis=dim)
        cells = jnp.concatenate(
            [
                lax.ppermute(tail, axis, [(i, (i + 1) % count) for i in range(ends)]),
                cells,
                lax.ppermute(head, axis, [((i + 1) % count, i) for i in range(ends)]),
            ],
            axis=dim,
        )
    return cells


def from_behind(value, axis, by):
    size = lax.axis_size(axis)
    pairs = [(i, i + by) for i in range(size) if 0 <= i + by < size]
    return lax.ppermute(value, axis, pairs)


def block_length(total_rows):
    block_size = total_rows
    while block_size > 768 and block_size % 2 == 0:
        block_size = block_size // 2
    return block_size


def fold_keys(partial_state, key_value, query_block, mask_row, rows_span):
    keys_piece, values_piece = key_value
    heads_dev = query_block.shape[1]
    piece_rows = keys_piece.shape[0]
    length = block_length(piece_rows)
    span_count = mask_row.shape[0]
    score_scale = 1.0 / math.sqrt(HD)
    span_ids = jnp.arange(span_count, dtype=jnp.int32)

    def one_block(carry_state, block_index):
        running_max, running_sum, weighted = carry_state
        offset = block_index * length
        key_block = lax.dynamic_slice_in_dim(keys_piece, offset, length, 0).reshape(
            length, heads_dev, HD
        )
        value_block = lax.dynamic_slice_in_dim(values_piece, offset, length, 0).reshape(
            length, heads_dev, HD
        )
        key_span = (offset + jnp.arange(length, dtype=jnp.int32)) // rows_span
        allowed = (
            jnp.sum(jnp.where(key_span[:, None] == span_ids[None, :], mask_row[None, :], 0), axis=1)
            > 0
        )
        scores = (
            jnp.einsum("qhd,khd->hqk", query_block, key_block, preferred_element_type=jnp.float32)
            * score_scale
        )
        scores = jnp.where(allowed[None, None, :], scores, neg_big)
        new_max = jnp.maximum(running_max, jnp.max(scores, axis=2))
        weights = jnp.where(allowed[None, None, :], jnp.exp(scores - new_max[:, :, None]), 0.0)
        factor = jnp.exp(running_max - new_max)
        running_sum = running_sum * factor + jnp.sum(weights, axis=2)
        weighted = weighted * factor.T[:, :, None] + jnp.einsum(
            "hqk,khd->qhd",
            weights.astype(jnp.bfloat16),
            value_block,
            preferred_element_type=jnp.float32,
        )
        return ((new_max, running_sum, weighted), None)

    result, unused = lax.scan(
        one_block, partial_state, jnp.arange(piece_rows // length, dtype=jnp.int32)
    )
    return result


def gathered_plan(
    queries,
    keys,
    values,
    span_mask,
    head_gain,
    head_shift,
    patch_weight,
    noisy_latent,
    conv_weight,
    conv_bias,
):
    heads_dev = queries.shape[1] // HD
    slab_count = lax.axis_size("slab")
    col_dev = TCOLS // slab_count
    slab_place = lax.axis_index("slab")
    span_place = lax.axis_index("span")
    mask_row = lax.dynamic_slice_in_dim(span_mask, span_place, 1, 0)[0]
    token_grid = queries.reshape(FRAMES_SPAN, TROWS, TCOLS, queries.shape[-1])
    picked = lax.dynamic_slice_in_dim(token_grid, slab_place * col_dev, col_dev, 2)
    own_queries = picked.reshape(FRAMES_SPAN * TROWS * col_dev, queries.shape[-1]).reshape(
        -1, heads_dev, HD
    )
    query_rows = own_queries.shape[0]
    rows_span = keys.shape[0] * slab_count
    running_max, running_sum, weighted = fold_keys(
        (
            jnp.full((heads_dev, query_rows), neg_big, jnp.float32),
            jnp.zeros((heads_dev, query_rows), jnp.float32),
            jnp.zeros((query_rows, heads_dev, HD), jnp.float32),
        ),
        (
            lax.all_gather(keys, ("span", "slab"), axis=0, tiled=True),
            lax.all_gather(values, ("span", "slab"), axis=0, tiled=True),
        ),
        own_queries,
        mask_row,
        rows_span,
    )
    attended = (
        (weighted / running_sum.T[:, :, None])
        .astype(jnp.bfloat16)
        .reshape(query_rows, heads_dev * HD)
    )
    feature_width = HEADS * HD
    values32 = attended.astype(jnp.float32)
    row_total = jnp.sum(values32, axis=1)
    row_squares = jnp.sum(values32 * values32, axis=1)
    row_total, row_squares = lax.psum((row_total, row_squares), "head")
    row_mean = row_total / feature_width
    spread = row_squares / feature_width - row_mean * row_mean
    normed = (
        (values32 - row_mean[:, None]) * lax.rsqrt(spread + norm_eps)[:, None] * head_gain[None, :]
        + head_shift[None, :]
    ).astype(jnp.bfloat16)
    normed_grid = normed.reshape(FRAMES_SPAN, TROWS, col_dev, normed.shape[-1])
    own_rows = TROWS // lax.axis_size("head")
    picked = normed_grid
    product = jnp.dot(
        picked.reshape(-1, picked.shape[-1]), patch_weight, preferred_element_type=jnp.float32
    )
    velocity = lax.psum_scatter(
        product.reshape(
            FRAMES_SPAN, own_rows * lax.axis_size("head"), col_dev * patch_weight.shape[1]
        )
        .transpose(1, 0, 2)
        .reshape(own_rows * lax.axis_size("head"), -1)
        .astype(jnp.bfloat16),
        "head",
        scatter_dimension=0,
        tiled=True,
    ).astype(jnp.float32)
    rows_dev = velocity.shape[0]
    patch_cells = (
        velocity.reshape(rows_dev, FRAMES_SPAN, col_dev, 2, 2, LAT_CH)
        .transpose(1, 0, 3, 2, 4, 5)
        .reshape(FRAMES_SPAN, 2 * rows_dev, 2 * col_dev, LAT_CH)
    )
    clean_latent = noisy_latent - noise_level * patch_cells
    latent_input = clean_latent.astype(jnp.bfloat16)
    framed = with_halo(latent_input, (("head", 1), ("slab", 2)), 1)
    earlier = from_behind(framed[FRAMES_SPAN - 2 :], "span", 1)
    stacked = jnp.concatenate([earlier, framed], axis=0)
    height = clean_latent.shape[1]
    breadth = clean_latent.shape[2]
    columns = jnp.concatenate(
        [
            stacked[
                frame_tap : frame_tap + FRAMES_SPAN,
                row_tap : row_tap + height,
                col_tap : col_tap + breadth,
                :,
            ]
            for frame_tap in range(3)
            for row_tap in range(3)
            for col_tap in range(3)
        ],
        axis=-1,
    )
    decoded = (
        jnp.dot(
            columns.reshape(FRAMES_SPAN * height * breadth, 27 * LAT_CH),
            conv_weight,
            preferred_element_type=jnp.float32,
        )
        + conv_bias[None, :]
    )
    decoded = decoded.astype(jnp.bfloat16).reshape(
        FRAMES_SPAN, height, breadth, conv_weight.shape[1]
    )
    return (clean_latent, decoded)


NEAR_HEADS = 4
MIDDLE_HEADS = 4
FAR_HEADS = 2
MIDDLE = NEAR_HEADS
FAR = NEAR_HEADS + MIDDLE_HEADS
STAT_ROWS = 8
SLOTS = 3
QUERY_ROWS = 192
SWAP = [(0, 1), (1, 0)]
WINDOW = 32
GRANT = 20 << 20

OWN, OTHER, DOWN, UP, MAIN, MAIN_CAP, FINAL, FINAL_CAP, PLACE, SLAB = range(10)


def plan_fits(heads_dev, span_count, slab_count, head_count):
    return (
        span_count == 4
        and slab_count == 2
        and head_count == 2
        and heads_dev == slab_count * (NEAR_HEADS + MIDDLE_HEADS + FAR_HEADS)
    )


def scalar_operand(heads):
    by_place = np.zeros((4, 12), np.int32)
    by_place[:, OTHER] = heads
    by_place[:, DOWN] = [MIDDLE, MIDDLE, 0, MIDDLE]
    by_place[:, UP] = [0, MIDDLE, 0, 0]
    by_place[:, MAIN] = [MIDDLE, 0, MIDDLE, 0]
    by_place[:, MAIN_CAP] = [3, 3, 3, 0]
    by_place[:, FINAL] = [FAR, 0, 0, FAR]
    by_place[:, FINAL_CAP] = [1, 3, 0, 1]
    by_place[:, PLACE] = range(4)
    by_slab = np.zeros(12, np.int32)
    by_slab[[OWN, OTHER, SLAB]] = heads, -heads, 1
    row = lax.dynamic_slice_in_dim(jnp.array(by_place), lax.axis_index("span"), 1, 0)[0]
    return row + lax.axis_index("slab") * jnp.array(by_slab)


def pack_kernel(inputs, messages, copies, scalars, *refs):
    ins, rest = refs[:inputs], refs[inputs:]
    outs, staged = rest[:messages], rest[messages:-2]
    arrive, leave = rest[-2:]
    arriving = []
    for number, (source, row, rows, entries, shift, target, at, heads) in enumerate(copies):
        head = shift
        for entry in entries:
            head = head + scalars[entry]
        column = pl.multiple_of(head * HD, HD)
        place = staged[target].at[pl.ds(at, rows), :]
        copy = pltpu.make_async_copy(
            ins[source].at[pl.ds(row, rows), pl.ds(column, heads * HD)], place, arrive.at[number]
        )
        copy.start()
        onward = pltpu.make_async_copy(
            place, outs[target].at[pl.ds(at, rows), :], leave.at[number]
        )
        arriving.append((copy, onward))
    for copy, onward in arriving:
        copy.wait()
        onward.start()
    for _, onward in arriving:
        onward.wait()


def pack(scalars, arrays, shapes, copies, name):
    moved = sum(2 * 2 * rows * heads * HD for _, _, rows, _, _, _, _, heads in copies)
    out_shape = [pltpu.HBM(shape, jnp.bfloat16) for shape in shapes]
    in_specs = [pl.BlockSpec(memory_space=pl.ANY)] * len(arrays)
    out_specs = [pl.BlockSpec(memory_space=pl.ANY)] * len(shapes)
    return pl.pallas_call(
        functools.partial(pack_kernel, len(arrays), len(shapes), copies),
        name=name,
        out_shape=out_shape,
        grid_spec=pltpu.PrefetchScalarGridSpec(
            num_scalar_prefetch=1,
            grid=(1,),
            in_specs=in_specs,
            out_specs=out_specs,
            scratch_shapes=[pltpu.VMEM(shape, jnp.bfloat16) for shape in shapes]
            + [
                pltpu.SemaphoreType.DMA((len(copies),)),
                pltpu.SemaphoreType.DMA((len(copies),)),
            ],
        ),
        compiler_params=pltpu.CompilerParams(vmem_limit_bytes=GRANT),
        cost_estimate=pl.CostEstimate(flops=0, bytes_accessed=moved, transcendentals=0),
    )(scalars, *arrays)


def hand_kernel(heads, keys, values, out, arrive):
    column = pl.multiple_of((1 - lax.axis_index("slab")) * heads * HD, heads * HD)
    half = keys.shape[0]
    copies = []
    for number, source in enumerate((keys, values)):
        copy = pltpu.make_async_copy(
            source.at[:, pl.ds(column, heads * HD)],
            out.at[pl.ds(number * half, half), :],
            arrive.at[number],
        )
        copy.start()
        copies.append(copy)
    for copy in copies:
        copy.wait()


def pack_handed(keys, values, heads):
    shape = (2 * keys.shape[0], heads * HD)
    return pl.pallas_call(
        functools.partial(hand_kernel, heads),
        name="pack_handed",
        out_shape=jax.ShapeDtypeStruct(shape, keys.dtype),
        in_specs=[pl.BlockSpec(memory_space=pl.ANY)] * 2,
        out_specs=pl.BlockSpec(memory_space=pltpu.VMEM),
        scratch_shapes=[pltpu.SemaphoreType.DMA((2,))],
        compiler_params=pltpu.CompilerParams(vmem_limit_bytes=GRANT),
        cost_estimate=pl.CostEstimate(
            flops=0, bytes_accessed=4 * math.prod(shape), transcendentals=0
        ),
    )(keys, values)


def message(scalars, pieces, arrays, name):
    copies, shapes = [], []
    for target, parts in enumerate(pieces):
        at = 0
        for source, row, rows, entries, shift, heads in parts:
            copies.append((source, row, rows, entries, shift, target, at, heads))
            at += rows
        shapes.append((at, parts[0][5] * HD))
    return pack(scalars, arrays, shapes, copies, name)


class Tokens(typing.NamedTuple):
    query: int | None = None
    pairs: tuple = ()
    extra: int | None = None


OWN_TOKENS = Tokens()


def attend_kernel(variants, extra, span_count, fresh, scalars, mask, *refs):
    query_own, key_own, value_own, received, weight, gain = refs[:6]
    more = refs[6 : 6 + extra]
    mine_out, theirs_out, folded, squares, carried, moved = refs[-6:]
    payloads = refs[6 + extra : -6] if fresh else refs[6 + extra : -8]
    rows = query_own.shape[0]
    half = rows // 2
    step = pl.program_id(0)
    to_exp2 = math.log2(math.e) / math.sqrt(HD)
    active = functools.reduce(
        lambda a, b: a | b, [scalars[PLACE] == place for place in variants]
    )

    last_step = step == pl.num_programs(0) - 1
    part = carried.shape[1] // 2
    halves = [
        carried.at[:, pl.ds(pl.multiple_of(number * part, part), part)]
        for number in (scalars[SLAB], 1 - scalars[SLAB])
    ]
    fetches = (
        []
        if fresh
        else [
            pltpu.make_async_copy(refs[number - 8], halves[number], moved.at[number])
            for number in range(2)
        ]
    )

    @pl.when((step == 0) & active)
    def _():
        folded[...] = jnp.zeros_like(folded)
        squares[...] = jnp.zeros_like(squares)
        for fetch in fetches:
            fetch.start()

    def query_of(source):
        if source is OWN_TOKENS:
            return query_own[...]
        if source.extra is not None:
            return more[0][:, source.extra * HD : (source.extra + 1) * HD]
        return payloads[source.query][:rows]

    def pair_of(source):
        if source is OWN_TOKENS:
            parts = (key_own[...], received[:half], value_own[...], received[half:])
        elif source.extra is not None:
            lanes = slice(source.extra * HD, (source.extra + 1) * HD)
            parts = (more[1][:, lanes], more[3][:half, lanes], more[2][:, lanes], more[3][half:, lanes])
        elif len(source.pairs) == 2:
            one, two = (payloads[number] for number in source.pairs)
            parts = (one[:half], two[:half], one[half:], two[half:])
        else:
            payload = payloads[source.pairs[0]]
            start = payload.shape[0] - 2 * rows
            return payload[start : start + rows], payload[start + rows :]
        return jnp.concatenate(parts[:2], axis=0), jnp.concatenate(parts[2:], axis=0)

    def projector(extra_head):
        if extra_head is None:
            scaled = weight[...].astype(jnp.float32) * gain[...]
        else:
            lanes = slice(extra_head * HD, (extra_head + 1) * HD)
            scaled = more[4][:, lanes].astype(jnp.float32) * more[5][:, lanes]
        high = scaled.astype(jnp.bfloat16)
        low = (scaled - high.astype(jnp.float32)).astype(jnp.bfloat16)
        return jnp.concatenate([high, low, jnp.ones((16, HD), jnp.bfloat16)], axis=0)

    def one_query(source, slot, query_span, key_sources):
        query = query_of(source)
        pairs = [pair_of(key_source) for key_source, _ in key_sources]
        open_to = [
            None if key_span == query_span else mask[query_span * span_count + key_span] > 0
            for _, key_span in key_sources
        ]
        keys_in = jnp.concatenate([pair[0] for pair in pairs], axis=0)
        ones_block = jnp.ones((rows, HD), jnp.bfloat16)
        values_in = jnp.concatenate(
            [jnp.concatenate([pair[1], ones_block], axis=1) for pair in pairs], axis=0
        )
        pieces = []
        for row in range(0, rows, QUERY_ROWS):
            score = lax.dot_general(
                query[row : row + QUERY_ROWS],
                keys_in,
                (((1,), (1,)), ((), ())),
                preferred_element_type=jnp.float32,
            )
            best = None
            for number, is_open in enumerate(open_to):
                start = number * rows
                block = score[:, start : start + HD]
                for lane in range(HD, rows, HD):
                    block = jnp.maximum(block, score[:, start + lane : start + lane + HD])
                if is_open is not None:
                    block = jnp.where(is_open, block, neg_big)
                best = block if best is None else jnp.maximum(best, block)
            top = jnp.max(best, axis=1, keepdims=True)
            weights = []
            for number, is_open in enumerate(open_to):
                start = number * rows
                shift = top if is_open is None else jnp.where(is_open, top, -neg_big)
                weights.append(
                    jnp.exp2((score[:, start : start + rows] - shift) * to_exp2).astype(jnp.bfloat16)
                )
            both = jnp.dot(
                jnp.concatenate(weights, axis=1), values_in, preferred_element_type=jnp.float32
            )
            pieces.append((both[:, :HD] / both[:, HD:]).astype(jnp.bfloat16))
        attended = jnp.concatenate(pieces, axis=0)
        folded[slot] += lax.dot_general(
            projector(source.extra),
            attended,
            (((1,), (1,)), ((), ())),
            preferred_element_type=jnp.float32,
        )
        wide = attended.astype(jnp.float32)
        squares[slot] += wide * wide

    for place, (steps, tasks) in variants.items():

        @pl.when((scalars[PLACE] == place) & (step < steps))
        def _():
            for task in tasks:
                one_query(*task)

    def store():
        copies = [
            pltpu.make_async_copy(halves[number], out, moved.at[2 + number])
            for number, out in enumerate((mine_out, theirs_out))
        ]
        for copy in copies:
            copy.start()
        for copy in copies:
            copy.wait()

    if fresh:

        @pl.when(last_step & jnp.logical_not(active))
        def _():
            carried[...] = jnp.zeros_like(carried)
            store()

    @pl.when(last_step & active)
    def _():
        ones_rows = jnp.ones((STAT_ROWS, HD), jnp.bfloat16)
        patch = weight.shape[0]
        for fetch in fetches:
            fetch.wait()
        if fresh:
            carried[...] = jnp.zeros_like(carried)

        def finish_slot(slot):
            left = squares[slot]
            total = jnp.zeros((STAT_ROWS, rows), jnp.float32)
            for _ in range(3):
                piece = left.astype(jnp.bfloat16)
                left = left - piece.astype(jnp.float32)
                total = total + lax.dot_general(
                    ones_rows, piece, (((1,), (1,)), ((), ())), preferred_element_type=jnp.float32
                )
            done = folded[slot]
            carried[slot] += jnp.concatenate(
                [
                    done[:patch] + done[patch : 2 * patch],
                    done[2 * patch : 2 * patch + STAT_ROWS],
                    total,
                ],
                axis=0,
            )

        for place, (_, tasks) in variants.items():

            @pl.when(scalars[PLACE] == place)
            def _():
                for slot in sorted({task[1] for task in tasks}):
                    finish_slot(slot)

        store()


def attend(steps, first, cap, own, scalars, mask, sums, payloads, variants, more, name, cost=1):
    queries, keys, values, received, weight, gain = own
    rows = queries.shape[0]
    half = rows // 2
    patch = weight.shape[0]

    def moving(i, scalars):
        return jnp.minimum(i, scalars[cap])

    def column(height, own_column):
        def index(i, scalars, mask):
            head = scalars[first] + moving(i, scalars)
            return (0, head + scalars[OWN] if own_column else head)

        return pl.BlockSpec((height, HD), index)

    def two_columns(height, own_column):
        def index(i, scalars, mask):
            pair = jnp.minimum(moving(i, scalars), 1)
            return (0, pair + scalars[OWN] // 2 if own_column else pair)

        return pl.BlockSpec((height, 2 * HD), index)

    def payload_column(payload):
        last = payload.shape[1] // HD - 1

        def index(i, scalars, mask):
            return (0, jnp.minimum(moving(i, scalars), last))

        return pl.BlockSpec((payload.shape[0], HD), index)

    in_specs = [
        column(rows, True),
        column(half, True),
        column(half, True),
        column(rows, False),
        column(patch, True),
        column(1, True),
    ]
    arrays = [queries, keys, values, received, weight, gain]
    extra = 0
    if more:
        extra = 6
        in_specs += [
            two_columns(rows, True),
            two_columns(half, True),
            two_columns(half, True),
            two_columns(rows, False),
            two_columns(patch, True),
            two_columns(1, True),
        ]
        arrays += [queries, keys, values, received, weight, gain]
    in_specs += [payload_column(payload) for payload in payloads]
    arrays += payloads
    fresh = sums is None
    sums_shape = (SLOTS, patch + 2 * STAT_ROWS, rows)
    aliases = {}
    if not fresh:
        aliases = {2 + len(arrays): 0, 3 + len(arrays): 1}
        in_specs += [pl.BlockSpec(memory_space=pl.ANY)] * 2
        arrays += sums
    pairs = max(
        count * sum(len(task[3]) for task in tasks) for count, tasks in variants.values()
    )
    span_count = math.isqrt(mask.shape[0])
    return pl.pallas_call(
        functools.partial(attend_kernel, variants, extra, span_count, fresh),
        name=name,
        out_shape=[pltpu.HBM((SLOTS, sums_shape[1] // 2, rows), jnp.float32)] * 2,
        input_output_aliases=aliases,
        grid_spec=pltpu.PrefetchScalarGridSpec(
            num_scalar_prefetch=2,
            grid=(steps,),
            in_specs=in_specs,
            out_specs=[pl.BlockSpec(memory_space=pl.ANY)] * 2,
            scratch_shapes=[
                pltpu.VMEM((SLOTS, 2 * patch + 16, rows), jnp.float32),
                pltpu.VMEM((SLOTS, rows, HD), jnp.float32),
                pltpu.VMEM(sums_shape, jnp.float32),
                pltpu.SemaphoreType.DMA((4,)),
            ],
        ),
        compiler_params=pltpu.CompilerParams(vmem_limit_bytes=GRANT),
        cost_estimate=pl.CostEstimate(
            flops=cost * pairs * 4 * rows * rows * HD,
            bytes_accessed=steps * HD * 2 * sum(spec.block_shape[0] for spec in in_specs[:4]),
            transcendentals=cost * pairs * rows * rows,
        ),
    )(scalars, mask, *arrays)


def token_sums(
    scalars, queries, keys, values, span_mask, head_gain, patch_weight, prepare
):
    rows = queries.shape[0]
    half = rows // 2
    heads = NEAR_HEADS + MIDDLE_HEADS + FAR_HEADS
    in_place = lambda array: pltpu.with_memory_space_constraint(array, pltpu.HBM)
    queries, keys, values = (in_place(array) for array in (queries, keys, values))

    def send(value, *pairs):
        return in_place(lax.ppermute(value, "span", list(pairs)))

    def tokens(entry, shift, count):
        return [(0, 0, rows, (OWN, entry) if entry else (OWN,), shift, count)]

    def pairs_of(entry, shift, count):
        entries = (entry,) if entry else ()
        return [
            piece
            for part in (1, 2)
            for piece in (
                (part, 0, half, (OWN,) + entries, shift, count),
                (3, (part - 1) * half, half, entries, shift, count),
            )
        ]

    handed = pack_handed(keys, values, heads)
    received = lax.ppermute(handed, "slab", SWAP)
    up, down = message(
        scalars,
        [
            pairs_of(UP, 0, NEAR_HEADS),
            tokens(DOWN, 0, MIDDLE_HEADS) + pairs_of(DOWN, 0, MIDDLE_HEADS),
        ],
        (queries, keys, values, received),
        "pack_first",
    )
    source, _ = lax.optimization_barrier((received, down))
    up = send(up, (0, 1), (1, 2))
    down = send(down, (1, 0), (2, 1), (3, 2))
    up_two, two, far_all, far_pair = message(
        scalars,
        [
            pairs_of(None, MIDDLE, MIDDLE_HEADS),
            tokens(None, 0, NEAR_HEADS) + pairs_of(None, 0, NEAR_HEADS),
            tokens(None, FAR, FAR_HEADS) + pairs_of(None, FAR, FAR_HEADS),
            pairs_of(None, FAR, FAR_HEADS),
        ],
        (queries, keys, values, source),
        "pack_second",
    )
    anchor = two
    up_two = send(up_two, (0, 2))
    two = send(two, (3, 1))
    far_next = send(far_all, (2, 3), (1, 0))
    far_pair, prepared = lax.optimization_barrier((far_pair, prepare(anchor)))
    far_two = send(far_pair, (1, 3))
    far_three = send(far_pair, (0, 3))

    span_mask, head_gain, patch_weight, _ = lax.optimization_barrier(
        (span_mask, head_gain, patch_weight, anchor)
    )
    mask = span_mask.reshape(-1)
    weight = patch_weight.T
    own = (queries, keys, values, received, weight, head_gain[None, :])
    run = functools.partial(attend, own=own, scalars=scalars, mask=mask)

    here, back_one, on_one = OWN_TOKENS, Tokens(None, (0,)), Tokens(1, (1,))
    back_two = Tokens(None, (2,))
    sums = run(
        MIDDLE_HEADS,
        MAIN,
        MAIN_CAP,
        sums=None,
        payloads=[up, down, up_two],
        variants={
            0: (4, [(here, 0, 0, [(here, 0)]), (on_one, 1, 1, [(here, 0), (on_one, 1)])]),
            1: (
                4,
                [
                    (on_one, 1, 2, [(back_one, 0), (here, 1), (on_one, 2)]),
                    (here, 0, 1, [(back_one, 0), (here, 1)]),
                ],
            ),
            2: (
                4,
                [
                    (on_one, 1, 3, [(back_two, 0), (back_one, 1), (here, 2), (on_one, 3)]),
                    (here, 0, 2, [(back_two, 0), (back_one, 1), (here, 2)]),
                ],
            ),
        },
        more=False,
        name="main_heads",
    )
    on_two, beside = Tokens(2, (2,)), Tokens(3, (3,))
    two_back, three_back = Tokens(None, (4,)), Tokens(None, (5,))
    extras = [Tokens(None, (), lane) for lane in range(2)]
    sums, prepared = lax.optimization_barrier((sums, prepared))
    sums = run(
        NEAR_HEADS,
        FINAL,
        FINAL_CAP,
        sums=sums,
        payloads=[up, down, two, far_next, far_two, far_three],
        variants={
            0: (
                FAR_HEADS,
                [(here, 0, 0, [(here, 0)]), (beside, 1, 1, [(here, 0), (beside, 1)])]
                + [(head, 0, 0, [(head, 0)]) for head in extras],
            ),
            1: (
                NEAR_HEADS,
                [(on_two, 2, 3, [(back_one, 0), (here, 1), (on_one, 2), (on_two, 3)])],
            ),
            3: (
                FAR_HEADS,
                [
                    (here, 0, 3, [(three_back, 0), (two_back, 1), (beside, 2), (here, 3)]),
                    (beside, 2, 2, [(three_back, 0), (two_back, 1), (beside, 2)]),
                ],
            ),
        },
        more=True,
        name="final_heads",
        cost=4,
    )
    return sums, prepared


def noise_window(grid, constants):
    height, breadth, _ = grid.shape
    slab = lax.axis_index("slab")
    edge = jnp.where(slab == 0, grid[:, breadth - 1], grid[:, 0])
    edge = lax.ppermute(edge, "slab", SWAP)[:, None]
    grid = jnp.concatenate(
        [
            jnp.where(slab == 1, edge, 0.0),
            grid,
            jnp.where(slab == 0, edge, 0.0),
            jnp.zeros((height, WINDOW - breadth - 2, grid.shape[2]), grid.dtype),
        ],
        axis=1,
    )
    head = lax.axis_index("head")
    edge = jnp.where(head == 0, grid[height - 1], grid[0])
    count = constants.shape[1]
    extra = jnp.pad(constants, ((0, 8 - constants.shape[0]), (0, HD - count)))
    edge = jnp.pad(edge, ((0, 0), (0, HD - edge.shape[1])))
    sent = lax.ppermute(jnp.concatenate([edge, extra], axis=0), "head", SWAP)
    edge = sent[None, :WINDOW, : grid.shape[2]]
    constants = constants + sent[WINDOW : WINDOW + constants.shape[0], :count]
    grid = jnp.concatenate(
        [jnp.where(head == 1, edge, 0.0), grid, jnp.where(head == 0, edge, 0.0)], axis=0
    )
    return grid.reshape((height + 2) * WINDOW, grid.shape[2]), constants.T


def cell_selector(height, breadth):
    cell = lax.broadcasted_iota(jnp.int32, ((height + 2) * WINDOW, 4 * TROWS * TCOLS), 0)
    column = lax.broadcasted_iota(jnp.int32, cell.shape, 1)
    y = lax.axis_index("head") * height + cell // WINDOW - 1
    x = lax.axis_index("slab") * breadth + cell % WINDOW - 1
    inside = (y >= 0) & (y < 2 * TROWS) & (x >= 0) & (x < 2 * TCOLS)
    inside = inside & (cell % WINDOW < breadth + 2)
    target = ((y % 2) * 2 + x % 2) * (TROWS * TCOLS) + (y // 2) * TCOLS + x // 2
    return (inside & (column == target)).astype(jnp.bfloat16)


def band_kernel(weight, band):
    outputs = weight.shape[1]
    band[...] = jnp.zeros_like(band)
    for row_tap in range(3):
        for col_tap in range(3):
            for frame_tap in range(3):
                start = ((3 * frame_tap + row_tap) * 3 + col_tap) * LAT_CH
                block = weight[start : start + LAT_CH]
                for frame in range(FRAMES_SPAN):
                    at = (col_tap * (FRAMES_SPAN + 2) + frame + frame_tap) * LAT_CH
                    band[
                        row_tap, at : at + LAT_CH, frame * outputs : (frame + 1) * outputs
                    ] = block


def banded_weight(conv_weight):
    shape = (3, 3 * (FRAMES_SPAN + 2) * LAT_CH, FRAMES_SPAN * conv_weight.shape[1])
    return pl.pallas_call(
        band_kernel,
        name="band",
        out_shape=jax.ShapeDtypeStruct(shape, conv_weight.dtype),
        in_specs=[pl.BlockSpec(memory_space=pltpu.VMEM)],
        out_specs=pl.BlockSpec(memory_space=pltpu.VMEM),
        compiler_params=pltpu.CompilerParams(vmem_limit_bytes=GRANT),
        cost_estimate=pl.CostEstimate(
            flops=0, bytes_accessed=2 * math.prod(shape), transcendentals=0
        ),
    )(conv_weight)


def finish_kernel(
    scalars, mine, other, noise, before, selector, band, bias, constants, clean, decoded, cells
):
    frames, height, breadth, channels = clean.shape
    patch = constants.shape[0]
    first = scalars[SLAB] == 0
    sums = jnp.concatenate(
        [jnp.where(first, mine[...], other[...]), jnp.where(first, other[...], mine[...])], axis=0
    )
    feature_width = HEADS * HD
    row_mean = sums[patch : patch + 1] / feature_width
    spread = sums[patch + STAT_ROWS : patch + STAT_ROWS + 1] / feature_width - row_mean * row_mean
    velocity = (
        lax.rsqrt(spread + norm_eps) * (sums[:patch] - constants[:, 0:1] * row_mean)
        + constants[:, 1:2]
    )
    tokens = TROWS * TCOLS
    lane = lax.broadcasted_iota(jnp.int32, velocity.shape, 1)
    velocity = jnp.where((lane >= 2 * tokens) | (scalars[PLACE] > 0), velocity, 0.0)
    columns = jnp.concatenate(
        [
            jnp.concatenate(
                [
                    velocity[
                        part * channels : (part + 1) * channels,
                        frame * tokens : (frame + 1) * tokens,
                    ]
                    for part in range(4)
                ],
                axis=1,
            )
            for frame in range(frames + 2)
        ],
        axis=0,
    )
    high = columns.astype(jnp.bfloat16)
    low = (columns - high.astype(jnp.float32)).astype(jnp.bfloat16)
    chosen = sum(
        lax.dot_general(
            selector[...], part, (((1,), (1,)), ((), ())), preferred_element_type=jnp.float32
        )
        for part in (high, low)
    )
    count = (height + 2) * WINDOW
    cells[:count] = (
        jnp.concatenate([before[...], noise[...]], axis=1) - noise_level * chosen
    )
    cells[count:] = jnp.zeros_like(cells[count:])
    for frame in range(frames):
        lanes = slice((frame + 2) * channels, (frame + 3) * channels)
        for y in range(height):
            start = (y + 1) * WINDOW + 1
            clean[frame, y] = cells[start : start + breadth, lanes]
    shifted = jnp.concatenate(
        [cells[tap : tap + count] for tap in range(3)], axis=1
    ).astype(jnp.bfloat16)
    total = jnp.broadcast_to(bias[...], (height * breadth, bias.shape[1]))
    for tap in range(3):
        block = jnp.concatenate(
            [
                shifted[(y + tap) * WINDOW : (y + tap) * WINDOW + breadth]
                for y in range(height)
            ],
            axis=0,
        )
        total = total + jnp.dot(block, band[tap], preferred_element_type=jnp.float32)
    outputs = decoded.shape[3]
    total = total.astype(decoded.dtype)
    for frame in range(frames):
        decoded[frame] = total[:, frame * outputs : (frame + 1) * outputs].reshape(
            height, breadth, outputs
        )


def finish(
    scalars, mine, other, noise, before, selector, band, bias, constants, shape, outputs
):
    whole = pl.BlockSpec(memory_space=pltpu.VMEM)
    frames, height, breadth, channels = shape
    rows = (height + 2) * WINDOW
    return pl.pallas_call(
        finish_kernel,
        name="finish",
        out_shape=(
            jax.ShapeDtypeStruct(shape, jnp.float32),
            jax.ShapeDtypeStruct((frames, height, breadth, outputs), jnp.bfloat16),
        ),
        in_specs=[pl.BlockSpec(memory_space=pltpu.SMEM)] + [whole] * 8,
        out_specs=(whole, whole),
        scratch_shapes=[pltpu.VMEM((rows + 8, (frames + 2) * channels), jnp.float32)],
        compiler_params=pltpu.CompilerParams(vmem_limit_bytes=GRANT),
    )(scalars, mine, other, noise, before, selector, band, bias, constants)


def per_device(
    queries,
    keys,
    values,
    span_mask,
    head_gain,
    head_shift,
    patch_weight,
    noisy_latent,
    conv_weight,
    conv_bias,
):
    heads_dev = queries.shape[1] // HD
    if not plan_fits(
        heads_dev, lax.axis_size("span"), lax.axis_size("slab"), lax.axis_size("head")
    ):
        return gathered_plan(
            queries,
            keys,
            values,
            span_mask,
            head_gain,
            head_shift,
            patch_weight,
            noisy_latent,
            conv_weight,
            conv_bias,
        )
    place = lax.axis_index("span")
    slab = lax.axis_index("slab")
    scalars = scalar_operand(heads_dev // lax.axis_size("slab"))
    def prepare(anchor):
        noise, weight, gain, shift, taps, bias, _ = lax.optimization_barrier(
            (noisy_latent, patch_weight, head_gain, head_shift, conv_weight, conv_bias, anchor)
        )
        _, height, breadth, _ = noise.shape
        noise = noise.transpose(1, 2, 0, 3).reshape(height, breadth, -1)
        wide_weight = weight.T.astype(jnp.float32)
        constants = jnp.stack(
            [
                jnp.sum(wide_weight * gain[None, :], axis=1),
                jnp.sum(wide_weight * shift[None, :], axis=1),
            ]
        )
        window, constants = noise_window(noise, constants)
        return (
            window,
            window[:, -2 * LAT_CH :].reshape(16, -1),
            constants,
            cell_selector(height, breadth),
            banded_weight(taps),
            jnp.tile(bias, FRAMES_SPAN)[None, :],
        )

    (mine, theirs), (noise, ahead, constants, selector, band, bias) = token_sums(
        scalars,
        queries,
        keys,
        values,
        span_mask,
        head_gain,
        patch_weight,
        prepare,
    )
    mine = mine + lax.ppermute(theirs, "slab", SWAP)
    own, after, third = mine[0], mine[1], mine[2]
    skip = TROWS * TCOLS
    from_one = lax.ppermute(
        jnp.concatenate([jnp.concatenate([own[:, skip:], after], axis=1), ahead], axis=0),
        "span",
        [(0, 1), (1, 2), (2, 3)],
    )
    before = from_one[own.shape[0] :].reshape(-1, 2 * LAT_CH)
    from_one = from_one[: own.shape[0]]
    to_current = lax.ppermute(third, "span", [(1, 3), (3, 2)])
    to_before = lax.ppermute(after[:, skip:], "span", [(0, 2), (1, 3)])
    kept = jnp.concatenate([jnp.where(place == 3, third[:, skip:], 0.0), own], axis=1)
    total = kept + from_one + jnp.concatenate([to_before, to_current], axis=1)
    total = total + lax.ppermute(total, "head", SWAP)
    other = lax.ppermute(total, "slab", SWAP)
    return finish(
        scalars,
        total,
        other,
        noise,
        before,
        selector,
        band,
        bias,
        constants,
        noisy_latent.shape,
        conv_weight.shape[1],
    )


def solution(mesh):
    placed = (
        P(("groups", "span"), "head"),
        P(("groups", "span", "slab"), "head"),
        P(("groups", "span", "slab"), "head"),
        P("groups", None),
        P("head"),
        P("head"),
        P("head", None),
        P(("groups", "span"), "head", "slab", None),
        P(),
        P(),
    )
    return jax.shard_map(
        per_device,
        mesh=mesh,
        in_specs=placed,
        out_specs=(
            P(("groups", "span"), "head", "slab", None),
            P(("groups", "span"), "head", "slab", None),
        ),
        check_vma=False,
    )
```

```python
import functools
import math
import typing

import jax
import jax.numpy as jnp
import numpy as np
from jax import lax
from jax.experimental import pallas as pl
from jax.experimental.pallas import tpu as pltpu
from jax.sharding import PartitionSpec as P

HEADS = 40
HD = 128
LAT_CH = 16
FRAMES_SPAN = 3
TROWS = 8
TCOLS = 16


neg_big = -1e30
noise_level = 0.75
norm_eps = 1e-06


def with_halo(cells, sides, width):
    for axis, dim in sides:
        count = lax.axis_size(axis)
        ends = count - 1
        head = lax.slice_in_dim(cells, 0, width, axis=dim)
        tail = lax.slice_in_dim(cells, cells.shape[dim] - width, cells.shape[dim], axis=dim)
        cells = jnp.concatenate(
            [
                lax.ppermute(tail, axis, [(i, (i + 1) % count) for i in range(ends)]),
                cells,
                lax.ppermute(head, axis, [((i + 1) % count, i) for i in range(ends)]),
            ],
            axis=dim,
        )
    return cells


def from_behind(value, axis, by):
    size = lax.axis_size(axis)
    pairs = [(i, i + by) for i in range(size) if 0 <= i + by < size]
    return lax.ppermute(value, axis, pairs)


def block_length(total_rows):
    block_size = total_rows
    while block_size > 768 and block_size % 2 == 0:
        block_size = block_size // 2
    return block_size


def fold_keys(partial_state, key_value, query_block, mask_row, rows_span):
    keys_piece, values_piece = key_value
    heads_dev = query_block.shape[1]
    piece_rows = keys_piece.shape[0]
    length = block_length(piece_rows)
    span_count = mask_row.shape[0]
    score_scale = 1.0 / math.sqrt(HD)
    span_ids = jnp.arange(span_count, dtype=jnp.int32)

    def one_block(carry_state, block_index):
        running_max, running_sum, weighted = carry_state
        offset = block_index * length
        key_block = lax.dynamic_slice_in_dim(keys_piece, offset, length, 0).reshape(
            length, heads_dev, HD
        )
        value_block = lax.dynamic_slice_in_dim(values_piece, offset, length, 0).reshape(
            length, heads_dev, HD
        )
        key_span = (offset + jnp.arange(length, dtype=jnp.int32)) // rows_span
        allowed = (
            jnp.sum(jnp.where(key_span[:, None] == span_ids[None, :], mask_row[None, :], 0), axis=1)
            > 0
        )
        scores = (
            jnp.einsum("qhd,khd->hqk", query_block, key_block, preferred_element_type=jnp.float32)
            * score_scale
        )
        scores = jnp.where(allowed[None, None, :], scores, neg_big)
        new_max = jnp.maximum(running_max, jnp.max(scores, axis=2))
        weights = jnp.where(allowed[None, None, :], jnp.exp(scores - new_max[:, :, None]), 0.0)
        factor = jnp.exp(running_max - new_max)
        running_sum = running_sum * factor + jnp.sum(weights, axis=2)
        weighted = weighted * factor.T[:, :, None] + jnp.einsum(
            "hqk,khd->qhd",
            weights.astype(jnp.bfloat16),
            value_block,
            preferred_element_type=jnp.float32,
        )
        return ((new_max, running_sum, weighted), None)

    result, unused = lax.scan(
        one_block, partial_state, jnp.arange(piece_rows // length, dtype=jnp.int32)
    )
    return result


def gathered_plan(
    queries,
    keys,
    values,
    span_mask,
    head_gain,
    head_shift,
    patch_weight,
    noisy_latent,
    conv_weight,
    conv_bias,
):
    heads_dev = queries.shape[1] // HD
    slab_count = lax.axis_size("slab")
    col_dev = TCOLS // slab_count
    slab_place = lax.axis_index("slab")
    span_place = lax.axis_index("span")
    mask_row = lax.dynamic_slice_in_dim(span_mask, span_place, 1, 0)[0]
    token_grid = queries.reshape(FRAMES_SPAN, TROWS, TCOLS, queries.shape[-1])
    picked = lax.dynamic_slice_in_dim(token_grid, slab_place * col_dev, col_dev, 2)
    own_queries = picked.reshape(FRAMES_SPAN * TROWS * col_dev, queries.shape[-1]).reshape(
        -1, heads_dev, HD
    )
    query_rows = own_queries.shape[0]
    rows_span = keys.shape[0] * slab_count
    running_max, running_sum, weighted = fold_keys(
        (
            jnp.full((heads_dev, query_rows), neg_big, jnp.float32),
            jnp.zeros((heads_dev, query_rows), jnp.float32),
            jnp.zeros((query_rows, heads_dev, HD), jnp.float32),
        ),
        (
            lax.all_gather(keys, ("span", "slab"), axis=0, tiled=True),
            lax.all_gather(values, ("span", "slab"), axis=0, tiled=True),
        ),
        own_queries,
        mask_row,
        rows_span,
    )
    attended = (
        (weighted / running_sum.T[:, :, None])
        .astype(jnp.bfloat16)
        .reshape(query_rows, heads_dev * HD)
    )
    feature_width = HEADS * HD
    values32 = attended.astype(jnp.float32)
    row_total = jnp.sum(values32, axis=1)
    row_squares = jnp.sum(values32 * values32, axis=1)
    row_total, row_squares = lax.psum((row_total, row_squares), "head")
    row_mean = row_total / feature_width
    spread = row_squares / feature_width - row_mean * row_mean
    normed = (
        (values32 - row_mean[:, None]) * lax.rsqrt(spread + norm_eps)[:, None] * head_gain[None, :]
        + head_shift[None, :]
    ).astype(jnp.bfloat16)
    normed_grid = normed.reshape(FRAMES_SPAN, TROWS, col_dev, normed.shape[-1])
    own_rows = TROWS // lax.axis_size("head")
    picked = normed_grid
    product = jnp.dot(
        picked.reshape(-1, picked.shape[-1]), patch_weight, preferred_element_type=jnp.float32
    )
    velocity = lax.psum_scatter(
        product.reshape(
            FRAMES_SPAN, own_rows * lax.axis_size("head"), col_dev * patch_weight.shape[1]
        )
        .transpose(1, 0, 2)
        .reshape(own_rows * lax.axis_size("head"), -1)
        .astype(jnp.bfloat16),
        "head",
        scatter_dimension=0,
        tiled=True,
    ).astype(jnp.float32)
    rows_dev = velocity.shape[0]
    patch_cells = (
        velocity.reshape(rows_dev, FRAMES_SPAN, col_dev, 2, 2, LAT_CH)
        .transpose(1, 0, 3, 2, 4, 5)
        .reshape(FRAMES_SPAN, 2 * rows_dev, 2 * col_dev, LAT_CH)
    )
    clean_latent = noisy_latent - noise_level * patch_cells
    latent_input = clean_latent.astype(jnp.bfloat16)
    framed = with_halo(latent_input, (("head", 1), ("slab", 2)), 1)
    earlier = from_behind(framed[FRAMES_SPAN - 2 :], "span", 1)
    stacked = jnp.concatenate([earlier, framed], axis=0)
    height = clean_latent.shape[1]
    breadth = clean_latent.shape[2]
    columns = jnp.concatenate(
        [
            stacked[
                frame_tap : frame_tap + FRAMES_SPAN,
                row_tap : row_tap + height,
                col_tap : col_tap + breadth,
                :,
            ]
            for frame_tap in range(3)
            for row_tap in range(3)
            for col_tap in range(3)
        ],
        axis=-1,
    )
    decoded = (
        jnp.dot(
            columns.reshape(FRAMES_SPAN * height * breadth, 27 * LAT_CH),
            conv_weight,
            preferred_element_type=jnp.float32,
        )
        + conv_bias[None, :]
    )
    decoded = decoded.astype(jnp.bfloat16).reshape(
        FRAMES_SPAN, height, breadth, conv_weight.shape[1]
    )
    return (clean_latent, decoded)


NEAR_HEADS = 4
MIDDLE_HEADS = 4
FAR_HEADS = 2
MIDDLE = NEAR_HEADS
FAR = NEAR_HEADS + MIDDLE_HEADS
STAT_ROWS = 8
SLOTS = 3
QUERY_ROWS = 192
SWAP = [(0, 1), (1, 0)]
WINDOW = 32
GRANT = 20 << 20

OWN, OTHER, DOWN, UP, MAIN, MAIN_CAP, FINAL, FINAL_CAP, PLACE, SLAB = range(10)


def plan_fits(heads_dev, span_count, slab_count, head_count):
    return (
        span_count == 4
        and slab_count == 2
        and head_count == 2
        and heads_dev == slab_count * (NEAR_HEADS + MIDDLE_HEADS + FAR_HEADS)
    )


def scalar_operand(heads):
    by_place = np.zeros((4, 12), np.int32)
    by_place[:, OTHER] = heads
    by_place[:, DOWN] = [MIDDLE, MIDDLE, 0, MIDDLE]
    by_place[:, UP] = [0, MIDDLE, 0, 0]
    by_place[:, MAIN] = [MIDDLE, 0, MIDDLE, 0]
    by_place[:, MAIN_CAP] = [3, 3, 3, 0]
    by_place[:, FINAL] = [FAR, 0, 0, FAR]
    by_place[:, FINAL_CAP] = [1, 3, 0, 1]
    by_place[:, PLACE] = range(4)
    by_slab = np.zeros(12, np.int32)
    by_slab[[OWN, OTHER, SLAB]] = heads, -heads, 1
    row = lax.dynamic_slice_in_dim(jnp.array(by_place), lax.axis_index("span"), 1, 0)[0]
    return row + lax.axis_index("slab") * jnp.array(by_slab)


def pack_kernel(inputs, messages, copies, scalars, *refs):
    ins, outs, arrive = refs[:inputs], refs[inputs:-1], refs[-1]
    arriving = []
    for number, (source, row, rows, entries, shift, target, at, heads) in enumerate(copies):
        head = shift
        for entry in entries:
            head = head + scalars[entry]
        column = pl.multiple_of(head * HD, HD)
        copy = pltpu.make_async_copy(
            ins[source].at[pl.ds(row, rows), pl.ds(column, heads * HD)],
            outs[target].at[pl.ds(at, rows), :],
            arrive.at[number],
        )
        copy.start()
        arriving.append(copy)
    for copy in arriving:
        copy.wait()


def pack(scalars, arrays, shapes, copies, name):
    moved = sum(2 * 2 * rows * heads * HD for _, _, rows, _, _, _, _, heads in copies)
    return pl.pallas_call(
        functools.partial(pack_kernel, len(arrays), len(shapes), copies),
        name=name,
        out_shape=[jax.ShapeDtypeStruct(shape, jnp.bfloat16) for shape in shapes],
        in_specs=[pl.BlockSpec(memory_space=pltpu.SMEM)]
        + [pl.BlockSpec(memory_space=pl.ANY)] * len(arrays),
        out_specs=[pl.BlockSpec(memory_space=pltpu.VMEM)] * len(shapes),
        scratch_shapes=[pltpu.SemaphoreType.DMA((len(copies),))],
        compiler_params=pltpu.CompilerParams(vmem_limit_bytes=GRANT),
        cost_estimate=pl.CostEstimate(flops=0, bytes_accessed=moved, transcendentals=0),
    )(scalars, *arrays)


def hand_kernel(heads, keys, values, out, arrive):
    column = pl.multiple_of((1 - lax.axis_index("slab")) * heads * HD, heads * HD)
    half = keys.shape[0]
    copies = []
    for number, source in enumerate((keys, values)):
        copy = pltpu.make_async_copy(
            source.at[:, pl.ds(column, heads * HD)],
            out.at[pl.ds(number * half, half), :],
            arrive.at[number],
        )
        copy.start()
        copies.append(copy)
    for copy in copies:
        copy.wait()


def pack_handed(keys, values, heads):
    shape = (2 * keys.shape[0], heads * HD)
    return pl.pallas_call(
        functools.partial(hand_kernel, heads),
        name="pack_handed",
        out_shape=jax.ShapeDtypeStruct(shape, keys.dtype),
        in_specs=[pl.BlockSpec(memory_space=pl.ANY)] * 2,
        out_specs=pl.BlockSpec(memory_space=pltpu.VMEM),
        scratch_shapes=[pltpu.SemaphoreType.DMA((2,))],
        compiler_params=pltpu.CompilerParams(vmem_limit_bytes=GRANT),
        cost_estimate=pl.CostEstimate(
            flops=0, bytes_accessed=4 * math.prod(shape), transcendentals=0
        ),
    )(keys, values)


def message(scalars, pieces, arrays, name):
    copies, shapes = [], []
    for target, parts in enumerate(pieces):
        at = 0
        for source, row, rows, entries, shift, heads in parts:
            copies.append((source, row, rows, entries, shift, target, at, heads))
            at += rows
        shapes.append((at, parts[0][5] * HD))
    return pack(scalars, arrays, shapes, copies, name)


class Tokens(typing.NamedTuple):
    query: int | None = None
    pairs: tuple = ()
    extra: int | None = None


OWN_TOKENS = Tokens()


def attend_kernel(variants, extra, span_count, fresh, scalars, mask, *refs):
    query_own, key_own, value_own, received, weight, gain = refs[:6]
    more = refs[6 : 6 + extra]
    mine_out, theirs_out, folded, squares, carried, moved = refs[-6:]
    payloads = refs[6 + extra : -6] if fresh else refs[6 + extra : -8]
    rows = query_own.shape[0]
    half = rows // 2
    step = pl.program_id(0)
    to_exp2 = math.log2(math.e) / math.sqrt(HD)
    active = functools.reduce(
        lambda a, b: a | b, [scalars[PLACE] == place for place in variants]
    )

    last_step = step == pl.num_programs(0) - 1
    part = carried.shape[1] // 2
    halves = [
        carried.at[:, pl.ds(pl.multiple_of(number * part, part), part)]
        for number in (scalars[SLAB], 1 - scalars[SLAB])
    ]
    fetches = (
        []
        if fresh
        else [
            pltpu.make_async_copy(refs[number - 8], halves[number], moved.at[number])
            for number in range(2)
        ]
    )

    @pl.when((step == 0) & active)
    def _():
        folded[...] = jnp.zeros_like(folded)
        squares[...] = jnp.zeros_like(squares)
        for fetch in fetches:
            fetch.start()

    def query_of(source):
        if source is OWN_TOKENS:
            return query_own[...]
        if source.extra is not None:
            return more[0][:, source.extra * HD : (source.extra + 1) * HD]
        return payloads[source.query][:rows]

    def pair_of(source):
        if source is OWN_TOKENS:
            parts = (key_own[...], received[:half], value_own[...], received[half:])
        elif source.extra is not None:
            lanes = slice(source.extra * HD, (source.extra + 1) * HD)
            parts = (more[1][:, lanes], more[3][:half, lanes], more[2][:, lanes], more[3][half:, lanes])
        elif len(source.pairs) == 2:
            one, two = (payloads[number] for number in source.pairs)
            parts = (one[:half], two[:half], one[half:], two[half:])
        else:
            payload = payloads[source.pairs[0]]
            start = payload.shape[0] - 2 * rows
            return payload[start : start + rows], payload[start + rows :]
        return jnp.concatenate(parts[:2], axis=0), jnp.concatenate(parts[2:], axis=0)

    def projector(extra_head):
        if extra_head is None:
            scaled = weight[...].astype(jnp.float32) * gain[...]
        else:
            lanes = slice(extra_head * HD, (extra_head + 1) * HD)
            scaled = more[4][:, lanes].astype(jnp.float32) * more[5][:, lanes]
        high = scaled.astype(jnp.bfloat16)
        low = (scaled - high.astype(jnp.float32)).astype(jnp.bfloat16)
        return jnp.concatenate([high, low, jnp.ones((16, HD), jnp.bfloat16)], axis=0)

    def one_query(source, slot, query_span, key_sources):
        query = query_of(source)
        pairs = [pair_of(key_source) for key_source, _ in key_sources]
        open_to = [
            None if key_span == query_span else mask[query_span * span_count + key_span] > 0
            for _, key_span in key_sources
        ]
        keys_in = jnp.concatenate([pair[0] for pair in pairs], axis=0)
        ones_block = jnp.ones((rows, HD), jnp.bfloat16)
        values_in = jnp.concatenate(
            [jnp.concatenate([pair[1], ones_block], axis=1) for pair in pairs], axis=0
        )
        pieces = []
        for row in range(0, rows, QUERY_ROWS):
            score = lax.dot_general(
                query[row : row + QUERY_ROWS],
                keys_in,
                (((1,), (1,)), ((), ())),
                preferred_element_type=jnp.float32,
            )
            best = None
            for number, is_open in enumerate(open_to):
                start = number * rows
                block = score[:, start : start + HD]
                for lane in range(HD, rows, HD):
                    block = jnp.maximum(block, score[:, start + lane : start + lane + HD])
                if is_open is not None:
                    block = jnp.where(is_open, block, neg_big)
                best = block if best is None else jnp.maximum(best, block)
            top = jnp.max(best, axis=1, keepdims=True)
            weights = []
            for number, is_open in enumerate(open_to):
                start = number * rows
                shift = top if is_open is None else jnp.where(is_open, top, -neg_big)
                weights.append(
                    jnp.exp2((score[:, start : start + rows] - shift) * to_exp2).astype(jnp.bfloat16)
                )
            both = jnp.dot(
                jnp.concatenate(weights, axis=1), values_in, preferred_element_type=jnp.float32
            )
            pieces.append((both[:, :HD] / both[:, HD:]).astype(jnp.bfloat16))
        attended = jnp.concatenate(pieces, axis=0)
        folded[slot] += lax.dot_general(
            projector(source.extra),
            attended,
            (((1,), (1,)), ((), ())),
            preferred_element_type=jnp.float32,
        )
        wide = attended.astype(jnp.float32)
        squares[slot] += wide * wide

    for place, (steps, tasks) in variants.items():

        @pl.when((scalars[PLACE] == place) & (step < steps))
        def _():
            for task in tasks:
                one_query(*task)

    def store():
        copies = [
            pltpu.make_async_copy(halves[number], out, moved.at[2 + number])
            for number, out in enumerate((mine_out, theirs_out))
        ]
        for copy in copies:
            copy.start()
        for copy in copies:
            copy.wait()

    if fresh:

        @pl.when(last_step & jnp.logical_not(active))
        def _():
            carried[...] = jnp.zeros_like(carried)
            store()

    @pl.when(last_step & active)
    def _():
        ones_rows = jnp.ones((STAT_ROWS, HD), jnp.bfloat16)
        patch = weight.shape[0]
        for fetch in fetches:
            fetch.wait()
        if fresh:
            carried[...] = jnp.zeros_like(carried)

        def finish_slot(slot):
            left = squares[slot]
            total = jnp.zeros((STAT_ROWS, rows), jnp.float32)
            for _ in range(3):
                piece = left.astype(jnp.bfloat16)
                left = left - piece.astype(jnp.float32)
                total = total + lax.dot_general(
                    ones_rows, piece, (((1,), (1,)), ((), ())), preferred_element_type=jnp.float32
                )
            done = folded[slot]
            carried[slot] += jnp.concatenate(
                [
                    done[:patch] + done[patch : 2 * patch],
                    done[2 * patch : 2 * patch + STAT_ROWS],
                    total,
                ],
                axis=0,
            )

        for place, (_, tasks) in variants.items():

            @pl.when(scalars[PLACE] == place)
            def _():
                for slot in sorted({task[1] for task in tasks}):
                    finish_slot(slot)

        store()


def attend(steps, first, cap, own, scalars, mask, sums, payloads, variants, more, name, cost=1):
    queries, keys, values, received, weight, gain = own
    rows = queries.shape[0]
    half = rows // 2
    patch = weight.shape[0]

    def moving(i, scalars):
        return jnp.minimum(i, scalars[cap])

    def column(height, own_column):
        def index(i, scalars, mask):
            head = scalars[first] + moving(i, scalars)
            return (0, head + scalars[OWN] if own_column else head)

        return pl.BlockSpec((height, HD), index)

    def two_columns(height, own_column):
        def index(i, scalars, mask):
            pair = jnp.minimum(moving(i, scalars), 1)
            return (0, pair + scalars[OWN] // 2 if own_column else pair)

        return pl.BlockSpec((height, 2 * HD), index)

    def payload_column(payload):
        last = payload.shape[1] // HD - 1

        def index(i, scalars, mask):
            return (0, jnp.minimum(moving(i, scalars), last))

        return pl.BlockSpec((payload.shape[0], HD), index)

    in_specs = [
        column(rows, True),
        column(half, True),
        column(half, True),
        column(rows, False),
        column(patch, True),
        column(1, True),
    ]
    arrays = [queries, keys, values, received, weight, gain]
    extra = 0
    if more:
        extra = 6
        in_specs += [
            two_columns(rows, True),
            two_columns(half, True),
            two_columns(half, True),
            two_columns(rows, False),
            two_columns(patch, True),
            two_columns(1, True),
        ]
        arrays += [queries, keys, values, received, weight, gain]
    in_specs += [payload_column(payload) for payload in payloads]
    arrays += payloads
    fresh = sums is None
    sums_shape = (SLOTS, patch + 2 * STAT_ROWS, rows)
    aliases = {}
    if not fresh:
        aliases = {2 + len(arrays): 0, 3 + len(arrays): 1}
        in_specs += [pl.BlockSpec(memory_space=pl.ANY)] * 2
        arrays += sums
    pairs = max(
        count * sum(len(task[3]) for task in tasks) for count, tasks in variants.values()
    )
    span_count = math.isqrt(mask.shape[0])
    return pl.pallas_call(
        functools.partial(attend_kernel, variants, extra, span_count, fresh),
        name=name,
        out_shape=[pltpu.HBM((SLOTS, sums_shape[1] // 2, rows), jnp.float32)] * 2,
        input_output_aliases=aliases,
        grid_spec=pltpu.PrefetchScalarGridSpec(
            num_scalar_prefetch=2,
            grid=(steps,),
            in_specs=in_specs,
            out_specs=[pl.BlockSpec(memory_space=pl.ANY)] * 2,
            scratch_shapes=[
                pltpu.VMEM((SLOTS, 2 * patch + 16, rows), jnp.float32),
                pltpu.VMEM((SLOTS, rows, HD), jnp.float32),
                pltpu.VMEM(sums_shape, jnp.float32),
                pltpu.SemaphoreType.DMA((4,)),
            ],
        ),
        compiler_params=pltpu.CompilerParams(vmem_limit_bytes=GRANT),
        cost_estimate=pl.CostEstimate(
            flops=cost * pairs * 4 * rows * rows * HD,
            bytes_accessed=steps * HD * 2 * sum(spec.block_shape[0] for spec in in_specs[:4]),
            transcendentals=cost * pairs * rows * rows,
        ),
    )(scalars, mask, *arrays)


def token_sums(
    scalars, queries, keys, values, span_mask, head_gain, patch_weight, prepare
):
    rows = queries.shape[0]
    half = rows // 2
    heads = NEAR_HEADS + MIDDLE_HEADS + FAR_HEADS
    in_place = lambda array: pltpu.with_memory_space_constraint(array, pltpu.HBM)
    queries, keys, values = (in_place(array) for array in (queries, keys, values))

    def send(value, *pairs):
        return in_place(lax.ppermute(value, "span", list(pairs)))

    def tokens(entry, shift, count):
        return [(0, 0, rows, (OWN, entry) if entry else (OWN,), shift, count)]

    def pairs_of(entry, shift, count):
        entries = (entry,) if entry else ()
        return [
            piece
            for part in (1, 2)
            for piece in (
                (part, 0, half, (OWN,) + entries, shift, count),
                (3, (part - 1) * half, half, entries, shift, count),
            )
        ]

    handed = pack_handed(keys, values, heads)
    received = lax.ppermute(handed, "slab", SWAP)
    up, down = message(
        scalars,
        [
            pairs_of(UP, 0, NEAR_HEADS),
            tokens(DOWN, 0, MIDDLE_HEADS) + pairs_of(DOWN, 0, MIDDLE_HEADS),
        ],
        (queries, keys, values, received),
        "pack_first",
    )
    source, _ = lax.optimization_barrier((received, down))
    up = send(up, (0, 1), (1, 2))
    down = send(down, (1, 0), (2, 1), (3, 2))
    up_two, two, far_all, far_pair = message(
        scalars,
        [
            pairs_of(None, MIDDLE, MIDDLE_HEADS),
            tokens(None, 0, NEAR_HEADS) + pairs_of(None, 0, NEAR_HEADS),
            tokens(None, FAR, FAR_HEADS) + pairs_of(None, FAR, FAR_HEADS),
            pairs_of(None, FAR, FAR_HEADS),
        ],
        (queries, keys, values, source),
        "pack_second",
    )
    anchor = two
    up, up_two = lax.optimization_barrier((up, up_two))
    up_two = send(up_two, (0, 2))
    two = send(two, (3, 1))
    far_next = send(far_all, (2, 3), (1, 0))
    far_pair, prepared = lax.optimization_barrier((far_pair, prepare(anchor)))
    far_two = send(far_pair, (1, 3))
    far_three = send(far_pair, (0, 3))

    span_mask, head_gain, patch_weight, _ = lax.optimization_barrier(
        (span_mask, head_gain, patch_weight, anchor)
    )
    mask = span_mask.reshape(-1)
    weight = patch_weight.T
    own = (queries, keys, values, received, weight, head_gain[None, :])
    run = functools.partial(attend, own=own, scalars=scalars, mask=mask)

    here, back_one, on_one = OWN_TOKENS, Tokens(None, (0,)), Tokens(1, (1,))
    back_two = Tokens(None, (2,))
    sums = run(
        MIDDLE_HEADS,
        MAIN,
        MAIN_CAP,
        sums=None,
        payloads=[up, down, up_two],
        variants={
            0: (4, [(here, 0, 0, [(here, 0)]), (on_one, 1, 1, [(here, 0), (on_one, 1)])]),
            1: (
                4,
                [
                    (on_one, 1, 2, [(back_one, 0), (here, 1), (on_one, 2)]),
                    (here, 0, 1, [(back_one, 0), (here, 1)]),
                ],
            ),
            2: (
                4,
                [
                    (on_one, 1, 3, [(back_two, 0), (back_one, 1), (here, 2), (on_one, 3)]),
                    (here, 0, 2, [(back_two, 0), (back_one, 1), (here, 2)]),
                ],
            ),
        },
        more=False,
        name="main_heads",
    )
    on_two, beside = Tokens(2, (2,)), Tokens(3, (3,))
    two_back, three_back = Tokens(None, (4,)), Tokens(None, (5,))
    extras = [Tokens(None, (), lane) for lane in range(2)]
    sums, prepared = lax.optimization_barrier((sums, prepared))
    sums = run(
        NEAR_HEADS,
        FINAL,
        FINAL_CAP,
        sums=sums,
        payloads=[up, down, two, far_next, far_two, far_three],
        variants={
            0: (
                FAR_HEADS,
                [(here, 0, 0, [(here, 0)]), (beside, 1, 1, [(here, 0), (beside, 1)])]
                + [(head, 0, 0, [(head, 0)]) for head in extras],
            ),
            1: (
                NEAR_HEADS,
                [(on_two, 2, 3, [(back_one, 0), (here, 1), (on_one, 2), (on_two, 3)])],
            ),
            3: (
                FAR_HEADS,
                [
                    (here, 0, 3, [(three_back, 0), (two_back, 1), (beside, 2), (here, 3)]),
                    (beside, 2, 2, [(three_back, 0), (two_back, 1), (beside, 2)]),
                ],
            ),
        },
        more=True,
        name="final_heads",
        cost=4,
    )
    return sums, prepared


def noise_window(grid, constants):
    height, breadth, _ = grid.shape
    slab = lax.axis_index("slab")
    edge = jnp.where(slab == 0, grid[:, breadth - 1], grid[:, 0])
    edge = lax.ppermute(edge, "slab", SWAP)[:, None]
    grid = jnp.concatenate(
        [
            jnp.where(slab == 1, edge, 0.0),
            grid,
            jnp.where(slab == 0, edge, 0.0),
            jnp.zeros((height, WINDOW - breadth - 2, grid.shape[2]), grid.dtype),
        ],
        axis=1,
    )
    head = lax.axis_index("head")
    edge = jnp.where(head == 0, grid[height - 1], grid[0])
    count = constants.shape[1]
    extra = jnp.pad(constants, ((0, 8 - constants.shape[0]), (0, HD - count)))
    edge = jnp.pad(edge, ((0, 0), (0, HD - edge.shape[1])))
    sent = lax.ppermute(jnp.concatenate([edge, extra], axis=0), "head", SWAP)
    edge = sent[None, :WINDOW, : grid.shape[2]]
    constants = constants + sent[WINDOW : WINDOW + constants.shape[0], :count]
    grid = jnp.concatenate(
        [jnp.where(head == 1, edge, 0.0), grid, jnp.where(head == 0, edge, 0.0)], axis=0
    )
    return grid.reshape((height + 2) * WINDOW, grid.shape[2]), constants.T


def cell_selector(height, breadth):
    cell = lax.broadcasted_iota(jnp.int32, ((height + 2) * WINDOW, 4 * TROWS * TCOLS), 0)
    column = lax.broadcasted_iota(jnp.int32, cell.shape, 1)
    y = lax.axis_index("head") * height + cell // WINDOW - 1
    x = lax.axis_index("slab") * breadth + cell % WINDOW - 1
    inside = (y >= 0) & (y < 2 * TROWS) & (x >= 0) & (x < 2 * TCOLS)
    inside = inside & (cell % WINDOW < breadth + 2)
    target = ((y % 2) * 2 + x % 2) * (TROWS * TCOLS) + (y // 2) * TCOLS + x // 2
    return (inside & (column == target)).astype(jnp.bfloat16)


def band_kernel(weight, band):
    outputs = weight.shape[1]
    band[...] = jnp.zeros_like(band)
    for row_tap in range(3):
        for col_tap in range(3):
            for frame_tap in range(3):
                start = ((3 * frame_tap + row_tap) * 3 + col_tap) * LAT_CH
                block = weight[start : start + LAT_CH]
                for frame in range(FRAMES_SPAN):
                    at = (col_tap * (FRAMES_SPAN + 2) + frame + frame_tap) * LAT_CH
                    band[
                        row_tap, at : at + LAT_CH, frame * outputs : (frame + 1) * outputs
                    ] = block


def banded_weight(conv_weight):
    shape = (3, 3 * (FRAMES_SPAN + 2) * LAT_CH, FRAMES_SPAN * conv_weight.shape[1])
    return pl.pallas_call(
        band_kernel,
        name="band",
        out_shape=jax.ShapeDtypeStruct(shape, conv_weight.dtype),
        in_specs=[pl.BlockSpec(memory_space=pltpu.VMEM)],
        out_specs=pl.BlockSpec(memory_space=pltpu.VMEM),
        compiler_params=pltpu.CompilerParams(vmem_limit_bytes=GRANT),
        cost_estimate=pl.CostEstimate(
            flops=0, bytes_accessed=2 * math.prod(shape), transcendentals=0
        ),
    )(conv_weight)


def finish_kernel(
    scalars, mine, other, noise, before, selector, band, bias, constants, clean, decoded, cells
):
    frames, height, breadth, channels = clean.shape
    patch = constants.shape[0]
    first = scalars[SLAB] == 0
    sums = jnp.concatenate(
        [jnp.where(first, mine[...], other[...]), jnp.where(first, other[...], mine[...])], axis=0
    )
    feature_width = HEADS * HD
    row_mean = sums[patch : patch + 1] / feature_width
    spread = sums[patch + STAT_ROWS : patch + STAT_ROWS + 1] / feature_width - row_mean * row_mean
    velocity = (
        lax.rsqrt(spread + norm_eps) * (sums[:patch] - constants[:, 0:1] * row_mean)
        + constants[:, 1:2]
    )
    tokens = TROWS * TCOLS
    lane = lax.broadcasted_iota(jnp.int32, velocity.shape, 1)
    velocity = jnp.where((lane >= 2 * tokens) | (scalars[PLACE] > 0), velocity, 0.0)
    columns = jnp.concatenate(
        [
            jnp.concatenate(
                [
                    velocity[
                        part * channels : (part + 1) * channels,
                        frame * tokens : (frame + 1) * tokens,
                    ]
                    for part in range(4)
                ],
                axis=1,
            )
            for frame in range(frames + 2)
        ],
        axis=0,
    )
    high = columns.astype(jnp.bfloat16)
    low = (columns - high.astype(jnp.float32)).astype(jnp.bfloat16)
    chosen = sum(
        lax.dot_general(
            selector[...], part, (((1,), (1,)), ((), ())), preferred_element_type=jnp.float32
        )
        for part in (high, low)
    )
    count = (height + 2) * WINDOW
    cells[:count] = (
        jnp.concatenate([before[...], noise[...]], axis=1) - noise_level * chosen
    )
    cells[count:] = jnp.zeros_like(cells[count:])
    for frame in range(frames):
        lanes = slice((frame + 2) * channels, (frame + 3) * channels)
        for y in range(height):
            start = (y + 1) * WINDOW + 1
            clean[frame, y] = cells[start : start + breadth, lanes]
    shifted = jnp.concatenate(
        [cells[tap : tap + count] for tap in range(3)], axis=1
    ).astype(jnp.bfloat16)
    total = jnp.broadcast_to(bias[...], (height * breadth, bias.shape[1]))
    for tap in range(3):
        block = jnp.concatenate(
            [
                shifted[(y + tap) * WINDOW : (y + tap) * WINDOW + breadth]
                for y in range(height)
            ],
            axis=0,
        )
        total = total + jnp.dot(block, band[tap], preferred_element_type=jnp.float32)
    outputs = decoded.shape[3]
    total = total.astype(decoded.dtype)
    for frame in range(frames):
        decoded[frame] = total[:, frame * outputs : (frame + 1) * outputs].reshape(
            height, breadth, outputs
        )


def finish(
    scalars, mine, other, noise, before, selector, band, bias, constants, shape, outputs
):
    whole = pl.BlockSpec(memory_space=pltpu.VMEM)
    frames, height, breadth, channels = shape
    rows = (height + 2) * WINDOW
    return pl.pallas_call(
        finish_kernel,
        name="finish",
        out_shape=(
            jax.ShapeDtypeStruct(shape, jnp.float32),
            jax.ShapeDtypeStruct((frames, height, breadth, outputs), jnp.bfloat16),
        ),
        in_specs=[pl.BlockSpec(memory_space=pltpu.SMEM)] + [whole] * 8,
        out_specs=(whole, whole),
        scratch_shapes=[pltpu.VMEM((rows + 8, (frames + 2) * channels), jnp.float32)],
        compiler_params=pltpu.CompilerParams(vmem_limit_bytes=GRANT),
    )(scalars, mine, other, noise, before, selector, band, bias, constants)


def per_device(
    queries,
    keys,
    values,
    span_mask,
    head_gain,
    head_shift,
    patch_weight,
    noisy_latent,
    conv_weight,
    conv_bias,
):
    heads_dev = queries.shape[1] // HD
    if not plan_fits(
        heads_dev, lax.axis_size("span"), lax.axis_size("slab"), lax.axis_size("head")
    ):
        return gathered_plan(
            queries,
            keys,
            values,
            span_mask,
            head_gain,
            head_shift,
            patch_weight,
            noisy_latent,
            conv_weight,
            conv_bias,
        )
    place = lax.axis_index("span")
    slab = lax.axis_index("slab")
    scalars = scalar_operand(heads_dev // lax.axis_size("slab"))
    def prepare(anchor):
        noise, weight, gain, shift, taps, bias, _ = lax.optimization_barrier(
            (noisy_latent, patch_weight, head_gain, head_shift, conv_weight, conv_bias, anchor)
        )
        _, height, breadth, _ = noise.shape
        noise = noise.transpose(1, 2, 0, 3).reshape(height, breadth, -1)
        wide_weight = weight.T.astype(jnp.float32)
        constants = jnp.stack(
            [
                jnp.sum(wide_weight * gain[None, :], axis=1),
                jnp.sum(wide_weight * shift[None, :], axis=1),
            ]
        )
        window, constants = noise_window(noise, constants)
        return (
            window,
            window[:, -2 * LAT_CH :].reshape(16, -1),
            constants,
            cell_selector(height, breadth),
            banded_weight(taps),
            jnp.tile(bias, FRAMES_SPAN)[None, :],
        )

    (mine, theirs), (noise, ahead, constants, selector, band, bias) = token_sums(
        scalars,
        queries,
        keys,
        values,
        span_mask,
        head_gain,
        patch_weight,
        prepare,
    )
    mine = mine + lax.ppermute(theirs, "slab", SWAP)
    own, after, third = mine[0], mine[1], mine[2]
    skip = TROWS * TCOLS
    from_one = lax.ppermute(
        jnp.concatenate([jnp.concatenate([own[:, skip:], after], axis=1), ahead], axis=0),
        "span",
        [(0, 1), (1, 2), (2, 3)],
    )
    before = from_one[own.shape[0] :].reshape(-1, 2 * LAT_CH)
    from_one = from_one[: own.shape[0]]
    to_current = lax.ppermute(third, "span", [(1, 3), (3, 2)])
    to_before = lax.ppermute(after[:, skip:], "span", [(0, 2), (1, 3)])
    kept = jnp.concatenate([jnp.where(place == 3, third[:, skip:], 0.0), own], axis=1)
    total = kept + from_one + jnp.concatenate([to_before, to_current], axis=1)
    total = total + lax.ppermute(total, "head", SWAP)
    other = lax.ppermute(total, "slab", SWAP)
    return finish(
        scalars,
        total,
        other,
        noise,
        before,
        selector,
        band,
        bias,
        constants,
        noisy_latent.shape,
        conv_weight.shape[1],
    )


def solution(mesh):
    placed = (
        P(("groups", "span"), "head"),
        P(("groups", "span", "slab"), "head"),
        P(("groups", "span", "slab"), "head"),
        P("groups", None),
        P("head"),
        P("head"),
        P("head", None),
        P(("groups", "span"), "head", "slab", None),
        P(),
        P(),
    )
    return jax.shard_map(
        per_device,
        mesh=mesh,
        in_specs=placed,
        out_specs=(
            P(("groups", "span"), "head", "slab", None),
            P(("groups", "span"), "head", "slab", None),
        ),
        check_vma=False,
    )
```

```python
import functools
import math
import typing

import jax
import jax.numpy as jnp
import numpy as np
from jax import lax
from jax.experimental import pallas as pl
from jax.experimental.pallas import tpu as pltpu
from jax.sharding import PartitionSpec as P

HEADS = 40
HD = 128
LAT_CH = 16
FRAMES_SPAN = 3
TROWS = 8
TCOLS = 16


neg_big = -1e30
noise_level = 0.75
norm_eps = 1e-06


def with_halo(cells, sides, width):
    for axis, dim in sides:
        count = lax.axis_size(axis)
        ends = count - 1
        head = lax.slice_in_dim(cells, 0, width, axis=dim)
        tail = lax.slice_in_dim(cells, cells.shape[dim] - width, cells.shape[dim], axis=dim)
        cells = jnp.concatenate(
            [
                lax.ppermute(tail, axis, [(i, (i + 1) % count) for i in range(ends)]),
                cells,
                lax.ppermute(head, axis, [((i + 1) % count, i) for i in range(ends)]),
            ],
            axis=dim,
        )
    return cells


def from_behind(value, axis, by):
    size = lax.axis_size(axis)
    pairs = [(i, i + by) for i in range(size) if 0 <= i + by < size]
    return lax.ppermute(value, axis, pairs)


def block_length(total_rows):
    block_size = total_rows
    while block_size > 768 and block_size % 2 == 0:
        block_size = block_size // 2
    return block_size


def fold_keys(partial_state, key_value, query_block, mask_row, rows_span):
    keys_piece, values_piece = key_value
    heads_dev = query_block.shape[1]
    piece_rows = keys_piece.shape[0]
    length = block_length(piece_rows)
    span_count = mask_row.shape[0]
    score_scale = 1.0 / math.sqrt(HD)
    span_ids = jnp.arange(span_count, dtype=jnp.int32)

    def one_block(carry_state, block_index):
        running_max, running_sum, weighted = carry_state
        offset = block_index * length
        key_block = lax.dynamic_slice_in_dim(keys_piece, offset, length, 0).reshape(
            length, heads_dev, HD
        )
        value_block = lax.dynamic_slice_in_dim(values_piece, offset, length, 0).reshape(
            length, heads_dev, HD
        )
        key_span = (offset + jnp.arange(length, dtype=jnp.int32)) // rows_span
        allowed = (
            jnp.sum(jnp.where(key_span[:, None] == span_ids[None, :], mask_row[None, :], 0), axis=1)
            > 0
        )
        scores = (
            jnp.einsum("qhd,khd->hqk", query_block, key_block, preferred_element_type=jnp.float32)
            * score_scale
        )
        scores = jnp.where(allowed[None, None, :], scores, neg_big)
        new_max = jnp.maximum(running_max, jnp.max(scores, axis=2))
        weights = jnp.where(allowed[None, None, :], jnp.exp(scores - new_max[:, :, None]), 0.0)
        factor = jnp.exp(running_max - new_max)
        running_sum = running_sum * factor + jnp.sum(weights, axis=2)
        weighted = weighted * factor.T[:, :, None] + jnp.einsum(
            "hqk,khd->qhd",
            weights.astype(jnp.bfloat16),
            value_block,
            preferred_element_type=jnp.float32,
        )
        return ((new_max, running_sum, weighted), None)

    result, unused = lax.scan(
        one_block, partial_state, jnp.arange(piece_rows // length, dtype=jnp.int32)
    )
    return result


def gathered_plan(
    queries,
    keys,
    values,
    span_mask,
    head_gain,
    head_shift,
    patch_weight,
    noisy_latent,
    conv_weight,
    conv_bias,
):
    heads_dev = queries.shape[1] // HD
    slab_count = lax.axis_size("slab")
    col_dev = TCOLS // slab_count
    slab_place = lax.axis_index("slab")
    span_place = lax.axis_index("span")
    mask_row = lax.dynamic_slice_in_dim(span_mask, span_place, 1, 0)[0]
    token_grid = queries.reshape(FRAMES_SPAN, TROWS, TCOLS, queries.shape[-1])
    picked = lax.dynamic_slice_in_dim(token_grid, slab_place * col_dev, col_dev, 2)
    own_queries = picked.reshape(FRAMES_SPAN * TROWS * col_dev, queries.shape[-1]).reshape(
        -1, heads_dev, HD
    )
    query_rows = own_queries.shape[0]
    rows_span = keys.shape[0] * slab_count
    running_max, running_sum, weighted = fold_keys(
        (
            jnp.full((heads_dev, query_rows), neg_big, jnp.float32),
            jnp.zeros((heads_dev, query_rows), jnp.float32),
            jnp.zeros((query_rows, heads_dev, HD), jnp.float32),
        ),
        (
            lax.all_gather(keys, ("span", "slab"), axis=0, tiled=True),
            lax.all_gather(values, ("span", "slab"), axis=0, tiled=True),
        ),
        own_queries,
        mask_row,
        rows_span,
    )
    attended = (
        (weighted / running_sum.T[:, :, None])
        .astype(jnp.bfloat16)
        .reshape(query_rows, heads_dev * HD)
    )
    feature_width = HEADS * HD
    values32 = attended.astype(jnp.float32)
    row_total = jnp.sum(values32, axis=1)
    row_squares = jnp.sum(values32 * values32, axis=1)
    row_total, row_squares = lax.psum((row_total, row_squares), "head")
    row_mean = row_total / feature_width
    spread = row_squares / feature_width - row_mean * row_mean
    normed = (
        (values32 - row_mean[:, None]) * lax.rsqrt(spread + norm_eps)[:, None] * head_gain[None, :]
        + head_shift[None, :]
    ).astype(jnp.bfloat16)
    normed_grid = normed.reshape(FRAMES_SPAN, TROWS, col_dev, normed.shape[-1])
    own_rows = TROWS // lax.axis_size("head")
    picked = normed_grid
    product = jnp.dot(
        picked.reshape(-1, picked.shape[-1]), patch_weight, preferred_element_type=jnp.float32
    )
    velocity = lax.psum_scatter(
        product.reshape(
            FRAMES_SPAN, own_rows * lax.axis_size("head"), col_dev * patch_weight.shape[1]
        )
        .transpose(1, 0, 2)
        .reshape(own_rows * lax.axis_size("head"), -1)
        .astype(jnp.bfloat16),
        "head",
        scatter_dimension=0,
        tiled=True,
    ).astype(jnp.float32)
    rows_dev = velocity.shape[0]
    patch_cells = (
        velocity.reshape(rows_dev, FRAMES_SPAN, col_dev, 2, 2, LAT_CH)
        .transpose(1, 0, 3, 2, 4, 5)
        .reshape(FRAMES_SPAN, 2 * rows_dev, 2 * col_dev, LAT_CH)
    )
    clean_latent = noisy_latent - noise_level * patch_cells
    latent_input = clean_latent.astype(jnp.bfloat16)
    framed = with_halo(latent_input, (("head", 1), ("slab", 2)), 1)
    earlier = from_behind(framed[FRAMES_SPAN - 2 :], "span", 1)
    stacked = jnp.concatenate([earlier, framed], axis=0)
    height = clean_latent.shape[1]
    breadth = clean_latent.shape[2]
    columns = jnp.concatenate(
        [
            stacked[
                frame_tap : frame_tap + FRAMES_SPAN,
                row_tap : row_tap + height,
                col_tap : col_tap + breadth,
                :,
            ]
            for frame_tap in range(3)
            for row_tap in range(3)
            for col_tap in range(3)
        ],
        axis=-1,
    )
    decoded = (
        jnp.dot(
            columns.reshape(FRAMES_SPAN * height * breadth, 27 * LAT_CH),
            conv_weight,
            preferred_element_type=jnp.float32,
        )
        + conv_bias[None, :]
    )
    decoded = decoded.astype(jnp.bfloat16).reshape(
        FRAMES_SPAN, height, breadth, conv_weight.shape[1]
    )
    return (clean_latent, decoded)


NEAR_HEADS = 4
MIDDLE_HEADS = 4
FAR_HEADS = 2
MIDDLE = NEAR_HEADS
FAR = NEAR_HEADS + MIDDLE_HEADS
STAT_ROWS = 8
SLOTS = 3
QUERY_ROWS = 192
SWAP = [(0, 1), (1, 0)]
WINDOW = 32
GRANT = 20 << 20

OWN, OTHER, DOWN, UP, MAIN, MAIN_CAP, FINAL, FINAL_CAP, PLACE, SLAB = range(10)


def plan_fits(heads_dev, span_count, slab_count, head_count):
    return (
        span_count == 4
        and slab_count == 2
        and head_count == 2
        and heads_dev == slab_count * (NEAR_HEADS + MIDDLE_HEADS + FAR_HEADS)
    )


def scalar_operand(heads):
    by_place = np.zeros((4, 12), np.int32)
    by_place[:, OTHER] = heads
    by_place[:, DOWN] = [MIDDLE, MIDDLE, 0, MIDDLE]
    by_place[:, UP] = [0, MIDDLE, 0, 0]
    by_place[:, MAIN] = [MIDDLE, 0, MIDDLE, 0]
    by_place[:, MAIN_CAP] = [1, 1, 1, 0]
    by_place[:, FINAL] = [FAR, 0, 0, FAR]
    by_place[:, FINAL_CAP] = [0, 1, 0, 0]
    by_place[:, PLACE] = range(4)
    by_slab = np.zeros(12, np.int32)
    by_slab[[OWN, OTHER, SLAB]] = heads, -heads, 1
    row = lax.dynamic_slice_in_dim(jnp.array(by_place), lax.axis_index("span"), 1, 0)[0]
    return row + lax.axis_index("slab") * jnp.array(by_slab)


def pack_kernel(inputs, messages, copies, scalars, *refs):
    ins, rest = refs[:inputs], refs[inputs:]
    outs, staged = rest[:messages], rest[messages:-2]
    arrive, leave = rest[-2:]
    arriving = []
    for number, (source, row, rows, entries, shift, target, at, heads) in enumerate(copies):
        head = shift
        for entry in entries:
            head = head + scalars[entry]
        column = pl.multiple_of(head * HD, HD)
        place = staged[target].at[pl.ds(at, rows), :]
        copy = pltpu.make_async_copy(
            ins[source].at[pl.ds(row, rows), pl.ds(column, heads * HD)], place, arrive.at[number]
        )
        copy.start()
        onward = pltpu.make_async_copy(
            place, outs[target].at[pl.ds(at, rows), :], leave.at[number]
        )
        arriving.append((copy, onward))
    for copy, onward in arriving:
        copy.wait()
        onward.start()
    for _, onward in arriving:
        onward.wait()


def pack(scalars, arrays, shapes, copies, name):
    moved = sum(2 * 2 * rows * heads * HD for _, _, rows, _, _, _, _, heads in copies)
    out_shape = [pltpu.HBM(shape, jnp.bfloat16) for shape in shapes]
    in_specs = [pl.BlockSpec(memory_space=pl.ANY)] * len(arrays)
    out_specs = [pl.BlockSpec(memory_space=pl.ANY)] * len(shapes)
    return pl.pallas_call(
        functools.partial(pack_kernel, len(arrays), len(shapes), copies),
        name=name,
        out_shape=out_shape,
        grid_spec=pltpu.PrefetchScalarGridSpec(
            num_scalar_prefetch=1,
            grid=(1,),
            in_specs=in_specs,
            out_specs=out_specs,
            scratch_shapes=[pltpu.VMEM(shape, jnp.bfloat16) for shape in shapes]
            + [
                pltpu.SemaphoreType.DMA((len(copies),)),
                pltpu.SemaphoreType.DMA((len(copies),)),
            ],
        ),
        compiler_params=pltpu.CompilerParams(vmem_limit_bytes=GRANT),
        cost_estimate=pl.CostEstimate(flops=0, bytes_accessed=moved, transcendentals=0),
    )(scalars, *arrays)


def hand_kernel(heads, keys, values, out, arrive):
    column = pl.multiple_of((1 - lax.axis_index("slab")) * heads * HD, heads * HD)
    half = keys.shape[0]
    copies = []
    for number, source in enumerate((keys, values)):
        copy = pltpu.make_async_copy(
            source.at[:, pl.ds(column, heads * HD)],
            out.at[pl.ds(number * half, half), :],
            arrive.at[number],
        )
        copy.start()
        copies.append(copy)
    for copy in copies:
        copy.wait()


def pack_handed(keys, values, heads):
    shape = (2 * keys.shape[0], heads * HD)
    return pl.pallas_call(
        functools.partial(hand_kernel, heads),
        name="pack_handed",
        out_shape=jax.ShapeDtypeStruct(shape, keys.dtype),
        in_specs=[pl.BlockSpec(memory_space=pl.ANY)] * 2,
        out_specs=pl.BlockSpec(memory_space=pltpu.VMEM),
        scratch_shapes=[pltpu.SemaphoreType.DMA((2,))],
        compiler_params=pltpu.CompilerParams(vmem_limit_bytes=GRANT),
        cost_estimate=pl.CostEstimate(
            flops=0, bytes_accessed=4 * math.prod(shape), transcendentals=0
        ),
    )(keys, values)


def message(scalars, pieces, arrays, name):
    copies, shapes = [], []
    for target, parts in enumerate(pieces):
        at = 0
        for source, row, rows, entries, shift, heads in parts:
            copies.append((source, row, rows, entries, shift, target, at, heads))
            at += rows
        shapes.append((at, parts[0][5] * HD))
    return pack(scalars, arrays, shapes, copies, name)


class Tokens(typing.NamedTuple):
    query: int | None = None
    pairs: tuple = ()
    extra: int | None = None


OWN_TOKENS = Tokens()


def attend_kernel(variants, extra, span_count, fresh, wide, scalars, mask, *refs):
    query_own, key_own, value_own, received, weight, gain = refs[:6]
    more = refs[6 : 6 + extra]
    mine_out, theirs_out, folded, squares, carried, moved = refs[-6:]
    payloads = refs[6 + extra : -6] if fresh else refs[6 + extra : -8]
    rows = query_own.shape[0]
    half = rows // 2
    step = pl.program_id(0)
    to_exp2 = math.log2(math.e) / math.sqrt(HD)
    active = functools.reduce(
        lambda a, b: a | b, [scalars[PLACE] == place for place in variants]
    )

    last_step = step == pl.num_programs(0) - 1
    part = carried.shape[1] // 2
    halves = [
        carried.at[:, pl.ds(pl.multiple_of(number * part, part), part)]
        for number in (scalars[SLAB], 1 - scalars[SLAB])
    ]
    fetches = (
        []
        if fresh
        else [
            pltpu.make_async_copy(refs[number - 8], halves[number], moved.at[number])
            for number in range(2)
        ]
    )

    @pl.when((step == 0) & active)
    def _():
        folded[...] = jnp.zeros_like(folded)
        squares[...] = jnp.zeros_like(squares)
        for fetch in fetches:
            fetch.start()

    def lanes_of(head):
        return slice(head * HD, (head + 1) * HD)

    def query_of(source, lanes):
        if source is OWN_TOKENS:
            return query_own[:, lanes]
        if source.extra is not None:
            return more[0][:, lanes_of(source.extra)]
        return payloads[source.query][:rows, lanes]

    def pair_of(source, lanes):
        if source is OWN_TOKENS:
            parts = (
                key_own[:, lanes],
                received[:half, lanes],
                value_own[:, lanes],
                received[half:, lanes],
            )
        elif source.extra is not None:
            own = lanes_of(source.extra)
            parts = (more[1][:, own], more[3][:half, own], more[2][:, own], more[3][half:, own])
        else:
            payload = payloads[source.pairs[0]]
            start = payload.shape[0] - 2 * rows
            return payload[start : start + rows, lanes], payload[start + rows :, lanes]
        return jnp.concatenate(parts[:2], axis=0), jnp.concatenate(parts[2:], axis=0)

    def projector(extra_head, lanes):
        if extra_head is None:
            scaled = weight[:, lanes].astype(jnp.float32) * gain[:, lanes]
        else:
            own = lanes_of(extra_head)
            scaled = more[4][:, own].astype(jnp.float32) * more[5][:, own]
        high = scaled.astype(jnp.bfloat16)
        low = (scaled - high.astype(jnp.float32)).astype(jnp.bfloat16)
        return jnp.concatenate([high, low, jnp.ones((16, HD), jnp.bfloat16)], axis=0)

    def one_query(head, source, slot, query_span, key_sources):
        lanes = lanes_of(head)
        query = query_of(source, lanes)
        pairs = [pair_of(key_source, lanes) for key_source, _ in key_sources]
        open_to = [
            None if key_span == query_span else mask[query_span * span_count + key_span] > 0
            for _, key_span in key_sources
        ]
        keys_in = jnp.concatenate([pair[0] for pair in pairs], axis=0)
        ones_block = jnp.ones((rows, HD), jnp.bfloat16)
        values_in = jnp.concatenate(
            [jnp.concatenate([pair[1], ones_block], axis=1) for pair in pairs], axis=0
        )
        pieces = []
        for row in range(0, rows, QUERY_ROWS):
            score = lax.dot_general(
                query[row : row + QUERY_ROWS],
                keys_in,
                (((1,), (1,)), ((), ())),
                preferred_element_type=jnp.float32,
            )
            best = None
            for number, is_open in enumerate(open_to):
                start = number * rows
                block = score[:, start : start + HD]
                for lane in range(HD, rows, HD):
                    block = jnp.maximum(block, score[:, start + lane : start + lane + HD])
                if is_open is not None:
                    block = jnp.where(is_open, block, neg_big)
                best = block if best is None else jnp.maximum(best, block)
            top = jnp.max(best, axis=1, keepdims=True)
            weights = []
            for number, is_open in enumerate(open_to):
                start = number * rows
                shift = top if is_open is None else jnp.where(is_open, top, -neg_big)
                weights.append(
                    jnp.exp2((score[:, start : start + rows] - shift) * to_exp2).astype(jnp.bfloat16)
                )
            both = jnp.dot(
                jnp.concatenate(weights, axis=1), values_in, preferred_element_type=jnp.float32
            )
            pieces.append((both[:, :HD] / both[:, HD:]).astype(jnp.bfloat16))
        attended = jnp.concatenate(pieces, axis=0)
        folded[slot] += lax.dot_general(
            projector(source.extra, lanes),
            attended,
            (((1,), (1,)), ((), ())),
            preferred_element_type=jnp.float32,
        )
        wide = attended.astype(jnp.float32)
        squares[slot] += wide * wide

    for place, groups in variants.items():
        for steps, tasks in groups:

            @pl.when((scalars[PLACE] == place) & (step < steps))
            def _():
                for head in range(wide):
                    for task in tasks:
                        if head == 0 or task[0].extra is None:
                            one_query(head, *task)

    def store():
        copies = [
            pltpu.make_async_copy(halves[number], out, moved.at[2 + number])
            for number, out in enumerate((mine_out, theirs_out))
        ]
        for copy in copies:
            copy.start()
        for copy in copies:
            copy.wait()

    if fresh:

        @pl.when(last_step & jnp.logical_not(active))
        def _():
            carried[...] = jnp.zeros_like(carried)
            store()

    @pl.when(last_step & active)
    def _():
        ones_rows = jnp.ones((STAT_ROWS, HD), jnp.bfloat16)
        patch = weight.shape[0]
        for fetch in fetches:
            fetch.wait()
        if fresh:
            carried[...] = jnp.zeros_like(carried)

        def finish_slot(slot):
            left = squares[slot]
            total = jnp.zeros((STAT_ROWS, rows), jnp.float32)
            for _ in range(3):
                piece = left.astype(jnp.bfloat16)
                left = left - piece.astype(jnp.float32)
                total = total + lax.dot_general(
                    ones_rows, piece, (((1,), (1,)), ((), ())), preferred_element_type=jnp.float32
                )
            done = folded[slot]
            carried[slot] += jnp.concatenate(
                [
                    done[:patch] + done[patch : 2 * patch],
                    done[2 * patch : 2 * patch + STAT_ROWS],
                    total,
                ],
                axis=0,
            )

        for place, groups in variants.items():

            @pl.when(scalars[PLACE] == place)
            def _():
                for slot in sorted({task[1] for _, tasks in groups for task in tasks}):
                    finish_slot(slot)

        store()


def attend(
    steps, wide, first, cap, own, scalars, mask, sums, payloads, variants, more, name, cost=1
):
    queries, keys, values, received, weight, gain = own
    rows = queries.shape[0]
    half = rows // 2
    patch = weight.shape[0]

    def moving(i, scalars):
        return jnp.minimum(i, scalars[cap])

    def column(height, own_column):
        def index(i, scalars, mask):
            head = scalars[first] + scalars[OWN] if own_column else scalars[first]
            return (0, head // wide + moving(i, scalars))

        return pl.BlockSpec((height, wide * HD), index)

    def two_columns(height, own_column):
        def index(i, scalars, mask):
            return (0, i + scalars[OWN] // 2 if own_column else i)

        return pl.BlockSpec((height, 2 * HD), index)

    def payload_column(payload):
        last = payload.shape[1] // (wide * HD) - 1

        def index(i, scalars, mask):
            return (0, jnp.minimum(moving(i, scalars), last))

        return pl.BlockSpec((payload.shape[0], wide * HD), index)

    in_specs = [
        column(rows, True),
        column(half, True),
        column(half, True),
        column(rows, False),
        column(patch, True),
        column(1, True),
    ]
    arrays = [queries, keys, values, received, weight, gain]
    extra = 0
    if more:
        extra = 6
        in_specs += [
            two_columns(rows, True),
            two_columns(half, True),
            two_columns(half, True),
            two_columns(rows, False),
            two_columns(patch, True),
            two_columns(1, True),
        ]
        arrays += [queries, keys, values, received, weight, gain]
    in_specs += [payload_column(payload) for payload in payloads]
    arrays += payloads
    fresh = sums is None
    sums_shape = (SLOTS, patch + 2 * STAT_ROWS, rows)
    aliases = {}
    if not fresh:
        aliases = {2 + len(arrays): 0, 3 + len(arrays): 1}
        in_specs += [pl.BlockSpec(memory_space=pl.ANY)] * 2
        arrays += sums
    pairs = max(
        sum(count * wide * sum(len(task[3]) for task in tasks) for count, tasks in groups)
        for groups in variants.values()
    )
    span_count = math.isqrt(mask.shape[0])
    return pl.pallas_call(
        functools.partial(attend_kernel, variants, extra, span_count, fresh, wide),
        name=name,
        out_shape=[pltpu.HBM((SLOTS, sums_shape[1] // 2, rows), jnp.float32)] * 2,
        input_output_aliases=aliases,
        grid_spec=pltpu.PrefetchScalarGridSpec(
            num_scalar_prefetch=2,
            grid=(steps,),
            in_specs=in_specs,
            out_specs=[pl.BlockSpec(memory_space=pl.ANY)] * 2,
            scratch_shapes=[
                pltpu.VMEM((SLOTS, 2 * patch + 16, rows), jnp.float32),
                pltpu.VMEM((SLOTS, rows, HD), jnp.float32),
                pltpu.VMEM(sums_shape, jnp.float32),
                pltpu.SemaphoreType.DMA((4,)),
            ],
        ),
        compiler_params=pltpu.CompilerParams(vmem_limit_bytes=GRANT),
        cost_estimate=pl.CostEstimate(
            flops=cost * pairs * 4 * rows * rows * HD,
            bytes_accessed=steps * wide * HD * 2 * sum(spec.block_shape[0] for spec in in_specs[:4]),
            transcendentals=cost * pairs * rows * rows,
        ),
    )(scalars, mask, *arrays)


def token_sums(
    scalars, queries, keys, values, span_mask, head_gain, patch_weight, prepare
):
    rows = queries.shape[0]
    half = rows // 2
    heads = NEAR_HEADS + MIDDLE_HEADS + FAR_HEADS
    in_place = lambda array: pltpu.with_memory_space_constraint(array, pltpu.HBM)
    queries, keys, values = (in_place(array) for array in (queries, keys, values))

    def send(value, *pairs):
        return in_place(lax.ppermute(value, "span", list(pairs)))

    def tokens(entry, shift, count):
        return [(0, 0, rows, (OWN, entry) if entry else (OWN,), shift, count)]

    def pairs_of(entry, shift, count):
        entries = (entry,) if entry else ()
        return [
            piece
            for part in (1, 2)
            for piece in (
                (part, 0, half, (OWN,) + entries, shift, count),
                (3, (part - 1) * half, half, entries, shift, count),
            )
        ]

    handed = pack_handed(keys, values, heads)
    received = lax.ppermute(handed, "slab", SWAP)
    up, down = message(
        scalars,
        [
            pairs_of(UP, 0, NEAR_HEADS),
            tokens(DOWN, 0, MIDDLE_HEADS) + pairs_of(DOWN, 0, MIDDLE_HEADS),
        ],
        (queries, keys, values, received),
        "pack_first",
    )
    source, _ = lax.optimization_barrier((received, down))
    up = send(up, (0, 1), (1, 2))
    down = send(down, (1, 0), (2, 1), (3, 2))
    up_two, two, far_all, far_pair = message(
        scalars,
        [
            pairs_of(None, MIDDLE, MIDDLE_HEADS),
            tokens(None, 0, NEAR_HEADS) + pairs_of(None, 0, NEAR_HEADS),
            tokens(None, FAR, FAR_HEADS) + pairs_of(None, FAR, FAR_HEADS),
            pairs_of(None, FAR, FAR_HEADS),
        ],
        (queries, keys, values, source),
        "pack_second",
    )
    anchor = two
    up_two = send(up_two, (0, 2))
    two = send(two, (3, 1))
    far_next = send(far_all, (2, 3), (1, 0))
    far_pair, prepared = lax.optimization_barrier((far_pair, prepare(anchor)))
    far_two = send(far_pair, (1, 3))
    far_three = send(far_pair, (0, 3))

    span_mask, head_gain, patch_weight, _ = lax.optimization_barrier(
        (span_mask, head_gain, patch_weight, anchor)
    )
    mask = span_mask.reshape(-1)
    weight = patch_weight.T
    own = (queries, keys, values, received, weight, head_gain[None, :])
    run = functools.partial(attend, own=own, scalars=scalars, mask=mask)

    here, back_one, on_one = OWN_TOKENS, Tokens(None, (0,)), Tokens(1, (1,))
    back_two = Tokens(None, (2,))
    sums = run(
        MIDDLE_HEADS // 2,
        2,
        MAIN,
        MAIN_CAP,
        sums=None,
        payloads=[up, down, up_two],
        variants={
            0: [(2, [(here, 0, 0, [(here, 0)]), (on_one, 1, 1, [(here, 0), (on_one, 1)])])],
            1: [
                (
                    2,
                    [
                        (on_one, 1, 2, [(back_one, 0), (here, 1), (on_one, 2)]),
                        (here, 0, 1, [(back_one, 0), (here, 1)]),
                    ],
                )
            ],
            2: [
                (
                    2,
                    [
                        (on_one, 1, 3, [(back_two, 0), (back_one, 1), (here, 2), (on_one, 3)]),
                        (here, 0, 2, [(back_two, 0), (back_one, 1), (here, 2)]),
                    ],
                )
            ],
        },
        more=False,
        name="main_heads",
    )
    on_two, beside = Tokens(2, (2,)), Tokens(3, (3,))
    two_back, three_back = Tokens(None, (4,)), Tokens(None, (5,))
    extras = [Tokens(None, (), lane) for lane in range(2)]
    sums, prepared = lax.optimization_barrier((sums, prepared))
    sums = run(
        NEAR_HEADS // 2,
        2,
        FINAL,
        FINAL_CAP,
        sums=sums,
        payloads=[up, down, two, far_next, far_two, far_three],
        variants={
            0: [
                (1, [(here, 0, 0, [(here, 0)]), (beside, 1, 1, [(here, 0), (beside, 1)])]),
                (2, [(head, 0, 0, [(head, 0)]) for head in extras]),
            ],
            1: [(2, [(on_two, 2, 3, [(back_one, 0), (here, 1), (on_one, 2), (on_two, 3)])])],
            3: [
                (
                    1,
                    [
                        (here, 0, 3, [(three_back, 0), (two_back, 1), (beside, 2), (here, 3)]),
                        (beside, 2, 2, [(three_back, 0), (two_back, 1), (beside, 2)]),
                    ],
                )
            ],
        },
        more=True,
        name="final_heads",
        cost=4,
    )
    return sums, prepared


def noise_window(grid, constants):
    height, breadth, _ = grid.shape
    slab = lax.axis_index("slab")
    edge = jnp.where(slab == 0, grid[:, breadth - 1], grid[:, 0])
    edge = lax.ppermute(edge, "slab", SWAP)[:, None]
    grid = jnp.concatenate(
        [
            jnp.where(slab == 1, edge, 0.0),
            grid,
            jnp.where(slab == 0, edge, 0.0),
            jnp.zeros((height, WINDOW - breadth - 2, grid.shape[2]), grid.dtype),
        ],
        axis=1,
    )
    head = lax.axis_index("head")
    edge = jnp.where(head == 0, grid[height - 1], grid[0])
    count = constants.shape[1]
    extra = jnp.pad(constants, ((0, 8 - constants.shape[0]), (0, HD - count)))
    edge = jnp.pad(edge, ((0, 0), (0, HD - edge.shape[1])))
    sent = lax.ppermute(jnp.concatenate([edge, extra], axis=0), "head", SWAP)
    edge = sent[None, :WINDOW, : grid.shape[2]]
    constants = constants + sent[WINDOW : WINDOW + constants.shape[0], :count]
    grid = jnp.concatenate(
        [jnp.where(head == 1, edge, 0.0), grid, jnp.where(head == 0, edge, 0.0)], axis=0
    )
    return grid.reshape((height + 2) * WINDOW, grid.shape[2]), constants.T


def cell_selector(height, breadth):
    cell = lax.broadcasted_iota(jnp.int32, ((height + 2) * WINDOW, 4 * TROWS * TCOLS), 0)
    column = lax.broadcasted_iota(jnp.int32, cell.shape, 1)
    y = lax.axis_index("head") * height + cell // WINDOW - 1
    x = lax.axis_index("slab") * breadth + cell % WINDOW - 1
    inside = (y >= 0) & (y < 2 * TROWS) & (x >= 0) & (x < 2 * TCOLS)
    inside = inside & (cell % WINDOW < breadth + 2)
    target = ((y % 2) * 2 + x % 2) * (TROWS * TCOLS) + (y // 2) * TCOLS + x // 2
    return (inside & (column == target)).astype(jnp.bfloat16)


def band_kernel(weight, band):
    outputs = weight.shape[1]
    band[...] = jnp.zeros_like(band)
    for row_tap in range(3):
        for col_tap in range(3):
            for frame_tap in range(3):
                start = ((3 * frame_tap + row_tap) * 3 + col_tap) * LAT_CH
                block = weight[start : start + LAT_CH]
                for frame in range(FRAMES_SPAN):
                    at = (col_tap * (FRAMES_SPAN + 2) + frame + frame_tap) * LAT_CH
                    band[
                        row_tap, at : at + LAT_CH, frame * outputs : (frame + 1) * outputs
                    ] = block


def banded_weight(conv_weight):
    shape = (3, 3 * (FRAMES_SPAN + 2) * LAT_CH, FRAMES_SPAN * conv_weight.shape[1])
    return pl.pallas_call(
        band_kernel,
        name="band",
        out_shape=jax.ShapeDtypeStruct(shape, conv_weight.dtype),
        in_specs=[pl.BlockSpec(memory_space=pltpu.VMEM)],
        out_specs=pl.BlockSpec(memory_space=pltpu.VMEM),
        compiler_params=pltpu.CompilerParams(vmem_limit_bytes=GRANT),
        cost_estimate=pl.CostEstimate(
            flops=0, bytes_accessed=2 * math.prod(shape), transcendentals=0
        ),
    )(conv_weight)


def finish_kernel(
    scalars, mine, other, noise, before, selector, band, bias, constants, clean, decoded, cells
):
    frames, height, breadth, channels = clean.shape
    patch = constants.shape[0]
    first = scalars[SLAB] == 0
    sums = jnp.concatenate(
        [jnp.where(first, mine[...], other[...]), jnp.where(first, other[...], mine[...])], axis=0
    )
    feature_width = HEADS * HD
    row_mean = sums[patch : patch + 1] / feature_width
    spread = sums[patch + STAT_ROWS : patch + STAT_ROWS + 1] / feature_width - row_mean * row_mean
    velocity = (
        lax.rsqrt(spread + norm_eps) * (sums[:patch] - constants[:, 0:1] * row_mean)
        + constants[:, 1:2]
    )
    tokens = TROWS * TCOLS
    lane = lax.broadcasted_iota(jnp.int32, velocity.shape, 1)
    velocity = jnp.where((lane >= 2 * tokens) | (scalars[PLACE] > 0), velocity, 0.0)
    columns = jnp.concatenate(
        [
            jnp.concatenate(
                [
                    velocity[
                        part * channels : (part + 1) * channels,
                        frame * tokens : (frame + 1) * tokens,
                    ]
                    for part in range(4)
                ],
                axis=1,
            )
            for frame in range(frames + 2)
        ],
        axis=0,
    )
    high = columns.astype(jnp.bfloat16)
    low = (columns - high.astype(jnp.float32)).astype(jnp.bfloat16)
    chosen = sum(
        lax.dot_general(
            selector[...], part, (((1,), (1,)), ((), ())), preferred_element_type=jnp.float32
        )
        for part in (high, low)
    )
    count = (height + 2) * WINDOW
    cells[:count] = (
        jnp.concatenate([before[...], noise[...]], axis=1) - noise_level * chosen
    )
    cells[count:] = jnp.zeros_like(cells[count:])
    for frame in range(frames):
        lanes = slice((frame + 2) * channels, (frame + 3) * channels)
        for y in range(height):
            start = (y + 1) * WINDOW + 1
            clean[frame, y] = cells[start : start + breadth, lanes]
    shifted = jnp.concatenate(
        [cells[tap : tap + count] for tap in range(3)], axis=1
    ).astype(jnp.bfloat16)
    total = jnp.broadcast_to(bias[...], (height * breadth, bias.shape[1]))
    for tap in range(3):
        block = jnp.concatenate(
            [
                shifted[(y + tap) * WINDOW : (y + tap) * WINDOW + breadth]
                for y in range(height)
            ],
            axis=0,
        )
        total = total + jnp.dot(block, band[tap], preferred_element_type=jnp.float32)
    outputs = decoded.shape[3]
    total = total.astype(decoded.dtype)
    for frame in range(frames):
        decoded[frame] = total[:, frame * outputs : (frame + 1) * outputs].reshape(
            height, breadth, outputs
        )


def finish(
    scalars, mine, other, noise, before, selector, band, bias, constants, shape, outputs
):
    whole = pl.BlockSpec(memory_space=pltpu.VMEM)
    frames, height, breadth, channels = shape
    rows = (height + 2) * WINDOW
    return pl.pallas_call(
        finish_kernel,
        name="finish",
        out_shape=(
            jax.ShapeDtypeStruct(shape, jnp.float32),
            jax.ShapeDtypeStruct((frames, height, breadth, outputs), jnp.bfloat16),
        ),
        in_specs=[pl.BlockSpec(memory_space=pltpu.SMEM)] + [whole] * 8,
        out_specs=(whole, whole),
        scratch_shapes=[pltpu.VMEM((rows + 8, (frames + 2) * channels), jnp.float32)],
        compiler_params=pltpu.CompilerParams(vmem_limit_bytes=GRANT),
    )(scalars, mine, other, noise, before, selector, band, bias, constants)


def per_device(
    queries,
    keys,
    values,
    span_mask,
    head_gain,
    head_shift,
    patch_weight,
    noisy_latent,
    conv_weight,
    conv_bias,
):
    heads_dev = queries.shape[1] // HD
    if not plan_fits(
        heads_dev, lax.axis_size("span"), lax.axis_size("slab"), lax.axis_size("head")
    ):
        return gathered_plan(
            queries,
            keys,
            values,
            span_mask,
            head_gain,
            head_shift,
            patch_weight,
            noisy_latent,
            conv_weight,
            conv_bias,
        )
    place = lax.axis_index("span")
    slab = lax.axis_index("slab")
    scalars = scalar_operand(heads_dev // lax.axis_size("slab"))
    def prepare(anchor):
        noise, weight, gain, shift, taps, bias, _ = lax.optimization_barrier(
            (noisy_latent, patch_weight, head_gain, head_shift, conv_weight, conv_bias, anchor)
        )
        _, height, breadth, _ = noise.shape
        noise = noise.transpose(1, 2, 0, 3).reshape(height, breadth, -1)
        wide_weight = weight.T.astype(jnp.float32)
        constants = jnp.stack(
            [
                jnp.sum(wide_weight * gain[None, :], axis=1),
                jnp.sum(wide_weight * shift[None, :], axis=1),
            ]
        )
        window, constants = noise_window(noise, constants)
        return (
            window,
            window[:, -2 * LAT_CH :].reshape(16, -1),
            constants,
            cell_selector(height, breadth),
            banded_weight(taps),
            jnp.tile(bias, FRAMES_SPAN)[None, :],
        )

    (mine, theirs), (noise, ahead, constants, selector, band, bias) = token_sums(
        scalars,
        queries,
        keys,
        values,
        span_mask,
        head_gain,
        patch_weight,
        prepare,
    )
    mine = mine + lax.ppermute(theirs, "slab", SWAP)
    own, after, third = mine[0], mine[1], mine[2]
    skip = TROWS * TCOLS
    from_one = lax.ppermute(
        jnp.concatenate([jnp.concatenate([own[:, skip:], after], axis=1), ahead], axis=0),
        "span",
        [(0, 1), (1, 2), (2, 3)],
    )
    before = from_one[own.shape[0] :].reshape(-1, 2 * LAT_CH)
    from_one = from_one[: own.shape[0]]
    to_current = lax.ppermute(third, "span", [(1, 3), (3, 2)])
    to_before = lax.ppermute(after[:, skip:], "span", [(0, 2), (1, 3)])
    kept = jnp.concatenate([jnp.where(place == 3, third[:, skip:], 0.0), own], axis=1)
    total = kept + from_one + jnp.concatenate([to_before, to_current], axis=1)
    total = total + lax.ppermute(total, "head", SWAP)
    other = lax.ppermute(total, "slab", SWAP)
    return finish(
        scalars,
        total,
        other,
        noise,
        before,
        selector,
        band,
        bias,
        constants,
        noisy_latent.shape,
        conv_weight.shape[1],
    )


def solution(mesh):
    placed = (
        P(("groups", "span"), "head"),
        P(("groups", "span", "slab"), "head"),
        P(("groups", "span", "slab"), "head"),
        P("groups", None),
        P("head"),
        P("head"),
        P("head", None),
        P(("groups", "span"), "head", "slab", None),
        P(),
        P(),
    )
    return jax.shard_map(
        per_device,
        mesh=mesh,
        in_specs=placed,
        out_specs=(
            P(("groups", "span"), "head", "slab", None),
            P(("groups", "span"), "head", "slab", None),
        ),
        check_vma=False,
    )
```

```python
import functools
import math
import typing

import jax
import jax.numpy as jnp
import numpy as np
from jax import lax
from jax.experimental import pallas as pl
from jax.experimental.pallas import tpu as pltpu
from jax.sharding import PartitionSpec as P

HEADS = 40
HD = 128
LAT_CH = 16
FRAMES_SPAN = 3
TROWS = 8
TCOLS = 16


neg_big = -1e30
noise_level = 0.75
norm_eps = 1e-06


def with_halo(cells, sides, width):
    for axis, dim in sides:
        count = lax.axis_size(axis)
        ends = count - 1
        head = lax.slice_in_dim(cells, 0, width, axis=dim)
        tail = lax.slice_in_dim(cells, cells.shape[dim] - width, cells.shape[dim], axis=dim)
        cells = jnp.concatenate(
            [
                lax.ppermute(tail, axis, [(i, (i + 1) % count) for i in range(ends)]),
                cells,
                lax.ppermute(head, axis, [((i + 1) % count, i) for i in range(ends)]),
            ],
            axis=dim,
        )
    return cells


def from_behind(value, axis, by):
    size = lax.axis_size(axis)
    pairs = [(i, i + by) for i in range(size) if 0 <= i + by < size]
    return lax.ppermute(value, axis, pairs)


def block_length(total_rows):
    block_size = total_rows
    while block_size > 768 and block_size % 2 == 0:
        block_size = block_size // 2
    return block_size


def fold_keys(partial_state, key_value, query_block, mask_row, rows_span):
    keys_piece, values_piece = key_value
    heads_dev = query_block.shape[1]
    piece_rows = keys_piece.shape[0]
    length = block_length(piece_rows)
    span_count = mask_row.shape[0]
    score_scale = 1.0 / math.sqrt(HD)
    span_ids = jnp.arange(span_count, dtype=jnp.int32)

    def one_block(carry_state, block_index):
        running_max, running_sum, weighted = carry_state
        offset = block_index * length
        key_block = lax.dynamic_slice_in_dim(keys_piece, offset, length, 0).reshape(
            length, heads_dev, HD
        )
        value_block = lax.dynamic_slice_in_dim(values_piece, offset, length, 0).reshape(
            length, heads_dev, HD
        )
        key_span = (offset + jnp.arange(length, dtype=jnp.int32)) // rows_span
        allowed = (
            jnp.sum(jnp.where(key_span[:, None] == span_ids[None, :], mask_row[None, :], 0), axis=1)
            > 0
        )
        scores = (
            jnp.einsum("qhd,khd->hqk", query_block, key_block, preferred_element_type=jnp.float32)
            * score_scale
        )
        scores = jnp.where(allowed[None, None, :], scores, neg_big)
        new_max = jnp.maximum(running_max, jnp.max(scores, axis=2))
        weights = jnp.where(allowed[None, None, :], jnp.exp(scores - new_max[:, :, None]), 0.0)
        factor = jnp.exp(running_max - new_max)
        running_sum = running_sum * factor + jnp.sum(weights, axis=2)
        weighted = weighted * factor.T[:, :, None] + jnp.einsum(
            "hqk,khd->qhd",
            weights.astype(jnp.bfloat16),
            value_block,
            preferred_element_type=jnp.float32,
        )
        return ((new_max, running_sum, weighted), None)

    result, unused = lax.scan(
        one_block, partial_state, jnp.arange(piece_rows // length, dtype=jnp.int32)
    )
    return result


def gathered_plan(
    queries,
    keys,
    values,
    span_mask,
    head_gain,
    head_shift,
    patch_weight,
    noisy_latent,
    conv_weight,
    conv_bias,
):
    heads_dev = queries.shape[1] // HD
    slab_count = lax.axis_size("slab")
    col_dev = TCOLS // slab_count
    slab_place = lax.axis_index("slab")
    span_place = lax.axis_index("span")
    mask_row = lax.dynamic_slice_in_dim(span_mask, span_place, 1, 0)[0]
    token_grid = queries.reshape(FRAMES_SPAN, TROWS, TCOLS, queries.shape[-1])
    picked = lax.dynamic_slice_in_dim(token_grid, slab_place * col_dev, col_dev, 2)
    own_queries = picked.reshape(FRAMES_SPAN * TROWS * col_dev, queries.shape[-1]).reshape(
        -1, heads_dev, HD
    )
    query_rows = own_queries.shape[0]
    rows_span = keys.shape[0] * slab_count
    running_max, running_sum, weighted = fold_keys(
        (
            jnp.full((heads_dev, query_rows), neg_big, jnp.float32),
            jnp.zeros((heads_dev, query_rows), jnp.float32),
            jnp.zeros((query_rows, heads_dev, HD), jnp.float32),
        ),
        (
            lax.all_gather(keys, ("span", "slab"), axis=0, tiled=True),
            lax.all_gather(values, ("span", "slab"), axis=0, tiled=True),
        ),
        own_queries,
        mask_row,
        rows_span,
    )
    attended = (
        (weighted / running_sum.T[:, :, None])
        .astype(jnp.bfloat16)
        .reshape(query_rows, heads_dev * HD)
    )
    feature_width = HEADS * HD
    values32 = attended.astype(jnp.float32)
    row_total = jnp.sum(values32, axis=1)
    row_squares = jnp.sum(values32 * values32, axis=1)
    row_total, row_squares = lax.psum((row_total, row_squares), "head")
    row_mean = row_total / feature_width
    spread = row_squares / feature_width - row_mean * row_mean
    normed = (
        (values32 - row_mean[:, None]) * lax.rsqrt(spread + norm_eps)[:, None] * head_gain[None, :]
        + head_shift[None, :]
    ).astype(jnp.bfloat16)
    normed_grid = normed.reshape(FRAMES_SPAN, TROWS, col_dev, normed.shape[-1])
    own_rows = TROWS // lax.axis_size("head")
    picked = normed_grid
    product = jnp.dot(
        picked.reshape(-1, picked.shape[-1]), patch_weight, preferred_element_type=jnp.float32
    )
    velocity = lax.psum_scatter(
        product.reshape(
            FRAMES_SPAN, own_rows * lax.axis_size("head"), col_dev * patch_weight.shape[1]
        )
        .transpose(1, 0, 2)
        .reshape(own_rows * lax.axis_size("head"), -1)
        .astype(jnp.bfloat16),
        "head",
        scatter_dimension=0,
        tiled=True,
    ).astype(jnp.float32)
    rows_dev = velocity.shape[0]
    patch_cells = (
        velocity.reshape(rows_dev, FRAMES_SPAN, col_dev, 2, 2, LAT_CH)
        .transpose(1, 0, 3, 2, 4, 5)
        .reshape(FRAMES_SPAN, 2 * rows_dev, 2 * col_dev, LAT_CH)
    )
    clean_latent = noisy_latent - noise_level * patch_cells
    latent_input = clean_latent.astype(jnp.bfloat16)
    framed = with_halo(latent_input, (("head", 1), ("slab", 2)), 1)
    earlier = from_behind(framed[FRAMES_SPAN - 2 :], "span", 1)
    stacked = jnp.concatenate([earlier, framed], axis=0)
    height = clean_latent.shape[1]
    breadth = clean_latent.shape[2]
    columns = jnp.concatenate(
        [
            stacked[
                frame_tap : frame_tap + FRAMES_SPAN,
                row_tap : row_tap + height,
                col_tap : col_tap + breadth,
                :,
            ]
            for frame_tap in range(3)
            for row_tap in range(3)
            for col_tap in range(3)
        ],
        axis=-1,
    )
    decoded = (
        jnp.dot(
            columns.reshape(FRAMES_SPAN * height * breadth, 27 * LAT_CH),
            conv_weight,
            preferred_element_type=jnp.float32,
        )
        + conv_bias[None, :]
    )
    decoded = decoded.astype(jnp.bfloat16).reshape(
        FRAMES_SPAN, height, breadth, conv_weight.shape[1]
    )
    return (clean_latent, decoded)


NEAR_HEADS = 4
MIDDLE_HEADS = 4
FAR_HEADS = 2
MIDDLE = NEAR_HEADS
FAR = NEAR_HEADS + MIDDLE_HEADS
STAT_ROWS = 8
SLOTS = 3
QUERY_ROWS = 192
SWAP = [(0, 1), (1, 0)]
WINDOW = 32
GRANT = 20 << 20

OWN, OTHER, DOWN, UP, MAIN, MAIN_CAP, FINAL, FINAL_CAP, PLACE, SLAB = range(10)


def plan_fits(heads_dev, span_count, slab_count, head_count):
    return (
        span_count == 4
        and slab_count == 2
        and head_count == 2
        and heads_dev == slab_count * (NEAR_HEADS + MIDDLE_HEADS + FAR_HEADS)
    )


def scalar_operand(heads):
    by_place = np.zeros((4, 12), np.int32)
    by_place[:, OTHER] = heads
    by_place[:, DOWN] = [MIDDLE, MIDDLE, 0, MIDDLE]
    by_place[:, UP] = [0, MIDDLE, 0, 0]
    by_place[:, MAIN] = [MIDDLE, 0, MIDDLE, 0]
    by_place[:, MAIN_CAP] = [1, 1, 1, 0]
    by_place[:, FINAL] = [FAR, 0, 0, FAR]
    by_place[:, FINAL_CAP] = [0, 1, 0, 0]
    by_place[:, PLACE] = range(4)
    by_slab = np.zeros(12, np.int32)
    by_slab[[OWN, OTHER, SLAB]] = heads, -heads, 1
    row = lax.dynamic_slice_in_dim(jnp.array(by_place), lax.axis_index("span"), 1, 0)[0]
    return row + lax.axis_index("slab") * jnp.array(by_slab)


def pack_kernel(inputs, messages, copies, scalars, *refs):
    ins, rest = refs[:inputs], refs[inputs:]
    outs, staged = rest[:messages], rest[messages:-2]
    arrive, leave = rest[-2:]
    arriving = []
    for number, (source, row, rows, entries, shift, target, at, heads) in enumerate(copies):
        head = shift
        for entry in entries:
            head = head + scalars[entry]
        column = pl.multiple_of(head * HD, HD)
        place = staged[target].at[pl.ds(at, rows), :]
        copy = pltpu.make_async_copy(
            ins[source].at[pl.ds(row, rows), pl.ds(column, heads * HD)], place, arrive.at[number]
        )
        copy.start()
        onward = pltpu.make_async_copy(
            place, outs[target].at[pl.ds(at, rows), :], leave.at[number]
        )
        arriving.append((copy, onward))
    for copy, onward in arriving:
        copy.wait()
        onward.start()
    for _, onward in arriving:
        onward.wait()


def pack(scalars, arrays, shapes, copies, name):
    moved = sum(2 * 2 * rows * heads * HD for _, _, rows, _, _, _, _, heads in copies)
    out_shape = [pltpu.HBM(shape, jnp.bfloat16) for shape in shapes]
    in_specs = [pl.BlockSpec(memory_space=pl.ANY)] * len(arrays)
    out_specs = [pl.BlockSpec(memory_space=pl.ANY)] * len(shapes)
    return pl.pallas_call(
        functools.partial(pack_kernel, len(arrays), len(shapes), copies),
        name=name,
        out_shape=out_shape,
        grid_spec=pltpu.PrefetchScalarGridSpec(
            num_scalar_prefetch=1,
            grid=(1,),
            in_specs=in_specs,
            out_specs=out_specs,
            scratch_shapes=[pltpu.VMEM(shape, jnp.bfloat16) for shape in shapes]
            + [
                pltpu.SemaphoreType.DMA((len(copies),)),
                pltpu.SemaphoreType.DMA((len(copies),)),
            ],
        ),
        compiler_params=pltpu.CompilerParams(vmem_limit_bytes=GRANT),
        cost_estimate=pl.CostEstimate(flops=0, bytes_accessed=moved, transcendentals=0),
    )(scalars, *arrays)


def hand_kernel(heads, keys, values, out, arrive):
    column = pl.multiple_of((1 - lax.axis_index("slab")) * heads * HD, heads * HD)
    half = keys.shape[0]
    copies = []
    for number, source in enumerate((keys, values)):
        copy = pltpu.make_async_copy(
            source.at[:, pl.ds(column, heads * HD)],
            out.at[pl.ds(number * half, half), :],
            arrive.at[number],
        )
        copy.start()
        copies.append(copy)
    for copy in copies:
        copy.wait()


def pack_handed(keys, values, heads):
    shape = (2 * keys.shape[0], heads * HD)
    return pl.pallas_call(
        functools.partial(hand_kernel, heads),
        name="pack_handed",
        out_shape=jax.ShapeDtypeStruct(shape, keys.dtype),
        in_specs=[pl.BlockSpec(memory_space=pl.ANY)] * 2,
        out_specs=pl.BlockSpec(memory_space=pltpu.VMEM),
        scratch_shapes=[pltpu.SemaphoreType.DMA((2,))],
        compiler_params=pltpu.CompilerParams(vmem_limit_bytes=GRANT),
        cost_estimate=pl.CostEstimate(
            flops=0, bytes_accessed=4 * math.prod(shape), transcendentals=0
        ),
    )(keys, values)


def message(scalars, pieces, arrays, name):
    copies, shapes = [], []
    for target, parts in enumerate(pieces):
        at = 0
        for source, row, rows, entries, shift, heads in parts:
            copies.append((source, row, rows, entries, shift, target, at, heads))
            at += rows
        shapes.append((at, parts[0][5] * HD))
    return pack(scalars, arrays, shapes, copies, name)


class Tokens(typing.NamedTuple):
    query: int | None = None
    pairs: tuple = ()
    extra: int | None = None


OWN_TOKENS = Tokens()


def attend_kernel(variants, extra, span_count, fresh, wide, final, scalars, mask, *refs):
    if final:
        sources, (weight, gain), brought = refs[:4], refs[4:6], refs[6 : 6 + final]
        sums_in, (mine_out, theirs_out) = refs[6 + final : 8 + final], refs[8 + final : 10 + final]
        folded, squares, carried, moved, *own_refs = refs[10 + final : 18 + final]
        query_own, key_own, value_own, received = own_refs
        more, payloads, landed = refs[18 + final : 22 + final], refs[22 + final : -1], refs[-1]
    else:
        query_own, key_own, value_own, received, weight, gain = refs[:6]
        mine_out, theirs_out, folded, squares, carried, moved = refs[-6:]
        payloads, sums_in = refs[6:-6], None
    rows = query_own.shape[0]
    half = rows // 2
    step = pl.program_id(0)
    to_exp2 = math.log2(math.e) / math.sqrt(HD)
    active = functools.reduce(
        lambda a, b: a | b, [scalars[PLACE] == place for place in variants]
    )

    last_step = step == pl.num_programs(0) - 1
    part = carried.shape[1] // 2
    halves = [
        carried.at[:, pl.ds(pl.multiple_of(number * part, part), part)]
        for number in (scalars[SLAB], 1 - scalars[SLAB])
    ]
    fetches = (
        []
        if fresh
        else [
            pltpu.make_async_copy(sums_in[number], halves[number], moved.at[number])
            for number in range(2)
        ]
    )

    @pl.when((step == 0) & active)
    def _():
        folded[...] = jnp.zeros_like(folded)
        squares[...] = jnp.zeros_like(squares)
        for fetch in fetches:
            fetch.start()

    def lanes_of(head):
        return slice(head * HD, (head + 1) * HD)

    def query_of(source, lanes):
        if source is OWN_TOKENS:
            return query_own[:, lanes]
        if source.extra is not None:
            return more[0][:, lanes_of(source.extra)]
        return payloads[source.query][:rows, lanes]

    def pair_of(source, lanes):
        if source is OWN_TOKENS:
            parts = (
                key_own[:, lanes],
                received[:half, lanes],
                value_own[:, lanes],
                received[half:, lanes],
            )
        elif source.extra is not None:
            own = lanes_of(source.extra)
            parts = (more[1][:, own], more[3][:half, own], more[2][:, own], more[3][half:, own])
        else:
            payload = payloads[source.pairs[0]]
            start = payload.shape[0] - 2 * rows
            return payload[start : start + rows, lanes], payload[start + rows :, lanes]
        return jnp.concatenate(parts[:2], axis=0), jnp.concatenate(parts[2:], axis=0)

    def projector(extra_head, lanes):
        if final:
            head = scalars[OWN] + (
                scalars[FINAL] + lanes.start // HD if extra_head is None else extra_head
            )
            lanes = pl.ds(pl.multiple_of(head * HD, HD), HD)
        scaled = weight[:, lanes].astype(jnp.float32) * gain[:, lanes]
        high = scaled.astype(jnp.bfloat16)
        low = (scaled - high.astype(jnp.float32)).astype(jnp.bfloat16)
        return jnp.concatenate([high, low, jnp.ones((16, HD), jnp.bfloat16)], axis=0)

    def one_query(head, source, slot, query_span, key_sources):
        lanes = lanes_of(head)
        query = query_of(source, lanes)
        pairs = [pair_of(key_source, lanes) for key_source, _ in key_sources]
        open_to = [
            None if key_span == query_span else mask[query_span * span_count + key_span] > 0
            for _, key_span in key_sources
        ]
        keys_in = jnp.concatenate([pair[0] for pair in pairs], axis=0)
        ones_block = jnp.ones((rows, HD), jnp.bfloat16)
        values_in = jnp.concatenate(
            [jnp.concatenate([pair[1], ones_block], axis=1) for pair in pairs], axis=0
        )
        pieces = []
        for row in range(0, rows, QUERY_ROWS):
            score = lax.dot_general(
                query[row : row + QUERY_ROWS],
                keys_in,
                (((1,), (1,)), ((), ())),
                preferred_element_type=jnp.float32,
            )
            best = None
            for number, is_open in enumerate(open_to):
                start = number * rows
                block = score[:, start : start + HD]
                for lane in range(HD, rows, HD):
                    block = jnp.maximum(block, score[:, start + lane : start + lane + HD])
                if is_open is not None:
                    block = jnp.where(is_open, block, neg_big)
                best = block if best is None else jnp.maximum(best, block)
            top = jnp.max(best, axis=1, keepdims=True)
            weights = []
            for number, is_open in enumerate(open_to):
                start = number * rows
                shift = top if is_open is None else jnp.where(is_open, top, -neg_big)
                weights.append(
                    jnp.exp2((score[:, start : start + rows] - shift) * to_exp2).astype(jnp.bfloat16)
                )
            both = jnp.dot(
                jnp.concatenate(weights, axis=1), values_in, preferred_element_type=jnp.float32
            )
            pieces.append((both[:, :HD] / both[:, HD:]).astype(jnp.bfloat16))
        attended = jnp.concatenate(pieces, axis=0)
        folded[slot] += lax.dot_general(
            projector(source.extra, lanes),
            attended,
            (((1,), (1,)), ((), ())),
            preferred_element_type=jnp.float32,
        )
        wide = attended.astype(jnp.float32)
        squares[slot] += wide * wide

    def fetch_head(number, head, used):
        copies = []
        place = pl.ds(number * HD, HD)
        for index, (source, target) in enumerate(zip(sources, own_refs if used else more)):
            column = head if index == 3 else scalars[OWN] + head
            column = pl.ds(pl.multiple_of(column * HD, HD), HD)
            copies.append((source.at[:, column], target.at[:, place]))
        copies += [(brought[index].at[:, place], payloads[index].at[:, place]) for index in used]
        started = []
        for index, (source, target) in enumerate(copies):
            slot = number if used else 4 + number
            copy = pltpu.make_async_copy(source, target, landed.at[slot, index])
            copy.start()
            started.append(copy)
        return started

    for place, groups in variants.items():
        if final:
            count, tasks, extra_tasks = groups
            used = set()
            for source, _, _, key_sources in tasks:
                for tokens in [source] + [key_source for key_source, _ in key_sources]:
                    used |= set(tokens.pairs) | ({tokens.query} if tokens.query is not None else set())

            @pl.when(scalars[PLACE] == place)
            def _():
                waits = [
                    fetch_head(head, scalars[FINAL] + head, sorted(used)) for head in range(count)
                ]
                extra_waits = [
                    fetch_head(number, number, ()) for number in range(len(extra_tasks))
                ]
                for head in range(count):
                    for copy in waits[head]:
                        copy.wait()
                    for task in tasks:
                        one_query(head, *task)
                for copies, task in zip(extra_waits, extra_tasks):
                    for copy in copies:
                        copy.wait()
                    one_query(0, *task)

            continue
        for steps, tasks in groups:

            @pl.when((scalars[PLACE] == place) & (step < steps))
            def _():
                for head in range(wide):
                    for task in tasks:
                        one_query(head, *task)

    def store():
        copies = [
            pltpu.make_async_copy(halves[number], out, moved.at[2 + number])
            for number, out in enumerate((mine_out, theirs_out))
        ]
        for copy in copies:
            copy.start()
        for copy in copies:
            copy.wait()

    if fresh:

        @pl.when(last_step & jnp.logical_not(active))
        def _():
            carried[...] = jnp.zeros_like(carried)
            store()

    @pl.when(last_step & active)
    def _():
        ones_rows = jnp.ones((STAT_ROWS, HD), jnp.bfloat16)
        patch = weight.shape[0]
        for fetch in fetches:
            fetch.wait()
        if fresh:
            carried[...] = jnp.zeros_like(carried)

        def finish_slot(slot):
            left = squares[slot]
            total = jnp.zeros((STAT_ROWS, rows), jnp.float32)
            for _ in range(3):
                piece = left.astype(jnp.bfloat16)
                left = left - piece.astype(jnp.float32)
                total = total + lax.dot_general(
                    ones_rows, piece, (((1,), (1,)), ((), ())), preferred_element_type=jnp.float32
                )
            done = folded[slot]
            carried[slot] += jnp.concatenate(
                [
                    done[:patch] + done[patch : 2 * patch],
                    done[2 * patch : 2 * patch + STAT_ROWS],
                    total,
                ],
                axis=0,
            )

        for place, groups in variants.items():

            @pl.when(scalars[PLACE] == place)
            def _():
                tasks = groups[1] if final else [task for _, some in groups for task in some]
                for slot in sorted({task[1] for task in tasks}):
                    finish_slot(slot)

        store()


def attend(steps, wide, first, cap, own, scalars, mask, sums, payloads, variants, name, cost=1):
    queries, keys, values, received, weight, gain = own
    rows = queries.shape[0]
    half = rows // 2
    patch = weight.shape[0]

    def moving(i, scalars):
        return jnp.minimum(i, scalars[cap])

    def column(height, own_column):
        def index(i, scalars, mask):
            head = scalars[first] + scalars[OWN] if own_column else scalars[first]
            return (0, head // wide + moving(i, scalars))

        return pl.BlockSpec((height, wide * HD), index)

    def payload_column(payload):
        last = payload.shape[1] // (wide * HD) - 1

        def index(i, scalars, mask):
            return (0, jnp.minimum(moving(i, scalars), last))

        return pl.BlockSpec((payload.shape[0], wide * HD), index)

    in_specs = [
        column(rows, True),
        column(half, True),
        column(half, True),
        column(rows, False),
        column(patch, True),
        column(1, True),
    ]
    arrays = [queries, keys, values, received, weight, gain]
    in_specs += [payload_column(payload) for payload in payloads]
    arrays += payloads
    fresh = sums is None
    sums_shape = (SLOTS, patch + 2 * STAT_ROWS, rows)
    scratch = [
        pltpu.VMEM((SLOTS, 2 * patch + 16, rows), jnp.float32),
        pltpu.VMEM((SLOTS, rows, HD), jnp.float32),
        pltpu.VMEM(sums_shape, jnp.float32),
        pltpu.SemaphoreType.DMA((4,)),
    ]
    aliases = {}
    if not fresh:
        anywhere = pl.BlockSpec(memory_space=pl.ANY)
        whole = lambda array: pl.BlockSpec(array.shape, lambda i, scalars, mask: (0, 0))
        in_specs = [anywhere] * 4 + [whole(weight), whole(gain)] + [anywhere] * len(payloads)
        scratch += 2 * [
            pltpu.VMEM((height, 4 * HD), jnp.bfloat16) for height in (rows, half, half, rows)
        ]
        scratch += [pltpu.VMEM(payload.shape, payload.dtype) for payload in payloads]
        scratch.append(pltpu.SemaphoreType.DMA((8, 4 + len(payloads))))
        aliases = {2 + len(arrays): 0, 3 + len(arrays): 1}
        in_specs += [anywhere] * 2
        arrays += sums
    flops = 4 * rows * rows * HD * cost * 16
    span_count = math.isqrt(mask.shape[0])
    final = 0 if fresh else len(payloads)
    return pl.pallas_call(
        functools.partial(attend_kernel, variants, 0, span_count, fresh, wide, final),
        name=name,
        out_shape=[pltpu.HBM((SLOTS, sums_shape[1] // 2, rows), jnp.float32)] * 2,
        input_output_aliases=aliases,
        grid_spec=pltpu.PrefetchScalarGridSpec(
            num_scalar_prefetch=2,
            grid=(steps,),
            in_specs=in_specs,
            out_specs=[pl.BlockSpec(memory_space=pl.ANY)] * 2,
            scratch_shapes=scratch,
        ),
        compiler_params=pltpu.CompilerParams(vmem_limit_bytes=GRANT),
        cost_estimate=pl.CostEstimate(
            flops=flops,
            bytes_accessed=4 * HD * 2 * 3 * rows,
            transcendentals=flops // (4 * HD),
        ),
    )(scalars, mask, *arrays)


def token_sums(
    scalars, queries, keys, values, span_mask, head_gain, patch_weight, prepare
):
    rows = queries.shape[0]
    half = rows // 2
    heads = NEAR_HEADS + MIDDLE_HEADS + FAR_HEADS
    in_place = lambda array: pltpu.with_memory_space_constraint(array, pltpu.HBM)
    queries, keys, values = (in_place(array) for array in (queries, keys, values))

    def send(value, *pairs):
        return in_place(lax.ppermute(value, "span", list(pairs)))

    def tokens(entry, shift, count):
        return [(0, 0, rows, (OWN, entry) if entry else (OWN,), shift, count)]

    def pairs_of(entry, shift, count):
        entries = (entry,) if entry else ()
        return [
            piece
            for part in (1, 2)
            for piece in (
                (part, 0, half, (OWN,) + entries, shift, count),
                (3, (part - 1) * half, half, entries, shift, count),
            )
        ]

    handed = pack_handed(keys, values, heads)
    received = lax.ppermute(handed, "slab", SWAP)
    up, down = message(
        scalars,
        [
            pairs_of(UP, 0, NEAR_HEADS),
            tokens(DOWN, 0, MIDDLE_HEADS) + pairs_of(DOWN, 0, MIDDLE_HEADS),
        ],
        (queries, keys, values, received),
        "pack_first",
    )
    source, _ = lax.optimization_barrier((received, down))
    up = send(up, (0, 1), (1, 2))
    down = send(down, (1, 0), (2, 1), (3, 2))
    up_two, two, far_all, far_pair = message(
        scalars,
        [
            pairs_of(None, MIDDLE, MIDDLE_HEADS),
            tokens(None, 0, NEAR_HEADS) + pairs_of(None, 0, NEAR_HEADS),
            tokens(None, FAR, FAR_HEADS) + pairs_of(None, FAR, FAR_HEADS),
            pairs_of(None, FAR, FAR_HEADS),
        ],
        (queries, keys, values, source),
        "pack_second",
    )
    anchor = two
    up_two = send(up_two, (0, 2))
    two = send(two, (3, 1))
    far_next = send(far_all, (2, 3), (1, 0))
    far_pair, prepared = lax.optimization_barrier((far_pair, prepare(anchor)))
    far_two = send(far_pair, (1, 3))
    far_three = send(far_pair, (0, 3))

    span_mask, head_gain, patch_weight, _ = lax.optimization_barrier(
        (span_mask, head_gain, patch_weight, anchor)
    )
    mask = span_mask.reshape(-1)
    weight = patch_weight.T
    own = (queries, keys, values, received, weight, head_gain[None, :])
    run = functools.partial(attend, own=own, scalars=scalars, mask=mask)

    here, back_one, on_one = OWN_TOKENS, Tokens(None, (0,)), Tokens(1, (1,))
    back_two = Tokens(None, (2,))
    sums = run(
        MIDDLE_HEADS // 2,
        2,
        MAIN,
        MAIN_CAP,
        sums=None,
        payloads=[up, down, up_two],
        variants={
            0: [(2, [(here, 0, 0, [(here, 0)]), (on_one, 1, 1, [(here, 0), (on_one, 1)])])],
            1: [
                (
                    2,
                    [
                        (on_one, 1, 2, [(back_one, 0), (here, 1), (on_one, 2)]),
                        (here, 0, 1, [(back_one, 0), (here, 1)]),
                    ],
                )
            ],
            2: [
                (
                    2,
                    [
                        (on_one, 1, 3, [(back_two, 0), (back_one, 1), (here, 2), (on_one, 3)]),
                        (here, 0, 2, [(back_two, 0), (back_one, 1), (here, 2)]),
                    ],
                )
            ],
        },
        name="main_heads",
    )
    on_two, beside = Tokens(2, (2,)), Tokens(3, (3,))
    two_back, three_back = Tokens(None, (4,)), Tokens(None, (5,))
    extras = [Tokens(None, (), lane) for lane in range(NEAR_HEADS)]
    sums, prepared = lax.optimization_barrier((sums, prepared))
    sums = run(
        1,
        1,
        FINAL,
        FINAL_CAP,
        sums=sums,
        payloads=[up, down, two, far_next, far_two, far_three],
        variants={
            0: (
                FAR_HEADS,
                [(here, 0, 0, [(here, 0)]), (beside, 1, 1, [(here, 0), (beside, 1)])],
                [(head, 0, 0, [(head, 0)]) for head in extras],
            ),
            1: (
                NEAR_HEADS,
                [(on_two, 2, 3, [(back_one, 0), (here, 1), (on_one, 2), (on_two, 3)])],
                [],
            ),
            3: (
                FAR_HEADS,
                [
                    (here, 0, 3, [(three_back, 0), (two_back, 1), (beside, 2), (here, 3)]),
                    (beside, 2, 2, [(three_back, 0), (two_back, 1), (beside, 2)]),
                ],
                [],
            ),
        },
        name="final_heads",
        cost=4,
    )
    return sums, prepared


def noise_window(grid, constants):
    height, breadth, _ = grid.shape
    slab = lax.axis_index("slab")
    edge = jnp.where(slab == 0, grid[:, breadth - 1], grid[:, 0])
    edge = lax.ppermute(edge, "slab", SWAP)[:, None]
    grid = jnp.concatenate(
        [
            jnp.where(slab == 1, edge, 0.0),
            grid,
            jnp.where(slab == 0, edge, 0.0),
            jnp.zeros((height, WINDOW - breadth - 2, grid.shape[2]), grid.dtype),
        ],
        axis=1,
    )
    head = lax.axis_index("head")
    edge = jnp.where(head == 0, grid[height - 1], grid[0])
    count = constants.shape[1]
    extra = jnp.pad(constants, ((0, 8 - constants.shape[0]), (0, HD - count)))
    edge = jnp.pad(edge, ((0, 0), (0, HD - edge.shape[1])))
    sent = lax.ppermute(jnp.concatenate([edge, extra], axis=0), "head", SWAP)
    edge = sent[None, :WINDOW, : grid.shape[2]]
    constants = constants + sent[WINDOW : WINDOW + constants.shape[0], :count]
    grid = jnp.concatenate(
        [jnp.where(head == 1, edge, 0.0), grid, jnp.where(head == 0, edge, 0.0)], axis=0
    )
    return grid.reshape((height + 2) * WINDOW, grid.shape[2]), constants.T


def cell_selector(height, breadth):
    cell = lax.broadcasted_iota(jnp.int32, ((height + 2) * WINDOW, 4 * TROWS * TCOLS), 0)
    column = lax.broadcasted_iota(jnp.int32, cell.shape, 1)
    y = lax.axis_index("head") * height + cell // WINDOW - 1
    x = lax.axis_index("slab") * breadth + cell % WINDOW - 1
    inside = (y >= 0) & (y < 2 * TROWS) & (x >= 0) & (x < 2 * TCOLS)
    inside = inside & (cell % WINDOW < breadth + 2)
    target = ((y % 2) * 2 + x % 2) * (TROWS * TCOLS) + (y // 2) * TCOLS + x // 2
    return (inside & (column == target)).astype(jnp.bfloat16)


def band_kernel(weight, band):
    outputs = weight.shape[1]
    band[...] = jnp.zeros_like(band)
    for row_tap in range(3):
        for col_tap in range(3):
            for frame_tap in range(3):
                start = ((3 * frame_tap + row_tap) * 3 + col_tap) * LAT_CH
                block = weight[start : start + LAT_CH]
                for frame in range(FRAMES_SPAN):
                    at = (col_tap * (FRAMES_SPAN + 2) + frame + frame_tap) * LAT_CH
                    band[
                        row_tap, at : at + LAT_CH, frame * outputs : (frame + 1) * outputs
                    ] = block


def banded_weight(conv_weight):
    shape = (3, 3 * (FRAMES_SPAN + 2) * LAT_CH, FRAMES_SPAN * conv_weight.shape[1])
    return pl.pallas_call(
        band_kernel,
        name="band",
        out_shape=jax.ShapeDtypeStruct(shape, conv_weight.dtype),
        in_specs=[pl.BlockSpec(memory_space=pltpu.VMEM)],
        out_specs=pl.BlockSpec(memory_space=pltpu.VMEM),
        compiler_params=pltpu.CompilerParams(vmem_limit_bytes=GRANT),
        cost_estimate=pl.CostEstimate(
            flops=0, bytes_accessed=2 * math.prod(shape), transcendentals=0
        ),
    )(conv_weight)


def finish_kernel(
    scalars, mine, other, noise, before, selector, band, bias, constants, clean, decoded, cells
):
    frames, height, breadth, channels = clean.shape
    patch = constants.shape[0]
    first = scalars[SLAB] == 0
    sums = jnp.concatenate(
        [jnp.where(first, mine[...], other[...]), jnp.where(first, other[...], mine[...])], axis=0
    )
    feature_width = HEADS * HD
    row_mean = sums[patch : patch + 1] / feature_width
    spread = sums[patch + STAT_ROWS : patch + STAT_ROWS + 1] / feature_width - row_mean * row_mean
    velocity = (
        lax.rsqrt(spread + norm_eps) * (sums[:patch] - constants[:, 0:1] * row_mean)
        + constants[:, 1:2]
    )
    tokens = TROWS * TCOLS
    lane = lax.broadcasted_iota(jnp.int32, velocity.shape, 1)
    velocity = jnp.where((lane >= 2 * tokens) | (scalars[PLACE] > 0), velocity, 0.0)
    columns = jnp.concatenate(
        [
            jnp.concatenate(
                [
                    velocity[
                        part * channels : (part + 1) * channels,
                        frame * tokens : (frame + 1) * tokens,
                    ]
                    for part in range(4)
                ],
                axis=1,
            )
            for frame in range(frames + 2)
        ],
        axis=0,
    )
    high = columns.astype(jnp.bfloat16)
    low = (columns - high.astype(jnp.float32)).astype(jnp.bfloat16)
    chosen = sum(
        lax.dot_general(
            selector[...], part, (((1,), (1,)), ((), ())), preferred_element_type=jnp.float32
        )
        for part in (high, low)
    )
    count = (height + 2) * WINDOW
    cells[:count] = (
        jnp.concatenate([before[...], noise[...]], axis=1) - noise_level * chosen
    )
    cells[count:] = jnp.zeros_like(cells[count:])
    for frame in range(frames):
        lanes = slice((frame + 2) * channels, (frame + 3) * channels)
        for y in range(height):
            start = (y + 1) * WINDOW + 1
            clean[frame, y] = cells[start : start + breadth, lanes]
    shifted = jnp.concatenate(
        [cells[tap : tap + count] for tap in range(3)], axis=1
    ).astype(jnp.bfloat16)
    total = jnp.broadcast_to(bias[...], (height * breadth, bias.shape[1]))
    for tap in range(3):
        block = jnp.concatenate(
            [
                shifted[(y + tap) * WINDOW : (y + tap) * WINDOW + breadth]
                for y in range(height)
            ],
            axis=0,
        )
        total = total + jnp.dot(block, band[tap], preferred_element_type=jnp.float32)
    outputs = decoded.shape[3]
    total = total.astype(decoded.dtype)
    for frame in range(frames):
        decoded[frame] = total[:, frame * outputs : (frame + 1) * outputs].reshape(
            height, breadth, outputs
        )


def finish(
    scalars, mine, other, noise, before, selector, band, bias, constants, shape, outputs
):
    whole = pl.BlockSpec(memory_space=pltpu.VMEM)
    frames, height, breadth, channels = shape
    rows = (height + 2) * WINDOW
    return pl.pallas_call(
        finish_kernel,
        name="finish",
        out_shape=(
            jax.ShapeDtypeStruct(shape, jnp.float32),
            jax.ShapeDtypeStruct((frames, height, breadth, outputs), jnp.bfloat16),
        ),
        in_specs=[pl.BlockSpec(memory_space=pltpu.SMEM)] + [whole] * 8,
        out_specs=(whole, whole),
        scratch_shapes=[pltpu.VMEM((rows + 8, (frames + 2) * channels), jnp.float32)],
        compiler_params=pltpu.CompilerParams(vmem_limit_bytes=GRANT),
    )(scalars, mine, other, noise, before, selector, band, bias, constants)


def per_device(
    queries,
    keys,
    values,
    span_mask,
    head_gain,
    head_shift,
    patch_weight,
    noisy_latent,
    conv_weight,
    conv_bias,
):
    heads_dev = queries.shape[1] // HD
    if not plan_fits(
        heads_dev, lax.axis_size("span"), lax.axis_size("slab"), lax.axis_size("head")
    ):
        return gathered_plan(
            queries,
            keys,
            values,
            span_mask,
            head_gain,
            head_shift,
            patch_weight,
            noisy_latent,
            conv_weight,
            conv_bias,
        )
    place = lax.axis_index("span")
    slab = lax.axis_index("slab")
    scalars = scalar_operand(heads_dev // lax.axis_size("slab"))
    def prepare(anchor):
        noise, weight, gain, shift, taps, bias, _ = lax.optimization_barrier(
            (noisy_latent, patch_weight, head_gain, head_shift, conv_weight, conv_bias, anchor)
        )
        _, height, breadth, _ = noise.shape
        noise = noise.transpose(1, 2, 0, 3).reshape(height, breadth, -1)
        wide_weight = weight.T.astype(jnp.float32)
        constants = jnp.stack(
            [
                jnp.sum(wide_weight * gain[None, :], axis=1),
                jnp.sum(wide_weight * shift[None, :], axis=1),
            ]
        )
        window, constants = noise_window(noise, constants)
        return (
            window,
            window[:, -2 * LAT_CH :].reshape(16, -1),
            constants,
            cell_selector(height, breadth),
            banded_weight(taps),
            jnp.tile(bias, FRAMES_SPAN)[None, :],
        )

    (mine, theirs), (noise, ahead, constants, selector, band, bias) = token_sums(
        scalars,
        queries,
        keys,
        values,
        span_mask,
        head_gain,
        patch_weight,
        prepare,
    )
    mine = mine + lax.ppermute(theirs, "slab", SWAP)
    own, after, third = mine[0], mine[1], mine[2]
    skip = TROWS * TCOLS
    from_one = lax.ppermute(
        jnp.concatenate([jnp.concatenate([own[:, skip:], after], axis=1), ahead], axis=0),
        "span",
        [(0, 1), (1, 2), (2, 3)],
    )
    before = from_one[own.shape[0] :].reshape(-1, 2 * LAT_CH)
    from_one = from_one[: own.shape[0]]
    to_current = lax.ppermute(third, "span", [(1, 3), (3, 2)])
    to_before = lax.ppermute(after[:, skip:], "span", [(0, 2), (1, 3)])
    kept = jnp.concatenate([jnp.where(place == 3, third[:, skip:], 0.0), own], axis=1)
    total = kept + from_one + jnp.concatenate([to_before, to_current], axis=1)
    total = total + lax.ppermute(total, "head", SWAP)
    other = lax.ppermute(total, "slab", SWAP)
    return finish(
        scalars,
        total,
        other,
        noise,
        before,
        selector,
        band,
        bias,
        constants,
        noisy_latent.shape,
        conv_weight.shape[1],
    )


def solution(mesh):
    placed = (
        P(("groups", "span"), "head"),
        P(("groups", "span", "slab"), "head"),
        P(("groups", "span", "slab"), "head"),
        P("groups", None),
        P("head"),
        P("head"),
        P("head", None),
        P(("groups", "span"), "head", "slab", None),
        P(),
        P(),
    )
    return jax.shard_map(
        per_device,
        mesh=mesh,
        in_specs=placed,
        out_specs=(
            P(("groups", "span"), "head", "slab", None),
            P(("groups", "span"), "head", "slab", None),
        ),
        check_vma=False,
    )
```

```python
import functools
import math
import typing

import jax
import jax.numpy as jnp
import numpy as np
from jax import lax
from jax.experimental import pallas as pl
from jax.experimental.pallas import tpu as pltpu
from jax.sharding import PartitionSpec as P

HEADS = 40
HD = 128
LAT_CH = 16
FRAMES_SPAN = 3
TROWS = 8
TCOLS = 16


neg_big = -1e30
noise_level = 0.75
norm_eps = 1e-06


def with_halo(cells, sides, width):
    for axis, dim in sides:
        count = lax.axis_size(axis)
        ends = count - 1
        head = lax.slice_in_dim(cells, 0, width, axis=dim)
        tail = lax.slice_in_dim(cells, cells.shape[dim] - width, cells.shape[dim], axis=dim)
        cells = jnp.concatenate(
            [
                lax.ppermute(tail, axis, [(i, (i + 1) % count) for i in range(ends)]),
                cells,
                lax.ppermute(head, axis, [((i + 1) % count, i) for i in range(ends)]),
            ],
            axis=dim,
        )
    return cells


def from_behind(value, axis, by):
    size = lax.axis_size(axis)
    pairs = [(i, i + by) for i in range(size) if 0 <= i + by < size]
    return lax.ppermute(value, axis, pairs)


def block_length(total_rows):
    block_size = total_rows
    while block_size > 768 and block_size % 2 == 0:
        block_size = block_size // 2
    return block_size


def fold_keys(partial_state, key_value, query_block, mask_row, rows_span):
    keys_piece, values_piece = key_value
    heads_dev = query_block.shape[1]
    piece_rows = keys_piece.shape[0]
    length = block_length(piece_rows)
    span_count = mask_row.shape[0]
    score_scale = 1.0 / math.sqrt(HD)
    span_ids = jnp.arange(span_count, dtype=jnp.int32)

    def one_block(carry_state, block_index):
        running_max, running_sum, weighted = carry_state
        offset = block_index * length
        key_block = lax.dynamic_slice_in_dim(keys_piece, offset, length, 0).reshape(
            length, heads_dev, HD
        )
        value_block = lax.dynamic_slice_in_dim(values_piece, offset, length, 0).reshape(
            length, heads_dev, HD
        )
        key_span = (offset + jnp.arange(length, dtype=jnp.int32)) // rows_span
        allowed = (
            jnp.sum(jnp.where(key_span[:, None] == span_ids[None, :], mask_row[None, :], 0), axis=1)
            > 0
        )
        scores = (
            jnp.einsum("qhd,khd->hqk", query_block, key_block, preferred_element_type=jnp.float32)
            * score_scale
        )
        scores = jnp.where(allowed[None, None, :], scores, neg_big)
        new_max = jnp.maximum(running_max, jnp.max(scores, axis=2))
        weights = jnp.where(allowed[None, None, :], jnp.exp(scores - new_max[:, :, None]), 0.0)
        factor = jnp.exp(running_max - new_max)
        running_sum = running_sum * factor + jnp.sum(weights, axis=2)
        weighted = weighted * factor.T[:, :, None] + jnp.einsum(
            "hqk,khd->qhd",
            weights.astype(jnp.bfloat16),
            value_block,
            preferred_element_type=jnp.float32,
        )
        return ((new_max, running_sum, weighted), None)

    result, unused = lax.scan(
        one_block, partial_state, jnp.arange(piece_rows // length, dtype=jnp.int32)
    )
    return result


def gathered_plan(
    queries,
    keys,
    values,
    span_mask,
    head_gain,
    head_shift,
    patch_weight,
    noisy_latent,
    conv_weight,
    conv_bias,
):
    heads_dev = queries.shape[1] // HD
    slab_count = lax.axis_size("slab")
    col_dev = TCOLS // slab_count
    slab_place = lax.axis_index("slab")
    span_place = lax.axis_index("span")
    mask_row = lax.dynamic_slice_in_dim(span_mask, span_place, 1, 0)[0]
    token_grid = queries.reshape(FRAMES_SPAN, TROWS, TCOLS, queries.shape[-1])
    picked = lax.dynamic_slice_in_dim(token_grid, slab_place * col_dev, col_dev, 2)
    own_queries = picked.reshape(FRAMES_SPAN * TROWS * col_dev, queries.shape[-1]).reshape(
        -1, heads_dev, HD
    )
    query_rows = own_queries.shape[0]
    rows_span = keys.shape[0] * slab_count
    running_max, running_sum, weighted = fold_keys(
        (
            jnp.full((heads_dev, query_rows), neg_big, jnp.float32),
            jnp.zeros((heads_dev, query_rows), jnp.float32),
            jnp.zeros((query_rows, heads_dev, HD), jnp.float32),
        ),
        (
            lax.all_gather(keys, ("span", "slab"), axis=0, tiled=True),
            lax.all_gather(values, ("span", "slab"), axis=0, tiled=True),
        ),
        own_queries,
        mask_row,
        rows_span,
    )
    attended = (
        (weighted / running_sum.T[:, :, None])
        .astype(jnp.bfloat16)
        .reshape(query_rows, heads_dev * HD)
    )
    feature_width = HEADS * HD
    values32 = attended.astype(jnp.float32)
    row_total = jnp.sum(values32, axis=1)
    row_squares = jnp.sum(values32 * values32, axis=1)
    row_total, row_squares = lax.psum((row_total, row_squares), "head")
    row_mean = row_total / feature_width
    spread = row_squares / feature_width - row_mean * row_mean
    normed = (
        (values32 - row_mean[:, None]) * lax.rsqrt(spread + norm_eps)[:, None] * head_gain[None, :]
        + head_shift[None, :]
    ).astype(jnp.bfloat16)
    normed_grid = normed.reshape(FRAMES_SPAN, TROWS, col_dev, normed.shape[-1])
    own_rows = TROWS // lax.axis_size("head")
    picked = normed_grid
    product = jnp.dot(
        picked.reshape(-1, picked.shape[-1]), patch_weight, preferred_element_type=jnp.float32
    )
    velocity = lax.psum_scatter(
        product.reshape(
            FRAMES_SPAN, own_rows * lax.axis_size("head"), col_dev * patch_weight.shape[1]
        )
        .transpose(1, 0, 2)
        .reshape(own_rows * lax.axis_size("head"), -1)
        .astype(jnp.bfloat16),
        "head",
        scatter_dimension=0,
        tiled=True,
    ).astype(jnp.float32)
    rows_dev = velocity.shape[0]
    patch_cells = (
        velocity.reshape(rows_dev, FRAMES_SPAN, col_dev, 2, 2, LAT_CH)
        .transpose(1, 0, 3, 2, 4, 5)
        .reshape(FRAMES_SPAN, 2 * rows_dev, 2 * col_dev, LAT_CH)
    )
    clean_latent = noisy_latent - noise_level * patch_cells
    latent_input = clean_latent.astype(jnp.bfloat16)
    framed = with_halo(latent_input, (("head", 1), ("slab", 2)), 1)
    earlier = from_behind(framed[FRAMES_SPAN - 2 :], "span", 1)
    stacked = jnp.concatenate([earlier, framed], axis=0)
    height = clean_latent.shape[1]
    breadth = clean_latent.shape[2]
    columns = jnp.concatenate(
        [
            stacked[
                frame_tap : frame_tap + FRAMES_SPAN,
                row_tap : row_tap + height,
                col_tap : col_tap + breadth,
                :,
            ]
            for frame_tap in range(3)
            for row_tap in range(3)
            for col_tap in range(3)
        ],
        axis=-1,
    )
    decoded = (
        jnp.dot(
            columns.reshape(FRAMES_SPAN * height * breadth, 27 * LAT_CH),
            conv_weight,
            preferred_element_type=jnp.float32,
        )
        + conv_bias[None, :]
    )
    decoded = decoded.astype(jnp.bfloat16).reshape(
        FRAMES_SPAN, height, breadth, conv_weight.shape[1]
    )
    return (clean_latent, decoded)


NEAR_HEADS = 4
MIDDLE_HEADS = 4
FAR_HEADS = 2
MIDDLE = NEAR_HEADS
FAR = NEAR_HEADS + MIDDLE_HEADS
STAT_ROWS = 8
SLOTS = 3
QUERY_ROWS = 192
SWAP = [(0, 1), (1, 0)]
WINDOW = 32
GRANT = 20 << 20

OWN, OTHER, DOWN, UP, MAIN, MAIN_CAP, FINAL, FINAL_CAP, PLACE, SLAB = range(10)


def plan_fits(heads_dev, span_count, slab_count, head_count):
    return (
        span_count == 4
        and slab_count == 2
        and head_count == 2
        and heads_dev == slab_count * (NEAR_HEADS + MIDDLE_HEADS + FAR_HEADS)
    )


def scalar_operand(heads):
    by_place = np.zeros((4, 12), np.int32)
    by_place[:, OTHER] = heads
    by_place[:, DOWN] = [MIDDLE, MIDDLE, 0, MIDDLE]
    by_place[:, UP] = [0, MIDDLE, 0, 0]
    by_place[:, MAIN] = [MIDDLE, 0, MIDDLE, 0]
    by_place[:, MAIN_CAP] = [1, 1, 1, 0]
    by_place[:, FINAL] = [FAR, 0, 0, FAR]
    by_place[:, FINAL_CAP] = [0, 1, 0, 0]
    by_place[:, PLACE] = range(4)
    by_slab = np.zeros(12, np.int32)
    by_slab[[OWN, OTHER, SLAB]] = heads, -heads, 1
    row = lax.dynamic_slice_in_dim(jnp.array(by_place), lax.axis_index("span"), 1, 0)[0]
    return row + lax.axis_index("slab") * jnp.array(by_slab)


def pack_kernel(inputs, messages, copies, scalars, *refs):
    ins, rest = refs[:inputs], refs[inputs:]
    outs, staged = rest[:messages], rest[messages:-2]
    arrive, leave = rest[-2:]
    arriving = []
    for number, (source, row, rows, entries, shift, target, at, heads) in enumerate(copies):
        head = shift
        for entry in entries:
            head = head + scalars[entry]
        column = pl.multiple_of(head * HD, HD)
        place = staged[target].at[pl.ds(at, rows), :]
        copy = pltpu.make_async_copy(
            ins[source].at[pl.ds(row, rows), pl.ds(column, heads * HD)], place, arrive.at[number]
        )
        copy.start()
        onward = pltpu.make_async_copy(
            place, outs[target].at[pl.ds(at, rows), :], leave.at[number]
        )
        arriving.append((copy, onward))
    for copy, onward in arriving:
        copy.wait()
        onward.start()
    for _, onward in arriving:
        onward.wait()


def pack(scalars, arrays, shapes, copies, name):
    moved = sum(2 * 2 * rows * heads * HD for _, _, rows, _, _, _, _, heads in copies)
    out_shape = [pltpu.HBM(shape, jnp.bfloat16) for shape in shapes]
    in_specs = [pl.BlockSpec(memory_space=pl.ANY)] * len(arrays)
    out_specs = [pl.BlockSpec(memory_space=pl.ANY)] * len(shapes)
    return pl.pallas_call(
        functools.partial(pack_kernel, len(arrays), len(shapes), copies),
        name=name,
        out_shape=out_shape,
        grid_spec=pltpu.PrefetchScalarGridSpec(
            num_scalar_prefetch=1,
            grid=(1,),
            in_specs=in_specs,
            out_specs=out_specs,
            scratch_shapes=[pltpu.VMEM(shape, jnp.bfloat16) for shape in shapes]
            + [
                pltpu.SemaphoreType.DMA((len(copies),)),
                pltpu.SemaphoreType.DMA((len(copies),)),
            ],
        ),
        compiler_params=pltpu.CompilerParams(vmem_limit_bytes=GRANT),
        cost_estimate=pl.CostEstimate(flops=0, bytes_accessed=moved, transcendentals=0),
    )(scalars, *arrays)


def hand_kernel(heads, keys, values, out, arrive):
    column = pl.multiple_of((1 - lax.axis_index("slab")) * heads * HD, heads * HD)
    half = keys.shape[0]
    copies = []
    for number, source in enumerate((keys, values)):
        copy = pltpu.make_async_copy(
            source.at[:, pl.ds(column, heads * HD)],
            out.at[pl.ds(number * half, half), :],
            arrive.at[number],
        )
        copy.start()
        copies.append(copy)
    for copy in copies:
        copy.wait()


def pack_handed(keys, values, heads):
    shape = (2 * keys.shape[0], heads * HD)
    return pl.pallas_call(
        functools.partial(hand_kernel, heads),
        name="pack_handed",
        out_shape=jax.ShapeDtypeStruct(shape, keys.dtype),
        in_specs=[pl.BlockSpec(memory_space=pl.ANY)] * 2,
        out_specs=pl.BlockSpec(memory_space=pltpu.VMEM),
        scratch_shapes=[pltpu.SemaphoreType.DMA((2,))],
        compiler_params=pltpu.CompilerParams(vmem_limit_bytes=GRANT),
        cost_estimate=pl.CostEstimate(
            flops=0, bytes_accessed=4 * math.prod(shape), transcendentals=0
        ),
    )(keys, values)


def message(scalars, pieces, arrays, name):
    copies, shapes = [], []
    for target, parts in enumerate(pieces):
        at = 0
        for source, row, rows, entries, shift, heads in parts:
            copies.append((source, row, rows, entries, shift, target, at, heads))
            at += rows
        shapes.append((at, parts[0][5] * HD))
    return pack(scalars, arrays, shapes, copies, name)


class Tokens(typing.NamedTuple):
    query: int | None = None
    pairs: tuple = ()
    extra: int | None = None


OWN_TOKENS = Tokens()


def attend_kernel(variants, extra, span_count, fresh, wide, final, scalars, mask, *refs):
    if final:
        sources, (weight, gain), brought = refs[:4], refs[4:6], refs[6 : 6 + final]
        sums_in, (mine_out, theirs_out) = refs[6 + final : 8 + final], refs[8 + final : 10 + final]
        folded, squares, carried, moved, *own_refs = refs[10 + final : 18 + final]
        query_own, key_own, value_own, received = own_refs
        more, payloads, landed = refs[18 + final : 22 + final], refs[22 + final : -1], refs[-1]
    else:
        query_own, key_own, value_own, received, weight, gain = refs[:6]
        mine_out, theirs_out, folded, squares, carried, moved = refs[-6:]
        payloads, sums_in = refs[6:-6], None
    rows = query_own.shape[0]
    half = rows // 2
    step = pl.program_id(0)
    to_exp2 = math.log2(math.e) / math.sqrt(HD)
    active = functools.reduce(
        lambda a, b: a | b, [scalars[PLACE] == place for place in variants]
    )

    last_step = step == pl.num_programs(0) - 1
    part = carried.shape[1] // 2
    halves = [
        carried.at[:, pl.ds(pl.multiple_of(number * part, part), part)]
        for number in (scalars[SLAB], 1 - scalars[SLAB])
    ]
    fetches = (
        []
        if fresh
        else [
            pltpu.make_async_copy(sums_in[number], halves[number], moved.at[number])
            for number in range(2)
        ]
    )

    @pl.when((step == 0) & active)
    def _():
        folded[...] = jnp.zeros_like(folded)
        squares[...] = jnp.zeros_like(squares)
        for fetch in fetches:
            fetch.start()

    def lanes_of(head):
        return slice(head * HD, (head + 1) * HD)

    def query_of(source, lanes):
        if source is OWN_TOKENS:
            return query_own[:, lanes]
        if source.extra is not None:
            return more[0][:, lanes_of(source.extra)]
        return payloads[source.query][:rows, lanes]

    def pair_of(source, lanes):
        if source is OWN_TOKENS:
            parts = (
                key_own[:, lanes],
                received[:half, lanes],
                value_own[:, lanes],
                received[half:, lanes],
            )
        elif source.extra is not None:
            own = lanes_of(source.extra)
            parts = (more[1][:, own], more[3][:half, own], more[2][:, own], more[3][half:, own])
        else:
            payload = payloads[source.pairs[0]]
            start = payload.shape[0] - 2 * rows
            return payload[start : start + rows, lanes], payload[start + rows :, lanes]
        return jnp.concatenate(parts[:2], axis=0), jnp.concatenate(parts[2:], axis=0)

    def projector(extra_head, lanes):
        if final:
            head = scalars[OWN] + (
                scalars[FINAL] + lanes.start // HD if extra_head is None else extra_head
            )
            lanes = pl.ds(pl.multiple_of(head * HD, HD), HD)
        scaled = weight[:, lanes].astype(jnp.float32) * gain[:, lanes]
        high = scaled.astype(jnp.bfloat16)
        low = (scaled - high.astype(jnp.float32)).astype(jnp.bfloat16)
        return jnp.concatenate([high, low, jnp.ones((16, HD), jnp.bfloat16)], axis=0)

    def one_query(head, source, slot, query_span, key_sources):
        lanes = lanes_of(head)
        query = query_of(source, lanes)
        pairs = [pair_of(key_source, lanes) for key_source, _ in key_sources]
        open_to = [
            None if key_span == query_span else mask[query_span * span_count + key_span] > 0
            for _, key_span in key_sources
        ]
        keys_in = jnp.concatenate([pair[0] for pair in pairs], axis=0)
        ones_block = jnp.ones((rows, HD), jnp.bfloat16)
        values_in = jnp.concatenate(
            [jnp.concatenate([pair[1], ones_block], axis=1) for pair in pairs], axis=0
        )
        pieces = []
        for row in range(0, rows, QUERY_ROWS):
            score = lax.dot_general(
                query[row : row + QUERY_ROWS],
                keys_in,
                (((1,), (1,)), ((), ())),
                preferred_element_type=jnp.float32,
            )
            best = None
            for number, is_open in enumerate(open_to):
                start = number * rows
                block = score[:, start : start + HD]
                for lane in range(HD, rows, HD):
                    block = jnp.maximum(block, score[:, start + lane : start + lane + HD])
                if is_open is not None:
                    block = jnp.where(is_open, block, neg_big)
                best = block if best is None else jnp.maximum(best, block)
            top = jnp.max(best, axis=1, keepdims=True)
            weights = []
            for number, is_open in enumerate(open_to):
                start = number * rows
                shift = top if is_open is None else jnp.where(is_open, top, -neg_big)
                weights.append(
                    jnp.exp2((score[:, start : start + rows] - shift) * to_exp2).astype(jnp.bfloat16)
                )
            both = jnp.dot(
                jnp.concatenate(weights, axis=1), values_in, preferred_element_type=jnp.float32
            )
            pieces.append((both[:, :HD] / both[:, HD:]).astype(jnp.bfloat16))
        attended = jnp.concatenate(pieces, axis=0)
        folded[slot] += lax.dot_general(
            projector(source.extra, lanes),
            attended,
            (((1,), (1,)), ((), ())),
            preferred_element_type=jnp.float32,
        )
        wide = attended.astype(jnp.float32)
        squares[slot] += wide * wide

    def fetch_head(number, head, used):
        copies = []
        place = pl.ds(number * HD, HD)
        for index, (source, target) in enumerate(zip(sources, own_refs if used else more)):
            column = head if index == 3 else scalars[OWN] + head
            column = pl.ds(pl.multiple_of(column * HD, HD), HD)
            copies.append((source.at[:, column], target.at[:, place]))
        copies += [(brought[index].at[:, place], payloads[index].at[:, place]) for index in used]
        started = []
        for index, (source, target) in enumerate(copies):
            slot = number if used else 4 + number
            copy = pltpu.make_async_copy(source, target, landed.at[slot, index])
            copy.start()
            started.append(copy)
        return started

    for place, groups in variants.items():
        if final:
            count, tasks, extra_tasks = groups
            used = set()
            for source, _, _, key_sources in tasks:
                for tokens in [source] + [key_source for key_source, _ in key_sources]:
                    used |= set(tokens.pairs) | ({tokens.query} if tokens.query is not None else set())

            @pl.when(scalars[PLACE] == place)
            def _():
                waits = [
                    fetch_head(head, scalars[FINAL] + head, sorted(used)) for head in range(count)
                ]
                extra_waits = [
                    fetch_head(number, number, ()) for number in range(len(extra_tasks))
                ]
                for head in range(count):
                    for copy in waits[head]:
                        copy.wait()
                    for task in tasks:
                        one_query(head, *task)
                for copies, task in zip(extra_waits, extra_tasks):
                    for copy in copies:
                        copy.wait()
                    one_query(0, *task)

            continue
        for steps, tasks in groups:

            @pl.when((scalars[PLACE] == place) & (step < steps))
            def _():
                for head in range(wide):
                    for task in tasks:
                        one_query(head, *task)

    def store():
        copies = [
            pltpu.make_async_copy(halves[number], out, moved.at[2 + number])
            for number, out in enumerate((mine_out, theirs_out))
        ]
        for copy in copies:
            copy.start()
        for copy in copies:
            copy.wait()

    if fresh:

        @pl.when(last_step & jnp.logical_not(active))
        def _():
            carried[...] = jnp.zeros_like(carried)
            store()

    @pl.when(last_step & active)
    def _():
        ones_rows = jnp.ones((STAT_ROWS, HD), jnp.bfloat16)
        patch = weight.shape[0]
        for fetch in fetches:
            fetch.wait()
        if fresh:
            carried[...] = jnp.zeros_like(carried)

        def finish_slot(slot):
            left = squares[slot]
            total = jnp.zeros((STAT_ROWS, rows), jnp.float32)
            for _ in range(3):
                piece = left.astype(jnp.bfloat16)
                left = left - piece.astype(jnp.float32)
                total = total + lax.dot_general(
                    ones_rows, piece, (((1,), (1,)), ((), ())), preferred_element_type=jnp.float32
                )
            done = folded[slot]
            carried[slot] += jnp.concatenate(
                [
                    done[:patch] + done[patch : 2 * patch],
                    done[2 * patch : 2 * patch + STAT_ROWS],
                    total,
                ],
                axis=0,
            )

        for place, groups in variants.items():

            @pl.when(scalars[PLACE] == place)
            def _():
                tasks = groups[1] if final else [task for _, some in groups for task in some]
                for slot in sorted({task[1] for task in tasks}):
                    finish_slot(slot)

        store()


def attend(steps, wide, first, cap, own, scalars, mask, sums, payloads, variants, name, cost=1):
    queries, keys, values, received, weight, gain = own
    rows = queries.shape[0]
    half = rows // 2
    patch = weight.shape[0]

    def moving(i, scalars):
        return jnp.minimum(i, scalars[cap])

    def column(height, own_column):
        def index(i, scalars, mask):
            head = scalars[first] + scalars[OWN] if own_column else scalars[first]
            return (0, head // wide + moving(i, scalars))

        return pl.BlockSpec((height, wide * HD), index)

    def payload_column(payload):
        last = payload.shape[1] // (wide * HD) - 1

        def index(i, scalars, mask):
            return (0, jnp.minimum(moving(i, scalars), last))

        return pl.BlockSpec((payload.shape[0], wide * HD), index)

    in_specs = [
        column(rows, True),
        column(half, True),
        column(half, True),
        column(rows, False),
        column(patch, True),
        column(1, True),
    ]
    arrays = [queries, keys, values, received, weight, gain]
    in_specs += [payload_column(payload) for payload in payloads]
    arrays += payloads
    fresh = sums is None
    sums_shape = (SLOTS, patch + 2 * STAT_ROWS, rows)
    scratch = [
        pltpu.VMEM((SLOTS, 2 * patch + 16, rows), jnp.float32),
        pltpu.VMEM((SLOTS, rows, HD), jnp.float32),
        pltpu.VMEM(sums_shape, jnp.float32),
        pltpu.SemaphoreType.DMA((4,)),
    ]
    aliases = {}
    if not fresh:
        anywhere = pl.BlockSpec(memory_space=pl.ANY)
        whole = lambda array: pl.BlockSpec(array.shape, lambda i, scalars, mask: (0, 0))
        in_specs = [anywhere] * 4 + [whole(weight), whole(gain)] + [anywhere] * len(payloads)
        scratch += 2 * [
            pltpu.VMEM((height, 4 * HD), jnp.bfloat16) for height in (rows, half, half, rows)
        ]
        scratch += [pltpu.VMEM(payload.shape, payload.dtype) for payload in payloads]
        scratch.append(pltpu.SemaphoreType.DMA((8, 4 + len(payloads))))
        aliases = {2 + len(arrays): 0, 3 + len(arrays): 1}
        in_specs += [anywhere] * 2
        arrays += sums
    flops = 4 * rows * rows * HD * cost * 16
    span_count = math.isqrt(mask.shape[0])
    final = 0 if fresh else len(payloads)
    return pl.pallas_call(
        functools.partial(attend_kernel, variants, 0, span_count, fresh, wide, final),
        name=name,
        out_shape=[pltpu.HBM((SLOTS, sums_shape[1] // 2, rows), jnp.float32)] * 2,
        input_output_aliases=aliases,
        grid_spec=pltpu.PrefetchScalarGridSpec(
            num_scalar_prefetch=2,
            grid=(steps,),
            in_specs=in_specs,
            out_specs=[pl.BlockSpec(memory_space=pl.ANY)] * 2,
            scratch_shapes=scratch,
        ),
        compiler_params=pltpu.CompilerParams(vmem_limit_bytes=GRANT),
        cost_estimate=pl.CostEstimate(
            flops=flops,
            bytes_accessed=4 * HD * 2 * 3 * rows,
            transcendentals=flops // (4 * HD),
        ),
    )(scalars, mask, *arrays)


def token_sums(
    scalars, queries, keys, values, span_mask, head_gain, patch_weight, prepare
):
    rows = queries.shape[0]
    half = rows // 2
    heads = NEAR_HEADS + MIDDLE_HEADS + FAR_HEADS
    in_place = lambda array: pltpu.with_memory_space_constraint(array, pltpu.HBM)
    queries, keys, values = (in_place(array) for array in (queries, keys, values))

    def send(value, *pairs):
        return in_place(lax.ppermute(value, "span", list(pairs)))

    def tokens(entry, shift, count):
        return [(0, 0, rows, (OWN, entry) if entry else (OWN,), shift, count)]

    def pairs_of(entry, shift, count):
        entries = (entry,) if entry else ()
        return [
            piece
            for part in (1, 2)
            for piece in (
                (part, 0, half, (OWN,) + entries, shift, count),
                (3, (part - 1) * half, half, entries, shift, count),
            )
        ]

    handed = pack_handed(keys, values, heads)
    received = lax.ppermute(handed, "slab", SWAP)
    up, down = message(
        scalars,
        [
            pairs_of(UP, 0, NEAR_HEADS),
            tokens(DOWN, 0, MIDDLE_HEADS) + pairs_of(DOWN, 0, MIDDLE_HEADS),
        ],
        (queries, keys, values, received),
        "pack_first",
    )
    source, _ = lax.optimization_barrier((received, down))
    up = send(up, (0, 1), (1, 2))
    down = send(down, (1, 0), (2, 1), (3, 2))
    up_two, two, far_all, far_pair = message(
        scalars,
        [
            pairs_of(None, MIDDLE, MIDDLE_HEADS),
            tokens(None, 0, NEAR_HEADS) + pairs_of(None, 0, NEAR_HEADS),
            tokens(None, FAR, FAR_HEADS) + pairs_of(None, FAR, FAR_HEADS),
            pairs_of(None, FAR, FAR_HEADS),
        ],
        (queries, keys, values, source),
        "pack_second",
    )
    anchor = two
    up_two = send(up_two, (0, 2))
    two = send(two, (3, 1))
    far_next = send(far_all, (2, 3), (1, 0))
    far_pair, prepared = lax.optimization_barrier((far_pair, prepare(anchor)))
    far_two = send(far_pair, (1, 3))
    far_three = send(far_pair, (0, 3))

    span_mask, head_gain, patch_weight, _ = lax.optimization_barrier(
        (span_mask, head_gain, patch_weight, anchor)
    )
    mask = span_mask.reshape(-1)
    weight = patch_weight.T
    own = (queries, keys, values, received, weight, head_gain[None, :])
    run = functools.partial(attend, own=own, scalars=scalars, mask=mask)

    here, back_one, on_one = OWN_TOKENS, Tokens(None, (0,)), Tokens(1, (1,))
    back_two = Tokens(None, (2,))
    sums = run(
        MIDDLE_HEADS // 2,
        2,
        MAIN,
        MAIN_CAP,
        sums=None,
        payloads=[up, down, up_two],
        variants={
            0: [(2, [(here, 0, 0, [(here, 0)]), (on_one, 1, 1, [(here, 0), (on_one, 1)])])],
            1: [
                (
                    2,
                    [
                        (on_one, 1, 2, [(back_one, 0), (here, 1), (on_one, 2)]),
                        (here, 0, 1, [(back_one, 0), (here, 1)]),
                    ],
                )
            ],
            2: [
                (
                    2,
                    [
                        (on_one, 1, 3, [(back_two, 0), (back_one, 1), (here, 2), (on_one, 3)]),
                        (here, 0, 2, [(back_two, 0), (back_one, 1), (here, 2)]),
                    ],
                )
            ],
        },
        name="main_heads",
    )
    on_two, beside = Tokens(2, (2,)), Tokens(3, (3,))
    two_back, three_back = Tokens(None, (4,)), Tokens(None, (5,))
    extras = [Tokens(None, (), lane) for lane in range(NEAR_HEADS)]
    sums, prepared = lax.optimization_barrier((sums, prepared))
    sums = run(
        1,
        1,
        FINAL,
        FINAL_CAP,
        sums=sums,
        payloads=[up, down, two, far_next, far_two, far_three],
        variants={
            0: (
                FAR_HEADS,
                [(here, 0, 0, [(here, 0)]), (beside, 1, 1, [(here, 0), (beside, 1)])],
                [(head, 0, 0, [(head, 0)]) for head in extras],
            ),
            1: (
                NEAR_HEADS,
                [(on_two, 2, 3, [(back_one, 0), (here, 1), (on_one, 2), (on_two, 3)])],
                [],
            ),
            3: (
                FAR_HEADS,
                [
                    (here, 0, 3, [(three_back, 0), (two_back, 1), (beside, 2), (here, 3)]),
                    (beside, 2, 2, [(three_back, 0), (two_back, 1), (beside, 2)]),
                ],
                [],
            ),
        },
        name="final_heads",
        cost=4,
    )
    return sums, prepared


def noise_window(grid, constants):
    height, breadth, _ = grid.shape
    slab = lax.axis_index("slab")
    edge = jnp.where(slab == 0, grid[:, breadth - 1], grid[:, 0])
    edge = lax.ppermute(edge, "slab", SWAP)[:, None]
    grid = jnp.concatenate(
        [
            jnp.where(slab == 1, edge, 0.0),
            grid,
            jnp.where(slab == 0, edge, 0.0),
            jnp.zeros((height, WINDOW - breadth - 2, grid.shape[2]), grid.dtype),
        ],
        axis=1,
    )
    head = lax.axis_index("head")
    edge = jnp.where(head == 0, grid[height - 1], grid[0])
    count = constants.shape[1]
    extra = jnp.pad(constants, ((0, 8 - constants.shape[0]), (0, HD - count)))
    edge = jnp.pad(edge, ((0, 0), (0, HD - edge.shape[1])))
    sent = lax.ppermute(jnp.concatenate([edge, extra], axis=0), "head", SWAP)
    edge = sent[None, :WINDOW, : grid.shape[2]]
    constants = constants + sent[WINDOW : WINDOW + constants.shape[0], :count]
    grid = jnp.concatenate(
        [jnp.where(head == 1, edge, 0.0), grid, jnp.where(head == 0, edge, 0.0)], axis=0
    )
    return grid.reshape((height + 2) * WINDOW, grid.shape[2]), constants.T


def cell_selector(height, breadth):
    cell = lax.broadcasted_iota(jnp.int32, ((height + 2) * WINDOW, 4 * TROWS * TCOLS), 0)
    column = lax.broadcasted_iota(jnp.int32, cell.shape, 1)
    y = lax.axis_index("head") * height + cell // WINDOW - 1
    x = lax.axis_index("slab") * breadth + cell % WINDOW - 1
    inside = (y >= 0) & (y < 2 * TROWS) & (x >= 0) & (x < 2 * TCOLS)
    inside = inside & (cell % WINDOW < breadth + 2)
    target = ((y % 2) * 2 + x % 2) * (TROWS * TCOLS) + (y // 2) * TCOLS + x // 2
    return (inside & (column == target)).astype(jnp.bfloat16)


def band_kernel(weight, band):
    outputs = weight.shape[1]
    band[...] = jnp.zeros_like(band)
    for row_tap in range(3):
        for col_tap in range(3):
            for frame_tap in range(3):
                start = ((3 * frame_tap + row_tap) * 3 + col_tap) * LAT_CH
                block = weight[start : start + LAT_CH]
                for frame in range(FRAMES_SPAN):
                    at = (col_tap * (FRAMES_SPAN + 2) + frame + frame_tap) * LAT_CH
                    band[
                        row_tap, at : at + LAT_CH, frame * outputs : (frame + 1) * outputs
                    ] = block


def banded_weight(conv_weight):
    shape = (3, 3 * (FRAMES_SPAN + 2) * LAT_CH, FRAMES_SPAN * conv_weight.shape[1])
    return pl.pallas_call(
        band_kernel,
        name="band",
        out_shape=jax.ShapeDtypeStruct(shape, conv_weight.dtype),
        in_specs=[pl.BlockSpec(memory_space=pltpu.VMEM)],
        out_specs=pl.BlockSpec(memory_space=pltpu.VMEM),
        compiler_params=pltpu.CompilerParams(vmem_limit_bytes=GRANT),
        cost_estimate=pl.CostEstimate(
            flops=0, bytes_accessed=2 * math.prod(shape), transcendentals=0
        ),
    )(conv_weight)


def finish_kernel(
    scalars, mine, other, noise, before, selector, band, bias, constants, clean, decoded, cells
):
    frames, height, breadth, channels = clean.shape
    patch = constants.shape[0]
    first = scalars[SLAB] == 0
    sums = jnp.concatenate(
        [jnp.where(first, mine[...], other[...]), jnp.where(first, other[...], mine[...])], axis=0
    )
    feature_width = HEADS * HD
    row_mean = sums[patch : patch + 1] / feature_width
    spread = sums[patch + STAT_ROWS : patch + STAT_ROWS + 1] / feature_width - row_mean * row_mean
    velocity = (
        lax.rsqrt(spread + norm_eps) * (sums[:patch] - constants[:, 0:1] * row_mean)
        + constants[:, 1:2]
    )
    tokens = TROWS * TCOLS
    lane = lax.broadcasted_iota(jnp.int32, velocity.shape, 1)
    velocity = jnp.where((lane >= 2 * tokens) | (scalars[PLACE] > 0), velocity, 0.0)
    columns = jnp.concatenate(
        [
            jnp.concatenate(
                [
                    velocity[
                        part * channels : (part + 1) * channels,
                        frame * tokens : (frame + 1) * tokens,
                    ]
                    for part in range(4)
                ],
                axis=1,
            )
            for frame in range(frames + 2)
        ],
        axis=0,
    )
    high = columns.astype(jnp.bfloat16)
    low = (columns - high.astype(jnp.float32)).astype(jnp.bfloat16)
    chosen = sum(
        lax.dot_general(
            selector[...], part, (((1,), (1,)), ((), ())), preferred_element_type=jnp.float32
        )
        for part in (high, low)
    )
    count = (height + 2) * WINDOW
    cells[:count] = (
        jnp.concatenate([before[...], noise[...]], axis=1) - noise_level * chosen
    )
    cells[count:] = jnp.zeros_like(cells[count:])
    for frame in range(frames):
        lanes = slice((frame + 2) * channels, (frame + 3) * channels)
        for y in range(height):
            start = (y + 1) * WINDOW + 1
            clean[frame, y] = cells[start : start + breadth, lanes]
    shifted = jnp.concatenate(
        [cells[tap : tap + count] for tap in range(3)], axis=1
    ).astype(jnp.bfloat16)
    total = jnp.broadcast_to(bias[...], (height * breadth, bias.shape[1]))
    for tap in range(3):
        block = jnp.concatenate(
            [
                shifted[(y + tap) * WINDOW : (y + tap) * WINDOW + breadth]
                for y in range(height)
            ],
            axis=0,
        )
        total = total + jnp.dot(block, band[tap], preferred_element_type=jnp.float32)
    outputs = decoded.shape[3]
    total = total.astype(decoded.dtype)
    for frame in range(frames):
        decoded[frame] = total[:, frame * outputs : (frame + 1) * outputs].reshape(
            height, breadth, outputs
        )


def finish(
    scalars, mine, other, noise, before, selector, band, bias, constants, shape, outputs
):
    whole = pl.BlockSpec(memory_space=pltpu.VMEM)
    frames, height, breadth, channels = shape
    rows = (height + 2) * WINDOW
    return pl.pallas_call(
        finish_kernel,
        name="finish",
        out_shape=(
            jax.ShapeDtypeStruct(shape, jnp.float32),
            jax.ShapeDtypeStruct((frames, height, breadth, outputs), jnp.bfloat16),
        ),
        in_specs=[pl.BlockSpec(memory_space=pltpu.SMEM)] + [whole] * 8,
        out_specs=(whole, whole),
        scratch_shapes=[pltpu.VMEM((rows + 8, (frames + 2) * channels), jnp.float32)],
        compiler_params=pltpu.CompilerParams(vmem_limit_bytes=GRANT),
    )(scalars, mine, other, noise, before, selector, band, bias, constants)


def per_device(
    queries,
    keys,
    values,
    span_mask,
    head_gain,
    head_shift,
    patch_weight,
    noisy_latent,
    conv_weight,
    conv_bias,
):
    heads_dev = queries.shape[1] // HD
    if not plan_fits(
        heads_dev, lax.axis_size("span"), lax.axis_size("slab"), lax.axis_size("head")
    ):
        return gathered_plan(
            queries,
            keys,
            values,
            span_mask,
            head_gain,
            head_shift,
            patch_weight,
            noisy_latent,
            conv_weight,
            conv_bias,
        )
    place = lax.axis_index("span")
    slab = lax.axis_index("slab")
    scalars = scalar_operand(heads_dev // lax.axis_size("slab"))
    def prepare(anchor):
        noise, weight, gain, shift, taps, bias, _ = lax.optimization_barrier(
            (noisy_latent, patch_weight, head_gain, head_shift, conv_weight, conv_bias, anchor)
        )
        _, height, breadth, _ = noise.shape
        noise = noise.transpose(1, 2, 0, 3).reshape(height, breadth, -1)
        wide_weight = weight.T.astype(jnp.float32)
        constants = jnp.stack(
            [
                jnp.sum(wide_weight * gain[None, :], axis=1),
                jnp.sum(wide_weight * shift[None, :], axis=1),
            ]
        )
        window, constants = noise_window(noise, constants)
        return (
            window,
            window[:, -2 * LAT_CH :].reshape(16, -1),
            constants,
            cell_selector(height, breadth),
            banded_weight(taps),
            jnp.tile(bias, FRAMES_SPAN)[None, :],
        )

    (mine, theirs), (noise, ahead, constants, selector, band, bias) = token_sums(
        scalars,
        queries,
        keys,
        values,
        span_mask,
        head_gain,
        patch_weight,
        prepare,
    )
    mine = mine + lax.ppermute(theirs, "slab", SWAP)
    own, after, third = mine[0], mine[1], mine[2]
    skip = TROWS * TCOLS
    ahead = jnp.concatenate([jnp.concatenate([own[:, skip:], after], axis=1), ahead], axis=0)
    from_one = lax.ppermute(ahead, "span", [(0, 1), (1, 2), (2, 3)])
    sent_current, sent_before, _ = lax.optimization_barrier((third, after[:, skip:], ahead))
    before = from_one[own.shape[0] :].reshape(-1, 2 * LAT_CH)
    from_one = from_one[: own.shape[0]]
    to_current = lax.ppermute(sent_current, "span", [(1, 3), (3, 2)])
    to_before = lax.ppermute(sent_before, "span", [(0, 2), (1, 3)])
    kept = jnp.concatenate([jnp.where(place == 3, third[:, skip:], 0.0), own], axis=1)
    total = kept + from_one + jnp.concatenate([to_before, to_current], axis=1)
    total = total + lax.ppermute(total, "head", SWAP)
    other = lax.ppermute(total, "slab", SWAP)
    return finish(
        scalars,
        total,
        other,
        noise,
        before,
        selector,
        band,
        bias,
        constants,
        noisy_latent.shape,
        conv_weight.shape[1],
    )


def solution(mesh):
    placed = (
        P(("groups", "span"), "head"),
        P(("groups", "span", "slab"), "head"),
        P(("groups", "span", "slab"), "head"),
        P("groups", None),
        P("head"),
        P("head"),
        P("head", None),
        P(("groups", "span"), "head", "slab", None),
        P(),
        P(),
    )
    return jax.shard_map(
        per_device,
        mesh=mesh,
        in_specs=placed,
        out_specs=(
            P(("groups", "span"), "head", "slab", None),
            P(("groups", "span"), "head", "slab", None),
        ),
        check_vma=False,
    )
```

```python
import functools
import math
import typing

import jax
import jax.numpy as jnp
import numpy as np
from jax import lax
from jax.experimental import pallas as pl
from jax.experimental.pallas import tpu as pltpu
from jax.sharding import PartitionSpec as P

HEADS = 40
HD = 128
LAT_CH = 16
FRAMES_SPAN = 3
TROWS = 8
TCOLS = 16


neg_big = -1e30
noise_level = 0.75
norm_eps = 1e-06


def with_halo(cells, sides, width):
    for axis, dim in sides:
        count = lax.axis_size(axis)
        ends = count - 1
        head = lax.slice_in_dim(cells, 0, width, axis=dim)
        tail = lax.slice_in_dim(cells, cells.shape[dim] - width, cells.shape[dim], axis=dim)
        cells = jnp.concatenate(
            [
                lax.ppermute(tail, axis, [(i, (i + 1) % count) for i in range(ends)]),
                cells,
                lax.ppermute(head, axis, [((i + 1) % count, i) for i in range(ends)]),
            ],
            axis=dim,
        )
    return cells


def from_behind(value, axis, by):
    size = lax.axis_size(axis)
    pairs = [(i, i + by) for i in range(size) if 0 <= i + by < size]
    return lax.ppermute(value, axis, pairs)


def block_length(total_rows):
    block_size = total_rows
    while block_size > 768 and block_size % 2 == 0:
        block_size = block_size // 2
    return block_size


def fold_keys(partial_state, key_value, query_block, mask_row, rows_span):
    keys_piece, values_piece = key_value
    heads_dev = query_block.shape[1]
    piece_rows = keys_piece.shape[0]
    length = block_length(piece_rows)
    span_count = mask_row.shape[0]
    score_scale = 1.0 / math.sqrt(HD)
    span_ids = jnp.arange(span_count, dtype=jnp.int32)

    def one_block(carry_state, block_index):
        running_max, running_sum, weighted = carry_state
        offset = block_index * length
        key_block = lax.dynamic_slice_in_dim(keys_piece, offset, length, 0).reshape(
            length, heads_dev, HD
        )
        value_block = lax.dynamic_slice_in_dim(values_piece, offset, length, 0).reshape(
            length, heads_dev, HD
        )
        key_span = (offset + jnp.arange(length, dtype=jnp.int32)) // rows_span
        allowed = (
            jnp.sum(jnp.where(key_span[:, None] == span_ids[None, :], mask_row[None, :], 0), axis=1)
            > 0
        )
        scores = (
            jnp.einsum("qhd,khd->hqk", query_block, key_block, preferred_element_type=jnp.float32)
            * score_scale
        )
        scores = jnp.where(allowed[None, None, :], scores, neg_big)
        new_max = jnp.maximum(running_max, jnp.max(scores, axis=2))
        weights = jnp.where(allowed[None, None, :], jnp.exp(scores - new_max[:, :, None]), 0.0)
        factor = jnp.exp(running_max - new_max)
        running_sum = running_sum * factor + jnp.sum(weights, axis=2)
        weighted = weighted * factor.T[:, :, None] + jnp.einsum(
            "hqk,khd->qhd",
            weights.astype(jnp.bfloat16),
            value_block,
            preferred_element_type=jnp.float32,
        )
        return ((new_max, running_sum, weighted), None)

    result, unused = lax.scan(
        one_block, partial_state, jnp.arange(piece_rows // length, dtype=jnp.int32)
    )
    return result


def gathered_plan(
    queries,
    keys,
    values,
    span_mask,
    head_gain,
    head_shift,
    patch_weight,
    noisy_latent,
    conv_weight,
    conv_bias,
):
    heads_dev = queries.shape[1] // HD
    slab_count = lax.axis_size("slab")
    col_dev = TCOLS // slab_count
    slab_place = lax.axis_index("slab")
    span_place = lax.axis_index("span")
    mask_row = lax.dynamic_slice_in_dim(span_mask, span_place, 1, 0)[0]
    token_grid = queries.reshape(FRAMES_SPAN, TROWS, TCOLS, queries.shape[-1])
    picked = lax.dynamic_slice_in_dim(token_grid, slab_place * col_dev, col_dev, 2)
    own_queries = picked.reshape(FRAMES_SPAN * TROWS * col_dev, queries.shape[-1]).reshape(
        -1, heads_dev, HD
    )
    query_rows = own_queries.shape[0]
    rows_span = keys.shape[0] * slab_count
    running_max, running_sum, weighted = fold_keys(
        (
            jnp.full((heads_dev, query_rows), neg_big, jnp.float32),
            jnp.zeros((heads_dev, query_rows), jnp.float32),
            jnp.zeros((query_rows, heads_dev, HD), jnp.float32),
        ),
        (
            lax.all_gather(keys, ("span", "slab"), axis=0, tiled=True),
            lax.all_gather(values, ("span", "slab"), axis=0, tiled=True),
        ),
        own_queries,
        mask_row,
        rows_span,
    )
    attended = (
        (weighted / running_sum.T[:, :, None])
        .astype(jnp.bfloat16)
        .reshape(query_rows, heads_dev * HD)
    )
    feature_width = HEADS * HD
    values32 = attended.astype(jnp.float32)
    row_total = jnp.sum(values32, axis=1)
    row_squares = jnp.sum(values32 * values32, axis=1)
    row_total, row_squares = lax.psum((row_total, row_squares), "head")
    row_mean = row_total / feature_width
    spread = row_squares / feature_width - row_mean * row_mean
    normed = (
        (values32 - row_mean[:, None]) * lax.rsqrt(spread + norm_eps)[:, None] * head_gain[None, :]
        + head_shift[None, :]
    ).astype(jnp.bfloat16)
    normed_grid = normed.reshape(FRAMES_SPAN, TROWS, col_dev, normed.shape[-1])
    own_rows = TROWS // lax.axis_size("head")
    picked = normed_grid
    product = jnp.dot(
        picked.reshape(-1, picked.shape[-1]), patch_weight, preferred_element_type=jnp.float32
    )
    velocity = lax.psum_scatter(
        product.reshape(
            FRAMES_SPAN, own_rows * lax.axis_size("head"), col_dev * patch_weight.shape[1]
        )
        .transpose(1, 0, 2)
        .reshape(own_rows * lax.axis_size("head"), -1)
        .astype(jnp.bfloat16),
        "head",
        scatter_dimension=0,
        tiled=True,
    ).astype(jnp.float32)
    rows_dev = velocity.shape[0]
    patch_cells = (
        velocity.reshape(rows_dev, FRAMES_SPAN, col_dev, 2, 2, LAT_CH)
        .transpose(1, 0, 3, 2, 4, 5)
        .reshape(FRAMES_SPAN, 2 * rows_dev, 2 * col_dev, LAT_CH)
    )
    clean_latent = noisy_latent - noise_level * patch_cells
    latent_input = clean_latent.astype(jnp.bfloat16)
    framed = with_halo(latent_input, (("head", 1), ("slab", 2)), 1)
    earlier = from_behind(framed[FRAMES_SPAN - 2 :], "span", 1)
    stacked = jnp.concatenate([earlier, framed], axis=0)
    height = clean_latent.shape[1]
    breadth = clean_latent.shape[2]
    columns = jnp.concatenate(
        [
            stacked[
                frame_tap : frame_tap + FRAMES_SPAN,
                row_tap : row_tap + height,
                col_tap : col_tap + breadth,
                :,
            ]
            for frame_tap in range(3)
            for row_tap in range(3)
            for col_tap in range(3)
        ],
        axis=-1,
    )
    decoded = (
        jnp.dot(
            columns.reshape(FRAMES_SPAN * height * breadth, 27 * LAT_CH),
            conv_weight,
            preferred_element_type=jnp.float32,
        )
        + conv_bias[None, :]
    )
    decoded = decoded.astype(jnp.bfloat16).reshape(
        FRAMES_SPAN, height, breadth, conv_weight.shape[1]
    )
    return (clean_latent, decoded)


NEAR_HEADS = 4
MIDDLE_HEADS = 4
FAR_HEADS = 2
MIDDLE = NEAR_HEADS
FAR = NEAR_HEADS + MIDDLE_HEADS
STAT_ROWS = 8
SLOTS = 3
QUERY_ROWS = 192
SWAP = [(0, 1), (1, 0)]
WINDOW = 32
GRANT = 20 << 20

OWN, OTHER, DOWN, UP, MAIN, MAIN_CAP, FINAL, FINAL_CAP, PLACE, SLAB = range(10)


def plan_fits(heads_dev, span_count, slab_count, head_count):
    return (
        span_count == 4
        and slab_count == 2
        and head_count == 2
        and heads_dev == slab_count * (NEAR_HEADS + MIDDLE_HEADS + FAR_HEADS)
    )


def scalar_operand(heads):
    by_place = np.zeros((4, 12), np.int32)
    by_place[:, OTHER] = heads
    by_place[:, DOWN] = [MIDDLE, MIDDLE, 0, MIDDLE]
    by_place[:, UP] = [0, MIDDLE, 0, 0]
    by_place[:, MAIN] = [MIDDLE, 0, MIDDLE, 0]
    by_place[:, MAIN_CAP] = [1, 1, 1, 0]
    by_place[:, FINAL] = [FAR, 0, 0, FAR]
    by_place[:, FINAL_CAP] = [0, 1, 0, 0]
    by_place[:, PLACE] = range(4)
    by_slab = np.zeros(12, np.int32)
    by_slab[[OWN, OTHER, SLAB]] = heads, -heads, 1
    row = lax.dynamic_slice_in_dim(jnp.array(by_place), lax.axis_index("span"), 1, 0)[0]
    return row + lax.axis_index("slab") * jnp.array(by_slab)


def pack_kernel(inputs, messages, copies, scalars, *refs):
    ins, rest = refs[:inputs], refs[inputs:]
    outs, staged = rest[:messages], rest[messages:-2]
    arrive, leave = rest[-2:]
    arriving = []
    for number, (source, row, rows, entries, shift, target, at, heads) in enumerate(copies):
        head = shift
        for entry in entries:
            head = head + scalars[entry]
        column = pl.multiple_of(head * HD, HD)
        place = staged[target].at[pl.ds(at, rows), :]
        copy = pltpu.make_async_copy(
            ins[source].at[pl.ds(row, rows), pl.ds(column, heads * HD)], place, arrive.at[number]
        )
        copy.start()
        onward = pltpu.make_async_copy(
            place, outs[target].at[pl.ds(at, rows), :], leave.at[number]
        )
        arriving.append((copy, onward))
    for copy, onward in arriving:
        copy.wait()
        onward.start()
    for _, onward in arriving:
        onward.wait()


def pack(scalars, arrays, shapes, copies, name):
    moved = sum(2 * 2 * rows * heads * HD for _, _, rows, _, _, _, _, heads in copies)
    out_shape = [pltpu.HBM(shape, jnp.bfloat16) for shape in shapes]
    in_specs = [pl.BlockSpec(memory_space=pl.ANY)] * len(arrays)
    out_specs = [pl.BlockSpec(memory_space=pl.ANY)] * len(shapes)
    return pl.pallas_call(
        functools.partial(pack_kernel, len(arrays), len(shapes), copies),
        name=name,
        out_shape=out_shape,
        grid_spec=pltpu.PrefetchScalarGridSpec(
            num_scalar_prefetch=1,
            grid=(1,),
            in_specs=in_specs,
            out_specs=out_specs,
            scratch_shapes=[pltpu.VMEM(shape, jnp.bfloat16) for shape in shapes]
            + [
                pltpu.SemaphoreType.DMA((len(copies),)),
                pltpu.SemaphoreType.DMA((len(copies),)),
            ],
        ),
        compiler_params=pltpu.CompilerParams(vmem_limit_bytes=GRANT),
        cost_estimate=pl.CostEstimate(flops=0, bytes_accessed=moved, transcendentals=0),
    )(scalars, *arrays)


def hand_kernel(heads, keys, values, out, arrive):
    column = pl.multiple_of((1 - lax.axis_index("slab")) * heads * HD, heads * HD)
    half = keys.shape[0]
    copies = []
    for number, source in enumerate((keys, values)):
        copy = pltpu.make_async_copy(
            source.at[:, pl.ds(column, heads * HD)],
            out.at[pl.ds(number * half, half), :],
            arrive.at[number],
        )
        copy.start()
        copies.append(copy)
    for copy in copies:
        copy.wait()


def pack_handed(keys, values, heads):
    shape = (2 * keys.shape[0], heads * HD)
    return pl.pallas_call(
        functools.partial(hand_kernel, heads),
        name="pack_handed",
        out_shape=jax.ShapeDtypeStruct(shape, keys.dtype),
        in_specs=[pl.BlockSpec(memory_space=pl.ANY)] * 2,
        out_specs=pl.BlockSpec(memory_space=pltpu.VMEM),
        scratch_shapes=[pltpu.SemaphoreType.DMA((2,))],
        compiler_params=pltpu.CompilerParams(vmem_limit_bytes=GRANT),
        cost_estimate=pl.CostEstimate(
            flops=0, bytes_accessed=4 * math.prod(shape), transcendentals=0
        ),
    )(keys, values)


def message(scalars, pieces, arrays, name):
    copies, shapes = [], []
    for target, parts in enumerate(pieces):
        at = 0
        for source, row, rows, entries, shift, heads in parts:
            copies.append((source, row, rows, entries, shift, target, at, heads))
            at += rows
        shapes.append((at, parts[0][5] * HD))
    return pack(scalars, arrays, shapes, copies, name)


class Tokens(typing.NamedTuple):
    query: int | None = None
    pairs: tuple = ()
    extra: int | None = None


OWN_TOKENS = Tokens()


def attend_kernel(variants, extra, span_count, fresh, wide, final, scalars, mask, *refs):
    if final:
        sources, (weight, gain), brought = refs[:4], refs[4:6], refs[6 : 6 + final]
        sums_in, (mine_out, theirs_out) = refs[6 + final : 8 + final], refs[8 + final : 10 + final]
        folded, squares, carried, moved, *own_refs = refs[10 + final : 18 + final]
        query_own, key_own, value_own, received = own_refs
        more, payloads, landed = refs[18 + final : 22 + final], refs[22 + final : -1], refs[-1]
    else:
        query_own, key_own, value_own, received, weight, gain = refs[:6]
        mine_out, theirs_out, folded, squares, carried, moved = refs[-6:]
        payloads, sums_in = refs[6:-6], None
    rows = query_own.shape[0]
    half = rows // 2
    step = pl.program_id(0)
    to_exp2 = math.log2(math.e) / math.sqrt(HD)
    active = functools.reduce(
        lambda a, b: a | b, [scalars[PLACE] == place for place in variants]
    )

    last_step = step == pl.num_programs(0) - 1
    part = carried.shape[1] // 2
    halves = [
        carried.at[:, pl.ds(pl.multiple_of(number * part, part), part)]
        for number in (scalars[SLAB], 1 - scalars[SLAB])
    ]
    fetches = (
        []
        if fresh
        else [
            pltpu.make_async_copy(sums_in[number], halves[number], moved.at[number])
            for number in range(2)
        ]
    )

    @pl.when((step == 0) & active)
    def _():
        folded[...] = jnp.zeros_like(folded)
        squares[...] = jnp.zeros_like(squares)
        for fetch in fetches:
            fetch.start()

    def lanes_of(head):
        return slice(head * HD, (head + 1) * HD)

    def query_of(source, lanes):
        if source is OWN_TOKENS:
            return query_own[:, lanes]
        if source.extra is not None:
            return more[0][:, lanes_of(source.extra)]
        return payloads[source.query][:rows, lanes]

    def pair_of(source, lanes):
        if source is OWN_TOKENS:
            parts = (
                key_own[:, lanes],
                received[:half, lanes],
                value_own[:, lanes],
                received[half:, lanes],
            )
        elif source.extra is not None:
            own = lanes_of(source.extra)
            parts = (more[1][:, own], more[3][:half, own], more[2][:, own], more[3][half:, own])
        else:
            payload = payloads[source.pairs[0]]
            start = payload.shape[0] - 2 * rows
            return payload[start : start + rows, lanes], payload[start + rows :, lanes]
        return jnp.concatenate(parts[:2], axis=0), jnp.concatenate(parts[2:], axis=0)

    def projector(extra_head, lanes):
        if final:
            head = scalars[OWN] + (
                scalars[FINAL] + lanes.start // HD if extra_head is None else extra_head
            )
            lanes = pl.ds(pl.multiple_of(head * HD, HD), HD)
        scaled = weight[:, lanes].astype(jnp.float32) * gain[:, lanes]
        high = scaled.astype(jnp.bfloat16)
        low = (scaled - high.astype(jnp.float32)).astype(jnp.bfloat16)
        return jnp.concatenate([high, low, jnp.ones((16, HD), jnp.bfloat16)], axis=0)

    def one_query(head, source, slot, query_span, key_sources):
        lanes = lanes_of(head)
        query = query_of(source, lanes)
        pairs = [pair_of(key_source, lanes) for key_source, _ in key_sources]
        open_to = [
            None if key_span == query_span else mask[query_span * span_count + key_span] > 0
            for _, key_span in key_sources
        ]
        keys_in = jnp.concatenate([pair[0] for pair in pairs], axis=0)
        ones_block = jnp.ones((rows, HD), jnp.bfloat16)
        values_in = jnp.concatenate(
            [jnp.concatenate([pair[1], ones_block], axis=1) for pair in pairs], axis=0
        )
        pieces = []
        for row in range(0, rows, QUERY_ROWS):
            score = lax.dot_general(
                query[row : row + QUERY_ROWS],
                keys_in,
                (((1,), (1,)), ((), ())),
                preferred_element_type=jnp.float32,
            )
            best = None
            for number, is_open in enumerate(open_to):
                start = number * rows
                block = score[:, start : start + HD]
                for lane in range(HD, rows, HD):
                    block = jnp.maximum(block, score[:, start + lane : start + lane + HD])
                if is_open is not None:
                    block = jnp.where(is_open, block, neg_big)
                best = block if best is None else jnp.maximum(best, block)
            top = jnp.max(best, axis=1, keepdims=True)
            weights = []
            for number, is_open in enumerate(open_to):
                start = number * rows
                shift = top if is_open is None else jnp.where(is_open, top, -neg_big)
                weights.append(
                    jnp.exp2((score[:, start : start + rows] - shift) * to_exp2).astype(jnp.bfloat16)
                )
            both = jnp.dot(
                jnp.concatenate(weights, axis=1), values_in, preferred_element_type=jnp.float32
            )
            pieces.append((both[:, :HD] / both[:, HD:]).astype(jnp.bfloat16))
        attended = jnp.concatenate(pieces, axis=0)
        folded[slot] += lax.dot_general(
            projector(source.extra, lanes),
            attended,
            (((1,), (1,)), ((), ())),
            preferred_element_type=jnp.float32,
        )
        wide = attended.astype(jnp.float32)
        squares[slot] += wide * wide

    def fetch_head(number, head, used):
        copies = []
        place = pl.ds(number * HD, HD)
        for index, (source, target) in enumerate(zip(sources, own_refs if used else more)):
            column = head if index == 3 else scalars[OWN] + head
            column = pl.ds(pl.multiple_of(column * HD, HD), HD)
            copies.append((source.at[:, column], target.at[:, place]))
        copies += [(brought[index].at[:, place], payloads[index].at[:, place]) for index in used]
        started = []
        for index, (source, target) in enumerate(copies):
            slot = number if used else 4 + number
            copy = pltpu.make_async_copy(source, target, landed.at[slot, index])
            copy.start()
            started.append(copy)
        return started

    for place, groups in variants.items():
        if final:
            count, tasks, extra_tasks = groups
            used = set()
            for source, _, _, key_sources in tasks:
                for tokens in [source] + [key_source for key_source, _ in key_sources]:
                    used |= set(tokens.pairs) | ({tokens.query} if tokens.query is not None else set())

            @pl.when(scalars[PLACE] == place)
            def _():
                waits = [
                    fetch_head(head, scalars[FINAL] + head, sorted(used)) for head in range(count)
                ]
                extra_waits = [
                    fetch_head(number, number, ()) for number in range(len(extra_tasks))
                ]
                for head in range(count):
                    for copy in waits[head]:
                        copy.wait()
                    for task in tasks:
                        one_query(head, *task)
                for copies, task in zip(extra_waits, extra_tasks):
                    for copy in copies:
                        copy.wait()
                    one_query(0, *task)

            continue
        for steps, tasks in groups:

            @pl.when((scalars[PLACE] == place) & (step < steps))
            def _():
                for head in range(wide):
                    for task in tasks:
                        one_query(head, *task)

    def store():
        copies = [
            pltpu.make_async_copy(halves[number], out, moved.at[2 + number])
            for number, out in enumerate((mine_out, theirs_out))
        ]
        for copy in copies:
            copy.start()
        for copy in copies:
            copy.wait()

    if fresh:

        @pl.when(last_step & jnp.logical_not(active))
        def _():
            carried[...] = jnp.zeros_like(carried)
            store()

    @pl.when(last_step & active)
    def _():
        ones_rows = jnp.ones((STAT_ROWS, HD), jnp.bfloat16)
        patch = weight.shape[0]
        for fetch in fetches:
            fetch.wait()
        if fresh:
            carried[...] = jnp.zeros_like(carried)

        def finish_slot(slot):
            left = squares[slot]
            total = jnp.zeros((STAT_ROWS, rows), jnp.float32)
            for _ in range(3):
                piece = left.astype(jnp.bfloat16)
                left = left - piece.astype(jnp.float32)
                total = total + lax.dot_general(
                    ones_rows, piece, (((1,), (1,)), ((), ())), preferred_element_type=jnp.float32
                )
            done = folded[slot]
            carried[slot] += jnp.concatenate(
                [
                    done[:patch] + done[patch : 2 * patch],
                    done[2 * patch : 2 * patch + STAT_ROWS],
                    total,
                ],
                axis=0,
            )

        for place, groups in variants.items():

            @pl.when(scalars[PLACE] == place)
            def _():
                tasks = groups[1] if final else [task for _, some in groups for task in some]
                for slot in sorted({task[1] for task in tasks}):
                    finish_slot(slot)

        store()


def attend(steps, wide, first, cap, own, scalars, mask, sums, payloads, variants, name, cost=1):
    queries, keys, values, received, weight, gain = own
    rows = queries.shape[0]
    half = rows // 2
    patch = weight.shape[0]

    def moving(i, scalars):
        return jnp.minimum(i, scalars[cap])

    def column(height, own_column):
        def index(i, scalars, mask):
            head = scalars[first] + scalars[OWN] if own_column else scalars[first]
            return (0, head // wide + moving(i, scalars))

        return pl.BlockSpec((height, wide * HD), index)

    def payload_column(payload):
        last = payload.shape[1] // (wide * HD) - 1

        def index(i, scalars, mask):
            return (0, jnp.minimum(moving(i, scalars), last))

        return pl.BlockSpec((payload.shape[0], wide * HD), index)

    in_specs = [
        column(rows, True),
        column(half, True),
        column(half, True),
        column(rows, False),
        column(patch, True),
        column(1, True),
    ]
    arrays = [queries, keys, values, received, weight, gain]
    in_specs += [payload_column(payload) for payload in payloads]
    arrays += payloads
    fresh = sums is None
    sums_shape = (SLOTS, patch + 2 * STAT_ROWS, rows)
    scratch = [
        pltpu.VMEM((SLOTS, 2 * patch + 16, rows), jnp.float32),
        pltpu.VMEM((SLOTS, rows, HD), jnp.float32),
        pltpu.VMEM(sums_shape, jnp.float32),
        pltpu.SemaphoreType.DMA((4,)),
    ]
    aliases = {}
    if not fresh:
        anywhere = pl.BlockSpec(memory_space=pl.ANY)
        whole = lambda array: pl.BlockSpec(array.shape, lambda i, scalars, mask: (0, 0))
        in_specs = [anywhere] * 4 + [whole(weight), whole(gain)] + [anywhere] * len(payloads)
        scratch += 2 * [
            pltpu.VMEM((height, 4 * HD), jnp.bfloat16) for height in (rows, half, half, rows)
        ]
        scratch += [pltpu.VMEM(payload.shape, payload.dtype) for payload in payloads]
        scratch.append(pltpu.SemaphoreType.DMA((8, 4 + len(payloads))))
        aliases = {2 + len(arrays): 0, 3 + len(arrays): 1}
        in_specs += [anywhere] * 2
        arrays += sums
    flops = 4 * rows * rows * HD * cost * 16
    span_count = math.isqrt(mask.shape[0])
    final = 0 if fresh else len(payloads)
    return pl.pallas_call(
        functools.partial(attend_kernel, variants, 0, span_count, fresh, wide, final),
        name=name,
        out_shape=[pltpu.HBM((SLOTS, sums_shape[1] // 2, rows), jnp.float32)] * 2,
        input_output_aliases=aliases,
        grid_spec=pltpu.PrefetchScalarGridSpec(
            num_scalar_prefetch=2,
            grid=(steps,),
            in_specs=in_specs,
            out_specs=[pl.BlockSpec(memory_space=pl.ANY)] * 2,
            scratch_shapes=scratch,
        ),
        compiler_params=pltpu.CompilerParams(vmem_limit_bytes=GRANT),
        cost_estimate=pl.CostEstimate(
            flops=flops,
            bytes_accessed=4 * HD * 2 * 3 * rows,
            transcendentals=flops // (4 * HD),
        ),
    )(scalars, mask, *arrays)


def token_sums(
    scalars, queries, keys, values, span_mask, head_gain, patch_weight, prepare
):
    rows = queries.shape[0]
    half = rows // 2
    heads = NEAR_HEADS + MIDDLE_HEADS + FAR_HEADS
    in_place = lambda array: pltpu.with_memory_space_constraint(array, pltpu.HBM)
    queries, keys, values = (in_place(array) for array in (queries, keys, values))

    def send(value, *pairs):
        return in_place(lax.ppermute(value, "span", list(pairs)))

    def tokens(entry, shift, count):
        return [(0, 0, rows, (OWN, entry) if entry else (OWN,), shift, count)]

    def pairs_of(entry, shift, count):
        entries = (entry,) if entry else ()
        return [
            piece
            for part in (1, 2)
            for piece in (
                (part, 0, half, (OWN,) + entries, shift, count),
                (3, (part - 1) * half, half, entries, shift, count),
            )
        ]

    handed = pack_handed(keys, values, heads)
    received = lax.ppermute(handed, "slab", SWAP)
    up, down = message(
        scalars,
        [
            pairs_of(UP, 0, NEAR_HEADS),
            tokens(DOWN, 0, MIDDLE_HEADS) + pairs_of(DOWN, 0, MIDDLE_HEADS),
        ],
        (queries, keys, values, received),
        "pack_first",
    )
    source, _ = lax.optimization_barrier((received, down))
    up = send(up, (0, 1), (1, 2))
    down = send(down, (1, 0), (2, 1), (3, 2))
    up_two, two, far_all, far_pair = message(
        scalars,
        [
            pairs_of(None, MIDDLE, MIDDLE_HEADS),
            tokens(None, 0, NEAR_HEADS) + pairs_of(None, 0, NEAR_HEADS),
            tokens(None, FAR, FAR_HEADS) + pairs_of(None, FAR, FAR_HEADS),
            pairs_of(None, FAR, FAR_HEADS),
        ],
        (queries, keys, values, source),
        "pack_second",
    )
    anchor = two
    up_two = send(up_two, (0, 2))
    two = send(two, (3, 1))
    far_next = send(far_all, (2, 3), (1, 0))
    prepared = prepare(anchor)
    far_two = send(far_pair, (1, 3))
    far_three = send(far_pair, (0, 3))

    span_mask, head_gain, patch_weight, _ = lax.optimization_barrier(
        (span_mask, head_gain, patch_weight, anchor)
    )
    mask = span_mask.reshape(-1)
    weight = patch_weight.T
    own = (queries, keys, values, received, weight, head_gain[None, :])
    run = functools.partial(attend, own=own, scalars=scalars, mask=mask)

    here, back_one, on_one = OWN_TOKENS, Tokens(None, (0,)), Tokens(1, (1,))
    back_two = Tokens(None, (2,))
    sums = run(
        MIDDLE_HEADS // 2,
        2,
        MAIN,
        MAIN_CAP,
        sums=None,
        payloads=[up, down, up_two],
        variants={
            0: [(2, [(here, 0, 0, [(here, 0)]), (on_one, 1, 1, [(here, 0), (on_one, 1)])])],
            1: [
                (
                    2,
                    [
                        (on_one, 1, 2, [(back_one, 0), (here, 1), (on_one, 2)]),
                        (here, 0, 1, [(back_one, 0), (here, 1)]),
                    ],
                )
            ],
            2: [
                (
                    2,
                    [
                        (on_one, 1, 3, [(back_two, 0), (back_one, 1), (here, 2), (on_one, 3)]),
                        (here, 0, 2, [(back_two, 0), (back_one, 1), (here, 2)]),
                    ],
                )
            ],
        },
        name="main_heads",
    )
    on_two, beside = Tokens(2, (2,)), Tokens(3, (3,))
    two_back, three_back = Tokens(None, (4,)), Tokens(None, (5,))
    extras = [Tokens(None, (), lane) for lane in range(NEAR_HEADS)]
    sums, prepared = lax.optimization_barrier((sums, prepared))
    sums = run(
        1,
        1,
        FINAL,
        FINAL_CAP,
        sums=sums,
        payloads=[up, down, two, far_next, far_two, far_three],
        variants={
            0: (
                FAR_HEADS,
                [(here, 0, 0, [(here, 0)]), (beside, 1, 1, [(here, 0), (beside, 1)])],
                [(head, 0, 0, [(head, 0)]) for head in extras],
            ),
            1: (
                NEAR_HEADS,
                [(on_two, 2, 3, [(back_one, 0), (here, 1), (on_one, 2), (on_two, 3)])],
                [],
            ),
            3: (
                FAR_HEADS,
                [
                    (here, 0, 3, [(three_back, 0), (two_back, 1), (beside, 2), (here, 3)]),
                    (beside, 2, 2, [(three_back, 0), (two_back, 1), (beside, 2)]),
                ],
                [],
            ),
        },
        name="final_heads",
        cost=4,
    )
    return sums, prepared


def noise_window(grid, constants):
    height, breadth, _ = grid.shape
    slab = lax.axis_index("slab")
    edge = jnp.where(slab == 0, grid[:, breadth - 1], grid[:, 0])
    edge = lax.ppermute(edge, "slab", SWAP)[:, None]
    grid = jnp.concatenate(
        [
            jnp.where(slab == 1, edge, 0.0),
            grid,
            jnp.where(slab == 0, edge, 0.0),
            jnp.zeros((height, WINDOW - breadth - 2, grid.shape[2]), grid.dtype),
        ],
        axis=1,
    )
    head = lax.axis_index("head")
    edge = jnp.where(head == 0, grid[height - 1], grid[0])
    count = constants.shape[1]
    extra = jnp.pad(constants, ((0, 8 - constants.shape[0]), (0, HD - count)))
    edge = jnp.pad(edge, ((0, 0), (0, HD - edge.shape[1])))
    sent = lax.ppermute(jnp.concatenate([edge, extra], axis=0), "head", SWAP)
    edge = sent[None, :WINDOW, : grid.shape[2]]
    constants = constants + sent[WINDOW : WINDOW + constants.shape[0], :count]
    grid = jnp.concatenate(
        [jnp.where(head == 1, edge, 0.0), grid, jnp.where(head == 0, edge, 0.0)], axis=0
    )
    return grid.reshape((height + 2) * WINDOW, grid.shape[2]), constants.T


def cell_selector(height, breadth):
    cell = lax.broadcasted_iota(jnp.int32, ((height + 2) * WINDOW, 4 * TROWS * TCOLS), 0)
    column = lax.broadcasted_iota(jnp.int32, cell.shape, 1)
    y = lax.axis_index("head") * height + cell // WINDOW - 1
    x = lax.axis_index("slab") * breadth + cell % WINDOW - 1
    inside = (y >= 0) & (y < 2 * TROWS) & (x >= 0) & (x < 2 * TCOLS)
    inside = inside & (cell % WINDOW < breadth + 2)
    target = ((y % 2) * 2 + x % 2) * (TROWS * TCOLS) + (y // 2) * TCOLS + x // 2
    return (inside & (column == target)).astype(jnp.bfloat16)


def band_kernel(weight, band):
    outputs = weight.shape[1]
    band[...] = jnp.zeros_like(band)
    for row_tap in range(3):
        for col_tap in range(3):
            for frame_tap in range(3):
                start = ((3 * frame_tap + row_tap) * 3 + col_tap) * LAT_CH
                block = weight[start : start + LAT_CH]
                for frame in range(FRAMES_SPAN):
                    at = (col_tap * (FRAMES_SPAN + 2) + frame + frame_tap) * LAT_CH
                    band[
                        row_tap, at : at + LAT_CH, frame * outputs : (frame + 1) * outputs
                    ] = block


def banded_weight(conv_weight):
    shape = (3, 3 * (FRAMES_SPAN + 2) * LAT_CH, FRAMES_SPAN * conv_weight.shape[1])
    return pl.pallas_call(
        band_kernel,
        name="band",
        out_shape=jax.ShapeDtypeStruct(shape, conv_weight.dtype),
        in_specs=[pl.BlockSpec(memory_space=pltpu.VMEM)],
        out_specs=pl.BlockSpec(memory_space=pltpu.VMEM),
        compiler_params=pltpu.CompilerParams(vmem_limit_bytes=GRANT),
        cost_estimate=pl.CostEstimate(
            flops=0, bytes_accessed=2 * math.prod(shape), transcendentals=0
        ),
    )(conv_weight)


def finish_kernel(
    scalars, mine, other, noise, before, selector, band, bias, constants, clean, decoded, cells
):
    frames, height, breadth, channels = clean.shape
    patch = constants.shape[0]
    first = scalars[SLAB] == 0
    sums = jnp.concatenate(
        [jnp.where(first, mine[...], other[...]), jnp.where(first, other[...], mine[...])], axis=0
    )
    feature_width = HEADS * HD
    row_mean = sums[patch : patch + 1] / feature_width
    spread = sums[patch + STAT_ROWS : patch + STAT_ROWS + 1] / feature_width - row_mean * row_mean
    velocity = (
        lax.rsqrt(spread + norm_eps) * (sums[:patch] - constants[:, 0:1] * row_mean)
        + constants[:, 1:2]
    )
    tokens = TROWS * TCOLS
    lane = lax.broadcasted_iota(jnp.int32, velocity.shape, 1)
    velocity = jnp.where((lane >= 2 * tokens) | (scalars[PLACE] > 0), velocity, 0.0)
    columns = jnp.concatenate(
        [
            jnp.concatenate(
                [
                    velocity[
                        part * channels : (part + 1) * channels,
                        frame * tokens : (frame + 1) * tokens,
                    ]
                    for part in range(4)
                ],
                axis=1,
            )
            for frame in range(frames + 2)
        ],
        axis=0,
    )
    high = columns.astype(jnp.bfloat16)
    low = (columns - high.astype(jnp.float32)).astype(jnp.bfloat16)
    chosen = sum(
        lax.dot_general(
            selector[...], part, (((1,), (1,)), ((), ())), preferred_element_type=jnp.float32
        )
        for part in (high, low)
    )
    count = (height + 2) * WINDOW
    cells[:count] = (
        jnp.concatenate([before[...], noise[...]], axis=1) - noise_level * chosen
    )
    cells[count:] = jnp.zeros_like(cells[count:])
    for frame in range(frames):
        lanes = slice((frame + 2) * channels, (frame + 3) * channels)
        for y in range(height):
            start = (y + 1) * WINDOW + 1
            clean[frame, y] = cells[start : start + breadth, lanes]
    shifted = jnp.concatenate(
        [cells[tap : tap + count] for tap in range(3)], axis=1
    ).astype(jnp.bfloat16)
    total = jnp.broadcast_to(bias[...], (height * breadth, bias.shape[1]))
    for tap in range(3):
        block = jnp.concatenate(
            [
                shifted[(y + tap) * WINDOW : (y + tap) * WINDOW + breadth]
                for y in range(height)
            ],
            axis=0,
        )
        total = total + jnp.dot(block, band[tap], preferred_element_type=jnp.float32)
    outputs = decoded.shape[3]
    total = total.astype(decoded.dtype)
    for frame in range(frames):
        decoded[frame] = total[:, frame * outputs : (frame + 1) * outputs].reshape(
            height, breadth, outputs
        )


def finish(
    scalars, mine, other, noise, before, selector, band, bias, constants, shape, outputs
):
    whole = pl.BlockSpec(memory_space=pltpu.VMEM)
    frames, height, breadth, channels = shape
    rows = (height + 2) * WINDOW
    return pl.pallas_call(
        finish_kernel,
        name="finish",
        out_shape=(
            jax.ShapeDtypeStruct(shape, jnp.float32),
            jax.ShapeDtypeStruct((frames, height, breadth, outputs), jnp.bfloat16),
        ),
        in_specs=[pl.BlockSpec(memory_space=pltpu.SMEM)] + [whole] * 8,
        out_specs=(whole, whole),
        scratch_shapes=[pltpu.VMEM((rows + 8, (frames + 2) * channels), jnp.float32)],
        compiler_params=pltpu.CompilerParams(vmem_limit_bytes=GRANT),
    )(scalars, mine, other, noise, before, selector, band, bias, constants)


def per_device(
    queries,
    keys,
    values,
    span_mask,
    head_gain,
    head_shift,
    patch_weight,
    noisy_latent,
    conv_weight,
    conv_bias,
):
    heads_dev = queries.shape[1] // HD
    if not plan_fits(
        heads_dev, lax.axis_size("span"), lax.axis_size("slab"), lax.axis_size("head")
    ):
        return gathered_plan(
            queries,
            keys,
            values,
            span_mask,
            head_gain,
            head_shift,
            patch_weight,
            noisy_latent,
            conv_weight,
            conv_bias,
        )
    place = lax.axis_index("span")
    slab = lax.axis_index("slab")
    scalars = scalar_operand(heads_dev // lax.axis_size("slab"))
    def prepare(anchor):
        noise, weight, gain, shift, taps, bias, _ = lax.optimization_barrier(
            (noisy_latent, patch_weight, head_gain, head_shift, conv_weight, conv_bias, anchor)
        )
        _, height, breadth, _ = noise.shape
        noise = noise.transpose(1, 2, 0, 3).reshape(height, breadth, -1)
        wide_weight = weight.T.astype(jnp.float32)
        constants = jnp.stack(
            [
                jnp.sum(wide_weight * gain[None, :], axis=1),
                jnp.sum(wide_weight * shift[None, :], axis=1),
            ]
        )
        window, constants = noise_window(noise, constants)
        return (
            window,
            window[:, -2 * LAT_CH :].reshape(16, -1),
            constants,
            cell_selector(height, breadth),
            banded_weight(taps),
            jnp.tile(bias, FRAMES_SPAN)[None, :],
        )

    (mine, theirs), (noise, ahead, constants, selector, band, bias) = token_sums(
        scalars,
        queries,
        keys,
        values,
        span_mask,
        head_gain,
        patch_weight,
        prepare,
    )
    mine = mine + lax.ppermute(theirs, "slab", SWAP)
    own, after, third = mine[0], mine[1], mine[2]
    skip = TROWS * TCOLS
    ahead = jnp.concatenate([jnp.concatenate([own[:, skip:], after], axis=1), ahead], axis=0)
    from_one = lax.ppermute(ahead, "span", [(0, 1), (1, 2), (2, 3)])
    sent_current, sent_before, _ = lax.optimization_barrier((third, after[:, skip:], ahead))
    before = from_one[own.shape[0] :].reshape(-1, 2 * LAT_CH)
    from_one = from_one[: own.shape[0]]
    to_current = lax.ppermute(sent_current, "span", [(1, 3), (3, 2)])
    to_before = lax.ppermute(sent_before, "span", [(0, 2), (1, 3)])
    kept = jnp.concatenate([jnp.where(place == 3, third[:, skip:], 0.0), own], axis=1)
    total = kept + from_one + jnp.concatenate([to_before, to_current], axis=1)
    total = total + lax.ppermute(total, "head", SWAP)
    other = lax.ppermute(total, "slab", SWAP)
    return finish(
        scalars,
        total,
        other,
        noise,
        before,
        selector,
        band,
        bias,
        constants,
        noisy_latent.shape,
        conv_weight.shape[1],
    )


def solution(mesh):
    placed = (
        P(("groups", "span"), "head"),
        P(("groups", "span", "slab"), "head"),
        P(("groups", "span", "slab"), "head"),
        P("groups", None),
        P("head"),
        P("head"),
        P("head", None),
        P(("groups", "span"), "head", "slab", None),
        P(),
        P(),
    )
    return jax.shard_map(
        per_device,
        mesh=mesh,
        in_specs=placed,
        out_specs=(
            P(("groups", "span"), "head", "slab", None),
            P(("groups", "span"), "head", "slab", None),
        ),
        check_vma=False,
    )
```
